32 devices in a mesh: scene: 2 (over x), seq: 16 (over z, y, core).
Axes of the slice: x: 2, y: 2, z: 4, core: 2. Of those that a mesh axis runs over, the one named last changes fastest.
Arguments:
- tokens: bfloat16 [2, 4096, 1024], P('scene', 'seq'), may hold values from -6 to 6
- surface_mask: int32 [2, 4096], P('scene', 'seq'), may hold values 0 or 1
- out_grad: bfloat16 [2, 4096, 1024], P('scene', 'seq'), may hold values from -6 to 6
- w_query: bfloat16 [1024, 1024], replicated, may hold values from -0.1875 to 0.1875
- w_key: bfloat16 [1024, 1024], replicated, may hold values from -0.1875 to 0.1875
- w_value: bfloat16 [1024, 1024], replicated, may hold values from -0.1875 to 0.1875
- w_out: bfloat16 [1024, 1024], replicated, may hold values from -6 to 6
- w_up: bfloat16 [1024, 4096], replicated, may hold values from -0.1875 to 0.1875
- w_down: bfloat16 [4096, 1024], replicated, may hold values from -0.09375 to 0.09375
- b_query: float32 [1024], replicated, may hold values from -3 to 3
- b_value: float32 [1024], replicated, may hold values from -3 to 3
- b_out: float32 [1024], replicated, may hold values from -3 to 3
- b_up: float32 [4096], replicated, may hold values from -3 to 3
- b_down: float32 [1024], replicated, may hold values from -3 to 3
- gain_one: float32 [1024], replicated, may hold values from 0.1 to 1.9
- shift_one: float32 [1024], replicated, may hold values from -3 to 3
- gain_two: float32 [1024], replicated, may hold values from 0.1 to 1.9
- shift_two: float32 [1024], replicated, may hold values from -3 to 3
Outputs:
- block_out: bfloat16 [2, 4096, 1024], P('scene', 'seq')
- tokens_grad: bfloat16 [2, 4096, 1024], P('scene', 'seq')
- query_grad: float32 [1024, 1024], P(('scene', 'seq'))
- key_grad: float32 [1024, 1024], P(('scene', 'seq'))
- value_grad: float32 [1024, 1024], P(('scene', 'seq'))
- out_proj_grad: float32 [1024, 1024], P(('scene', 'seq'))
- up_grad: float32 [1024, 4096], P(('scene', 'seq'))
- down_grad: float32 [4096, 1024], P(('scene', 'seq'))
- query_bias_grad: float32 [1024], P(('scene', 'seq'))
- value_bias_grad: float32 [1024], P(('scene', 'seq'))
- out_bias_grad: float32 [1024], P(('scene', 'seq'))
- up_bias_grad: float32 [4096], P(('scene', 'seq'))
- down_bias_grad: float32 [1024], P(('scene', 'seq'))
- gain_one_grad: float32 [1024], P(('scene', 'seq'))
- shift_one_grad: float32 [1024], P(('scene', 'seq'))
- gain_two_grad: float32 [1024], P(('scene', 'seq'))
- shift_two_grad: float32 [1024], P(('scene', 'seq'))
The draws below stay inside these ranges and needn't reach their ends.
All inputs are finite; a program needn't handle non-finite values. No bound on the sum of `surface_mask` on one device may be relied on, other than what follows from the above.
Results may differ from the reference program's by a relative error of at most 0.014.
Values may be sent and summed in bfloat16 or wider, within the bound.
A program may use at most 320 MiB of HBM per device.

```python
import jax
import jax.numpy as jnp
from jax import lax

HEADS = 16
HEAD_DIM = 64
FF = 4096
D = 1024
SCENES = 2
LEN = 4096


def plant(values, key, smallest, top_value):
    longest = values.shape.index(max(values.shape))
    spots = []
    for shift in (0, 1):
        where = [jax.random.randint(jax.random.fold_in(key, axis), (), 0, length) for axis, length in enumerate(values.shape)]
        where[longest] = (where[longest] + shift) % values.shape[longest]
        spots.append(tuple(where))
    return values.at[spots[0]].set(smallest).at[spots[1]].set(top_value)


def strengthened(values, key, source, target, parts, factor):
    def block_of(axis_at):
        return (jnp.arange(values.shape[axis_at]) // (values.shape[axis_at] // parts)).reshape((-1,) + (1,) * (values.ndim - 1 - axis_at))

    one_side = jax.random.permutation(key, parts)[block_of(target)]
    other_side = (block_of(target) + parts // 2) % parts
    return jnp.where((block_of(source) == one_side) | (block_of(source) == other_side), factor * values, values)


def steps_of(key, shape, shards, least, high):
    def one(axis_at, parts):
        heights = jax.random.uniform(jax.random.fold_in(jax.random.fold_in(key, 6), axis_at), (parts,), jnp.float32, least / len(shards), high / len(shards))
        return jnp.repeat(jnp.exp(heights), shape[axis_at] // parts).reshape((-1,) + (1,) * (len(shape) - axis_at - 1))

    factor_of = one(*shards[0])
    for cut in shards[1:]:
        factor_of = factor_of * one(*cut)
    return factor_of


def gaussian(own_key, dims, scale, reach, shards=(), kind=jnp.bfloat16):
    level = steps_of(own_key, dims, shards, -0.22, 0.18) if shards else 1.0
    drawn = jax.random.normal(own_key, dims, jnp.float32) * scale * level
    return jnp.minimum(jnp.maximum(drawn, -reach), reach).astype(kind)


def heavy_noise(stream_key, dims, scale, most, shards, heavy, held_as=jnp.bfloat16):
    entries = scale * jax.random.normal(stream_key, dims, jnp.float32)
    if shards:
        entries = entries * steps_of(stream_key, dims, shards, -0.22, 0.18)
    return jnp.clip(strengthened(entries, jax.random.fold_in(stream_key, 3), *heavy), -most, most).astype(held_as)


def setup_inputs(seed: int = 0) -> dict:
    arg_keys = jax.random.split(jax.random.key(seed), 19)
    tokens = heavy_noise(arg_keys[0], (SCENES, LEN, D), 1.0, 6.0, ((0, 2), (1, 16)), (1, 2, 16, 2.0))
    surface_mask = plant((jax.random.randint(arg_keys[1], (SCENES, LEN), 0, 4) < 3).astype(jnp.int32), jax.random.fold_in(arg_keys[1], 1), 0, 1)
    out_grad = gaussian(arg_keys[2], (SCENES, LEN, D), 1.0, 6.0, ((0, 2), (1, 16)))
    w_query = gaussian(arg_keys[3], (D, D), D ** -0.5, 0.1875)
    w_key = gaussian(arg_keys[4], (D, D), D ** -0.5, 0.1875)
    w_value = gaussian(arg_keys[5], (D, D), D ** -0.5, 0.1875)
    w_out = gaussian(arg_keys[6], (D, D), (max(1, 2 * D // LEN)) ** -0.5, 6.0)
    w_up = gaussian(arg_keys[7], (D, FF), D ** -0.5, 0.1875)
    w_down = gaussian(arg_keys[8], (FF, D), FF ** -0.5, 0.09375)
    b_query = gaussian(arg_keys[9], (D,), 0.5, 3.0, (), jnp.float32)
    b_value = gaussian(arg_keys[10], (D,), 0.5, 3.0, (), jnp.float32)
    b_out = gaussian(arg_keys[11], (D,), 0.5, 3.0, (), jnp.float32)
    b_up = gaussian(arg_keys[12], (FF,), 0.5, 3.0, (), jnp.float32)
    b_down = gaussian(arg_keys[13], (D,), 0.5, 3.0, (), jnp.float32)
    gain_one = jnp.clip(1.0 + 0.18 * jax.random.normal(arg_keys[14], (D,), jnp.float32), 0.1, 1.9)
    shift_one = gaussian(arg_keys[15], (D,), 0.5, 3.0, (), jnp.float32)
    gain_two = jnp.clip(1.0 + 0.18 * jax.random.normal(arg_keys[16], (D,), jnp.float32), 0.1, 1.9)
    shift_two = gaussian(arg_keys[17], (D,), 0.5, 3.0, (), jnp.float32)
    return dict(tokens=tokens, surface_mask=surface_mask, out_grad=out_grad, w_query=w_query, w_key=w_key, w_value=w_value, w_out=w_out, w_up=w_up, w_down=w_down, b_query=b_query, b_value=b_value, b_out=b_out, b_up=b_up, b_down=b_down, gain_one=gain_one, shift_one=shift_one, gain_two=gain_two, shift_two=shift_two)


@jax.custom_vjp
def low(v):
    return lax.optimization_barrier(v.astype(jnp.bfloat16)).astype(jnp.float32)

@jax.custom_vjp
def low_back(v):
    return v

def low_keep(v):
    return (low(v), None)

def low_pass(kept, grad):
    return (grad,)

def back_keep(v):
    return (v, None)

def back_low(kept, grad):
    return (low(grad),)
low.defvjp(low_keep, low_pass)
low_back.defvjp(back_keep, back_low)
highest = lax.Precision.HIGHEST
norm_eps = 1e-05
score_scale = 0.125
gelu_coef = 0.7978845608028654

def matmul(left, right):
    return jnp.dot(left, right, precision=highest, preferred_element_type=jnp.float32)

def norm_rows(values, gain, shift):
    row_mean = lax.optimization_barrier(jnp.mean(values, axis=-1, keepdims=True))
    centred = values - row_mean
    row_var = lax.optimization_barrier(jnp.mean(centred * centred, axis=-1, keepdims=True))
    return centred * lax.rsqrt(row_var + norm_eps) * gain + shift

def gelu_tanh(values):
    return 0.5 * values * (1.0 + jnp.tanh(gelu_coef * (values + 0.044715 * values * values * values)))

def attend_head(inputs):
    q_head, k_head, v_head = inputs
    scores = low_back(jnp.einsum('qe,ke->qk', q_head, k_head, precision=highest) * score_scale)
    row_max = lax.optimization_barrier(jnp.max(scores, axis=-1, keepdims=True))
    shifted = jnp.exp(scores - row_max)
    attn_prob = shifted / lax.optimization_barrier(jnp.sum(shifted, axis=-1, keepdims=True))
    return jnp.einsum('qk,ke->qe', low(attn_prob), v_head, precision=highest)

def scene_layer(tokens, params):
    w_query, w_key, w_value, w_out, w_up, w_down, b_query, b_value, b_out, b_up, b_down, gain_one, shift_one, gain_two, shift_two = params
    length = tokens.shape[0]
    normed = low(norm_rows(tokens, gain_one, shift_one))
    queries = low(low_back(matmul(normed, w_query) + b_query))
    keys_all = low(low_back(matmul(normed, w_key)))
    values = low(low_back(matmul(normed, w_value) + b_value))

    def by_head(array_in):
        return array_in.reshape(length, HEADS, HEAD_DIM).transpose(1, 0, 2)
    head_outs = lax.map(jax.checkpoint(attend_head), (by_head(queries), by_head(keys_all), by_head(values)))
    attended = low(low_back(head_outs.transpose(1, 0, 2).reshape(length, D)))
    residual = tokens + low_back(matmul(attended, w_out) + b_out)
    normed_two = low(norm_rows(residual, gain_two, shift_two))
    hidden = low_back(matmul(normed_two, w_up) + b_up)
    activated = low(gelu_tanh(hidden))
    return residual + low_back(matmul(activated, w_down) + b_down)

def reference(tokens, surface_mask, out_grad, w_query, w_key, w_value, w_out, w_up, w_down, b_query, b_value, b_out, b_up, b_down, gain_one, shift_one, gain_two, shift_two):
    params = jax.tree.map(lambda member: member.astype(jnp.float32), (w_query, w_key, w_value, w_out, w_up, w_down, b_query, b_value, b_out, b_up, b_down, gain_one, shift_one, gain_two, shift_two))
    tokens_f = tokens.astype(jnp.float32)
    cotangent = out_grad.astype(jnp.float32) * surface_mask.astype(jnp.float32)[..., None]
    zeros = jax.tree.map(jnp.zeros_like, params)

    def scene_step(totals, inputs):
        scene_tokens, scene_cot = inputs
        result, pullback = jax.vjp(scene_layer, scene_tokens, params)
        scene_grad, param_grads = pullback(scene_cot)
        totals = jax.tree.map(jnp.add, totals, param_grads)
        return (totals, (result.astype(jnp.bfloat16), scene_grad.astype(jnp.bfloat16)))
    totals, (block_out, tokens_grad) = lax.scan(scene_step, zeros, (tokens_f, cotangent))
    return (block_out, tokens_grad, totals[0], totals[1], totals[2], totals[3], totals[4], totals[5], totals[6], totals[7], totals[8], totals[9], totals[10], totals[11], totals[12], totals[13], totals[14])
```

```python
import functools

import jax
import jax.numpy as jnp
from jax import lax
from jax.experimental import pallas as pl
from jax.experimental.pallas import tpu as pltpu
from jax.sharding import PartitionSpec as P

HEADS = 16
HEAD_DIM = 64
MESH = pl.DeviceIdType.MESH
f32 = jnp.float32
bf16 = jnp.bfloat16

norm_eps = 1e-05
score_scale = 0.125
gelu_coef = 0.7978845608028654


def matmul(left, right):
    return jnp.dot(left, right, preferred_element_type=jnp.float32)


def contract(left, right, left_dim, right_dim):
    return lax.dot_general(
        left, right, (((left_dim,), (right_dim,)), ((), ())), preferred_element_type=jnp.float32
    )


def matmul_tn(left, right):
    return contract(left, right, 0, 0)


def matmul_nt(left, right):
    return contract(left, right, 1, 1)


def greet(partners):
    barrier = pltpu.get_barrier_semaphore()
    for partner in partners:
        pl.semaphore_signal(barrier, inc=1, device_id=partner, device_id_type=MESH)
    pl.semaphore_wait(barrier, len(partners))


def remote(src, dst, send_sem, recv_sem, device):
    return pltpu.make_async_remote_copy(
        src_ref=src,
        dst_ref=dst,
        send_sem=send_sem,
        recv_sem=recv_sem,
        device_id=device,
        device_id_type=MESH,
    )


def forward_kernel(
    n,
    tok,
    qt_ref,
    kt_ref,
    vt_ref,
    att_ref,
    q_out,
    k_out,
    v_out,
    o_out,
    lse_out,
    q_all,
    k_all,
    v_all,
    k_nat,
    o_all,
    lse_all,
    att_send,
    in_send,
    in_recv,
    in_local,
    out_send,
    out_recv,
    out_local,
    save_sem,
):
    me = lax.axis_index("seq")
    scene = lax.axis_index("scene")
    chip, core = me // 2, lax.rem(me, 2)
    chips = n // 2
    length = n * tok
    others = [lax.rem(me + j, n) for j in range(1, n)]
    greet([(scene, other) for other in others])

    def rows(head):
        return pl.ds(pl.multiple_of(head * HEAD_DIM, HEAD_DIM), HEAD_DIM)

    def lanes(block, width=tok):
        return pl.ds(pl.multiple_of(block * width, width), width)

    pairs = ((kt_ref, k_all), (vt_ref, v_all), (qt_ref, q_all))
    copies = {}
    for a, (src, dst) in enumerate(pairs):
        for j in range(1, n):
            head = lax.rem(me + j, n)
            copies[a, j] = remote(
                src.at[rows(head), :],
                dst.at[:, lanes(me)],
                in_send.at[a, j],
                in_recv.at[a, j],
                (scene, head),
            )
            copies[a, j].start()
    local = [
        pltpu.make_async_copy(src.at[rows(me), :], dst.at[:, lanes(me)], in_local.at[a])
        for a, (src, dst) in enumerate(pairs)
    ]
    for copy in local:
        copy.start()
    for copy in local:
        copy.wait()
    for a in range(3):
        for j in range(1, n):
            copies[a, j].wait_recv()
    k_nat[...] = k_all[...].T
    saves = [
        pltpu.make_async_copy(src, dst, save_sem.at[a])
        for a, (src, dst) in enumerate(((q_all, q_out), (k_all, k_out), (v_all, v_out)))
    ]
    for copy in saves:
        copy.start()

    wide = 2 * tok
    key_block = length // 2

    def queries(step):
        target = lax.rem(chip + step, chips)
        span = lanes(target, wide)
        q_here = q_all[:, span]
        top = total = acc = None
        for block in range(length // key_block):
            keys = slice(block * key_block, (block + 1) * key_block)
            scores = contract(k_nat[keys, :], q_here, 1, 0)
            here = jnp.max(scores, axis=0, keepdims=True)
            new_top = here if top is None else jnp.maximum(top, here)
            shifted = jnp.exp(scores - new_top)
            part_sum = jnp.sum(shifted, axis=0, keepdims=True)
            part = contract(v_all[:, keys], shifted.astype(bf16), 1, 0)
            if top is None:
                total, acc = part_sum, part
            else:
                fade = jnp.exp(top - new_top)
                total, acc = total * fade + part_sum, acc * fade + part
            top = new_top
        out = acc / total
        o_all[:, span] = out
        lse_all[:, span] = jnp.broadcast_to(top + jnp.log(total), (8, wide))
        low = out.astype(bf16)
        att_send[step, 0] = low[:, :tok]
        att_send[step, 1] = low[:, tok:]
        return target

    def out_copy(step, target, flip):
        device = 2 * target + lax.rem(core + flip, 2)
        return remote(
            att_send.at[step, lax.rem(core + flip, 2)],
            att_ref.at[rows(me), :],
            out_send.at[step, flip],
            out_recv.at[step, flip],
            (scene, device),
        )

    queries(0)
    mine = pltpu.make_async_copy(att_send.at[0, core], att_ref.at[rows(me), :], out_local)
    mine.start()
    out_copy(0, chip, 1).start()

    def step_body(step, carry):
        target = queries(step)
        out_copy(step, target, 0).start()
        out_copy(step, target, 1).start()
        return carry

    lax.fori_loop(1, chips, step_body, 0)
    o_save = pltpu.make_async_copy(o_all, o_out, save_sem.at[3])
    l_save = pltpu.make_async_copy(lse_all, lse_out, save_sem.at[4])
    o_save.start()
    l_save.start()
    for a in range(3):
        for j in range(1, n):
            copies[a, j].wait_send()
    mine.wait()
    out_copy(0, chip, 1).wait()

    def drain(step, carry):
        target = lax.rem(chip + step, chips)
        out_copy(step, target, 0).wait()
        out_copy(step, target, 1).wait()
        return carry

    lax.fori_loop(1, chips, drain, 0)
    for copy in saves + [o_save, l_save]:
        copy.wait()


def attention_forward(n, q_t, k_t, v_t):
    tok = q_t.shape[1]
    length = n * tok
    any_spec = pl.BlockSpec(memory_space=pl.ANY)
    head_all = jax.ShapeDtypeStruct((HEAD_DIM, length), bf16)
    dma = pltpu.SemaphoreType.DMA
    return pl.pallas_call(
        functools.partial(forward_kernel, n, tok),
        out_shape=(
            jax.ShapeDtypeStruct(q_t.shape, bf16),
            head_all,
            head_all,
            head_all,
            jax.ShapeDtypeStruct((HEAD_DIM, length), f32),
            jax.ShapeDtypeStruct((8, length), f32),
        ),
        in_specs=[any_spec] * 3,
        out_specs=[any_spec] * 6,
        scratch_shapes=[
            pltpu.VMEM((HEAD_DIM, length), bf16),
            pltpu.VMEM((HEAD_DIM, length), bf16),
            pltpu.VMEM((HEAD_DIM, length), bf16),
            pltpu.VMEM((length, HEAD_DIM), bf16),
            pltpu.VMEM((HEAD_DIM, length), f32),
            pltpu.VMEM((8, length), f32),
            pltpu.VMEM((n // 2, 2, HEAD_DIM, tok), bf16),
            dma((3, n)),
            dma((3, n)),
            dma((3,)),
            dma((n // 2, 2)),
            dma((n // 2, 2)),
            dma,
            dma((5,)),
        ],
        compiler_params=pltpu.CompilerParams(
            collective_id=0, has_side_effects=True, vmem_limit_bytes=48 << 20
        ),
        name="attention_forward",
    )(q_t, k_t, v_t)


def backward_kernel(
    n,
    tok,
    dt_ref,
    q_all,
    k_all,
    v_all,
    o_all,
    lse_all,
    dq_ref,
    dk_ref,
    dv_ref,
    heads_ref,
    d_all,
    q_nat,
    k_nat,
    v_nat,
    d_nat,
    delta,
    dq_acc,
    low,
    in_send,
    in_recv,
    in_local,
    kv_send,
    kv_recv,
    kv_local,
    q_send,
    q_recv,
    q_local,
    save_sem,
):
    me = lax.axis_index("seq")
    scene = lax.axis_index("scene")
    chip, core = me // 2, lax.rem(me, 2)
    chips = n // 2
    length = n * tok
    wide = 2 * tok
    greet([(scene, lax.rem(me + j, n)) for j in range(1, n)])

    def rows(head):
        return pl.ds(pl.multiple_of(head * HEAD_DIM, HEAD_DIM), HEAD_DIM)

    def lanes(block, width=tok):
        return pl.ds(pl.multiple_of(block * width, width), width)

    copies = []
    for j in range(1, n):
        head = lax.rem(me + j, n)
        copies.append(
            remote(
                dt_ref.at[rows(head), :],
                d_all.at[:, lanes(me)],
                in_send.at[j],
                in_recv.at[j],
                (scene, head),
            )
        )
        copies[-1].start()
    local = pltpu.make_async_copy(dt_ref.at[rows(me), :], d_all.at[:, lanes(me)], in_local)
    local.start()
    q_nat[...] = q_all[...].T
    k_nat[...] = k_all[...].T
    v_nat[...] = v_all[...].T
    dq_acc[...] = jnp.zeros_like(dq_acc)
    local.wait()
    for copy in copies:
        copy.wait_recv()
    d_nat[...] = d_all[...].T
    delta[...] = jnp.broadcast_to(
        jnp.sum(d_all[...].astype(f32) * o_all[...], axis=0, keepdims=True), delta.shape
    )

    def q_copy(step, flip):
        target = lax.rem(chip + step, chips)
        device = 2 * target + lax.rem(core + flip, 2)
        return remote(
            low.at[0, :, lanes(device)],
            dq_ref.at[rows(me), :],
            q_send.at[step, flip],
            q_recv.at[step, flip],
            (scene, device),
        )

    def kv_copy(a, step, flip):
        target = lax.rem(chip + step, chips)
        device = 2 * target + lax.rem(core + flip, 2)
        return remote(
            low.at[1 + a, :, lanes(device)],
            (dk_ref, dv_ref)[a].at[rows(me), :],
            kv_send.at[a, step, flip],
            kv_recv.at[a, step, flip],
            (scene, device),
        )

    mine = [
        pltpu.make_async_copy(low.at[0, :, lanes(me)], dq_ref.at[rows(me), :], q_local),
        pltpu.make_async_copy(low.at[1, :, lanes(me)], dk_ref.at[rows(me), :], kv_local.at[0]),
        pltpu.make_async_copy(low.at[2, :, lanes(me)], dv_ref.at[rows(me), :], kv_local.at[1]),
    ]

    def keys(step, last):
        target = lax.rem(chip + step, chips)
        span = lanes(target, wide)
        k_here, v_here, kt_here = k_nat[span, :], v_nat[span, :], k_all[:, span]
        dk = dv = None
        for i in range(chips):
            if last:
                block = lax.rem(chip + i, chips)
                there = lanes(block, wide)
            else:
                there = slice(i * wide, (i + 1) * wide)
            scores = contract(k_here, q_all[:, there], 1, 0)
            prob = jnp.exp(scores - lse_all[0:1, there])
            dprob = contract(v_here, d_all[:, there], 1, 0)
            dscore = (prob * (dprob - delta[0:1, there])).astype(bf16)
            v_part = contract(prob.astype(bf16), d_nat[there, :], 1, 0)
            k_part = contract(dscore, q_nat[there, :], 1, 0)
            dk = k_part if dk is None else dk + k_part
            dv = v_part if dv is None else dv + v_part
            dq = dq_acc[:, there] + contract(kt_here, dscore, 1, 0)
            if last:
                low[0, :, there] = (dq * score_scale).astype(bf16)
                if i == 0:
                    mine[0].start()
                else:
                    q_copy(i, 0).start()
                q_copy(i, 1).start()
            else:
                dq_acc[:, there] = dq
        low[1, :, span] = dk.astype(bf16).T
        low[2, :, span] = dv.astype(bf16).T

    keys(0, False)
    mine[1].start()
    mine[2].start()
    kv_copy(0, 0, 1).start()
    kv_copy(1, 0, 1).start()

    def send_kv(step):
        for a in range(2):
            kv_copy(a, step, 0).start()
            kv_copy(a, step, 1).start()

    def step_body(step, carry):
        keys(step, False)
        send_kv(step)
        return carry

    lax.fori_loop(1, chips - 1, step_body, 0)
    keys(chips - 1, True)
    send_kv(chips - 1)
    save = pltpu.make_async_copy(low, heads_ref, save_sem)
    save.start()
    for copy in copies:
        copy.wait_send()
    for copy in mine:
        copy.wait()
    for step in range(chips):
        for flip in range(2):
            if step == 0 and flip == 0:
                continue
            kv_copy(0, step, flip).wait()
            kv_copy(1, step, flip).wait()
            q_copy(step, flip).wait()
    save.wait()


def attention_backward(n, d_t, q_all, k_all, v_all, o_all, lse_all):
    tok = d_t.shape[1]
    length = n * tok
    chips = n // 2
    any_spec = pl.BlockSpec(memory_space=pl.ANY)
    vmem = pl.BlockSpec(memory_space=pltpu.VMEM)
    dma = pltpu.SemaphoreType.DMA
    part = jax.ShapeDtypeStruct(d_t.shape, bf16)
    return pl.pallas_call(
        functools.partial(backward_kernel, n, tok),
        out_shape=(part, part, part, jax.ShapeDtypeStruct((3, HEAD_DIM, length), bf16)),
        in_specs=[any_spec] + [vmem] * 5,
        out_specs=[any_spec] * 4,
        scratch_shapes=[
            pltpu.VMEM((HEAD_DIM, length), bf16),
            pltpu.VMEM((length, HEAD_DIM), bf16),
            pltpu.VMEM((length, HEAD_DIM), bf16),
            pltpu.VMEM((length, HEAD_DIM), bf16),
            pltpu.VMEM((length, HEAD_DIM), bf16),
            pltpu.VMEM((8, length), f32),
            pltpu.VMEM((HEAD_DIM, length), f32),
            pltpu.VMEM((3, HEAD_DIM, length), bf16),
            dma((n,)),
            dma((n,)),
            dma,
            dma((2, chips, 2)),
            dma((2, chips, 2)),
            dma((2,)),
            dma((chips, 2)),
            dma((chips, 2)),
            dma,
            dma,
        ],
        compiler_params=pltpu.CompilerParams(
            collective_id=1, has_side_effects=True, vmem_limit_bytes=48 << 20
        ),
        name="attention_backward",
    )(d_t, q_all, k_all, v_all, o_all, lse_all)


def halving_kernel(
    down_ref,
    up_ref,
    out_ref,
    down_sum,
    up_sum,
    out_sum,
    own,
    got0,
    got1a,
    got1b,
    got2,
    got3,
    got4,
    load_sem,
    send_sem,
    recv_sem,
):
    me = lax.axis_index("seq")
    x = lax.axis_index("scene")
    core = lax.rem(me, 2)
    y = lax.rem(me // 2, 2)
    z0 = lax.rem(me // 4, 2)
    z1 = me // 8
    at_core = (x, me + 1 - 2 * core)
    at_x = (1 - x, me)
    at_y = (x, me + 2 - 4 * y)
    at_z0 = (x, me + 4 - 8 * z0)
    at_z1 = (x, me + 8 - 16 * z1)
    greet([at_core, at_x, at_y, at_z0, at_z1])

    every = slice(None)
    pieces = (
        [(down_ref, down_sum, slice(32 * i, 32 * i + 32), every) for i in range(4)]
        + [(up_ref, up_sum, every, slice(1024 * i, 1024 * i + 1024)) for i in range(4)]
        + [(out_ref, out_sum, every, every)]
    )
    top, low = slice(0, 16), slice(16, 32)
    started = []
    flight = {}

    def send(src, dst, chunk, slot, device):
        copy = remote(src, dst, send_sem.at[chunk, slot], recv_sem.at[chunk, slot], device)
        copy.start()
        started.append(copy)
        return copy

    for c, (ref, _, rows, columns) in enumerate(pieces):
        load = pltpu.make_async_copy(
            ref.at[:, :, :, core, rows, columns], own.at[c], load_sem.at[c]
        )
        load.start()
        flight[c, 0] = (
            load,
            send(ref.at[:, :, :, 1 - core, rows, columns], got0.at[c], c, 0, at_core),
        )

    def stage1(c):
        flight[c, 0][0].wait()
        flight[c, 0][1].wait_recv()
        own[c] = own[c] + got0[c]
        flight[c, 1] = (
            send(own.at[c, 1 - x, :, :, top, :], got1a.at[c], c, 1, at_x),
            send(own.at[c, :, :, 1 - y, low, :], got1b.at[c], c, 2, at_y),
        )

    def stage2(c):
        flight[c, 1][0].wait_recv()
        got1a[c] = own[c, x, :, :, top, :] + got1a[c]
        first = send(got1a.at[c, :, 1 - y], got2.at[c, :, top, :], c, 3, at_y)
        flight[c, 1][1].wait_recv()
        got1b[c] = own[c, :, :, y, low, :] + got1b[c]
        flight[c, 2] = (first, send(got1b.at[c, 1 - x], got2.at[c, :, low, :], c, 4, at_x))

    def stage3(c):
        flight[c, 2][0].wait_recv()
        got2[c, :, top, :] = got1a[c, :, y] + got2[c, :, top, :]
        flight[c, 2][1].wait_recv()
        got2[c, :, low, :] = got1b[c, x] + got2[c, :, low, :]
        flight[c, 3] = (
            send(got2.at[c, 1 - z0], got3.at[c, 0], c, 5, at_z0),
            send(got2.at[c, 3 - z0], got3.at[c, 1], c, 6, at_z0),
        )

    def stage4(c):
        flight[c, 3][0].wait_recv()
        flight[c, 3][1].wait_recv()
        got3[c, 0] = got2[c, z0] + got3[c, 0]
        got3[c, 1] = got2[c, 2 + z0] + got3[c, 1]
        flight[c, 4] = (send(got3.at[c, 1 - z1], got4.at[c], c, 7, at_z1),)

    def stage5(c):
        flight[c, 4][0].wait_recv()
        _, ref, rows, columns = pieces[c]
        ref[rows, columns] = got3[c, z1].astype(f32) + got4[c].astype(f32)

    stages = (stage1, stage2, stage3, stage4, stage5)
    for tick in range(len(pieces) + len(stages) - 1):
        for depth in reversed(range(len(stages))):
            if 0 <= tick - depth < len(pieces):
                stages[depth](tick - depth)
    for copy in started:
        copy.wait_send()


def halving_sum(down, up, out):
    shards = 32
    any_spec = pl.BlockSpec(memory_space=pl.ANY)
    vmem = pl.BlockSpec(memory_space=pltpu.VMEM)
    dma = pltpu.SemaphoreType.DMA
    arrays = [down, up, out]
    chunks = 9
    return pl.pallas_call(
        halving_kernel,
        out_shape=tuple(
            jax.ShapeDtypeStruct((a.shape[0] // shards, a.shape[1]), f32) for a in arrays
        ),
        in_specs=[any_spec] * 3,
        out_specs=[vmem] * 3,
        scratch_shapes=[
            pltpu.VMEM((chunks, 2, 4, 2, 32, 1024), bf16),
            pltpu.VMEM((chunks, 2, 4, 2, 32, 1024), bf16),
            pltpu.VMEM((chunks, 4, 2, 16, 1024), bf16),
            pltpu.VMEM((chunks, 2, 4, 16, 1024), bf16),
            pltpu.VMEM((chunks, 4, 32, 1024), bf16),
            pltpu.VMEM((chunks, 2, 32, 1024), bf16),
            pltpu.VMEM((chunks, 32, 1024), bf16),
            dma((chunks,)),
            dma((chunks, 8)),
            dma((chunks, 8)),
        ],
        compiler_params=pltpu.CompilerParams(
            collective_id=2, has_side_effects=True, vmem_limit_bytes=48 << 20
        ),
        name="halving_sum",
    )(*(a.reshape(2, 4, 2, 2, a.shape[0] // shards, a.shape[1]) for a in arrays))


def exchange_kernel(scenes, n, count, *refs):
    sources, sinks = refs[:count], refs[count : 2 * count]
    send_sem, recv_sem, local_sem = refs[2 * count :]
    me = lax.axis_index("seq")
    scene = lax.axis_index("scene")
    mine = scene * n + me
    devices = scenes * n

    def peer(j):
        index = lax.rem(mine + j, devices)
        return index, (index // n, lax.rem(index, n))

    greet([peer(j)[1] for j in range(1, devices)])
    copies = []
    for a in range(count):
        copies.append(
            pltpu.make_async_copy(sources[a].at[mine], sinks[a].at[mine], local_sem.at[a])
        )
        copies[-1].start()
    for j in range(1, devices):
        index, device = peer(j)
        for a in range(count):
            copies.append(
                remote(
                    sources[a].at[index],
                    sinks[a].at[mine],
                    send_sem.at[a, j],
                    recv_sem.at[a, j],
                    device,
                )
            )
            copies[-1].start()
    for copy in copies:
        copy.wait()


def exchange(scenes, n, *arrays):
    any_spec = pl.BlockSpec(memory_space=pl.ANY)
    dma = pltpu.SemaphoreType.DMA
    count, devices = len(arrays), scenes * n
    return pl.pallas_call(
        functools.partial(exchange_kernel, scenes, n, count),
        out_shape=tuple(jax.ShapeDtypeStruct(a.shape, a.dtype) for a in arrays),
        in_specs=[any_spec] * count,
        out_specs=[any_spec] * count,
        scratch_shapes=[dma((count, devices)), dma((count, devices)), dma((count,))],
        compiler_params=pltpu.CompilerParams(collective_id=3, has_side_effects=True),
        name="exchange",
    )(*arrays)


def normalise(values):
    row_mean = jnp.mean(values, axis=-1, keepdims=True)
    centred = values - row_mean
    row_var = jnp.mean(centred * centred, axis=-1, keepdims=True)
    inverse = lax.rsqrt(row_var + norm_eps)
    return centred * inverse, inverse


def norm_back(grad, scaled, inverse, gain):
    weighted = grad * gain
    back = inverse * (
        weighted
        - jnp.mean(weighted, axis=-1, keepdims=True)
        - scaled * jnp.mean(weighted * scaled, axis=-1, keepdims=True)
    )
    return back, jnp.sum(grad * scaled, axis=0), jnp.sum(grad, axis=0)


def gelu_both(values):
    cubic = gelu_coef * (values + 0.044715 * values * values * values)
    bend = jnp.tanh(cubic)
    slope = gelu_coef * (1.0 + 3.0 * 0.044715 * values * values)
    grad = 0.5 * (1.0 + bend) + 0.5 * values * (1.0 - bend * bend) * slope
    return 0.5 * values * (1.0 + bend), grad


def layer_on_device(
    scenes,
    n,
    tokens,
    surface_mask,
    out_grad,
    w_query,
    w_key,
    w_value,
    w_out,
    w_up,
    w_down,
    b_query,
    b_value,
    b_out,
    b_up,
    b_down,
    gain_one,
    shift_one,
    gain_two,
    shift_two,
):
    _, tok, width = tokens.shape
    devices = scenes * n
    rows = tokens[0].astype(f32)
    scaled_one, inverse_one = normalise(rows)
    normed = (scaled_one * gain_one + shift_one).astype(bf16)
    normed_all = lax.all_gather(normed, "seq", axis=0, tiled=True)
    q_t = contract(w_query, normed, 0, 1) + b_query[:, None]
    q_t = (q_t.astype(bf16).astype(f32) * score_scale).astype(bf16)
    k_t = contract(w_key, normed, 0, 1).astype(bf16)
    v_t = (contract(w_value, normed, 0, 1) + b_value[:, None]).astype(bf16)
    att_t, q_all, k_all, v_all, o_all, lse_all = attention_forward(n, q_t, k_t, v_t)

    residual = rows + matmul_tn(att_t, w_out) + b_out
    scaled_two, inverse_two = normalise(residual)
    normed_two = (scaled_two * gain_two + shift_two).astype(bf16)
    hidden = matmul(normed_two, w_up) + b_up
    activated, gelu_grad = gelu_both(hidden)
    activated = activated.astype(bf16)
    block_out = (residual + matmul(activated, w_down) + b_down).astype(bf16)
    masked = out_grad[0] * surface_mask[0].astype(bf16)[:, None]
    grad_down = matmul_tn(activated, masked).astype(bf16)
    grad_bdown = jnp.sum(masked.astype(f32), axis=0)
    hidden_grad = (matmul_nt(masked, w_down) * gelu_grad).astype(bf16)
    grad_up = matmul_tn(normed_two, hidden_grad).astype(bf16)
    grad_bup = jnp.sum(hidden_grad.astype(f32), axis=0)
    norm_two_in = matmul_nt(hidden_grad, w_up)
    resid_part, grad_gain_two, grad_shift_two = norm_back(
        norm_two_in, scaled_two, inverse_two, gain_two
    )
    resid_grad = masked.astype(f32) + resid_part
    resid_low = resid_grad.astype(bf16)
    grad_out = matmul(att_t, resid_low).astype(bf16)
    grad_bout = jnp.sum(resid_low.astype(f32), axis=0)
    att_grad_t = matmul_nt(w_out, resid_low).astype(bf16)

    sum_down, sum_up, sum_out = halving_sum(grad_down, grad_up, grad_out)
    dq_t, dk_t, dv_t, heads_t = attention_backward(
        n, att_grad_t, q_all, k_all, v_all, o_all, lse_all
    )

    head_grads = matmul(heads_t.reshape(3 * HEAD_DIM, n * tok), normed_all)
    head_grads = head_grads.T.reshape(devices, width // devices, 3 * HEAD_DIM)
    norm_one_in = (
        contract(dq_t, w_query, 0, 1) + contract(dk_t, w_key, 0, 1) + contract(dv_t, w_value, 0, 1)
    )
    token_part, grad_gain_one, grad_shift_one = norm_back(
        norm_one_in, scaled_one, inverse_one, gain_one
    )
    tokens_grad = (resid_grad + token_part).astype(bf16)
    grad_bquery = jnp.sum(dq_t.astype(f32), axis=1)
    grad_bvalue = jnp.sum(dv_t.astype(f32), axis=1)
    small = [
        grad_bquery,
        grad_bvalue,
        grad_bout,
        grad_bup,
        grad_bdown,
        grad_gain_one,
        grad_shift_one,
        grad_gain_two,
        grad_shift_two,
    ]
    packed = jnp.concatenate([s.reshape(devices, -1) for s in small], axis=1)
    room = -packed.shape[1] % 1024
    packed = jnp.pad(packed, ((0, 0), (0, room))).reshape(devices, -1, 128)
    heads_got, small_got = exchange(scenes, n, head_grads, packed)
    heads_sum = heads_got.reshape(scenes, n, width // devices, 3, HEAD_DIM).sum(axis=0)
    weights = [
        jnp.moveaxis(heads_sum[:, :, i], 0, 1).reshape(width // devices, width) for i in range(3)
    ]
    vectors = small_got.reshape(devices, -1).sum(axis=0)
    parts, at = [], 0
    for s in small:
        size = s.shape[0] // devices
        parts.append(vectors[at : at + size])
        at += size
    bquery, bvalue, bout, bup, bdown, gone, sone, gtwo, stwo = parts
    return (
        block_out[None],
        tokens_grad[None],
        *weights,
        sum_out,
        sum_up,
        sum_down,
        bquery,
        bvalue,
        bout,
        bup,
        bdown,
        gone,
        sone,
        gtwo,
        stwo,
    )


def norm_rows(values, gain, shift):
    row_mean = jnp.mean(values, axis=-1, keepdims=True)
    centred = values - row_mean
    row_var = jnp.mean(centred * centred, axis=-1, keepdims=True)
    return centred * lax.rsqrt(row_var + norm_eps) * gain + shift


def gelu_tanh(values):
    return (
        0.5 * values * (1.0 + jnp.tanh(gelu_coef * (values + 0.044715 * values * values * values)))
    )


def take_pair(array_in, pair_index):
    pair_width = 2 * HEAD_DIM
    sliced = lax.dynamic_slice_in_dim(array_in, pair_index * pair_width, pair_width, 2)
    return sliced.reshape(sliced.shape[:2] + (2, HEAD_DIM))


def take_stats(array_in, pair_index):
    return lax.dynamic_slice_in_dim(array_in, pair_index * 2, 2, 1)


def join_pairs(stacked):
    moved = jnp.moveaxis(stacked, 0, 2)
    return moved.reshape(moved.shape[:2] + (moved.shape[2] * moved.shape[3],))


def join_stats(stacked):
    moved = jnp.moveaxis(stacked, 0, 1)
    return moved.reshape((moved.shape[0], moved.shape[1] * moved.shape[2], moved.shape[3]))


def merge_heads(pair_part):
    return pair_part.reshape(pair_part.shape[:2] + (2 * HEAD_DIM,))


def attend(q_scene, k_gathered, v_gathered):

    def attend_pair_step(unused, pair_index):
        q_pair = take_pair(q_scene, pair_index)
        k_pair = take_pair(k_gathered, pair_index)
        v_pair = take_pair(v_gathered, pair_index)
        scores = (
            jnp.einsum("sqhe,skhe->shqk", q_pair, k_pair, preferred_element_type=jnp.float32)
            * score_scale
        )
        row_max = jnp.max(scores, axis=-1, keepdims=True)
        shifted = jnp.exp(scores - row_max)
        row_sum = jnp.sum(shifted, axis=-1, keepdims=True)
        prob_low = (shifted / row_sum).astype(jnp.bfloat16)
        pair_out = jnp.einsum(
            "shqk,skhe->sqhe", prob_low, v_pair, preferred_element_type=jnp.float32
        )
        pair_lse = (row_max + jnp.log(row_sum))[..., 0]
        return (unused, (merge_heads(pair_out), pair_lse))

    pair_count = HEADS // 2
    _, (pair_outs, pair_lses) = lax.scan(
        attend_pair_step, jnp.zeros((), jnp.float32), jnp.arange(pair_count, dtype=jnp.int32)
    )
    return (join_pairs(pair_outs), join_stats(pair_lses))


def query_side(q_scene, k_gathered, v_gathered, row_lse, att_grad):

    def query_pair_step(unused, pair_index):
        q_pair = take_pair(q_scene, pair_index)
        k_pair = take_pair(k_gathered, pair_index)
        v_pair = take_pair(v_gathered, pair_index)
        d_pair = take_pair(att_grad, pair_index)
        l_pair = take_stats(row_lse, pair_index)
        scores = (
            jnp.einsum("sqhe,skhe->shqk", q_pair, k_pair, preferred_element_type=jnp.float32)
            * score_scale
        )
        attn_prob = jnp.exp(scores - l_pair[..., None])
        dprob = jnp.einsum("sqhe,skhe->shqk", d_pair, v_pair, preferred_element_type=jnp.float32)
        row_delta = jnp.sum(attn_prob * dprob, axis=-1)
        dscore = (attn_prob * (dprob - row_delta[..., None])).astype(jnp.bfloat16)
        q_part = (
            jnp.einsum("shqk,skhe->sqhe", dscore, k_pair, preferred_element_type=jnp.float32)
            * score_scale
        )
        results = (merge_heads(q_part), row_delta)
        prob_low = attn_prob.astype(jnp.bfloat16)
        k_part = (
            jnp.einsum("shqk,sqhe->skhe", dscore, q_pair, preferred_element_type=jnp.float32)
            * score_scale
        )
        v_part = jnp.einsum("shqk,sqhe->skhe", prob_low, d_pair, preferred_element_type=jnp.float32)
        results = results + (merge_heads(k_part), merge_heads(v_part))
        return (unused, results)

    pair_count = HEADS // 2
    _, results = lax.scan(
        query_pair_step, jnp.zeros((), jnp.float32), jnp.arange(pair_count, dtype=jnp.int32)
    )
    return results


def on_any_device(
    tokens,
    surface_mask,
    out_grad,
    w_query,
    w_key,
    w_value,
    w_out,
    w_up,
    w_down,
    b_query,
    b_value,
    b_out,
    b_up,
    b_down,
    gain_one,
    shift_one,
    gain_two,
    shift_two,
):
    scenes, local_len, model_width = tokens.shape
    row_count = scenes * local_len
    flat_rows = tokens.astype(jnp.float32).reshape(row_count, model_width)
    normed, norm_one_pull = jax.vjp(norm_rows, flat_rows, gain_one, shift_one)
    normed_low = normed.astype(jnp.bfloat16)
    q_low = (matmul(normed_low, w_query) + b_query).astype(jnp.bfloat16)
    k_low = matmul(normed_low, w_key).astype(jnp.bfloat16)
    v_low = (matmul(normed_low, w_value) + b_value).astype(jnp.bfloat16)
    q_scene = q_low.reshape(scenes, local_len, model_width)
    k_scene = k_low.reshape(scenes, local_len, model_width)
    v_scene = v_low.reshape(scenes, local_len, model_width)
    k_gathered, v_gathered = (
        lax.all_gather(k_scene, "seq", axis=1, tiled=True),
        lax.all_gather(v_scene, "seq", axis=1, tiled=True),
    )
    attended, row_lse = attend(q_scene, k_gathered, v_gathered)
    att_low = attended.reshape(row_count, model_width).astype(jnp.bfloat16)
    residual = flat_rows + matmul(att_low, w_out) + b_out
    normed_two, norm_two_pull = jax.vjp(norm_rows, residual, gain_two, shift_two)
    normed_two_low = normed_two.astype(jnp.bfloat16)
    hidden = matmul(normed_two_low, w_up) + b_up
    activated, gelu_pull = jax.vjp(gelu_tanh, hidden)
    act_low = activated.astype(jnp.bfloat16)
    block_rows = residual + matmul(act_low, w_down) + b_down
    block_out = block_rows.reshape(scenes, local_len, model_width).astype(jnp.bfloat16)
    masked_f = out_grad.astype(jnp.float32) * surface_mask.astype(jnp.float32)[..., None]
    masked_rows = masked_f.reshape(row_count, model_width)
    masked_low = masked_rows.astype(jnp.bfloat16)
    grad_down = matmul_tn(act_low, masked_low)
    grad_bdown = jnp.sum(masked_rows, axis=0)
    act_grad = matmul_nt(masked_low, w_down)
    hidden_low = gelu_pull(act_grad)[0].astype(jnp.bfloat16)
    grad_up = matmul_tn(normed_two_low, hidden_low)
    grad_bup = jnp.sum(hidden_low.astype(jnp.float32), axis=0)
    norm_two_in = matmul_nt(hidden_low, w_up)
    resid_part, grad_gain_two, grad_shift_two = norm_two_pull(norm_two_in)
    resid_grad = masked_rows + resid_part
    resid_low = resid_grad.astype(jnp.bfloat16)
    grad_out = matmul_tn(att_low, resid_low)
    grad_bout = jnp.sum(resid_low.astype(jnp.float32), axis=0)
    att_grad = (
        matmul_nt(resid_low, w_out).astype(jnp.bfloat16).reshape(scenes, local_len, model_width)
    )
    q_parts, delta_parts, k_parts, v_parts = query_side(
        q_scene, k_gathered, v_gathered, row_lse, att_grad
    )
    k_summed, v_summed = (
        lax.psum_scatter(
            k_parts.astype(jnp.bfloat16), "seq", scatter_dimension=2, tiled=True
        ).astype(jnp.float32),
        lax.psum_scatter(
            v_parts.astype(jnp.bfloat16), "seq", scatter_dimension=2, tiled=True
        ).astype(jnp.float32),
    )
    k_grad = join_pairs(k_summed)
    v_grad = join_pairs(v_summed)
    q_grad = join_pairs(q_parts)
    q_grad_low = q_grad.reshape(row_count, model_width).astype(jnp.bfloat16)
    k_grad_low = k_grad.reshape(row_count, model_width).astype(jnp.bfloat16)
    v_grad_low = v_grad.reshape(row_count, model_width).astype(jnp.bfloat16)
    grad_query = matmul_tn(normed_low, q_grad_low)
    grad_key = matmul_tn(normed_low, k_grad_low)
    grad_value = matmul_tn(normed_low, v_grad_low)
    grad_bquery = jnp.sum(q_grad_low.astype(jnp.float32), axis=0)
    grad_bvalue = jnp.sum(v_grad_low.astype(jnp.float32), axis=0)
    norm_one_in = (
        matmul_nt(q_grad_low, w_query)
        + matmul_nt(k_grad_low, w_key)
        + matmul_nt(v_grad_low, w_value)
    )
    token_part, grad_gain_one, grad_shift_one = norm_one_pull(norm_one_in)
    tokens_grad = (
        (resid_grad + token_part).reshape(scenes, local_len, model_width).astype(jnp.bfloat16)
    )
    (
        sum_query,
        sum_key,
        sum_value,
        sum_out,
        sum_bquery,
        sum_bvalue,
        sum_bout,
        sum_gain_one,
        sum_shift_one,
        sum_up,
        sum_down,
        sum_bup,
        sum_bdown,
        sum_gain_two,
        sum_shift_two,
    ) = (
        lax.psum_scatter(grad_query, ("scene", "seq"), scatter_dimension=0, tiled=True),
        lax.psum_scatter(grad_key, ("scene", "seq"), scatter_dimension=0, tiled=True),
        lax.psum_scatter(grad_value, ("scene", "seq"), scatter_dimension=0, tiled=True),
        lax.psum_scatter(grad_out, ("scene", "seq"), scatter_dimension=0, tiled=True),
        lax.psum_scatter(grad_bquery, ("scene", "seq"), scatter_dimension=0, tiled=True),
        lax.psum_scatter(grad_bvalue, ("scene", "seq"), scatter_dimension=0, tiled=True),
        lax.psum_scatter(grad_bout, ("scene", "seq"), scatter_dimension=0, tiled=True),
        lax.psum_scatter(grad_gain_one, ("scene", "seq"), scatter_dimension=0, tiled=True),
        lax.psum_scatter(grad_shift_one, ("scene", "seq"), scatter_dimension=0, tiled=True),
        lax.psum_scatter(grad_up, ("scene", "seq"), scatter_dimension=0, tiled=True),
        lax.psum_scatter(grad_down, ("scene", "seq"), scatter_dimension=0, tiled=True),
        lax.psum_scatter(grad_bup, ("scene", "seq"), scatter_dimension=0, tiled=True),
        lax.psum_scatter(grad_bdown, ("scene", "seq"), scatter_dimension=0, tiled=True),
        lax.psum_scatter(grad_gain_two, ("scene", "seq"), scatter_dimension=0, tiled=True),
        lax.psum_scatter(grad_shift_two, ("scene", "seq"), scatter_dimension=0, tiled=True),
    )
    return (
        block_out,
        tokens_grad,
        sum_query,
        sum_key,
        sum_value,
        sum_out,
        sum_up,
        sum_down,
        sum_bquery,
        sum_bvalue,
        sum_bout,
        sum_bup,
        sum_bdown,
        sum_gain_one,
        sum_shift_one,
        sum_gain_two,
        sum_shift_two,
    )


def solution(mesh):
    placed = (
        P("scene", "seq", None),
        P("scene", "seq"),
        P("scene", "seq", None),
        P(),
        P(),
        P(),
        P(),
        P(),
        P(),
        P(),
        P(),
        P(),
        P(),
        P(),
        P(),
        P(),
        P(),
        P(),
    )
    scenes, n = mesh.shape["scene"], mesh.shape["seq"]
    if (scenes, n) == (2, HEADS):
        on_device = functools.partial(layer_on_device, scenes, n)
    else:
        on_device = on_any_device
    return jax.shard_map(
        on_device,
        mesh=mesh,
        in_specs=placed,
        out_specs=(
            P("scene", "seq", None),
            P("scene", "seq", None),
            P(("scene", "seq"), None),
            P(("scene", "seq"), None),
            P(("scene", "seq"), None),
            P(("scene", "seq"), None),
            P(("scene", "seq"), None),
            P(("scene", "seq"), None),
            P(("scene", "seq")),
            P(("scene", "seq")),
            P(("scene", "seq")),
            P(("scene", "seq")),
            P(("scene", "seq")),
            P(("scene", "seq")),
            P(("scene", "seq")),
            P(("scene", "seq")),
            P(("scene", "seq")),
        ),
        check_vma=False,
    )
```

```python
import functools

import jax
import jax.numpy as jnp
from jax import lax
from jax.experimental import pallas as pl
from jax.experimental.pallas import tpu as pltpu
from jax.sharding import PartitionSpec as P

HEADS = 16
HEAD_DIM = 64
MESH = pl.DeviceIdType.MESH
f32 = jnp.float32
bf16 = jnp.bfloat16

norm_eps = 1e-05
score_scale = 0.125
gelu_coef = 0.7978845608028654


def matmul(left, right):
    return jnp.dot(left, right, preferred_element_type=jnp.float32)


def contract(left, right, left_dim, right_dim):
    return lax.dot_general(
        left, right, (((left_dim,), (right_dim,)), ((), ())), preferred_element_type=jnp.float32
    )


def matmul_tn(left, right):
    return contract(left, right, 0, 0)


def matmul_nt(left, right):
    return contract(left, right, 1, 1)


def greet(partners):
    barrier = pltpu.get_barrier_semaphore()
    for partner in partners:
        pl.semaphore_signal(barrier, inc=1, device_id=partner, device_id_type=MESH)
    pl.semaphore_wait(barrier, len(partners))


def remote(src, dst, send_sem, recv_sem, device):
    return pltpu.make_async_remote_copy(
        src_ref=src,
        dst_ref=dst,
        send_sem=send_sem,
        recv_sem=recv_sem,
        device_id=device,
        device_id_type=MESH,
    )


def forward_kernel(
    n,
    tok,
    qt_ref,
    kt_ref,
    vt_ref,
    att_ref,
    q_out,
    k_out,
    v_out,
    o_out,
    lse_out,
    q_all,
    k_all,
    v_all,
    k_nat,
    o_all,
    lse_all,
    att_send,
    in_send,
    in_recv,
    in_local,
    out_send,
    out_recv,
    out_local,
    save_sem,
):
    me = lax.axis_index("seq")
    scene = lax.axis_index("scene")
    chip, core = me // 2, lax.rem(me, 2)
    chips = n // 2
    length = n * tok
    others = [lax.rem(me + j, n) for j in range(1, n)]
    greet([(scene, other) for other in others])

    def rows(head):
        return pl.ds(pl.multiple_of(head * HEAD_DIM, HEAD_DIM), HEAD_DIM)

    def lanes(block, width=tok):
        return pl.ds(pl.multiple_of(block * width, width), width)

    pairs = ((kt_ref, k_all), (vt_ref, v_all), (qt_ref, q_all))
    copies = {}
    for a, (src, dst) in enumerate(pairs):
        for j in range(1, n):
            head = lax.rem(me + j, n)
            copies[a, j] = remote(
                src.at[rows(head), :],
                dst.at[:, lanes(me)],
                in_send.at[a, j],
                in_recv.at[a, j],
                (scene, head),
            )
            copies[a, j].start()
    local = [
        pltpu.make_async_copy(src.at[rows(me), :], dst.at[:, lanes(me)], in_local.at[a])
        for a, (src, dst) in enumerate(pairs)
    ]
    for copy in local:
        copy.start()
    for copy in local:
        copy.wait()
    for a in range(3):
        for j in range(1, n):
            copies[a, j].wait_recv()
    k_nat[...] = k_all[...].T
    saves = [
        pltpu.make_async_copy(src, dst, save_sem.at[a])
        for a, (src, dst) in enumerate(((q_all, q_out), (k_all, k_out), (v_all, v_out)))
    ]
    for copy in saves:
        copy.start()

    wide = 2 * tok
    key_block = length // 2

    def queries(step):
        target = lax.rem(chip + step, chips)
        span = lanes(target, wide)
        q_here = q_all[:, span]
        top = total = acc = None
        for block in range(length // key_block):
            keys = slice(block * key_block, (block + 1) * key_block)
            scores = contract(k_nat[keys, :], q_here, 1, 0)
            here = jnp.max(scores, axis=0, keepdims=True)
            new_top = here if top is None else jnp.maximum(top, here)
            shifted = jnp.exp(scores - new_top)
            part_sum = jnp.sum(shifted, axis=0, keepdims=True)
            part = contract(v_all[:, keys], shifted.astype(bf16), 1, 0)
            if top is None:
                total, acc = part_sum, part
            else:
                fade = jnp.exp(top - new_top)
                total, acc = total * fade + part_sum, acc * fade + part
            top = new_top
        out = acc / total
        o_all[:, span] = out
        lse_all[:, span] = jnp.broadcast_to(top + jnp.log(total), (8, wide))
        low = out.astype(bf16)
        att_send[step, 0] = low[:, :tok]
        att_send[step, 1] = low[:, tok:]
        return target

    def out_copy(step, target, flip):
        device = 2 * target + lax.rem(core + flip, 2)
        return remote(
            att_send.at[step, lax.rem(core + flip, 2)],
            att_ref.at[rows(me), :],
            out_send.at[step, flip],
            out_recv.at[step, flip],
            (scene, device),
        )

    queries(0)
    mine = pltpu.make_async_copy(att_send.at[0, core], att_ref.at[rows(me), :], out_local)
    mine.start()
    out_copy(0, chip, 1).start()

    def step_body(step, carry):
        target = queries(step)
        out_copy(step, target, 0).start()
        out_copy(step, target, 1).start()
        return carry

    lax.fori_loop(1, chips, step_body, 0)
    o_save = pltpu.make_async_copy(o_all, o_out, save_sem.at[3])
    l_save = pltpu.make_async_copy(lse_all, lse_out, save_sem.at[4])
    o_save.start()
    l_save.start()
    for a in range(3):
        for j in range(1, n):
            copies[a, j].wait_send()
    mine.wait()
    out_copy(0, chip, 1).wait()

    def drain(step, carry):
        target = lax.rem(chip + step, chips)
        out_copy(step, target, 0).wait()
        out_copy(step, target, 1).wait()
        return carry

    lax.fori_loop(1, chips, drain, 0)
    for copy in saves + [o_save, l_save]:
        copy.wait()


def attention_forward(n, q_t, k_t, v_t):
    tok = q_t.shape[1]
    length = n * tok
    any_spec = pl.BlockSpec(memory_space=pl.ANY)
    head_all = jax.ShapeDtypeStruct((HEAD_DIM, length), bf16)
    dma = pltpu.SemaphoreType.DMA
    return pl.pallas_call(
        functools.partial(forward_kernel, n, tok),
        out_shape=(
            jax.ShapeDtypeStruct(q_t.shape, bf16),
            head_all,
            head_all,
            head_all,
            jax.ShapeDtypeStruct((HEAD_DIM, length), f32),
            jax.ShapeDtypeStruct((8, length), f32),
        ),
        in_specs=[any_spec] * 3,
        out_specs=[any_spec] * 6,
        scratch_shapes=[
            pltpu.VMEM((HEAD_DIM, length), bf16),
            pltpu.VMEM((HEAD_DIM, length), bf16),
            pltpu.VMEM((HEAD_DIM, length), bf16),
            pltpu.VMEM((length, HEAD_DIM), bf16),
            pltpu.VMEM((HEAD_DIM, length), f32),
            pltpu.VMEM((8, length), f32),
            pltpu.VMEM((n // 2, 2, HEAD_DIM, tok), bf16),
            dma((3, n)),
            dma((3, n)),
            dma((3,)),
            dma((n // 2, 2)),
            dma((n // 2, 2)),
            dma,
            dma((5,)),
        ],
        compiler_params=pltpu.CompilerParams(
            collective_id=0, has_side_effects=True, vmem_limit_bytes=48 << 20
        ),
        name="attention_forward",
    )(q_t, k_t, v_t)


CHUNKS = 9
TICKS = CHUNKS + 4


def halving_plan(sources, own, got0, got1a, got1b, got2, got3, got4, total, sems):
    load_sem, send_sem, recv_sem = sems
    me = lax.axis_index("seq")
    x = lax.axis_index("scene")
    core = lax.rem(me, 2)
    y = lax.rem(me // 2, 2)
    z0 = lax.rem(me // 4, 2)
    z1 = me // 8
    at_core = (x, me + 1 - 2 * core)
    at_x = (1 - x, me)
    at_y = (x, me + 2 - 4 * y)
    at_z0 = (x, me + 4 - 8 * z0)
    at_z1 = (x, me + 8 - 16 * z1)
    top, low = slice(0, 16), slice(16, 32)

    def copy_of(slot, c):
        src, dst, device = (
            lambda: (got0.at[c], got0.at[c], at_core),
            lambda: (own.at[c, 1 - x, :, :, top, :], got1a.at[c], at_x),
            lambda: (own.at[c, :, :, 1 - y, low, :], got1b.at[c], at_y),
            lambda: (got1a.at[c, :, 1 - y], got2.at[c, :, top, :], at_y),
            lambda: (got1b.at[c, 1 - x], got2.at[c, :, low, :], at_x),
            lambda: (got2.at[c, 1 - z0], got3.at[c, 0], at_z0),
            lambda: (got2.at[c, 3 - z0], got3.at[c, 1], at_z0),
            lambda: (got3.at[c, 1 - z1], got4.at[c], at_z1),
        )[slot]()
        return remote(src, dst, send_sem.at[c, slot], recv_sem.at[c, slot], device)

    def first_copies(c):
        ref, rows, columns = sources[c]
        load = pltpu.make_async_copy(
            ref.at[:, :, :, core, rows, columns], own.at[c], load_sem.at[c]
        )
        over = remote(
            ref.at[:, :, :, 1 - core, rows, columns],
            got0.at[c],
            send_sem.at[c, 0],
            recv_sem.at[c, 0],
            at_core,
        )
        return load, over

    def begin():
        for c in range(CHUNKS):
            for copy in first_copies(c):
                copy.start()

    def stage1(c):
        pltpu.make_async_copy(own.at[c], own.at[c], load_sem.at[c]).wait()
        copy_of(0, c).wait_recv()
        own[c] = own[c] + got0[c]
        copy_of(1, c).start()
        copy_of(2, c).start()

    def stage2(c):
        copy_of(1, c).wait_recv()
        got1a[c] = own[c, x, :, :, top, :] + got1a[c]
        copy_of(3, c).start()
        copy_of(2, c).wait_recv()
        got1b[c] = own[c, :, :, y, low, :] + got1b[c]
        copy_of(4, c).start()

    def stage3(c):
        copy_of(3, c).wait_recv()
        got2[c, :, top, :] = got1a[c, :, y] + got2[c, :, top, :]
        copy_of(4, c).wait_recv()
        got2[c, :, low, :] = got1b[c, x] + got2[c, :, low, :]
        copy_of(5, c).start()
        copy_of(6, c).start()

    def stage4(c):
        copy_of(5, c).wait_recv()
        copy_of(6, c).wait_recv()
        got3[c, 0] = got2[c, z0] + got3[c, 0]
        got3[c, 1] = got2[c, 2 + z0] + got3[c, 1]
        copy_of(7, c).start()

    def stage5(c):
        copy_of(7, c).wait_recv()
        total[c] = got3[c, z1].astype(f32) + got4[c].astype(f32)

    stages = (stage1, stage2, stage3, stage4, stage5)

    def tick(when):
        for depth in reversed(range(len(stages))):
            c = when - depth

            @pl.when((c >= 0) & (c < CHUNKS))
            def _(stage=stages[depth], c=c):
                stage(c)

    def finish(sinks):
        for c, (ref, rows, columns) in enumerate(sinks):
            pltpu.make_async_copy(total.at[c], ref.at[rows, columns], load_sem.at[c]).start()
        for c in range(CHUNKS):
            for slot in range(8):
                copy_of(slot, c).wait_send()
        for c, (ref, rows, columns) in enumerate(sinks):
            pltpu.make_async_copy(total.at[c], ref.at[rows, columns], load_sem.at[c]).wait()

    return [at_core, at_x, at_y, at_z0, at_z1], begin, tick, finish


def halving_pieces(down, up, out):
    every = slice(None)
    return (
        [(down, slice(32 * i, 32 * i + 32), every) for i in range(4)]
        + [(up, every, slice(1024 * i, 1024 * i + 1024)) for i in range(4)]
        + [(out, every, every)]
    )


def halving_scratch():
    dma = pltpu.SemaphoreType.DMA
    return [
        pltpu.VMEM((CHUNKS, 2, 4, 2, 32, 1024), bf16),
        pltpu.VMEM((CHUNKS, 2, 4, 2, 32, 1024), bf16),
        pltpu.VMEM((CHUNKS, 4, 2, 16, 1024), bf16),
        pltpu.VMEM((CHUNKS, 2, 4, 16, 1024), bf16),
        pltpu.VMEM((CHUNKS, 4, 32, 1024), bf16),
        pltpu.VMEM((CHUNKS, 2, 32, 1024), bf16),
        pltpu.VMEM((CHUNKS, 32, 1024), bf16),
        pltpu.VMEM((CHUNKS, 32, 1024), f32),
        dma((CHUNKS,)),
        dma((CHUNKS, 8)),
        dma((CHUNKS, 8)),
    ]


def backward_kernel(
    n,
    tok,
    dt_ref,
    q_all,
    k_all,
    v_all,
    o_all,
    lse_all,
    down_ref,
    up_ref,
    out_ref,
    dq_ref,
    dk_ref,
    dv_ref,
    heads_ref,
    down_sum,
    up_sum,
    out_sum,
    d_all,
    q_nat,
    k_nat,
    v_nat,
    d_nat,
    delta,
    dq_acc,
    low,
    in_send,
    in_recv,
    in_local,
    kv_send,
    kv_recv,
    kv_local,
    q_send,
    q_recv,
    q_local,
    save_sem,
    *halving,
):
    me = lax.axis_index("seq")
    scene = lax.axis_index("scene")
    chip, core = me // 2, lax.rem(me, 2)
    chips = n // 2
    length = n * tok
    wide = 2 * tok
    partners, begin, tick, finish = halving_plan(
        halving_pieces(down_ref, up_ref, out_ref), *halving[:8], halving[8:]
    )
    greet([(scene, lax.rem(me + j, n)) for j in range(1, n)] + [partners[1]])

    def rows(head):
        return pl.ds(pl.multiple_of(head * HEAD_DIM, HEAD_DIM), HEAD_DIM)

    def lanes(block, width=tok):
        return pl.ds(pl.multiple_of(block * width, width), width)

    copies = []
    for j in range(1, n):
        head = lax.rem(me + j, n)
        copies.append(
            remote(
                dt_ref.at[rows(head), :],
                d_all.at[:, lanes(me)],
                in_send.at[j],
                in_recv.at[j],
                (scene, head),
            )
        )
        copies[-1].start()
    local = pltpu.make_async_copy(dt_ref.at[rows(me), :], d_all.at[:, lanes(me)], in_local)
    local.start()
    begin()
    q_nat[...] = q_all[...].T
    k_nat[...] = k_all[...].T
    v_nat[...] = v_all[...].T
    dq_acc[...] = jnp.zeros_like(dq_acc)
    local.wait()
    for copy in copies:
        copy.wait_recv()
    d_nat[...] = d_all[...].T
    delta[...] = jnp.broadcast_to(
        jnp.sum(d_all[...].astype(f32) * o_all[...], axis=0, keepdims=True), delta.shape
    )

    def q_copy(step, flip):
        target = lax.rem(chip + step, chips)
        device = 2 * target + lax.rem(core + flip, 2)
        return remote(
            low.at[0, :, lanes(device)],
            dq_ref.at[rows(me), :],
            q_send.at[step, flip],
            q_recv.at[step, flip],
            (scene, device),
        )

    def kv_copy(a, step, flip):
        target = lax.rem(chip + step, chips)
        device = 2 * target + lax.rem(core + flip, 2)
        return remote(
            low.at[1 + a, :, lanes(device)],
            (dk_ref, dv_ref)[a].at[rows(me), :],
            kv_send.at[a, step, flip],
            kv_recv.at[a, step, flip],
            (scene, device),
        )

    mine = [
        pltpu.make_async_copy(low.at[0, :, lanes(me)], dq_ref.at[rows(me), :], q_local),
        pltpu.make_async_copy(low.at[1, :, lanes(me)], dk_ref.at[rows(me), :], kv_local.at[0]),
        pltpu.make_async_copy(low.at[2, :, lanes(me)], dv_ref.at[rows(me), :], kv_local.at[1]),
    ]

    def keys(step, last):
        target = lax.rem(chip + step, chips)
        span = lanes(target, wide)
        k_here, v_here, kt_here = k_nat[span, :], v_nat[span, :], k_all[:, span]
        dk = dv = None
        for i in range(chips):
            if last:
                block = lax.rem(chip + i, chips)
                there = lanes(block, wide)
            else:
                there = slice(i * wide, (i + 1) * wide)
            scores = contract(k_here, q_all[:, there], 1, 0)
            prob = jnp.exp(scores - lse_all[0:1, there])
            dprob = contract(v_here, d_all[:, there], 1, 0)
            dscore = (prob * (dprob - delta[0:1, there])).astype(bf16)
            v_part = contract(prob.astype(bf16), d_nat[there, :], 1, 0)
            k_part = contract(dscore, q_nat[there, :], 1, 0)
            dk = k_part if dk is None else dk + k_part
            dv = v_part if dv is None else dv + v_part
            dq = dq_acc[:, there] + contract(kt_here, dscore, 1, 0)
            if last:
                low[0, :, there] = (dq * score_scale).astype(bf16)
                if i == 0:
                    mine[0].start()
                else:
                    q_copy(i, 0).start()
                q_copy(i, 1).start()
            else:
                dq_acc[:, there] = dq
        low[1, :, span] = dk.astype(bf16).T
        low[2, :, span] = dv.astype(bf16).T

    tick(0)
    keys(0, False)
    mine[1].start()
    mine[2].start()
    kv_copy(0, 0, 1).start()
    kv_copy(1, 0, 1).start()

    def send_kv(step):
        for a in range(2):
            kv_copy(a, step, 0).start()
            kv_copy(a, step, 1).start()

    def step_body(step, carry):
        tick(step)
        keys(step, False)
        send_kv(step)
        return carry

    lax.fori_loop(1, chips - 1, step_body, 0)
    tick(chips - 1)
    keys(chips - 1, True)
    send_kv(chips - 1)
    save = pltpu.make_async_copy(low, heads_ref, save_sem)
    save.start()

    def tick_body(when, carry):
        tick(when)
        return carry

    lax.fori_loop(chips, TICKS, tick_body, 0)
    finish(halving_pieces(down_sum, up_sum, out_sum))
    for copy in copies:
        copy.wait_send()
    for copy in mine:
        copy.wait()
    for step in range(chips):
        for flip in range(2):
            if step == 0 and flip == 0:
                continue
            kv_copy(0, step, flip).wait()
            kv_copy(1, step, flip).wait()
            q_copy(step, flip).wait()
    save.wait()


def attention_backward(n, d_t, q_all, k_all, v_all, o_all, lse_all, *weights):
    shards = 32
    tok = d_t.shape[1]
    length = n * tok
    chips = n // 2
    any_spec = pl.BlockSpec(memory_space=pl.ANY)
    vmem = pl.BlockSpec(memory_space=pltpu.VMEM)
    dma = pltpu.SemaphoreType.DMA
    part = jax.ShapeDtypeStruct(d_t.shape, bf16)
    return pl.pallas_call(
        functools.partial(backward_kernel, n, tok),
        out_shape=(part, part, part, jax.ShapeDtypeStruct((3, HEAD_DIM, length), bf16))
        + tuple(jax.ShapeDtypeStruct((w.shape[0] // shards, w.shape[1]), f32) for w in weights),
        in_specs=[any_spec] + [vmem] * 5 + [any_spec] * 3,
        out_specs=[any_spec] * 7,
        scratch_shapes=[
            pltpu.VMEM((HEAD_DIM, length), bf16),
            pltpu.VMEM((length, HEAD_DIM), bf16),
            pltpu.VMEM((length, HEAD_DIM), bf16),
            pltpu.VMEM((length, HEAD_DIM), bf16),
            pltpu.VMEM((length, HEAD_DIM), bf16),
            pltpu.VMEM((8, length), f32),
            pltpu.VMEM((HEAD_DIM, length), f32),
            pltpu.VMEM((3, HEAD_DIM, length), bf16),
            dma((n,)),
            dma((n,)),
            dma,
            dma((2, chips, 2)),
            dma((2, chips, 2)),
            dma((2,)),
            dma((chips, 2)),
            dma((chips, 2)),
            dma,
            dma,
        ]
        + halving_scratch(),
        compiler_params=pltpu.CompilerParams(
            collective_id=1, has_side_effects=True, vmem_limit_bytes=60 << 20
        ),
        name="attention_backward",
    )(
        d_t,
        q_all,
        k_all,
        v_all,
        o_all,
        lse_all,
        *(w.reshape(2, 4, 2, 2, w.shape[0] // shards, w.shape[1]) for w in weights),
    )


def exchange_kernel(scenes, n, count, *refs):
    sources, sinks = refs[:count], refs[count : 2 * count]
    send_sem, recv_sem, local_sem = refs[2 * count :]
    me = lax.axis_index("seq")
    scene = lax.axis_index("scene")
    mine = scene * n + me
    devices = scenes * n

    def peer(j):
        index = lax.rem(mine + j, devices)
        return index, (index // n, lax.rem(index, n))

    greet([peer(j)[1] for j in range(1, devices)])
    copies = []
    for a in range(count):
        copies.append(
            pltpu.make_async_copy(sources[a].at[mine], sinks[a].at[mine], local_sem.at[a])
        )
        copies[-1].start()
    for j in range(1, devices):
        index, device = peer(j)
        for a in range(count):
            copies.append(
                remote(
                    sources[a].at[index],
                    sinks[a].at[mine],
                    send_sem.at[a, j],
                    recv_sem.at[a, j],
                    device,
                )
            )
            copies[-1].start()
    for copy in copies:
        copy.wait()


def exchange(scenes, n, *arrays):
    any_spec = pl.BlockSpec(memory_space=pl.ANY)
    dma = pltpu.SemaphoreType.DMA
    count, devices = len(arrays), scenes * n
    return pl.pallas_call(
        functools.partial(exchange_kernel, scenes, n, count),
        out_shape=tuple(jax.ShapeDtypeStruct(a.shape, a.dtype) for a in arrays),
        in_specs=[any_spec] * count,
        out_specs=[any_spec] * count,
        scratch_shapes=[dma((count, devices)), dma((count, devices)), dma((count,))],
        compiler_params=pltpu.CompilerParams(collective_id=3, has_side_effects=True),
        name="exchange",
    )(*arrays)


def normalise(values):
    row_mean = jnp.mean(values, axis=-1, keepdims=True)
    centred = values - row_mean
    row_var = jnp.mean(centred * centred, axis=-1, keepdims=True)
    inverse = lax.rsqrt(row_var + norm_eps)
    return centred * inverse, inverse


def norm_back(grad, scaled, inverse, gain):
    weighted = grad * gain
    back = inverse * (
        weighted
        - jnp.mean(weighted, axis=-1, keepdims=True)
        - scaled * jnp.mean(weighted * scaled, axis=-1, keepdims=True)
    )
    return back, jnp.sum(grad * scaled, axis=0), jnp.sum(grad, axis=0)


def gelu_both(values):
    cubic = gelu_coef * (values + 0.044715 * values * values * values)
    bend = jnp.tanh(cubic)
    slope = gelu_coef * (1.0 + 3.0 * 0.044715 * values * values)
    grad = 0.5 * (1.0 + bend) + 0.5 * values * (1.0 - bend * bend) * slope
    return 0.5 * values * (1.0 + bend), grad


def layer_on_device(
    scenes,
    n,
    tokens,
    surface_mask,
    out_grad,
    w_query,
    w_key,
    w_value,
    w_out,
    w_up,
    w_down,
    b_query,
    b_value,
    b_out,
    b_up,
    b_down,
    gain_one,
    shift_one,
    gain_two,
    shift_two,
):
    _, tok, width = tokens.shape
    devices = scenes * n
    rows = tokens[0].astype(f32)
    scaled_one, inverse_one = normalise(rows)
    normed = (scaled_one * gain_one + shift_one).astype(bf16)
    normed_all = lax.all_gather(normed, "seq", axis=0, tiled=True)
    q_t = contract(w_query, normed, 0, 1) + b_query[:, None]
    q_t = (q_t.astype(bf16).astype(f32) * score_scale).astype(bf16)
    k_t = contract(w_key, normed, 0, 1).astype(bf16)
    v_t = (contract(w_value, normed, 0, 1) + b_value[:, None]).astype(bf16)
    att_t, q_all, k_all, v_all, o_all, lse_all = attention_forward(n, q_t, k_t, v_t)

    residual = rows + matmul_tn(att_t, w_out) + b_out
    scaled_two, inverse_two = normalise(residual)
    normed_two = (scaled_two * gain_two + shift_two).astype(bf16)
    hidden = matmul(normed_two, w_up) + b_up
    activated, gelu_grad = gelu_both(hidden)
    activated = activated.astype(bf16)
    block_out = (residual + matmul(activated, w_down) + b_down).astype(bf16)
    masked = out_grad[0] * surface_mask[0].astype(bf16)[:, None]
    grad_down = matmul_tn(activated, masked).astype(bf16)
    grad_bdown = jnp.sum(masked.astype(f32), axis=0)
    hidden_grad = (matmul_nt(masked, w_down) * gelu_grad).astype(bf16)
    grad_up = matmul_tn(normed_two, hidden_grad).astype(bf16)
    grad_bup = jnp.sum(hidden_grad.astype(f32), axis=0)
    norm_two_in = matmul_nt(hidden_grad, w_up)
    resid_part, grad_gain_two, grad_shift_two = norm_back(
        norm_two_in, scaled_two, inverse_two, gain_two
    )
    resid_grad = masked.astype(f32) + resid_part
    resid_low = resid_grad.astype(bf16)
    grad_out = matmul(att_t, resid_low).astype(bf16)
    grad_bout = jnp.sum(resid_low.astype(f32), axis=0)
    att_grad_t = matmul_nt(w_out, resid_low).astype(bf16)

    dq_t, dk_t, dv_t, heads_t, sum_down, sum_up, sum_out = attention_backward(
        n, att_grad_t, q_all, k_all, v_all, o_all, lse_all, grad_down, grad_up, grad_out
    )

    head_grads = matmul(heads_t.reshape(3 * HEAD_DIM, n * tok), normed_all)
    head_grads = head_grads.T.reshape(devices, width // devices, 3 * HEAD_DIM)
    norm_one_in = (
        contract(dq_t, w_query, 0, 1) + contract(dk_t, w_key, 0, 1) + contract(dv_t, w_value, 0, 1)
    )
    token_part, grad_gain_one, grad_shift_one = norm_back(
        norm_one_in, scaled_one, inverse_one, gain_one
    )
    tokens_grad = (resid_grad + token_part).astype(bf16)
    grad_bquery = jnp.sum(dq_t.astype(f32), axis=1)
    grad_bvalue = jnp.sum(dv_t.astype(f32), axis=1)
    small = [
        grad_bquery,
        grad_bvalue,
        grad_bout,
        grad_bup,
        grad_bdown,
        grad_gain_one,
        grad_shift_one,
        grad_gain_two,
        grad_shift_two,
    ]
    packed = jnp.concatenate([s.reshape(devices, -1) for s in small], axis=1)
    room = -packed.shape[1] % 1024
    packed = jnp.pad(packed, ((0, 0), (0, room))).reshape(devices, -1, 128)
    heads_got, small_got = exchange(scenes, n, head_grads, packed)
    heads_sum = heads_got.reshape(scenes, n, width // devices, 3, HEAD_DIM).sum(axis=0)
    weights = [
        jnp.moveaxis(heads_sum[:, :, i], 0, 1).reshape(width // devices, width) for i in range(3)
    ]
    vectors = small_got.reshape(devices, -1).sum(axis=0)
    parts, at = [], 0
    for s in small:
        size = s.shape[0] // devices
        parts.append(vectors[at : at + size])
        at += size
    bquery, bvalue, bout, bup, bdown, gone, sone, gtwo, stwo = parts
    return (
        block_out[None],
        tokens_grad[None],
        *weights,
        sum_out,
        sum_up,
        sum_down,
        bquery,
        bvalue,
        bout,
        bup,
        bdown,
        gone,
        sone,
        gtwo,
        stwo,
    )


def norm_rows(values, gain, shift):
    row_mean = jnp.mean(values, axis=-1, keepdims=True)
    centred = values - row_mean
    row_var = jnp.mean(centred * centred, axis=-1, keepdims=True)
    return centred * lax.rsqrt(row_var + norm_eps) * gain + shift


def gelu_tanh(values):
    return (
        0.5 * values * (1.0 + jnp.tanh(gelu_coef * (values + 0.044715 * values * values * values)))
    )


def take_pair(array_in, pair_index):
    pair_width = 2 * HEAD_DIM
    sliced = lax.dynamic_slice_in_dim(array_in, pair_index * pair_width, pair_width, 2)
    return sliced.reshape(sliced.shape[:2] + (2, HEAD_DIM))


def take_stats(array_in, pair_index):
    return lax.dynamic_slice_in_dim(array_in, pair_index * 2, 2, 1)


def join_pairs(stacked):
    moved = jnp.moveaxis(stacked, 0, 2)
    return moved.reshape(moved.shape[:2] + (moved.shape[2] * moved.shape[3],))


def join_stats(stacked):
    moved = jnp.moveaxis(stacked, 0, 1)
    return moved.reshape((moved.shape[0], moved.shape[1] * moved.shape[2], moved.shape[3]))


def merge_heads(pair_part):
    return pair_part.reshape(pair_part.shape[:2] + (2 * HEAD_DIM,))


def attend(q_scene, k_gathered, v_gathered):

    def attend_pair_step(unused, pair_index):
        q_pair = take_pair(q_scene, pair_index)
        k_pair = take_pair(k_gathered, pair_index)
        v_pair = take_pair(v_gathered, pair_index)
        scores = (
            jnp.einsum("sqhe,skhe->shqk", q_pair, k_pair, preferred_element_type=jnp.float32)
            * score_scale
        )
        row_max = jnp.max(scores, axis=-1, keepdims=True)
        shifted = jnp.exp(scores - row_max)
        row_sum = jnp.sum(shifted, axis=-1, keepdims=True)
        prob_low = (shifted / row_sum).astype(jnp.bfloat16)
        pair_out = jnp.einsum(
            "shqk,skhe->sqhe", prob_low, v_pair, preferred_element_type=jnp.float32
        )
        pair_lse = (row_max + jnp.log(row_sum))[..., 0]
        return (unused, (merge_heads(pair_out), pair_lse))

    pair_count = HEADS // 2
    _, (pair_outs, pair_lses) = lax.scan(
        attend_pair_step, jnp.zeros((), jnp.float32), jnp.arange(pair_count, dtype=jnp.int32)
    )
    return (join_pairs(pair_outs), join_stats(pair_lses))


def query_side(q_scene, k_gathered, v_gathered, row_lse, att_grad):

    def query_pair_step(unused, pair_index):
        q_pair = take_pair(q_scene, pair_index)
        k_pair = take_pair(k_gathered, pair_index)
        v_pair = take_pair(v_gathered, pair_index)
        d_pair = take_pair(att_grad, pair_index)
        l_pair = take_stats(row_lse, pair_index)
        scores = (
            jnp.einsum("sqhe,skhe->shqk", q_pair, k_pair, preferred_element_type=jnp.float32)
            * score_scale
        )
        attn_prob = jnp.exp(scores - l_pair[..., None])
        dprob = jnp.einsum("sqhe,skhe->shqk", d_pair, v_pair, preferred_element_type=jnp.float32)
        row_delta = jnp.sum(attn_prob * dprob, axis=-1)
        dscore = (attn_prob * (dprob - row_delta[..., None])).astype(jnp.bfloat16)
        q_part = (
            jnp.einsum("shqk,skhe->sqhe", dscore, k_pair, preferred_element_type=jnp.float32)
            * score_scale
        )
        results = (merge_heads(q_part), row_delta)
        prob_low = attn_prob.astype(jnp.bfloat16)
        k_part = (
            jnp.einsum("shqk,sqhe->skhe", dscore, q_pair, preferred_element_type=jnp.float32)
            * score_scale
        )
        v_part = jnp.einsum("shqk,sqhe->skhe", prob_low, d_pair, preferred_element_type=jnp.float32)
        results = results + (merge_heads(k_part), merge_heads(v_part))
        return (unused, results)

    pair_count = HEADS // 2
    _, results = lax.scan(
        query_pair_step, jnp.zeros((), jnp.float32), jnp.arange(pair_count, dtype=jnp.int32)
    )
    return results


def on_any_device(
    tokens,
    surface_mask,
    out_grad,
    w_query,
    w_key,
    w_value,
    w_out,
    w_up,
    w_down,
    b_query,
    b_value,
    b_out,
    b_up,
    b_down,
    gain_one,
    shift_one,
    gain_two,
    shift_two,
):
    scenes, local_len, model_width = tokens.shape
    row_count = scenes * local_len
    flat_rows = tokens.astype(jnp.float32).reshape(row_count, model_width)
    normed, norm_one_pull = jax.vjp(norm_rows, flat_rows, gain_one, shift_one)
    normed_low = normed.astype(jnp.bfloat16)
    q_low = (matmul(normed_low, w_query) + b_query).astype(jnp.bfloat16)
    k_low = matmul(normed_low, w_key).astype(jnp.bfloat16)
    v_low = (matmul(normed_low, w_value) + b_value).astype(jnp.bfloat16)
    q_scene = q_low.reshape(scenes, local_len, model_width)
    k_scene = k_low.reshape(scenes, local_len, model_width)
    v_scene = v_low.reshape(scenes, local_len, model_width)
    k_gathered, v_gathered = (
        lax.all_gather(k_scene, "seq", axis=1, tiled=True),
        lax.all_gather(v_scene, "seq", axis=1, tiled=True),
    )
    attended, row_lse = attend(q_scene, k_gathered, v_gathered)
    att_low = attended.reshape(row_count, model_width).astype(jnp.bfloat16)
    residual = flat_rows + matmul(att_low, w_out) + b_out
    normed_two, norm_two_pull = jax.vjp(norm_rows, residual, gain_two, shift_two)
    normed_two_low = normed_two.astype(jnp.bfloat16)
    hidden = matmul(normed_two_low, w_up) + b_up
    activated, gelu_pull = jax.vjp(gelu_tanh, hidden)
    act_low = activated.astype(jnp.bfloat16)
    block_rows = residual + matmul(act_low, w_down) + b_down
    block_out = block_rows.reshape(scenes, local_len, model_width).astype(jnp.bfloat16)
    masked_f = out_grad.astype(jnp.float32) * surface_mask.astype(jnp.float32)[..., None]
    masked_rows = masked_f.reshape(row_count, model_width)
    masked_low = masked_rows.astype(jnp.bfloat16)
    grad_down = matmul_tn(act_low, masked_low)
    grad_bdown = jnp.sum(masked_rows, axis=0)
    act_grad = matmul_nt(masked_low, w_down)
    hidden_low = gelu_pull(act_grad)[0].astype(jnp.bfloat16)
    grad_up = matmul_tn(normed_two_low, hidden_low)
    grad_bup = jnp.sum(hidden_low.astype(jnp.float32), axis=0)
    norm_two_in = matmul_nt(hidden_low, w_up)
    resid_part, grad_gain_two, grad_shift_two = norm_two_pull(norm_two_in)
    resid_grad = masked_rows + resid_part
    resid_low = resid_grad.astype(jnp.bfloat16)
    grad_out = matmul_tn(att_low, resid_low)
    grad_bout = jnp.sum(resid_low.astype(jnp.float32), axis=0)
    att_grad = (
        matmul_nt(resid_low, w_out).astype(jnp.bfloat16).reshape(scenes, local_len, model_width)
    )
    q_parts, delta_parts, k_parts, v_parts = query_side(
        q_scene, k_gathered, v_gathered, row_lse, att_grad
    )
    k_summed, v_summed = (
        lax.psum_scatter(
            k_parts.astype(jnp.bfloat16), "seq", scatter_dimension=2, tiled=True
        ).astype(jnp.float32),
        lax.psum_scatter(
            v_parts.astype(jnp.bfloat16), "seq", scatter_dimension=2, tiled=True
        ).astype(jnp.float32),
    )
    k_grad = join_pairs(k_summed)
    v_grad = join_pairs(v_summed)
    q_grad = join_pairs(q_parts)
    q_grad_low = q_grad.reshape(row_count, model_width).astype(jnp.bfloat16)
    k_grad_low = k_grad.reshape(row_count, model_width).astype(jnp.bfloat16)
    v_grad_low = v_grad.reshape(row_count, model_width).astype(jnp.bfloat16)
    grad_query = matmul_tn(normed_low, q_grad_low)
    grad_key = matmul_tn(normed_low, k_grad_low)
    grad_value = matmul_tn(normed_low, v_grad_low)
    grad_bquery = jnp.sum(q_grad_low.astype(jnp.float32), axis=0)
    grad_bvalue = jnp.sum(v_grad_low.astype(jnp.float32), axis=0)
    norm_one_in = (
        matmul_nt(q_grad_low, w_query)
        + matmul_nt(k_grad_low, w_key)
        + matmul_nt(v_grad_low, w_value)
    )
    token_part, grad_gain_one, grad_shift_one = norm_one_pull(norm_one_in)
    tokens_grad = (
        (resid_grad + token_part).reshape(scenes, local_len, model_width).astype(jnp.bfloat16)
    )
    (
        sum_query,
        sum_key,
        sum_value,
        sum_out,
        sum_bquery,
        sum_bvalue,
        sum_bout,
        sum_gain_one,
        sum_shift_one,
        sum_up,
        sum_down,
        sum_bup,
        sum_bdown,
        sum_gain_two,
        sum_shift_two,
    ) = (
        lax.psum_scatter(grad_query, ("scene", "seq"), scatter_dimension=0, tiled=True),
        lax.psum_scatter(grad_key, ("scene", "seq"), scatter_dimension=0, tiled=True),
        lax.psum_scatter(grad_value, ("scene", "seq"), scatter_dimension=0, tiled=True),
        lax.psum_scatter(grad_out, ("scene", "seq"), scatter_dimension=0, tiled=True),
        lax.psum_scatter(grad_bquery, ("scene", "seq"), scatter_dimension=0, tiled=True),
        lax.psum_scatter(grad_bvalue, ("scene", "seq"), scatter_dimension=0, tiled=True),
        lax.psum_scatter(grad_bout, ("scene", "seq"), scatter_dimension=0, tiled=True),
        lax.psum_scatter(grad_gain_one, ("scene", "seq"), scatter_dimension=0, tiled=True),
        lax.psum_scatter(grad_shift_one, ("scene", "seq"), scatter_dimension=0, tiled=True),
        lax.psum_scatter(grad_up, ("scene", "seq"), scatter_dimension=0, tiled=True),
        lax.psum_scatter(grad_down, ("scene", "seq"), scatter_dimension=0, tiled=True),
        lax.psum_scatter(grad_bup, ("scene", "seq"), scatter_dimension=0, tiled=True),
        lax.psum_scatter(grad_bdown, ("scene", "seq"), scatter_dimension=0, tiled=True),
        lax.psum_scatter(grad_gain_two, ("scene", "seq"), scatter_dimension=0, tiled=True),
        lax.psum_scatter(grad_shift_two, ("scene", "seq"), scatter_dimension=0, tiled=True),
    )
    return (
        block_out,
        tokens_grad,
        sum_query,
        sum_key,
        sum_value,
        sum_out,
        sum_up,
        sum_down,
        sum_bquery,
        sum_bvalue,
        sum_bout,
        sum_bup,
        sum_bdown,
        sum_gain_one,
        sum_shift_one,
        sum_gain_two,
        sum_shift_two,
    )


def solution(mesh):
    placed = (
        P("scene", "seq", None),
        P("scene", "seq"),
        P("scene", "seq", None),
        P(),
        P(),
        P(),
        P(),
        P(),
        P(),
        P(),
        P(),
        P(),
        P(),
        P(),
        P(),
        P(),
        P(),
        P(),
    )
    scenes, n = mesh.shape["scene"], mesh.shape["seq"]
    if (scenes, n) == (2, HEADS):
        on_device = functools.partial(layer_on_device, scenes, n)
    else:
        on_device = on_any_device
    return jax.shard_map(
        on_device,
        mesh=mesh,
        in_specs=placed,
        out_specs=(
            P("scene", "seq", None),
            P("scene", "seq", None),
            P(("scene", "seq"), None),
            P(("scene", "seq"), None),
            P(("scene", "seq"), None),
            P(("scene", "seq"), None),
            P(("scene", "seq"), None),
            P(("scene", "seq"), None),
            P(("scene", "seq")),
            P(("scene", "seq")),
            P(("scene", "seq")),
            P(("scene", "seq")),
            P(("scene", "seq")),
            P(("scene", "seq")),
            P(("scene", "seq")),
            P(("scene", "seq")),
            P(("scene", "seq")),
        ),
        check_vma=False,
    )
```

```python
import functools

import jax
import jax.numpy as jnp
from jax import lax
from jax.experimental import pallas as pl
from jax.experimental.pallas import tpu as pltpu
from jax.sharding import PartitionSpec as P

HEADS = 16
HEAD_DIM = 64
MESH = pl.DeviceIdType.MESH
f32 = jnp.float32
bf16 = jnp.bfloat16

norm_eps = 1e-05
score_scale = 0.125
gelu_coef = 0.7978845608028654


def matmul(left, right):
    return jnp.dot(left, right, preferred_element_type=jnp.float32)


def contract(left, right, left_dim, right_dim):
    return lax.dot_general(
        left, right, (((left_dim,), (right_dim,)), ((), ())), preferred_element_type=jnp.float32
    )


def matmul_tn(left, right):
    return contract(left, right, 0, 0)


def matmul_nt(left, right):
    return contract(left, right, 1, 1)


def greet(partners):
    barrier = pltpu.get_barrier_semaphore()
    for partner in partners:
        pl.semaphore_signal(barrier, inc=1, device_id=partner, device_id_type=MESH)
    pl.semaphore_wait(barrier, len(partners))


def remote(src, dst, send_sem, recv_sem, device):
    return pltpu.make_async_remote_copy(
        src_ref=src,
        dst_ref=dst,
        send_sem=send_sem,
        recv_sem=recv_sem,
        device_id=device,
        device_id_type=MESH,
    )


def forward_kernel(
    n,
    tok,
    qt_ref,
    kt_ref,
    vt_ref,
    att_ref,
    q_out,
    k_out,
    v_out,
    o_out,
    lse_out,
    q_all,
    k_all,
    v_all,
    k_nat,
    o_all,
    lse_all,
    att_send,
    in_send,
    in_recv,
    in_local,
    out_send,
    out_recv,
    out_local,
    save_sem,
):
    me = lax.axis_index("seq")
    scene = lax.axis_index("scene")
    chip, core = me // 2, lax.rem(me, 2)
    chips = n // 2
    length = n * tok
    others = [lax.rem(me + j, n) for j in range(1, n)]
    greet([(scene, other) for other in others])

    def rows(head):
        return pl.ds(pl.multiple_of(head * HEAD_DIM, HEAD_DIM), HEAD_DIM)

    def lanes(block, width=tok):
        return pl.ds(pl.multiple_of(block * width, width), width)

    pairs = ((kt_ref, k_all), (vt_ref, v_all), (qt_ref, q_all))
    copies = {}
    for a, (src, dst) in enumerate(pairs):
        for j in range(1, n):
            head = lax.rem(me + j, n)
            copies[a, j] = remote(
                src.at[rows(head), :],
                dst.at[:, lanes(me)],
                in_send.at[a, j],
                in_recv.at[a, j],
                (scene, head),
            )
            copies[a, j].start()
    local = [
        pltpu.make_async_copy(src.at[rows(me), :], dst.at[:, lanes(me)], in_local.at[a])
        for a, (src, dst) in enumerate(pairs)
    ]
    for copy in local:
        copy.start()
    for copy in local:
        copy.wait()
    for a in range(3):
        for j in range(1, n):
            copies[a, j].wait_recv()
    k_nat[...] = k_all[...].T
    saves = [
        pltpu.make_async_copy(src, dst, save_sem.at[a])
        for a, (src, dst) in enumerate(((q_all, q_out), (k_all, k_out), (v_all, v_out)))
    ]
    for copy in saves:
        copy.start()

    wide = 2 * tok
    key_block = length // 2

    def queries(step):
        target = lax.rem(chip + step, chips)
        span = lanes(target, wide)
        q_here = q_all[:, span]
        top = total = acc = None
        for block in range(length // key_block):
            keys = slice(block * key_block, (block + 1) * key_block)
            scores = contract(k_nat[keys, :], q_here, 1, 0)
            here = jnp.max(scores, axis=0, keepdims=True)
            new_top = here if top is None else jnp.maximum(top, here)
            shifted = jnp.exp(scores - new_top)
            part_sum = jnp.sum(shifted, axis=0, keepdims=True)
            part = contract(v_all[:, keys], shifted.astype(bf16), 1, 0)
            if top is None:
                total, acc = part_sum, part
            else:
                fade = jnp.exp(top - new_top)
                total, acc = total * fade + part_sum, acc * fade + part
            top = new_top
        out = acc / total
        o_all[:, span] = out
        lse_all[:, span] = jnp.broadcast_to(top + jnp.log(total), (8, wide))
        low = out.astype(bf16)
        att_send[step, 0] = low[:, :tok]
        att_send[step, 1] = low[:, tok:]
        return target

    def out_copy(step, target, flip):
        device = 2 * target + lax.rem(core + flip, 2)
        return remote(
            att_send.at[step, lax.rem(core + flip, 2)],
            att_ref.at[rows(me), :],
            out_send.at[step, flip],
            out_recv.at[step, flip],
            (scene, device),
        )

    queries(0)
    mine = pltpu.make_async_copy(att_send.at[0, core], att_ref.at[rows(me), :], out_local)
    mine.start()
    out_copy(0, chip, 1).start()

    def step_body(step, carry):
        target = queries(step)
        out_copy(step, target, 0).start()
        out_copy(step, target, 1).start()
        return carry

    lax.fori_loop(1, chips, step_body, 0)
    o_save = pltpu.make_async_copy(o_all, o_out, save_sem.at[3])
    l_save = pltpu.make_async_copy(lse_all, lse_out, save_sem.at[4])
    o_save.start()
    l_save.start()
    for a in range(3):
        for j in range(1, n):
            copies[a, j].wait_send()
    mine.wait()
    out_copy(0, chip, 1).wait()

    def drain(step, carry):
        target = lax.rem(chip + step, chips)
        out_copy(step, target, 0).wait()
        out_copy(step, target, 1).wait()
        return carry

    lax.fori_loop(1, chips, drain, 0)
    for copy in saves + [o_save, l_save]:
        copy.wait()


def attention_forward(n, q_t, k_t, v_t):
    tok = q_t.shape[1]
    length = n * tok
    any_spec = pl.BlockSpec(memory_space=pl.ANY)
    head_all = jax.ShapeDtypeStruct((HEAD_DIM, length), bf16)
    dma = pltpu.SemaphoreType.DMA
    return pl.pallas_call(
        functools.partial(forward_kernel, n, tok),
        out_shape=(
            jax.ShapeDtypeStruct(q_t.shape, bf16),
            head_all,
            head_all,
            head_all,
            jax.ShapeDtypeStruct((HEAD_DIM, length), f32),
            jax.ShapeDtypeStruct((8, length), f32),
        ),
        in_specs=[any_spec] * 3,
        out_specs=[any_spec] * 6,
        scratch_shapes=[
            pltpu.VMEM((HEAD_DIM, length), bf16),
            pltpu.VMEM((HEAD_DIM, length), bf16),
            pltpu.VMEM((HEAD_DIM, length), bf16),
            pltpu.VMEM((length, HEAD_DIM), bf16),
            pltpu.VMEM((HEAD_DIM, length), f32),
            pltpu.VMEM((8, length), f32),
            pltpu.VMEM((n // 2, 2, HEAD_DIM, tok), bf16),
            dma((3, n)),
            dma((3, n)),
            dma((3,)),
            dma((n // 2, 2)),
            dma((n // 2, 2)),
            dma,
            dma((5,)),
        ],
        compiler_params=pltpu.CompilerParams(
            collective_id=0, has_side_effects=True, vmem_limit_bytes=48 << 20
        ),
        name="attention_forward",
    )(q_t, k_t, v_t)


CHUNKS = 9
TICKS = CHUNKS + 4
SLOTS = 3


def halving_plan(full, got0, got1a, got1b, got2a, got2b, got3, got4, total, send_sem, recv_sem):
    me = lax.axis_index("seq")
    x = lax.axis_index("scene")
    core = lax.rem(me, 2)
    y = lax.rem(me // 2, 2)
    z0 = lax.rem(me // 4, 2)
    z1 = me // 8
    at_core = (x, me + 1 - 2 * core)
    at_x = (1 - x, me)
    at_y = (x, me + 2 - 4 * y)
    at_z0 = (x, me + 4 - 8 * z0)
    at_z1 = (x, me + 8 - 16 * z1)
    up, low = slice(0, 64), slice(64, 128)

    def copy_of(slot, c):
        src, dst, device = (
            lambda: (full.at[lax.rem(c, SLOTS), :, :, :, :, 1 - core], got0.at[c], at_core),
            lambda: (got0.at[c, 1 - x, :, :, :, up, :], got1a.at[c], at_x),
            lambda: (got0.at[c, :, :, :, 1 - y, low, :], got1b.at[c], at_y),
            lambda: (got1a.at[c, :, 1 - z0], got2a.at[c], at_z0),
            lambda: (got1b.at[c, 1 - x], got2b.at[c], at_x),
            lambda: (got2a.at[c, :, 1 - y], got3.at[c, :, up, :], at_y),
            lambda: (got2b.at[c, :, 1 - z0], got3.at[c, :, low, :], at_z0),
            lambda: (got3.at[c, 1 - z1], got4.at[c], at_z1),
        )[slot]()
        return remote(src, dst, send_sem.at[c, slot], recv_sem.at[c, slot], device)

    def sum1(c):
        copy_of(0, c).wait_recv()
        got0[c] = got0[c] + full[lax.rem(c, SLOTS), :, :, :, :, core]

    def start1(c):
        copy_of(1, c).start()
        copy_of(2, c).start()

    def stage2(c):
        copy_of(1, c).wait_recv()
        got1a[c] = got1a[c] + got0[c, x, :, :, :, up, :]
        copy_of(3, c).start()
        copy_of(2, c).wait_recv()
        got1b[c] = got1b[c] + got0[c, :, :, :, y, low, :]
        copy_of(4, c).start()

    def stage3(c):
        copy_of(3, c).wait_recv()
        got2a[c] = got2a[c] + got1a[c, :, z0]
        copy_of(5, c).start()
        copy_of(4, c).wait_recv()
        got2b[c] = got2b[c] + got1b[c, x]
        copy_of(6, c).start()

    def stage4(c):
        copy_of(5, c).wait_recv()
        got3[c, :, up, :] = got3[c, :, up, :] + got2a[c, :, y]
        copy_of(6, c).wait_recv()
        got3[c, :, low, :] = got3[c, :, low, :] + got2b[c, :, z0]
        copy_of(7, c).start()

    def stage5(c):
        copy_of(7, c).wait_recv()
        total[c] = got3[c, z1].astype(f32) + got4[c].astype(f32)

    def tick(when):
        for stage, c in (
            (stage5, when - 4),
            (stage4, when - 3),
            (stage3, when - 2),
            (stage2, when - 1),
            (start1, when + 1),
        ):

            @pl.when((c >= 0) & (c < CHUNKS))
            def _(stage=stage, c=c):
                stage(c)

    return copy_of, sum1, start1, tick


def tail_kernel(n, tok, *refs):
    (
        dt_ref,
        q_ref,
        k_ref,
        v_ref,
        o_ref,
        lse_ref,
        act_ref,
        masked_ref,
        two_ref,
        hidden_ref,
        att_ref,
        low_ref,
        normed_ref,
        wq_ref,
        wk_ref,
        wv_ref,
        tokens_ref,
        resid_ref,
        gain_ref,
        early_ref,
        early_up_ref,
        tokens_out,
        total,
        pack_got,
        small_got,
        small_up_got,
        q_all,
        k_all,
        v_all,
        d_all,
        q_nat,
        k_nat,
        v_nat,
        d_nat,
        o_all,
        lse_all,
        delta,
        dq_acc,
        low,
        act,
        masked,
        two,
        hidden,
        att,
        resid_low,
        act_t,
        two_t,
        full,
        got0,
        got1a,
        got1b,
        got2a,
        got2b,
        got3,
        got4,
        land,
        back_in,
        rows_in,
        resid,
        pack,
        small,
        small_up,
        load_sem,
        weight_sem,
        normed_sem,
        in_send,
        in_recv,
        in_local,
        kv_send,
        kv_recv,
        kv_local,
        q_send,
        q_recv,
        q_local,
        half_send,
        half_recv,
        pack_send,
        pack_recv,
        small_send,
        small_recv,
        small_up_send,
        small_up_recv,
        last_local,
    ) = refs
    me = lax.axis_index("seq")
    scene = lax.axis_index("scene")
    chip, core = me // 2, lax.rem(me, 2)
    chips = n // 2
    length = n * tok
    wide = 2 * tok
    devices = 2 * n
    width = masked.shape[1]
    mine = scene * n + me

    def rows(head):
        return pl.ds(pl.multiple_of(head * HEAD_DIM, HEAD_DIM), HEAD_DIM)

    def lanes(block, width=tok):
        return pl.ds(pl.multiple_of(block * width, width), width)

    def by_block(ref, block):
        return ref.at[:, 1024 * block : 1024 * block + 1024]

    loads = [
        pltpu.make_async_copy(src, dst, load_sem.at[i])
        for i, (src, dst) in enumerate(
            [(by_block(act_ref, i), act.at[tok * i : tok * i + tok, :]) for i in range(4)]
            + [
                (masked_ref, masked),
                (q_ref, q_all),
                (k_ref, k_all),
                (v_ref, v_all),
                (o_ref, o_all),
                (lse_ref, lse_all),
                (two_ref, two),
            ]
            + [(by_block(hidden_ref, i), hidden.at[tok * i : tok * i + tok, :]) for i in range(4)]
            + [
                (att_ref, att),
                (low_ref, resid_low),
                (early_ref, small.at[4:8]),
                (early_up_ref, small_up),
                (tokens_ref, rows_in),
                (resid_ref, resid),
            ]
        )
    ]
    for load in loads:
        load.start()

    def peer(j):
        index = lax.rem(mine + j, devices)
        return index, (index // n, lax.rem(index, n))

    greet([peer(j)[1] for j in range(1, devices)])

    copies = []
    for j in range(1, n):
        head = lax.rem(me + j, n)
        copies.append(
            remote(
                dt_ref.at[rows(head), :],
                d_all.at[:, lanes(me)],
                in_send.at[j],
                in_recv.at[j],
                (scene, head),
            )
        )
        copies[-1].start()
    local = pltpu.make_async_copy(dt_ref.at[rows(me), :], d_all.at[:, lanes(me)], in_local)
    local.start()

    half, sum1, start1, tick = halving_plan(
        full, got0, got1a, got1b, got2a, got2b, got3, got4, total, half_send, half_recv
    )

    def chunk_begin(c):
        @pl.when(c >= SLOTS)
        def _():
            half(0, c - SLOTS).wait_send()

        return lax.rem(c, SLOTS)

    def chunk_end(c):
        half(0, c).start()

        @pl.when(c >= 1)
        def _():
            sum1(c - 1)

    def down_chunk(c):
        slot = chunk_begin(c)
        columns = masked[:, lanes(c, 256)]
        for block in range(4):
            part = contract(act_t[1024 * block : 1024 * block + 1024, :], columns, 1, 0)
            full[slot, block // 2, block % 2] = part.astype(bf16).reshape(2, 2, 2, 128, 256)
        chunk_end(c)

    def narrow_chunk(c, left, right):
        slot = chunk_begin(c)
        for block in range(4):
            part = contract(left, right[:, 256 * block : 256 * block + 256], 1, 0)
            full[slot, :, :, :, :, :, 32 * block : 32 * block + 32, :] = part.astype(bf16).reshape(
                2, 2, 2, 2, 2, 32, 256
            )
        chunk_end(c)

    for block in range(4):
        loads[block].wait()
        act_t[1024 * block : 1024 * block + 1024, :] = act[tok * block : tok * block + tok, :].T
    loads[4].wait()

    def first_chunk(c, carry):
        down_chunk(c)

        @pl.when(c >= 1)
        def _():
            start1(c - 1)

        return carry

    lax.fori_loop(0, 3, first_chunk, 0)
    for load in loads[5:11]:
        load.wait()
    two_t[...] = two[...].T
    q_nat[...] = q_all[...].T
    k_nat[...] = k_all[...].T
    v_nat[...] = v_all[...].T
    dq_acc[...] = jnp.zeros_like(dq_acc)
    for load in loads[11:17]:
        load.wait()

    def chunk(step):
        @pl.when(step == 0)
        def _():
            down_chunk(step + 3)

        @pl.when((step >= 1) & (step < 5))
        def _():
            there = pl.ds(pl.multiple_of((step - 1) * tok, tok), tok)
            narrow_chunk(step + 3, two_t[...], hidden[there, :])

        @pl.when(step == 5)
        def _():
            narrow_chunk(step + 3, att[...], resid_low[...])

        @pl.when(step == 6)
        def _():
            sum1(CHUNKS - 1)

        @pl.when(step == 1)
        def _():
            normed_load(0).start()

        @pl.when(step == 5)
        def _():
            normed_load(1).start()

    def normed_load(i):
        return pltpu.make_async_copy(
            normed_ref.at[1024 * i : 1024 * i + 1024, :],
            (act, hidden)[i % 2],
            normed_sem.at[i % 2],
        )

    local.wait()
    for copy in copies:
        copy.wait_recv()
    d_nat[...] = d_all[...].T
    delta[...] = jnp.broadcast_to(
        jnp.sum(d_all[...].astype(f32) * o_all[...], axis=0, keepdims=True), delta.shape
    )

    def q_copy(step, flip):
        target = lax.rem(chip + step, chips)
        device = 2 * target + lax.rem(core + flip, 2)
        return remote(
            low.at[0, :, lanes(device)],
            land.at[0, rows(me), :],
            q_send.at[step, flip],
            q_recv.at[step, flip],
            (scene, device),
        )

    def kv_copy(a, step, flip):
        target = lax.rem(chip + step, chips)
        device = 2 * target + lax.rem(core + flip, 2)
        return remote(
            low.at[1 + a, :, lanes(device)],
            land.at[1 + a, rows(me), :],
            kv_send.at[a, step, flip],
            kv_recv.at[a, step, flip],
            (scene, device),
        )

    own = [
        pltpu.make_async_copy(low.at[a, :, lanes(me)], land.at[a, rows(me), :], sem)
        for a, sem in ((0, q_local), (1, kv_local.at[0]), (2, kv_local.at[1]))
    ]

    def keys(step, last):
        target = lax.rem(chip + step, chips)
        span = lanes(target, wide)
        k_here, v_here, kt_here = k_nat[span, :], v_nat[span, :], k_all[:, span]
        dk = dv = None
        for i in range(chips):
            if last:
                block = lax.rem(chip + i, chips)
                there = lanes(block, wide)
            else:
                there = slice(i * wide, (i + 1) * wide)
            scores = contract(k_here, q_all[:, there], 1, 0)
            prob = jnp.exp(scores - lse_all[0:1, there])
            dprob = contract(v_here, d_all[:, there], 1, 0)
            dscore = (prob * (dprob - delta[0:1, there])).astype(bf16)
            v_part = contract(prob.astype(bf16), d_nat[there, :], 1, 0)
            k_part = contract(dscore, q_nat[there, :], 1, 0)
            dk = k_part if dk is None else dk + k_part
            dv = v_part if dv is None else dv + v_part
            dq = dq_acc[:, there] + contract(kt_here, dscore, 1, 0)
            if last:
                low[0, :, there] = (dq * score_scale).astype(bf16)
                if i == 0:
                    own[0].start()
                else:
                    q_copy(i, 0).start()
                q_copy(i, 1).start()
            else:
                dq_acc[:, there] = dq
        low[1, :, span] = dk.astype(bf16).T
        low[2, :, span] = dv.astype(bf16).T

    def step_body(step, carry):
        chunk(step)
        tick(step + 1)
        keys(step, False)

        @pl.when(step == 0)
        def _():
            own[1].start()
            own[2].start()

        for a in range(2):

            @pl.when(step > 0)
            def _(a=a):
                kv_copy(a, step, 0).start()

            kv_copy(a, step, 1).start()
        return carry

    lax.fori_loop(0, chips - 1, step_body, 0)
    for c in range(CHUNKS - SLOTS, CHUNKS):
        half(0, c).wait_send()
    weight_loads = []
    for a, ref in enumerate((wq_ref, wk_ref, wv_ref)):
        for block in range(4):
            weight_loads.append(
                pltpu.make_async_copy(
                    ref.at[:, :, :, :, 256 * block : 256 * block + 256],
                    full.at[a, block // 2, block % 2],
                    weight_sem.at[a, block],
                )
            )
            weight_loads[-1].start()
    tick(8)
    keys(chips - 1, True)
    for a in range(2):
        kv_copy(a, chips - 1, 0).start()
        kv_copy(a, chips - 1, 1).start()
    tick(9)

    head_acc = None
    for i in range(length // 1024):
        normed_load(i).wait()
        left = low[:, :, 1024 * i : 1024 * i + 1024].reshape(3 * HEAD_DIM, 1024)
        part = contract(left, (act, hidden)[i % 2][...], 1, 0)
        head_acc = part if head_acc is None else head_acc + part
        if i + 2 < length // 1024:
            normed_load(i + 2).start()
    tick(10)
    by_row = head_acc.T
    share = width // devices
    pack[:, :share, :] = by_row[:, : 2 * HEAD_DIM].astype(bf16).reshape(devices, share, 2 * HEAD_DIM)
    third = by_row[:, 2 * HEAD_DIM :].astype(bf16).reshape(devices, 2, share // 2, HEAD_DIM)
    pack[:, share:, :] = jnp.concatenate([third[:, 0], third[:, 1]], axis=-1)

    def pack_copy(j):
        index, device = peer(j)
        return remote(
            pack.at[index], pack_got.at[mine], pack_send.at[j], pack_recv.at[j], device
        )

    def small_copy(j):
        index, device = peer(j)
        return remote(
            small.at[:, lanes(index // 4, 128)],
            small_got.at[mine],
            small_send.at[j],
            small_recv.at[j],
            device,
        )

    def small_up_copy(j):
        index, device = peer(j)
        return remote(
            small_up.at[index], small_up_got.at[mine], small_up_send.at[j], small_up_recv.at[j], device
        )

    kept = [
        pltpu.make_async_copy(pack.at[mine], pack_got.at[mine], last_local.at[0]),
        pltpu.make_async_copy(
            small.at[:, lanes(mine // 4, 128)], small_got.at[mine], last_local.at[1]
        ),
        pltpu.make_async_copy(small_up.at[mine], small_up_got.at[mine], last_local.at[2]),
    ]
    loads[17].wait()
    loads[18].wait()
    kept[0].start()
    kept[2].start()

    def pack_body(j, carry):
        pack_copy(j).start()
        small_up_copy(j).start()
        return carry

    lax.fori_loop(1, devices, pack_body, 0)
    tick(11)

    for copy in own:
        copy.wait()
    for step in range(chips):
        for flip in range(2):
            if step or flip:
                kv_copy(0, step, flip).wait_recv()
                kv_copy(1, step, flip).wait_recv()
                q_copy(step, flip).wait_recv()
    for load in loads[19:] + weight_loads:
        load.wait()
    for i in range(4):
        part = None
        for a in range(3):
            left = jnp.concatenate(
                [full[a, b // 2, b % 2, i // 2, i % 2].reshape(256, 256) for b in range(4)], axis=1
            )
            here = contract(left, land[a], 1, 0)
            part = here if part is None else part + here
        back_in[:, 256 * i : 256 * i + 256] = part.T
    back = back_in[...]
    scaled, inverse = normalise(rows_in[...].astype(f32))
    token_part, gain_grad, shift_grad = norm_back(back, scaled, inverse, gain_ref[...])
    tokens_out[...] = (resid[...] + token_part).astype(bf16)
    ones = jnp.ones((8, tok), bf16)
    small[0:1, :] = contract(ones, land[0], 1, 1)[0:1]
    small[1:2, :] = contract(ones, land[2], 1, 1)[0:1]
    small[2:3, :] = gain_grad[None]
    small[3:4, :] = shift_grad[None]
    kept[1].start()

    def small_body(j, carry):
        small_copy(j).start()
        return carry

    lax.fori_loop(1, devices, small_body, 0)

    tick(12)
    for copy in kept:
        copy.wait()

    def arrive(j, carry):
        pack_copy(j).wait()
        small_up_copy(j).wait()
        small_copy(j).wait()
        return carry

    lax.fori_loop(1, devices, arrive, 0)
    for copy in copies:
        copy.wait_send()
    for step in range(chips):
        for flip in range(2):
            if step or flip:
                kv_copy(0, step, flip).wait_send()
                kv_copy(1, step, flip).wait_send()
                q_copy(step, flip).wait_send()

    def settle(c, carry):
        for slot in range(1, 8):
            half(slot, c).wait_send()
        return carry

    lax.fori_loop(0, CHUNKS, settle, 0)


def tail(n, tok, width, hidden_width, *arrays):
    length = n * tok
    chips = n // 2
    devices = 2 * n
    share = width // devices
    any_spec = pl.BlockSpec(memory_space=pl.ANY)
    vmem = pl.BlockSpec(memory_space=pltpu.VMEM)
    dma = pltpu.SemaphoreType.DMA

    def space(*shape, kind=bf16):
        return pltpu.VMEM(shape, kind)

    def out(*shape, kind=f32):
        return jax.ShapeDtypeStruct(shape, kind)

    pieces = CHUNKS
    scratch = (
        [space(HEAD_DIM, length)] * 4
        + [space(length, HEAD_DIM)] * 4
        + [
            space(HEAD_DIM, length, kind=f32),
            space(8, length, kind=f32),
            space(8, length, kind=f32),
            space(HEAD_DIM, length, kind=f32),
            space(3, HEAD_DIM, length),
            space(hidden_width // 1024 * tok, 1024),
            space(tok, width),
            space(tok, width),
            space(hidden_width // 1024 * tok, 1024),
            space(width, tok),
            space(tok, width),
            space(hidden_width, tok),
            space(width, tok),
            space(SLOTS, 2, 2, 2, 2, 2, 128, 256),
            space(pieces, 2, 2, 2, 2, 128, 256),
            space(pieces, 2, 2, 2, 64, 256),
            space(pieces, 2, 2, 2, 64, 256),
            space(pieces, 2, 2, 64, 256),
            space(pieces, 2, 2, 64, 256),
            space(pieces, 2, 128, 256),
            space(pieces, 128, 256),
            space(3, width, tok),
            space(tok, width, kind=f32),
            space(tok, width),
            space(tok, width, kind=f32),
            space(devices, share + share // 2, 128),
            space(8, width, kind=f32),
            space(devices, 8, 128, kind=f32),
            dma((21,)),
            dma((3, 4)),
            dma((2,)),
            dma((n,)),
            dma((n,)),
            dma,
            dma((2, chips, 2)),
            dma((2, chips, 2)),
            dma((2,)),
            dma((chips, 2)),
            dma((chips, 2)),
            dma,
            dma((pieces, 8)),
            dma((pieces, 8)),
        ]
        + [dma((devices,))] * 6
        + [dma((3,))]
    )
    in_specs = [any_spec] * 21
    in_specs[18] = vmem
    return pl.pallas_call(
        functools.partial(tail_kernel, n, tok),
        out_shape=(
            out(tok, width, kind=bf16),
            out(pieces, 128, 256),
            out(devices, share + share // 2, 128, kind=bf16),
            out(devices, 8, 128),
            out(devices, 8, 128),
        ),
        in_specs=in_specs,
        out_specs=[vmem] * 5,
        scratch_shapes=scratch,
        compiler_params=pltpu.CompilerParams(
            collective_id=1, has_side_effects=True, vmem_limit_bytes=63 << 20
        ),
        name="tail",
    )(*arrays)


def finish_kernel(n, *refs):
    tokens_in, total, pack_got, small_got, small_up_got, tokens_out = refs[:6]
    query_out, key_out, value_out, out_out, up_out, down_out = refs[6:12]
    vectors, up_vector = refs[12:20], refs[20]
    tokens_out[...] = tokens_in[...]
    mine = lax.axis_index("scene") * n + lax.axis_index("seq")
    share = query_out.shape[0]
    for head in range(0, n, 2):
        pair = [
            pack_got[head + i].astype(f32) + pack_got[n + head + i].astype(f32) for i in range(2)
        ]
        columns = slice(head * HEAD_DIM, head * HEAD_DIM + 2 * HEAD_DIM)

        def joined(first, last, start):
            return jnp.concatenate(
                [part[first:last, start : start + HEAD_DIM] for part in pair], axis=1
            )

        query_out[:, columns] = joined(0, share, 0)
        key_out[:, columns] = joined(0, share, HEAD_DIM)
        value_out[: share // 2, columns] = joined(share, share + share // 2, 0)
        value_out[share // 2 :, columns] = joined(share, share + share // 2, HEAD_DIM)
    for i in range(4):
        down_out[:, 256 * i : 256 * i + 256] = total[i]
        out_out[:, 256 * i : 256 * i + 256] = total[8, 32 * i : 32 * i + 32, :]
    for i in range(16):
        up_out[:, 256 * i : 256 * i + 256] = total[4 + i // 4, 32 * (i % 4) : 32 * (i % 4) + 32, :]
    turn = lax.rem(128 - 32 * lax.rem(mine, 4), 128)
    sums = pltpu.roll(jnp.sum(small_got[...], axis=0), turn, 1)
    for i, vector in enumerate(vectors):
        vector[...] = sums[i, :share]
    up_vector[...] = jnp.sum(small_up_got[...], axis=0)[0]


def finish(n, tokens_grad, total, pack_got, small_got, small_up_got):
    tok, width = tokens_grad.shape
    devices = 2 * n
    share = width // devices
    vmem = pl.BlockSpec(memory_space=pltpu.VMEM)

    def out(*shape):
        return jax.ShapeDtypeStruct(shape, f32)

    return pl.pallas_call(
        functools.partial(finish_kernel, n),
        out_shape=(
            jax.ShapeDtypeStruct((tok, width), bf16),
            out(share, width),
            out(share, width),
            out(share, width),
            out(share, width),
            out(share, 4 * width),
            out(4 * share, width),
        )
        + (out(share),) * 8
        + (out(4 * share),),
        in_specs=[vmem] * 5,
        out_specs=[vmem] * 16,
        compiler_params=pltpu.CompilerParams(vmem_limit_bytes=60 << 20),
        name="finish",
    )(tokens_grad, total, pack_got, small_got, small_up_got)


def normalise(values):
    row_mean = jnp.mean(values, axis=-1, keepdims=True)
    centred = values - row_mean
    row_var = jnp.mean(centred * centred, axis=-1, keepdims=True)
    inverse = lax.rsqrt(row_var + norm_eps)
    return centred * inverse, inverse


def norm_back(grad, scaled, inverse, gain):
    weighted = grad * gain
    back = inverse * (
        weighted
        - jnp.mean(weighted, axis=-1, keepdims=True)
        - scaled * jnp.mean(weighted * scaled, axis=-1, keepdims=True)
    )
    return back, jnp.sum(grad * scaled, axis=0), jnp.sum(grad, axis=0)


def gelu_both(values):
    cubic = gelu_coef * (values + 0.044715 * values * values * values)
    bend = jnp.tanh(cubic)
    slope = gelu_coef * (1.0 + 3.0 * 0.044715 * values * values)
    grad = 0.5 * (1.0 + bend) + 0.5 * values * (1.0 - bend * bend) * slope
    return 0.5 * values * (1.0 + bend), grad


def layer_on_device(
    scenes,
    n,
    tokens,
    surface_mask,
    out_grad,
    w_query,
    w_key,
    w_value,
    w_out,
    w_up,
    w_down,
    b_query,
    b_value,
    b_out,
    b_up,
    b_down,
    gain_one,
    shift_one,
    gain_two,
    shift_two,
):
    _, tok, width = tokens.shape
    devices = scenes * n
    rows = tokens[0].astype(f32)
    scaled_one, inverse_one = normalise(rows)
    normed = (scaled_one * gain_one + shift_one).astype(bf16)
    normed_all = lax.all_gather(normed, "seq", axis=0, tiled=True)
    q_t = contract(w_query, normed, 0, 1) + b_query[:, None]
    q_t = (q_t.astype(bf16).astype(f32) * score_scale).astype(bf16)
    k_t = contract(w_key, normed, 0, 1).astype(bf16)
    v_t = (contract(w_value, normed, 0, 1) + b_value[:, None]).astype(bf16)
    att_t, q_all, k_all, v_all, o_all, lse_all = attention_forward(n, q_t, k_t, v_t)

    residual = rows + matmul_tn(att_t, w_out) + b_out
    scaled_two, inverse_two = normalise(residual)
    normed_two = (scaled_two * gain_two + shift_two).astype(bf16)
    hidden = matmul(normed_two, w_up) + b_up
    activated, gelu_grad = gelu_both(hidden)
    activated = activated.astype(bf16)
    block_out = (residual + matmul(activated, w_down) + b_down).astype(bf16)
    masked = out_grad[0] * surface_mask[0].astype(bf16)[:, None]
    grad_bdown = jnp.sum(masked.astype(f32), axis=0)
    hidden_grad = (matmul_nt(masked, w_down) * gelu_grad).astype(bf16)
    grad_bup = jnp.sum(hidden_grad.astype(f32), axis=0)
    norm_two_in = matmul_nt(hidden_grad, w_up)
    resid_part, grad_gain_two, grad_shift_two = norm_back(
        norm_two_in, scaled_two, inverse_two, gain_two
    )
    resid_grad = masked.astype(f32) + resid_part
    resid_low = resid_grad.astype(bf16)
    grad_bout = jnp.sum(resid_low.astype(f32), axis=0)
    att_grad_t = matmul_nt(w_out, resid_low).astype(bf16)

    early = jnp.stack([grad_bout, grad_bdown, grad_gain_two, grad_shift_two])
    early_up = jnp.broadcast_to(grad_bup.reshape(devices, 1, -1), (devices, 8, 128))
    arrived = tail(
        n,
        tok,
        width,
        w_up.shape[1],
        att_grad_t,
        q_all,
        k_all,
        v_all,
        o_all,
        lse_all,
        activated,
        masked,
        normed_two,
        hidden_grad,
        att_t,
        resid_low,
        normed_all,
        *(w.reshape(2, 2, 2, 128, width) for w in (w_query, w_key, w_value)),
        tokens[0],
        resid_grad,
        gain_one[None],
        early,
        early_up,
    )
    tokens_grad, *sums = finish(n, *arrived)
    bquery, bvalue, gone, sone, bout, bdown, gtwo, stwo, bup = sums[6:]
    return (
        block_out[None],
        tokens_grad[None],
        *sums[:6],
        bquery,
        bvalue,
        bout,
        bup,
        bdown,
        gone,
        sone,
        gtwo,
        stwo,
    )


def norm_rows(values, gain, shift):
    row_mean = jnp.mean(values, axis=-1, keepdims=True)
    centred = values - row_mean
    row_var = jnp.mean(centred * centred, axis=-1, keepdims=True)
    return centred * lax.rsqrt(row_var + norm_eps) * gain + shift


def gelu_tanh(values):
    return (
        0.5 * values * (1.0 + jnp.tanh(gelu_coef * (values + 0.044715 * values * values * values)))
    )


def take_pair(array_in, pair_index):
    pair_width = 2 * HEAD_DIM
    sliced = lax.dynamic_slice_in_dim(array_in, pair_index * pair_width, pair_width, 2)
    return sliced.reshape(sliced.shape[:2] + (2, HEAD_DIM))


def take_stats(array_in, pair_index):
    return lax.dynamic_slice_in_dim(array_in, pair_index * 2, 2, 1)


def join_pairs(stacked):
    moved = jnp.moveaxis(stacked, 0, 2)
    return moved.reshape(moved.shape[:2] + (moved.shape[2] * moved.shape[3],))


def join_stats(stacked):
    moved = jnp.moveaxis(stacked, 0, 1)
    return moved.reshape((moved.shape[0], moved.shape[1] * moved.shape[2], moved.shape[3]))


def merge_heads(pair_part):
    return pair_part.reshape(pair_part.shape[:2] + (2 * HEAD_DIM,))


def attend(q_scene, k_gathered, v_gathered):

    def attend_pair_step(unused, pair_index):
        q_pair = take_pair(q_scene, pair_index)
        k_pair = take_pair(k_gathered, pair_index)
        v_pair = take_pair(v_gathered, pair_index)
        scores = (
            jnp.einsum("sqhe,skhe->shqk", q_pair, k_pair, preferred_element_type=jnp.float32)
            * score_scale
        )
        row_max = jnp.max(scores, axis=-1, keepdims=True)
        shifted = jnp.exp(scores - row_max)
        row_sum = jnp.sum(shifted, axis=-1, keepdims=True)
        prob_low = (shifted / row_sum).astype(jnp.bfloat16)
        pair_out = jnp.einsum(
            "shqk,skhe->sqhe", prob_low, v_pair, preferred_element_type=jnp.float32
        )
        pair_lse = (row_max + jnp.log(row_sum))[..., 0]
        return (unused, (merge_heads(pair_out), pair_lse))

    pair_count = HEADS // 2
    _, (pair_outs, pair_lses) = lax.scan(
        attend_pair_step, jnp.zeros((), jnp.float32), jnp.arange(pair_count, dtype=jnp.int32)
    )
    return (join_pairs(pair_outs), join_stats(pair_lses))


def query_side(q_scene, k_gathered, v_gathered, row_lse, att_grad):

    def query_pair_step(unused, pair_index):
        q_pair = take_pair(q_scene, pair_index)
        k_pair = take_pair(k_gathered, pair_index)
        v_pair = take_pair(v_gathered, pair_index)
        d_pair = take_pair(att_grad, pair_index)
        l_pair = take_stats(row_lse, pair_index)
        scores = (
            jnp.einsum("sqhe,skhe->shqk", q_pair, k_pair, preferred_element_type=jnp.float32)
            * score_scale
        )
        attn_prob = jnp.exp(scores - l_pair[..., None])
        dprob = jnp.einsum("sqhe,skhe->shqk", d_pair, v_pair, preferred_element_type=jnp.float32)
        row_delta = jnp.sum(attn_prob * dprob, axis=-1)
        dscore = (attn_prob * (dprob - row_delta[..., None])).astype(jnp.bfloat16)
        q_part = (
            jnp.einsum("shqk,skhe->sqhe", dscore, k_pair, preferred_element_type=jnp.float32)
            * score_scale
        )
        results = (merge_heads(q_part), row_delta)
        prob_low = attn_prob.astype(jnp.bfloat16)
        k_part = (
            jnp.einsum("shqk,sqhe->skhe", dscore, q_pair, preferred_element_type=jnp.float32)
            * score_scale
        )
        v_part = jnp.einsum("shqk,sqhe->skhe", prob_low, d_pair, preferred_element_type=jnp.float32)
        results = results + (merge_heads(k_part), merge_heads(v_part))
        return (unused, results)

    pair_count = HEADS // 2
    _, results = lax.scan(
        query_pair_step, jnp.zeros((), jnp.float32), jnp.arange(pair_count, dtype=jnp.int32)
    )
    return results


def on_any_device(
    tokens,
    surface_mask,
    out_grad,
    w_query,
    w_key,
    w_value,
    w_out,
    w_up,
    w_down,
    b_query,
    b_value,
    b_out,
    b_up,
    b_down,
    gain_one,
    shift_one,
    gain_two,
    shift_two,
):
    scenes, local_len, model_width = tokens.shape
    row_count = scenes * local_len
    flat_rows = tokens.astype(jnp.float32).reshape(row_count, model_width)
    normed, norm_one_pull = jax.vjp(norm_rows, flat_rows, gain_one, shift_one)
    normed_low = normed.astype(jnp.bfloat16)
    q_low = (matmul(normed_low, w_query) + b_query).astype(jnp.bfloat16)
    k_low = matmul(normed_low, w_key).astype(jnp.bfloat16)
    v_low = (matmul(normed_low, w_value) + b_value).astype(jnp.bfloat16)
    q_scene = q_low.reshape(scenes, local_len, model_width)
    k_scene = k_low.reshape(scenes, local_len, model_width)
    v_scene = v_low.reshape(scenes, local_len, model_width)
    k_gathered, v_gathered = (
        lax.all_gather(k_scene, "seq", axis=1, tiled=True),
        lax.all_gather(v_scene, "seq", axis=1, tiled=True),
    )
    attended, row_lse = attend(q_scene, k_gathered, v_gathered)
    att_low = attended.reshape(row_count, model_width).astype(jnp.bfloat16)
    residual = flat_rows + matmul(att_low, w_out) + b_out
    normed_two, norm_two_pull = jax.vjp(norm_rows, residual, gain_two, shift_two)
    normed_two_low = normed_two.astype(jnp.bfloat16)
    hidden = matmul(normed_two_low, w_up) + b_up
    activated, gelu_pull = jax.vjp(gelu_tanh, hidden)
    act_low = activated.astype(jnp.bfloat16)
    block_rows = residual + matmul(act_low, w_down) + b_down
    block_out = block_rows.reshape(scenes, local_len, model_width).astype(jnp.bfloat16)
    masked_f = out_grad.astype(jnp.float32) * surface_mask.astype(jnp.float32)[..., None]
    masked_rows = masked_f.reshape(row_count, model_width)
    masked_low = masked_rows.astype(jnp.bfloat16)
    grad_down = matmul_tn(act_low, masked_low)
    grad_bdown = jnp.sum(masked_rows, axis=0)
    act_grad = matmul_nt(masked_low, w_down)
    hidden_low = gelu_pull(act_grad)[0].astype(jnp.bfloat16)
    grad_up = matmul_tn(normed_two_low, hidden_low)
    grad_bup = jnp.sum(hidden_low.astype(jnp.float32), axis=0)
    norm_two_in = matmul_nt(hidden_low, w_up)
    resid_part, grad_gain_two, grad_shift_two = norm_two_pull(norm_two_in)
    resid_grad = masked_rows + resid_part
    resid_low = resid_grad.astype(jnp.bfloat16)
    grad_out = matmul_tn(att_low, resid_low)
    grad_bout = jnp.sum(resid_low.astype(jnp.float32), axis=0)
    att_grad = (
        matmul_nt(resid_low, w_out).astype(jnp.bfloat16).reshape(scenes, local_len, model_width)
    )
    q_parts, delta_parts, k_parts, v_parts = query_side(
        q_scene, k_gathered, v_gathered, row_lse, att_grad
    )
    k_summed, v_summed = (
        lax.psum_scatter(
            k_parts.astype(jnp.bfloat16), "seq", scatter_dimension=2, tiled=True
        ).astype(jnp.float32),
        lax.psum_scatter(
            v_parts.astype(jnp.bfloat16), "seq", scatter_dimension=2, tiled=True
        ).astype(jnp.float32),
    )
    k_grad = join_pairs(k_summed)
    v_grad = join_pairs(v_summed)
    q_grad = join_pairs(q_parts)
    q_grad_low = q_grad.reshape(row_count, model_width).astype(jnp.bfloat16)
    k_grad_low = k_grad.reshape(row_count, model_width).astype(jnp.bfloat16)
    v_grad_low = v_grad.reshape(row_count, model_width).astype(jnp.bfloat16)
    grad_query = matmul_tn(normed_low, q_grad_low)
    grad_key = matmul_tn(normed_low, k_grad_low)
    grad_value = matmul_tn(normed_low, v_grad_low)
    grad_bquery = jnp.sum(q_grad_low.astype(jnp.float32), axis=0)
    grad_bvalue = jnp.sum(v_grad_low.astype(jnp.float32), axis=0)
    norm_one_in = (
        matmul_nt(q_grad_low, w_query)
        + matmul_nt(k_grad_low, w_key)
        + matmul_nt(v_grad_low, w_value)
    )
    token_part, grad_gain_one, grad_shift_one = norm_one_pull(norm_one_in)
    tokens_grad = (
        (resid_grad + token_part).reshape(scenes, local_len, model_width).astype(jnp.bfloat16)
    )
    (
        sum_query,
        sum_key,
        sum_value,
        sum_out,
        sum_bquery,
        sum_bvalue,
        sum_bout,
        sum_gain_one,
        sum_shift_one,
        sum_up,
        sum_down,
        sum_bup,
        sum_bdown,
        sum_gain_two,
        sum_shift_two,
    ) = (
        lax.psum_scatter(grad_query, ("scene", "seq"), scatter_dimension=0, tiled=True),
        lax.psum_scatter(grad_key, ("scene", "seq"), scatter_dimension=0, tiled=True),
        lax.psum_scatter(grad_value, ("scene", "seq"), scatter_dimension=0, tiled=True),
        lax.psum_scatter(grad_out, ("scene", "seq"), scatter_dimension=0, tiled=True),
        lax.psum_scatter(grad_bquery, ("scene", "seq"), scatter_dimension=0, tiled=True),
        lax.psum_scatter(grad_bvalue, ("scene", "seq"), scatter_dimension=0, tiled=True),
        lax.psum_scatter(grad_bout, ("scene", "seq"), scatter_dimension=0, tiled=True),
        lax.psum_scatter(grad_gain_one, ("scene", "seq"), scatter_dimension=0, tiled=True),
        lax.psum_scatter(grad_shift_one, ("scene", "seq"), scatter_dimension=0, tiled=True),
        lax.psum_scatter(grad_up, ("scene", "seq"), scatter_dimension=0, tiled=True),
        lax.psum_scatter(grad_down, ("scene", "seq"), scatter_dimension=0, tiled=True),
        lax.psum_scatter(grad_bup, ("scene", "seq"), scatter_dimension=0, tiled=True),
        lax.psum_scatter(grad_bdown, ("scene", "seq"), scatter_dimension=0, tiled=True),
        lax.psum_scatter(grad_gain_two, ("scene", "seq"), scatter_dimension=0, tiled=True),
        lax.psum_scatter(grad_shift_two, ("scene", "seq"), scatter_dimension=0, tiled=True),
    )
    return (
        block_out,
        tokens_grad,
        sum_query,
        sum_key,
        sum_value,
        sum_out,
        sum_up,
        sum_down,
        sum_bquery,
        sum_bvalue,
        sum_bout,
        sum_bup,
        sum_bdown,
        sum_gain_one,
        sum_shift_one,
        sum_gain_two,
        sum_shift_two,
    )


def solution(mesh):
    placed = (
        P("scene", "seq", None),
        P("scene", "seq"),
        P("scene", "seq", None),
        P(),
        P(),
        P(),
        P(),
        P(),
        P(),
        P(),
        P(),
        P(),
        P(),
        P(),
        P(),
        P(),
        P(),
        P(),
    )
    scenes, n = mesh.shape["scene"], mesh.shape["seq"]
    if (scenes, n) == (2, HEADS):
        on_device = functools.partial(layer_on_device, scenes, n)
    else:
        on_device = on_any_device
    return jax.shard_map(
        on_device,
        mesh=mesh,
        in_specs=placed,
        out_specs=(
            P("scene", "seq", None),
            P("scene", "seq", None),
            P(("scene", "seq"), None),
            P(("scene", "seq"), None),
            P(("scene", "seq"), None),
            P(("scene", "seq"), None),
            P(("scene", "seq"), None),
            P(("scene", "seq"), None),
            P(("scene", "seq")),
            P(("scene", "seq")),
            P(("scene", "seq")),
            P(("scene", "seq")),
            P(("scene", "seq")),
            P(("scene", "seq")),
            P(("scene", "seq")),
            P(("scene", "seq")),
            P(("scene", "seq")),
        ),
        check_vma=False,
    )
```

```python
import functools

import jax
import jax.numpy as jnp
from jax import lax
from jax.experimental import pallas as pl
from jax.experimental.pallas import tpu as pltpu
from jax.sharding import PartitionSpec as P

HEADS = 16
HEAD_DIM = 64
MESH = pl.DeviceIdType.MESH
f32 = jnp.float32
bf16 = jnp.bfloat16

norm_eps = 1e-05
score_scale = 0.125
FORWARD_LIMIT = 60 << 20
gelu_coef = 0.7978845608028654


def matmul(left, right):
    return jnp.dot(left, right, preferred_element_type=jnp.float32)


def contract(left, right, left_dim, right_dim):
    return lax.dot_general(
        left, right, (((left_dim,), (right_dim,)), ((), ())), preferred_element_type=jnp.float32
    )


def matmul_tn(left, right):
    return contract(left, right, 0, 0)


def matmul_nt(left, right):
    return contract(left, right, 1, 1)


def normalise(values):
    row_mean = jnp.mean(values, axis=-1, keepdims=True)
    centred = values - row_mean
    row_var = jnp.mean(centred * centred, axis=-1, keepdims=True)
    inverse = lax.rsqrt(row_var + norm_eps)
    return centred * inverse, inverse


def norm_back(grad, scaled, inverse, gain):
    weighted = grad * gain
    back = inverse * (
        weighted
        - jnp.mean(weighted, axis=-1, keepdims=True)
        - scaled * jnp.mean(weighted * scaled, axis=-1, keepdims=True)
    )
    return back, jnp.sum(grad * scaled, axis=0), jnp.sum(grad, axis=0)


def greet(partners):
    barrier = pltpu.get_barrier_semaphore()
    for partner in partners:
        pl.semaphore_signal(barrier, inc=1, device_id=partner, device_id_type=MESH)
    return lambda: pl.semaphore_wait(barrier, len(partners))


def remote(src, dst, send_sem, recv_sem, device):
    return pltpu.make_async_remote_copy(
        src_ref=src,
        dst_ref=dst,
        send_sem=send_sem,
        recv_sem=recv_sem,
        device_id=device,
        device_id_type=MESH,
    )


def flipped(index, other):
    out = 0
    for weight in (1, 2, 4, 8):
        bit, turn = lax.rem(index // weight, 2), lax.rem(other // weight, 2)
        out = out + weight * (bit + turn - 2 * bit * turn)
    return out


def forward_kernel(n, tok, *refs):
    (
        tokens_ref,
        gain_ref,
        shift_ref,
        wq_ref,
        wk_ref,
        wv_ref,
        bq_ref,
        bv_ref,
        att_ref,
        normed_out,
        q_out,
        k_out,
        v_out,
        o_out,
        lse_out,
        rows_in,
        gain,
        shift,
        b_query,
        b_value,
        land,
        w_pair,
        w_head,
        bias,
        q_all,
        k_all,
        v_all,
        k_nat,
        o_all,
        lse_all,
        stats,
        att_send,
        load_sem,
        gather_send,
        gather_recv,
        save_sem,
        out_send,
        out_recv,
        out_local,
        last_sem,
    ) = refs
    me = lax.axis_index("seq")
    scene = lax.axis_index("scene")
    core = lax.rem(me, 2)
    chips = n // 2
    wide = 2 * tok
    half_rows = tok // 2
    devices = [flipped(me, s) for s in range(n)]

    def rows(head):
        return pl.ds(pl.multiple_of(head * HEAD_DIM, HEAD_DIM), HEAD_DIM)

    def lanes(block, width=tok):
        return pl.ds(pl.multiple_of(block * width, width), width)

    tokens_load = pltpu.make_async_copy(tokens_ref, rows_in, load_sem.at[0])
    tokens_load.start()
    weight_loads = [
        pltpu.make_async_copy(ref.at[:, lanes(me // 2, 128)], w_pair.at[i], load_sem.at[1 + i])
        for i, ref in enumerate((wk_ref, wq_ref, wv_ref))
    ]
    vector_loads = [
        pltpu.make_async_copy(src, dst, load_sem.at[4 + i])
        for i, (src, dst) in enumerate(
            ((gain_ref, gain), (shift_ref, shift), (bq_ref, b_query), (bv_ref, b_value))
        )
    ]
    for load in vector_loads + weight_loads:
        load.start()
    all_here = greet([(scene, devices[s]) for s in range(1, n)])

    def gather_copy(slot, over, part):
        piece = slice(part * half_rows, (part + 1) * half_rows)
        there = slot ^ over
        return remote(
            land.at[slot, piece, :],
            land.at[there, piece, :],
            gather_send.at[there, part],
            gather_recv.at[there, part],
            (scene, devices[over]),
        )

    routes = {0: (4, 2, 8, 1), 8: (4, 2, 1), 4: (2, 1), 12: (2, 1), 2: (1,), 6: (1,), 10: (1,), 14: (1,)}

    def routes_of(slot, part):
        if part == 1 and slot == 12:
            return (1,)
        if part == 1 and slot == 10:
            return (4, 1)
        return routes.get(slot, ())

    def came_over(slot, part):
        for source in range(n):
            for over in routes_of(source, part):
                if source ^ over == slot:
                    return over

    sent = []
    saves = []

    def forward(slot, part):
        for over in routes_of(slot, part):
            copy = gather_copy(slot, over, part)
            copy.start()
            sent.append(copy)

    def arrive(slot, part):
        over = came_over(slot, part)
        gather_copy(slot ^ over, over, part).wait_recv()
        forward(slot, part)

    for load in [tokens_load] + vector_loads:
        load.wait()
    for part in range(2):
        piece = slice(part * half_rows, (part + 1) * half_rows)
        scaled, _ = normalise(rows_in[piece, :].astype(f32))
        land[0, piece, :] = (scaled * gain[...] + shift[...]).astype(bf16)
        if part == 0:
            all_here()
        forward(0, part)

    odd = core == 1
    for i, load in enumerate(weight_loads):
        load.wait()
        pair = w_pair[i].astype(f32)
        w_head[:, HEAD_DIM * i : HEAD_DIM * i + HEAD_DIM] = jnp.where(
            odd, pair[:, HEAD_DIM:], pair[:, :HEAD_DIM]
        ).astype(bf16)
    for i, ref in ((1, b_query), (2, b_value)):
        pair = ref[0:1, lanes(me // 2, 128)]
        bias[0:1, HEAD_DIM * i : HEAD_DIM * i + HEAD_DIM] = jnp.where(
            odd, pair[:, HEAD_DIM:], pair[:, :HEAD_DIM]
        )
    bias[0:1, :HEAD_DIM] = jnp.zeros((1, HEAD_DIM), f32)

    def project(slot):
        made = contract(land[slot], w_head[...], 1, 0) + bias[0:1, :]
        low = made.astype(bf16)
        turned = low.T
        span = slice(slot * tok, (slot + 1) * tok)
        k_nat[span, :] = low[:, :HEAD_DIM]
        k_all[:, span] = turned[:HEAD_DIM]
        q_all[:, span] = turned[HEAD_DIM : 2 * HEAD_DIM] * jnp.asarray(score_scale, bf16)
        v_all[:, span] = turned[2 * HEAD_DIM :]
        save = pltpu.make_async_copy(land.at[slot], normed_out.at[span, :], save_sem.at[slot])
        save.start()
        saves.append(save)

    def attend(span, first, state):
        top, total, acc = state
        keys = slice(first, first + chips // 2 * wide)
        scores = contract(k_nat[keys, :], q_all[:, span], 1, 0)
        here = jnp.max(scores, axis=0, keepdims=True)
        new_top = here if top is None else jnp.maximum(top, here)
        shifted = jnp.exp(scores - new_top)
        part_sum = jnp.sum(shifted, axis=0, keepdims=True)
        part = contract(v_all[:, keys], shifted.astype(bf16), 1, 0)
        if top is None:
            return new_top, part_sum, part
        fade = jnp.exp(top - new_top)
        return new_top, total * fade + part_sum, acc * fade + part

    middle = chips // 2 * wide

    def early(i):
        span = slice(i * wide, (i + 1) * wide)
        top, total, acc = attend(span, 0, (None, None, None))
        stats[0:1, span] = top
        stats[1:2, span] = total
        o_all[:, span] = acc

    def close(i, span, state):
        top, total, acc = state
        out = acc / total
        o_all[:, span] = out
        lse_all[:, span] = jnp.broadcast_to(top + jnp.log(total), (8, wide))
        low = out.astype(bf16)
        att_send[i, 0] = low[:, :tok]
        att_send[i, 1] = low[:, tok:]

    def out_copy(i, flip):
        return remote(
            att_send.at[i, flip],
            att_ref.at[rows(me), :],
            out_send.at[i, flip],
            out_recv.at[i, flip],
            (scene, flipped(me, 2 * i + flip)),
        )

    project(0)
    for part in range(2):
        arrive(1, part)
    project(1)
    for part in range(2):
        arrive(2, part)
        arrive(4, part)
    project(2)
    for slot in (3, 5):
        for part in range(2):
            arrive(slot, part)
    project(3)
    project(4)
    project(5)
    for part in range(2):
        arrive(8, part)
    for slot in (6, 7):
        for part in range(2):
            arrive(slot, part)
    project(6)
    project(7)
    early(0)
    early(1)
    arrive(9, 0)
    arrive(9, 1)
    project(8)
    project(9)
    for part in range(2):
        arrive(12, part)
        arrive(10, part)
    early(2)
    for slot in (11, 13):
        for part in range(2):
            arrive(slot, part)
    project(10)
    project(11)
    early(3)
    project(12)
    project(13)
    arrive(14, 0)
    arrive(14, 1)
    project(14)
    arrive(15, 0)
    arrive(15, 1)
    project(15)
    for i, (src, dst) in enumerate(((q_all, q_out), (k_all, k_out), (v_all, v_out))):
        save = pltpu.make_async_copy(src, dst, last_sem.at[i])
        save.start()
        saves.append(save)

    def late_body(j, carry):
        i = chips - 1 - j
        span = lanes(i, wide)
        close(i, span, attend(span, middle, attend(span, 0, (None, None, None))))
        out_copy(i, 0).start()
        out_copy(i, 1).start()
        return carry

    lax.fori_loop(0, chips // 2, late_body, 0)

    def rest(i, span):
        state = (stats[0:1, span], stats[1:2, span], o_all[:, span])
        close(i, span, attend(span, middle, state))

    def rest_body(j, carry):
        i = chips // 2 - 1 - j
        rest(i, lanes(i, wide))
        out_copy(i, 0).start()
        out_copy(i, 1).start()
        return carry

    lax.fori_loop(0, chips // 2 - 1, rest_body, 0)
    rest(0, slice(0, wide))
    mine = pltpu.make_async_copy(att_send.at[0, 0], att_ref.at[rows(me), :], out_local)
    mine.start()
    out_copy(0, 1).start()
    for i, (src, dst) in enumerate(((o_all, o_out), (lse_all, lse_out))):
        save = pltpu.make_async_copy(src, dst, last_sem.at[3 + i])
        save.start()
        saves.append(save)
    for copy in sent:
        copy.wait_send()
    mine.wait()
    out_copy(0, 1).wait()

    def drain(i, carry):
        out_copy(i, 0).wait()
        out_copy(i, 1).wait()
        return carry

    lax.fori_loop(1, chips, drain, 0)
    for save in saves:
        save.wait()


def attention_forward(n, tokens, gain, shift, w_query, w_key, w_value, b_query, b_value):
    tok, width = tokens.shape
    length = n * tok
    any_spec = pl.BlockSpec(memory_space=pl.ANY)
    head_all = jax.ShapeDtypeStruct((HEAD_DIM, length), bf16)
    dma = pltpu.SemaphoreType.DMA
    return pl.pallas_call(
        functools.partial(forward_kernel, n, tok),
        out_shape=(
            jax.ShapeDtypeStruct((width, tok), bf16),
            jax.ShapeDtypeStruct((length, width), bf16),
            head_all,
            head_all,
            head_all,
            jax.ShapeDtypeStruct((HEAD_DIM, length), f32),
            jax.ShapeDtypeStruct((8, length), f32),
        ),
        in_specs=[any_spec] * 8,
        out_specs=[any_spec] * 7,
        scratch_shapes=[
            pltpu.VMEM((tok, width), bf16),
            pltpu.VMEM((1, width), f32),
            pltpu.VMEM((1, width), f32),
            pltpu.VMEM((1, width), f32),
            pltpu.VMEM((1, width), f32),
            pltpu.VMEM((n, tok, width), bf16),
            pltpu.VMEM((3, width, 2 * HEAD_DIM), bf16),
            pltpu.VMEM((width, 3 * HEAD_DIM), bf16),
            pltpu.VMEM((8, 3 * HEAD_DIM), f32),
            pltpu.VMEM((HEAD_DIM, length), bf16),
            pltpu.VMEM((HEAD_DIM, length), bf16),
            pltpu.VMEM((HEAD_DIM, length), bf16),
            pltpu.VMEM((length, HEAD_DIM), bf16),
            pltpu.VMEM((HEAD_DIM, length), f32),
            pltpu.VMEM((8, length), f32),
            pltpu.VMEM((8, length), f32),
            pltpu.VMEM((n // 2, 2, HEAD_DIM, tok), bf16),
            dma((8,)),
            dma((n, 2)),
            dma((n, 2)),
            dma((n,)),
            dma((n // 2, 2)),
            dma((n // 2, 2)),
            dma,
            dma((5,)),
        ],
        compiler_params=pltpu.CompilerParams(
            collective_id=0, has_side_effects=True, vmem_limit_bytes=FORWARD_LIMIT
        ),
        name="attention_forward",
    )(
        tokens,
        gain[None],
        shift[None],
        w_query,
        w_key,
        w_value,
        b_query[None],
        b_value[None],
    )


CHUNKS = 9
TICKS = CHUNKS + 4
SLOTS = 3


def halving_plan(full, got0, got1a, got1b, got2a, got2b, got3, got4, total, send_sem, recv_sem):
    me = lax.axis_index("seq")
    x = lax.axis_index("scene")
    core = lax.rem(me, 2)
    y = lax.rem(me // 2, 2)
    z0 = lax.rem(me // 4, 2)
    z1 = me // 8
    at_core = (x, me + 1 - 2 * core)
    at_x = (1 - x, me)
    at_y = (x, me + 2 - 4 * y)
    at_z0 = (x, me + 4 - 8 * z0)
    at_z1 = (x, me + 8 - 16 * z1)
    up, low = slice(0, 64), slice(64, 128)

    def copy_of(slot, c):
        src, dst, device = (
            lambda: (full.at[lax.rem(c, SLOTS), :, :, :, :, 1 - core], got0.at[c], at_core),
            lambda: (got0.at[c, 1 - x, :, :, :, up, :], got1a.at[c], at_x),
            lambda: (got0.at[c, :, :, :, 1 - y, low, :], got1b.at[c], at_y),
            lambda: (got1a.at[c, :, 1 - z0], got2a.at[c], at_z0),
            lambda: (got1b.at[c, 1 - x], got2b.at[c], at_x),
            lambda: (got2a.at[c, :, 1 - y], got3.at[c, :, up, :], at_y),
            lambda: (got2b.at[c, :, 1 - z0], got3.at[c, :, low, :], at_z0),
            lambda: (got3.at[c, 1 - z1], got4.at[c], at_z1),
        )[slot]()
        return remote(src, dst, send_sem.at[c, slot], recv_sem.at[c, slot], device)

    def sum1(c):
        copy_of(0, c).wait_recv()
        got0[c] = got0[c] + full[lax.rem(c, SLOTS), :, :, :, :, core]

    def start1(c):
        copy_of(1, c).start()
        copy_of(2, c).start()

    def stage2(c):
        copy_of(1, c).wait_recv()
        got1a[c] = got1a[c] + got0[c, x, :, :, :, up, :]
        copy_of(3, c).start()
        copy_of(2, c).wait_recv()
        got1b[c] = got1b[c] + got0[c, :, :, :, y, low, :]
        copy_of(4, c).start()

    def stage3(c):
        copy_of(3, c).wait_recv()
        got2a[c] = got2a[c] + got1a[c, :, z0]
        copy_of(5, c).start()
        copy_of(4, c).wait_recv()
        got2b[c] = got2b[c] + got1b[c, x]
        copy_of(6, c).start()

    def stage4(c):
        copy_of(5, c).wait_recv()
        got3[c, :, up, :] = got3[c, :, up, :] + got2a[c, :, y]
        copy_of(6, c).wait_recv()
        got3[c, :, low, :] = got3[c, :, low, :] + got2b[c, :, z0]
        copy_of(7, c).start()

    def stage5(c):
        copy_of(7, c).wait_recv()
        total[c] = got3[c, z1].astype(f32) + got4[c].astype(f32)

    def tick(when):
        for stage, c in (
            (stage5, when - 4),
            (stage4, when - 3),
            (stage3, when - 2),
            (stage2, when - 1),
            (start1, when + 1),
        ):

            @pl.when((c >= 0) & (c < CHUNKS))
            def _(stage=stage, c=c):
                stage(c)

    return copy_of, sum1, start1, tick


def tail_kernel(n, tok, *refs):
    (
        q_ref,
        k_ref,
        v_ref,
        o_ref,
        lse_ref,
        act_ref,
        slope_ref,
        masked_ref,
        two_ref,
        residual_ref,
        att_ref,
        normed_ref,
        wd_ref,
        wu_ref,
        wo_ref,
        wq_ref,
        wk_ref,
        wv_ref,
        tokens_ref,
        gain_ref,
        gain_two_ref,
        b_down_ref,
        block_out,
        tokens_out,
        total,
        pack_got,
        small_got,
        small_up_got,
        q_all,
        k_all,
        v_all,
        d_all,
        d_send,
        o_all,
        lse_all,
        low,
        act,
        masked,
        two,
        hidden,
        att,
        resid_low,
        act_t,
        two_t,
        full,
        got0,
        got1a,
        got1b,
        got2a,
        got2b,
        got3,
        got4,
        land,
        rows_in,
        resid,
        gain_one,
        gain_two,
        b_down,
        pack,
        small,
        small_up,
        load_sem,
        ring_sem,
        weight_sem,
        normed_sem,
        in_send,
        in_recv,
        in_local,
        kv_send,
        kv_recv,
        kv_local,
        q_send,
        q_recv,
        q_local,
        half_send,
        half_recv,
        pack_send,
        pack_recv,
        small_send,
        small_recv,
        small_up_send,
        small_up_recv,
        last_local,
    ) = refs
    me = lax.axis_index("seq")
    scene = lax.axis_index("scene")
    chips = n // 2
    length = n * tok
    wide = 2 * tok
    devices = 2 * n
    width = masked.shape[1]
    mine = scene * n + me

    def rows(head):
        return pl.ds(pl.multiple_of(head * HEAD_DIM, HEAD_DIM), HEAD_DIM)

    def lanes(block, width=tok):
        return pl.ds(pl.multiple_of(block * width, width), width)

    def by_block(ref, block):
        return ref.at[:, 1024 * block : 1024 * block + 1024]

    loads = [
        pltpu.make_async_copy(src, dst, load_sem.at[i])
        for i, (src, dst) in enumerate(
            [(by_block(act_ref, i), act.at[tok * i : tok * i + tok, :]) for i in range(4)]
            + [
                (masked_ref, masked),
                (q_ref, q_all),
                (k_ref, k_all),
                (v_ref, v_all),
                (o_ref, o_all),
                (lse_ref, lse_all),
                (two_ref, two),
                (att_ref, att),
                (residual_ref, resid),
                (tokens_ref, rows_in),
                (gain_ref, gain_one),
                (gain_two_ref, gain_two),
                (b_down_ref, b_down),
            ]
        )
    ]
    for load in loads:
        load.start()

    def peer(j):
        index = lax.rem(mine + j, devices)
        return index, (index // n, lax.rem(index, n))

    all_here = greet([peer(j)[1] for j in range(1, devices)])

    half, sum1, start1, tick = halving_plan(
        full, got0, got1a, got1b, got2a, got2b, got3, got4, total, half_send, half_recv
    )

    def chunk_begin(c):
        @pl.when(c >= SLOTS)
        def _():
            half(0, c - SLOTS).wait_send()

        return lax.rem(c, SLOTS)

    def chunk_end(c):
        half(0, c).start()

        @pl.when((c >= 1) & (c != 4))
        def _():
            sum1(c - 1)

    def down_chunk(c):
        slot = chunk_begin(c)
        columns = masked[:, lanes(c, 256)]
        for block in range(4):
            part = contract(act_t[1024 * block : 1024 * block + 1024, :], columns, 1, 0)
            full[slot, block // 2, block % 2] = part.astype(bf16).reshape(2, 2, 2, 128, 256)
        chunk_end(c)

    def narrow_chunk(c, left, right):
        slot = chunk_begin(c)
        for block in range(4):
            part = contract(left, right[:, 256 * block : 256 * block + 256], 1, 0)
            full[slot, :, :, :, :, :, 32 * block : 32 * block + 32, :] = part.astype(bf16).reshape(
                2, 2, 2, 2, 2, 32, 256
            )
        chunk_end(c)

    for block in range(4):
        loads[block].wait()
        act_t[1024 * block : 1024 * block + 1024, :] = act[tok * block : tok * block + tok, :].T
    loads[4].wait()
    all_here()

    def first_chunk(c, carry):
        down_chunk(c)

        @pl.when((c >= 1) & (c <= 2))
        def _():
            start1(c - 1)

        return carry

    lax.fori_loop(0, 4, first_chunk, 0)

    def feed_forward(ring, slope, out_acc, two_acc):
        def weight_load(i):
            if i < 4:
                src = wd_ref.at[1024 * i : 1024 * i + 1024, :]
            elif i < 8:
                src = wu_ref.at[:, 1024 * (i - 4) : 1024 * (i - 4) + 1024]
            else:
                src = wo_ref
            return pltpu.make_async_copy(src, ring.at[i % 2], ring_sem.at[i % 2])

        def slope_load(i):
            return pltpu.make_async_copy(by_block(slope_ref, i), slope.at[i % 2], ring_sem.at[2 + i % 2])

        for i in range(2):
            weight_load(i).start()
            slope_load(i).start()
        for load in loads[10:]:
            load.wait()
        small[5:6, :] = jnp.sum(masked[...].astype(f32), axis=0, keepdims=True)
        for i in range(4):
            weight_load(i).wait()
            slope_load(i).wait()
            there = slice(tok * i, tok * i + tok)
            part = contract(act[there, :], ring[i % 2], 1, 0)
            out_acc[...] = resid[...] + b_down[...] + part if i == 0 else out_acc[...] + part
            grown = contract(masked[...], ring[i % 2], 1, 1) * slope[i % 2]
            weight_load(i + 2).start()
            if i < 2:
                slope_load(i + 2).start()
            grown = grown.astype(bf16)
            hidden[there, :] = grown
            sums = jnp.sum(grown.astype(f32), axis=0, keepdims=True)
            for j in range(8):
                small_up[8 * i + j] = jnp.broadcast_to(sums[:, 128 * j : 128 * j + 128], (8, 128))
            if i == 1:
                tick(1)
        block_out[...] = out_acc[...].astype(bf16)
        sum1(3)
        for i in range(4):
            weight_load(4 + i).wait()
            part = contract(hidden[tok * i : tok * i + tok, :], ring[i % 2], 1, 1)
            two_acc[...] = part if i == 0 else two_acc[...] + part
            if i < 3:
                weight_load(6 + i).start()
            if i == 1:
                tick(2)
        scaled, inverse = normalise(resid[...])
        part, gain_grad, shift_grad = norm_back(two_acc[...], scaled, inverse, gain_two[...])
        resid[...] = masked[...].astype(f32) + part
        resid_low[...] = resid[...].astype(bf16)
        small[4:5, :] = jnp.sum(resid_low[...].astype(f32), axis=0, keepdims=True)
        small[6:7, :] = gain_grad[None]
        small[7:8, :] = shift_grad[None]
        weight_load(8).wait()
        d_send[...] = contract(ring[0], resid_low[...], 1, 1).astype(bf16)

    pl.run_scoped(
        feed_forward,
        pltpu.VMEM((2, 1024, 1024), bf16),
        pltpu.VMEM((2, tok, 1024), f32),
        pltpu.VMEM((tok, width), f32),
        pltpu.VMEM((tok, width), f32),
    )

    copies = []
    for s in range(1, n):
        head = flipped(me, s)
        copies.append(
            remote(
                d_send.at[rows(head), :],
                d_all.at[:, s * tok : s * tok + tok],
                in_send.at[s],
                in_recv.at[s],
                (scene, head),
            )
        )
        copies[-1].start()
    local = pltpu.make_async_copy(d_send.at[rows(me), :], d_all.at[:, :tok], in_local)
    local.start()

    two_t[...] = two[...].T
    for load in loads[5:10]:
        load.wait()

    def chunk(step):
        @pl.when(step == 0)
        def _():
            narrow_chunk(step + 7, two_t[...], hidden[3 * tok :, :])
            normed_load(0).start()

        @pl.when(step == 1)
        def _():
            narrow_chunk(step + 7, att[...], resid_low[...])
            normed_load(1).start()

        @pl.when(step == 2)
        def _():
            sum1(CHUNKS - 1)

    def normed_load(i):
        return pltpu.make_async_copy(
            normed_ref.at[1024 * i : 1024 * i + 1024, :],
            (act, hidden)[i % 2],
            normed_sem.at[i % 2],
        )

    def q_copy(step, flip):
        slot = 2 * step + flip
        return remote(
            low.at[0, :, lanes(slot)],
            land.at[0, rows(me), :],
            q_send.at[step, flip],
            q_recv.at[step, flip],
            (scene, flipped(me, slot)),
        )

    def kv_copy(a, step, flip):
        slot = 2 * step + flip
        return remote(
            low.at[1 + a, :, lanes(slot)],
            land.at[1 + a, rows(me), :],
            kv_send.at[a, step, flip],
            kv_recv.at[a, step, flip],
            (scene, flipped(me, slot)),
        )

    own = [
        pltpu.make_async_copy(low.at[a, :, :tok], land.at[a, rows(me), :], sem)
        for a, sem in ((0, q_local), (1, kv_local.at[0]), (2, kv_local.at[1]))
    ]

    weight_loads = [
        pltpu.make_async_copy(
            ref.at[:, :, :, :, 256 * block : 256 * block + 256],
            full.at[a, block // 2, block % 2],
            weight_sem.at[a, block],
        )
        for a, ref in enumerate((wq_ref, wk_ref, wv_ref))
        for block in range(4)
    ]

    def load_weights():
        for c in range(CHUNKS - SLOTS, CHUNKS):
            half(0, c).wait_send()
        for load in weight_loads:
            load.start()

    def attention(q_nat, k_nat, v_nat, d_nat, delta, dq_acc):
        q_nat[...] = q_all[...].T
        k_nat[...] = k_all[...].T
        v_nat[...] = v_all[...].T
        dq_acc[...] = jnp.zeros_like(dq_acc)

        def middle_chunk(i, carry):
            there = pl.ds(pl.multiple_of(i * tok, tok), tok)
            narrow_chunk(4 + i, two_t[...], hidden[there, :])

            @pl.when(i == 1)
            def _():
                tick(3)

            return carry

        lax.fori_loop(0, 3, middle_chunk, 0)
        local.wait()
        for copy in copies:
            copy.wait_recv()
        d_nat[...] = d_all[...].T
        delta[...] = jnp.broadcast_to(
            jnp.sum(d_all[...].astype(f32) * o_all[...], axis=0, keepdims=True), delta.shape
        )

        def keys(step, last):
            span = lanes(step, wide)
            k_here, v_here, kt_here = k_nat[span, :], v_nat[span, :], k_all[:, span]
            dk = dv = None
            for i in reversed(range(chips)):
                there = slice(i * wide, (i + 1) * wide)
                scores = contract(k_here, q_all[:, there], 1, 0)
                prob = jnp.exp(scores - lse_all[0:1, there])
                dprob = contract(v_here, d_all[:, there], 1, 0)
                dscore = (prob * (dprob - delta[0:1, there])).astype(bf16)
                v_part = contract(prob.astype(bf16), d_nat[there, :], 1, 0)
                k_part = contract(dscore, q_nat[there, :], 1, 0)
                dk = k_part if dk is None else dk + k_part
                dv = v_part if dv is None else dv + v_part
                dq = dq_acc[:, there] + contract(kt_here, dscore, 1, 0)
                if last:
                    low[0, :, there] = (dq * score_scale).astype(bf16)
                    if i == 0:
                        own[0].start()
                    else:
                        q_copy(i, 0).start()
                    q_copy(i, 1).start()
                else:
                    dq_acc[:, there] = dq
            low[1, :, span] = dk.astype(bf16).T
            low[2, :, span] = dv.astype(bf16).T

        def step_body(step, carry):
            chunk(step)
            tick(step + 4)
            keys(step, False)

            @pl.when(step == 0)
            def _():
                own[1].start()
                own[2].start()

            for a in range(2):

                @pl.when(step > 0)
                def _(a=a):
                    kv_copy(a, step, 0).start()

                kv_copy(a, step, 1).start()
            return carry

        lax.fori_loop(0, chips - 1, step_body, 0)
        load_weights()
        tick(11)
        keys(chips - 1, True)
        for a in range(2):
            kv_copy(a, chips - 1, 0).start()
            kv_copy(a, chips - 1, 1).start()

    pl.run_scoped(
        attention,
        *(pltpu.VMEM((length, HEAD_DIM), bf16) for _ in range(4)),
        pltpu.VMEM((8, length), f32),
        pltpu.VMEM((HEAD_DIM, length), f32),
    )
    tick(12)

    head_acc = None
    for i in range(length // 1024):
        normed_load(i).wait()
        left = low[:, :, 1024 * i : 1024 * i + 1024].reshape(3 * HEAD_DIM, 1024)
        part = contract(left, (act, hidden)[i % 2][...], 1, 0)
        head_acc = part if head_acc is None else head_acc + part
        if i + 2 < length // 1024:
            normed_load(i + 2).start()
    by_row = head_acc.T
    share = width // devices
    pack[:, :share, :] = by_row[:, : 2 * HEAD_DIM].astype(bf16).reshape(devices, share, 2 * HEAD_DIM)
    third = by_row[:, 2 * HEAD_DIM :].astype(bf16).reshape(devices, 2, share // 2, HEAD_DIM)
    pack[:, share:, :] = jnp.concatenate([third[:, 0], third[:, 1]], axis=-1)

    def pack_copy(j):
        index, device = peer(j)
        return remote(
            pack.at[index], pack_got.at[mine], pack_send.at[j], pack_recv.at[j], device
        )

    def small_copy(j):
        index, device = peer(j)
        return remote(
            small.at[:, lanes(index // 4, 128)],
            small_got.at[mine],
            small_send.at[j],
            small_recv.at[j],
            device,
        )

    def small_up_copy(j):
        index, device = peer(j)
        return remote(
            small_up.at[index], small_up_got.at[mine], small_up_send.at[j], small_up_recv.at[j], device
        )

    kept = [
        pltpu.make_async_copy(pack.at[mine], pack_got.at[mine], last_local.at[0]),
        pltpu.make_async_copy(
            small.at[:, lanes(mine // 4, 128)], small_got.at[mine], last_local.at[1]
        ),
        pltpu.make_async_copy(small_up.at[mine], small_up_got.at[mine], last_local.at[2]),
    ]
    kept[0].start()
    kept[2].start()

    def pack_body(j, carry):
        pack_copy(j).start()
        small_up_copy(j).start()
        return carry

    lax.fori_loop(1, devices, pack_body, 0)

    for copy in own:
        copy.wait()
    for step in range(chips):
        for flip in range(2):
            if step or flip:
                kv_copy(0, step, flip).wait_recv()
                kv_copy(1, step, flip).wait_recv()
                q_copy(step, flip).wait_recv()
    for load in weight_loads:
        load.wait()
    def first_norm(back_in):
        for i in range(4):
            part = None
            for a in range(3):
                left = jnp.concatenate(
                    [full[a, b // 2, b % 2, i // 2, i % 2].reshape(256, 256) for b in range(4)],
                    axis=1,
                )
                here = contract(left, land[a], 1, 0)
                part = here if part is None else part + here
            back_in[:, 256 * i : 256 * i + 256] = part.T
        scaled, inverse = normalise(rows_in[...].astype(f32))
        token_part, gain_grad, shift_grad = norm_back(back_in[...], scaled, inverse, gain_one[...])
        tokens_out[...] = (resid[...] + token_part).astype(bf16)
        small[2:3, :] = gain_grad[None]
        small[3:4, :] = shift_grad[None]

    pl.run_scoped(first_norm, pltpu.VMEM((tok, width), f32))
    ones = jnp.ones((8, tok), bf16)
    small[0:1, :] = contract(ones, land[0], 1, 1)[0:1]
    small[1:2, :] = contract(ones, land[2], 1, 1)[0:1]
    kept[1].start()

    def small_body(j, carry):
        small_copy(j).start()
        return carry

    lax.fori_loop(1, devices, small_body, 0)

    for copy in kept:
        copy.wait()

    def arrive(j, carry):
        pack_copy(j).wait()
        small_up_copy(j).wait()
        small_copy(j).wait()
        return carry

    lax.fori_loop(1, devices, arrive, 0)
    for copy in copies:
        copy.wait_send()
    for step in range(chips):
        for flip in range(2):
            if step or flip:
                kv_copy(0, step, flip).wait_send()
                kv_copy(1, step, flip).wait_send()
                q_copy(step, flip).wait_send()

    def settle(c, carry):
        for slot in range(1, 8):
            half(slot, c).wait_send()
        return carry

    lax.fori_loop(0, CHUNKS, settle, 0)


def tail(n, tok, width, hidden_width, *arrays):
    length = n * tok
    chips = n // 2
    devices = 2 * n
    share = width // devices
    any_spec = pl.BlockSpec(memory_space=pl.ANY)
    vmem = pl.BlockSpec(memory_space=pltpu.VMEM)
    dma = pltpu.SemaphoreType.DMA

    def space(*shape, kind=bf16):
        return pltpu.VMEM(shape, kind)

    def out(*shape, kind=f32):
        return jax.ShapeDtypeStruct(shape, kind)

    pieces = CHUNKS
    scratch = (
        [space(HEAD_DIM, length)] * 4
        + [
            space(width, tok),
            space(HEAD_DIM, length, kind=f32),
            space(8, length, kind=f32),
            space(3, HEAD_DIM, length),
            space(hidden_width // 1024 * tok, 1024),
            space(tok, width),
            space(tok, width),
            space(hidden_width // 1024 * tok, 1024),
            space(width, tok),
            space(tok, width),
            space(hidden_width, tok),
            space(width, tok),
            space(SLOTS, 2, 2, 2, 2, 2, 128, 256),
            space(pieces, 2, 2, 2, 2, 128, 256),
            space(pieces, 2, 2, 2, 64, 256),
            space(pieces, 2, 2, 2, 64, 256),
            space(pieces, 2, 2, 64, 256),
            space(pieces, 2, 2, 64, 256),
            space(pieces, 2, 128, 256),
            space(pieces, 128, 256),
            space(3, width, tok),
            space(tok, width),
            space(tok, width, kind=f32),
            space(1, width, kind=f32),
            space(1, width, kind=f32),
            space(1, width, kind=f32),
            space(devices, share + share // 2, 128),
            space(8, width, kind=f32),
            space(devices, 8, 128, kind=f32),
            dma((17,)),
            dma((4,)),
            dma((3, 4)),
            dma((2,)),
            dma((n,)),
            dma((n,)),
            dma,
            dma((2, chips, 2)),
            dma((2, chips, 2)),
            dma((2,)),
            dma((chips, 2)),
            dma((chips, 2)),
            dma,
            dma((pieces, 8)),
            dma((pieces, 8)),
        ]
        + [dma((devices,))] * 6
        + [dma((3,))]
    )
    return pl.pallas_call(
        functools.partial(tail_kernel, n, tok),
        out_shape=(
            out(tok, width, kind=bf16),
            out(tok, width, kind=bf16),
            out(pieces, 128, 256),
            out(devices, share + share // 2, 128, kind=bf16),
            out(devices, 8, 128),
            out(devices, 8, 128),
        ),
        in_specs=[any_spec] * 22,
        out_specs=[vmem] * 6,
        scratch_shapes=scratch,
        compiler_params=pltpu.CompilerParams(
            collective_id=1, has_side_effects=True, vmem_limit_bytes=63 << 20
        ),
        name="tail",
    )(*arrays)


def finish_kernel(n, *refs):
    block_in, tokens_in, total, pack_got, small_got, small_up_got = refs[:6]
    block_out, tokens_out, query_out, key_out, value_out, out_out, up_out, down_out = refs[6:14]
    vectors, up_vector = refs[14:22], refs[22]
    block_out[...] = block_in[...]
    tokens_out[...] = tokens_in[...]
    mine = lax.axis_index("scene") * n + lax.axis_index("seq")
    share = query_out.shape[0]
    for head in range(0, n, 2):
        pair = [
            pack_got[head + i].astype(f32) + pack_got[n + head + i].astype(f32) for i in range(2)
        ]
        columns = slice(head * HEAD_DIM, head * HEAD_DIM + 2 * HEAD_DIM)

        def joined(first, last, start):
            return jnp.concatenate(
                [part[first:last, start : start + HEAD_DIM] for part in pair], axis=1
            )

        query_out[:, columns] = joined(0, share, 0)
        key_out[:, columns] = joined(0, share, HEAD_DIM)
        value_out[: share // 2, columns] = joined(share, share + share // 2, 0)
        value_out[share // 2 :, columns] = joined(share, share + share // 2, HEAD_DIM)
    for i in range(4):
        down_out[:, 256 * i : 256 * i + 256] = total[i]
        out_out[:, 256 * i : 256 * i + 256] = total[8, 32 * i : 32 * i + 32, :]
    for i in range(16):
        up_out[:, 256 * i : 256 * i + 256] = total[4 + i // 4, 32 * (i % 4) : 32 * (i % 4) + 32, :]
    turn = lax.rem(128 - 32 * lax.rem(mine, 4), 128)
    sums = pltpu.roll(jnp.sum(small_got[...], axis=0), turn, 1)
    for i, vector in enumerate(vectors):
        vector[...] = sums[i, :share]
    up_vector[...] = jnp.sum(small_up_got[...], axis=0)[0]


def finish(n, block_rows, tokens_grad, total, pack_got, small_got, small_up_got):
    tok, width = tokens_grad.shape
    devices = 2 * n
    share = width // devices
    vmem = pl.BlockSpec(memory_space=pltpu.VMEM)

    def out(*shape):
        return jax.ShapeDtypeStruct(shape, f32)

    return pl.pallas_call(
        functools.partial(finish_kernel, n),
        out_shape=(
            jax.ShapeDtypeStruct((tok, width), bf16),
            jax.ShapeDtypeStruct((tok, width), bf16),
            out(share, width),
            out(share, width),
            out(share, width),
            out(share, width),
            out(share, 4 * width),
            out(4 * share, width),
        )
        + (out(share),) * 8
        + (out(4 * share),),
        in_specs=[vmem] * 6,
        out_specs=[vmem] * 17,
        compiler_params=pltpu.CompilerParams(vmem_limit_bytes=60 << 20),
        name="finish",
    )(block_rows, tokens_grad, total, pack_got, small_got, small_up_got)


def gelu_both(values):
    cubic = gelu_coef * (values + 0.044715 * values * values * values)
    bend = jnp.tanh(cubic)
    slope = gelu_coef * (1.0 + 3.0 * 0.044715 * values * values)
    grad = 0.5 * (1.0 + bend) + 0.5 * values * (1.0 - bend * bend) * slope
    return 0.5 * values * (1.0 + bend), grad


def layer_on_device(
    scenes,
    n,
    tokens,
    surface_mask,
    out_grad,
    w_query,
    w_key,
    w_value,
    w_out,
    w_up,
    w_down,
    b_query,
    b_value,
    b_out,
    b_up,
    b_down,
    gain_one,
    shift_one,
    gain_two,
    shift_two,
):
    _, tok, width = tokens.shape
    rows = tokens[0].astype(f32)
    att_t, normed_all, q_all, k_all, v_all, o_all, lse_all = attention_forward(
        n, tokens[0], gain_one, shift_one, w_query, w_key, w_value, b_query, b_value
    )

    att_t, out_grad, surface_mask = lax.optimization_barrier((att_t, out_grad, surface_mask))
    residual = rows + matmul_tn(att_t, w_out) + b_out
    scaled_two, _ = normalise(residual)
    normed_two = (scaled_two * gain_two + shift_two).astype(bf16)
    activated, slope = gelu_both(matmul(normed_two, w_up) + b_up)
    activated = activated.astype(bf16)
    masked = out_grad[0] * surface_mask[0].astype(bf16)[:, None]
    arrived = tail(
        n,
        tok,
        width,
        w_up.shape[1],
        q_all,
        k_all,
        v_all,
        o_all,
        lse_all,
        activated,
        slope,
        masked,
        normed_two,
        residual,
        att_t,
        normed_all,
        w_down,
        w_up,
        w_out,
        *(w.reshape(2, 2, 2, 128, width) for w in (w_query, w_key, w_value)),
        tokens[0],
        gain_one[None],
        gain_two[None],
        b_down[None],
    )
    block_out, tokens_grad, *sums = finish(n, *arrived)
    bquery, bvalue, gone, sone, bout, bdown, gtwo, stwo, bup = sums[6:]
    return (
        block_out[None],
        tokens_grad[None],
        *sums[:6],
        bquery,
        bvalue,
        bout,
        bup,
        bdown,
        gone,
        sone,
        gtwo,
        stwo,
    )


def norm_rows(values, gain, shift):
    row_mean = jnp.mean(values, axis=-1, keepdims=True)
    centred = values - row_mean
    row_var = jnp.mean(centred * centred, axis=-1, keepdims=True)
    return centred * lax.rsqrt(row_var + norm_eps) * gain + shift


def gelu_tanh(values):
    return (
        0.5 * values * (1.0 + jnp.tanh(gelu_coef * (values + 0.044715 * values * values * values)))
    )


def take_pair(array_in, pair_index):
    pair_width = 2 * HEAD_DIM
    sliced = lax.dynamic_slice_in_dim(array_in, pair_index * pair_width, pair_width, 2)
    return sliced.reshape(sliced.shape[:2] + (2, HEAD_DIM))


def take_stats(array_in, pair_index):
    return lax.dynamic_slice_in_dim(array_in, pair_index * 2, 2, 1)


def join_pairs(stacked):
    moved = jnp.moveaxis(stacked, 0, 2)
    return moved.reshape(moved.shape[:2] + (moved.shape[2] * moved.shape[3],))


def join_stats(stacked):
    moved = jnp.moveaxis(stacked, 0, 1)
    return moved.reshape((moved.shape[0], moved.shape[1] * moved.shape[2], moved.shape[3]))


def merge_heads(pair_part):
    return pair_part.reshape(pair_part.shape[:2] + (2 * HEAD_DIM,))


def attend(q_scene, k_gathered, v_gathered):

    def attend_pair_step(unused, pair_index):
        q_pair = take_pair(q_scene, pair_index)
        k_pair = take_pair(k_gathered, pair_index)
        v_pair = take_pair(v_gathered, pair_index)
        scores = (
            jnp.einsum("sqhe,skhe->shqk", q_pair, k_pair, preferred_element_type=jnp.float32)
            * score_scale
        )
        row_max = jnp.max(scores, axis=-1, keepdims=True)
        shifted = jnp.exp(scores - row_max)
        row_sum = jnp.sum(shifted, axis=-1, keepdims=True)
        prob_low = (shifted / row_sum).astype(jnp.bfloat16)
        pair_out = jnp.einsum(
            "shqk,skhe->sqhe", prob_low, v_pair, preferred_element_type=jnp.float32
        )
        pair_lse = (row_max + jnp.log(row_sum))[..., 0]
        return (unused, (merge_heads(pair_out), pair_lse))

    pair_count = HEADS // 2
    _, (pair_outs, pair_lses) = lax.scan(
        attend_pair_step, jnp.zeros((), jnp.float32), jnp.arange(pair_count, dtype=jnp.int32)
    )
    return (join_pairs(pair_outs), join_stats(pair_lses))


def query_side(q_scene, k_gathered, v_gathered, row_lse, att_grad):

    def query_pair_step(unused, pair_index):
        q_pair = take_pair(q_scene, pair_index)
        k_pair = take_pair(k_gathered, pair_index)
        v_pair = take_pair(v_gathered, pair_index)
        d_pair = take_pair(att_grad, pair_index)
        l_pair = take_stats(row_lse, pair_index)
        scores = (
            jnp.einsum("sqhe,skhe->shqk", q_pair, k_pair, preferred_element_type=jnp.float32)
            * score_scale
        )
        attn_prob = jnp.exp(scores - l_pair[..., None])
        dprob = jnp.einsum("sqhe,skhe->shqk", d_pair, v_pair, preferred_element_type=jnp.float32)
        row_delta = jnp.sum(attn_prob * dprob, axis=-1)
        dscore = (attn_prob * (dprob - row_delta[..., None])).astype(jnp.bfloat16)
        q_part = (
            jnp.einsum("shqk,skhe->sqhe", dscore, k_pair, preferred_element_type=jnp.float32)
            * score_scale
        )
        results = (merge_heads(q_part), row_delta)
        prob_low = attn_prob.astype(jnp.bfloat16)
        k_part = (
            jnp.einsum("shqk,sqhe->skhe", dscore, q_pair, preferred_element_type=jnp.float32)
            * score_scale
        )
        v_part = jnp.einsum("shqk,sqhe->skhe", prob_low, d_pair, preferred_element_type=jnp.float32)
        results = results + (merge_heads(k_part), merge_heads(v_part))
        return (unused, results)

    pair_count = HEADS // 2
    _, results = lax.scan(
        query_pair_step, jnp.zeros((), jnp.float32), jnp.arange(pair_count, dtype=jnp.int32)
    )
    return results


def on_any_device(
    tokens,
    surface_mask,
    out_grad,
    w_query,
    w_key,
    w_value,
    w_out,
    w_up,
    w_down,
    b_query,
    b_value,
    b_out,
    b_up,
    b_down,
    gain_one,
    shift_one,
    gain_two,
    shift_two,
):
    scenes, local_len, model_width = tokens.shape
    row_count = scenes * local_len
    flat_rows = tokens.astype(jnp.float32).reshape(row_count, model_width)
    normed, norm_one_pull = jax.vjp(norm_rows, flat_rows, gain_one, shift_one)
    normed_low = normed.astype(jnp.bfloat16)
    q_low = (matmul(normed_low, w_query) + b_query).astype(jnp.bfloat16)
    k_low = matmul(normed_low, w_key).astype(jnp.bfloat16)
    v_low = (matmul(normed_low, w_value) + b_value).astype(jnp.bfloat16)
    q_scene = q_low.reshape(scenes, local_len, model_width)
    k_scene = k_low.reshape(scenes, local_len, model_width)
    v_scene = v_low.reshape(scenes, local_len, model_width)
    k_gathered, v_gathered = (
        lax.all_gather(k_scene, "seq", axis=1, tiled=True),
        lax.all_gather(v_scene, "seq", axis=1, tiled=True),
    )
    attended, row_lse = attend(q_scene, k_gathered, v_gathered)
    att_low = attended.reshape(row_count, model_width).astype(jnp.bfloat16)
    residual = flat_rows + matmul(att_low, w_out) + b_out
    normed_two, norm_two_pull = jax.vjp(norm_rows, residual, gain_two, shift_two)
    normed_two_low = normed_two.astype(jnp.bfloat16)
    hidden = matmul(normed_two_low, w_up) + b_up
    activated, gelu_pull = jax.vjp(gelu_tanh, hidden)
    act_low = activated.astype(jnp.bfloat16)
    block_rows = residual + matmul(act_low, w_down) + b_down
    block_out = block_rows.reshape(scenes, local_len, model_width).astype(jnp.bfloat16)
    masked_f = out_grad.astype(jnp.float32) * surface_mask.astype(jnp.float32)[..., None]
    masked_rows = masked_f.reshape(row_count, model_width)
    masked_low = masked_rows.astype(jnp.bfloat16)
    grad_down = matmul_tn(act_low, masked_low)
    grad_bdown = jnp.sum(masked_rows, axis=0)
    act_grad = matmul_nt(masked_low, w_down)
    hidden_low = gelu_pull(act_grad)[0].astype(jnp.bfloat16)
    grad_up = matmul_tn(normed_two_low, hidden_low)
    grad_bup = jnp.sum(hidden_low.astype(jnp.float32), axis=0)
    norm_two_in = matmul_nt(hidden_low, w_up)
    resid_part, grad_gain_two, grad_shift_two = norm_two_pull(norm_two_in)
    resid_grad = masked_rows + resid_part
    resid_low = resid_grad.astype(jnp.bfloat16)
    grad_out = matmul_tn(att_low, resid_low)
    grad_bout = jnp.sum(resid_low.astype(jnp.float32), axis=0)
    att_grad = (
        matmul_nt(resid_low, w_out).astype(jnp.bfloat16).reshape(scenes, local_len, model_width)
    )
    q_parts, delta_parts, k_parts, v_parts = query_side(
        q_scene, k_gathered, v_gathered, row_lse, att_grad
    )
    k_summed, v_summed = (
        lax.psum_scatter(
            k_parts.astype(jnp.bfloat16), "seq", scatter_dimension=2, tiled=True
        ).astype(jnp.float32),
        lax.psum_scatter(
            v_parts.astype(jnp.bfloat16), "seq", scatter_dimension=2, tiled=True
        ).astype(jnp.float32),
    )
    k_grad = join_pairs(k_summed)
    v_grad = join_pairs(v_summed)
    q_grad = join_pairs(q_parts)
    q_grad_low = q_grad.reshape(row_count, model_width).astype(jnp.bfloat16)
    k_grad_low = k_grad.reshape(row_count, model_width).astype(jnp.bfloat16)
    v_grad_low = v_grad.reshape(row_count, model_width).astype(jnp.bfloat16)
    grad_query = matmul_tn(normed_low, q_grad_low)
    grad_key = matmul_tn(normed_low, k_grad_low)
    grad_value = matmul_tn(normed_low, v_grad_low)
    grad_bquery = jnp.sum(q_grad_low.astype(jnp.float32), axis=0)
    grad_bvalue = jnp.sum(v_grad_low.astype(jnp.float32), axis=0)
    norm_one_in = (
        matmul_nt(q_grad_low, w_query)
        + matmul_nt(k_grad_low, w_key)
        + matmul_nt(v_grad_low, w_value)
    )
    token_part, grad_gain_one, grad_shift_one = norm_one_pull(norm_one_in)
    tokens_grad = (
        (resid_grad + token_part).reshape(scenes, local_len, model_width).astype(jnp.bfloat16)
    )
    (
        sum_query,
        sum_key,
        sum_value,
        sum_out,
        sum_bquery,
        sum_bvalue,
        sum_bout,
        sum_gain_one,
        sum_shift_one,
        sum_up,
        sum_down,
        sum_bup,
        sum_bdown,
        sum_gain_two,
        sum_shift_two,
    ) = (
        lax.psum_scatter(grad_query, ("scene", "seq"), scatter_dimension=0, tiled=True),
        lax.psum_scatter(grad_key, ("scene", "seq"), scatter_dimension=0, tiled=True),
        lax.psum_scatter(grad_value, ("scene", "seq"), scatter_dimension=0, tiled=True),
        lax.psum_scatter(grad_out, ("scene", "seq"), scatter_dimension=0, tiled=True),
        lax.psum_scatter(grad_bquery, ("scene", "seq"), scatter_dimension=0, tiled=True),
        lax.psum_scatter(grad_bvalue, ("scene", "seq"), scatter_dimension=0, tiled=True),
        lax.psum_scatter(grad_bout, ("scene", "seq"), scatter_dimension=0, tiled=True),
        lax.psum_scatter(grad_gain_one, ("scene", "seq"), scatter_dimension=0, tiled=True),
        lax.psum_scatter(grad_shift_one, ("scene", "seq"), scatter_dimension=0, tiled=True),
        lax.psum_scatter(grad_up, ("scene", "seq"), scatter_dimension=0, tiled=True),
        lax.psum_scatter(grad_down, ("scene", "seq"), scatter_dimension=0, tiled=True),
        lax.psum_scatter(grad_bup, ("scene", "seq"), scatter_dimension=0, tiled=True),
        lax.psum_scatter(grad_bdown, ("scene", "seq"), scatter_dimension=0, tiled=True),
        lax.psum_scatter(grad_gain_two, ("scene", "seq"), scatter_dimension=0, tiled=True),
        lax.psum_scatter(grad_shift_two, ("scene", "seq"), scatter_dimension=0, tiled=True),
    )
    return (
        block_out,
        tokens_grad,
        sum_query,
        sum_key,
        sum_value,
        sum_out,
        sum_up,
        sum_down,
        sum_bquery,
        sum_bvalue,
        sum_bout,
        sum_bup,
        sum_bdown,
        sum_gain_one,
        sum_shift_one,
        sum_gain_two,
        sum_shift_two,
    )


def solution(mesh):
    placed = (
        P("scene", "seq", None),
        P("scene", "seq"),
        P("scene", "seq", None),
        P(),
        P(),
        P(),
        P(),
        P(),
        P(),
        P(),
        P(),
        P(),
        P(),
        P(),
        P(),
        P(),
        P(),
        P(),
    )
    scenes, n = mesh.shape["scene"], mesh.shape["seq"]
    if (scenes, n) == (2, HEADS):
        on_device = functools.partial(layer_on_device, scenes, n)
    else:
        on_device = on_any_device
    return jax.shard_map(
        on_device,
        mesh=mesh,
        in_specs=placed,
        out_specs=(
            P("scene", "seq", None),
            P("scene", "seq", None),
            P(("scene", "seq"), None),
            P(("scene", "seq"), None),
            P(("scene", "seq"), None),
            P(("scene", "seq"), None),
            P(("scene", "seq"), None),
            P(("scene", "seq"), None),
            P(("scene", "seq")),
            P(("scene", "seq")),
            P(("scene", "seq")),
            P(("scene", "seq")),
            P(("scene", "seq")),
            P(("scene", "seq")),
            P(("scene", "seq")),
            P(("scene", "seq")),
            P(("scene", "seq")),
        ),
        check_vma=False,
    )
```

```python
import functools

import jax
import jax.numpy as jnp
from jax import lax
from jax.experimental import pallas as pl
from jax.experimental.pallas import tpu as pltpu
from jax.sharding import PartitionSpec as P

HEADS = 16
HEAD_DIM = 64
MESH = pl.DeviceIdType.MESH
f32 = jnp.float32
bf16 = jnp.bfloat16

norm_eps = 1e-05
score_scale = 0.125
FORWARD_LIMIT = 60 << 20
gelu_coef = 0.7978845608028654


def matmul(left, right):
    return jnp.dot(left, right, preferred_element_type=jnp.float32)


def contract(left, right, left_dim, right_dim):
    return lax.dot_general(
        left, right, (((left_dim,), (right_dim,)), ((), ())), preferred_element_type=jnp.float32
    )


def matmul_tn(left, right):
    return contract(left, right, 0, 0)


def matmul_nt(left, right):
    return contract(left, right, 1, 1)


def normalise(values):
    row_mean = jnp.mean(values, axis=-1, keepdims=True)
    centred = values - row_mean
    row_var = jnp.mean(centred * centred, axis=-1, keepdims=True)
    inverse = lax.rsqrt(row_var + norm_eps)
    return centred * inverse, inverse


def norm_back(grad, scaled, inverse, gain):
    weighted = grad * gain
    back = inverse * (
        weighted
        - jnp.mean(weighted, axis=-1, keepdims=True)
        - scaled * jnp.mean(weighted * scaled, axis=-1, keepdims=True)
    )
    return back, jnp.sum(grad * scaled, axis=0), jnp.sum(grad, axis=0)


def greet(partners):
    barrier = pltpu.get_barrier_semaphore()
    for partner in partners:
        pl.semaphore_signal(barrier, inc=1, device_id=partner, device_id_type=MESH)
    return lambda: pl.semaphore_wait(barrier, len(partners))


def remote(src, dst, send_sem, recv_sem, device):
    return pltpu.make_async_remote_copy(
        src_ref=src,
        dst_ref=dst,
        send_sem=send_sem,
        recv_sem=recv_sem,
        device_id=device,
        device_id_type=MESH,
    )


def flipped(index, other):
    out = 0
    for weight in (1, 2, 4, 8):
        bit, turn = lax.rem(index // weight, 2), lax.rem(other // weight, 2)
        out = out + weight * (bit + turn - 2 * bit * turn)
    return out


def forward_kernel(n, tok, *refs):
    (
        tokens_ref,
        gain_ref,
        shift_ref,
        wq_ref,
        wk_ref,
        wv_ref,
        bq_ref,
        bv_ref,
        att_ref,
        normed_out,
        q_out,
        k_out,
        v_out,
        o_out,
        lse_out,
        rows_in,
        gain,
        shift,
        b_query,
        b_value,
        land,
        w_pair,
        w_head,
        bias,
        q_all,
        k_all,
        v_all,
        k_nat,
        o_all,
        lse_all,
        stats,
        att_send,
        load_sem,
        gather_send,
        gather_recv,
        save_sem,
        out_send,
        out_recv,
        out_local,
        last_sem,
    ) = refs
    me = lax.axis_index("seq")
    scene = lax.axis_index("scene")
    core = lax.rem(me, 2)
    chips = n // 2
    wide = 2 * tok
    half_rows = tok // 2
    devices = [flipped(me, s) for s in range(n)]

    def rows(head):
        return pl.ds(pl.multiple_of(head * HEAD_DIM, HEAD_DIM), HEAD_DIM)

    def lanes(block, width=tok):
        return pl.ds(pl.multiple_of(block * width, width), width)

    tokens_load = pltpu.make_async_copy(tokens_ref, rows_in, load_sem.at[0])
    tokens_load.start()
    weight_loads = [
        pltpu.make_async_copy(ref.at[:, lanes(me // 2, 128)], w_pair.at[i], load_sem.at[1 + i])
        for i, ref in enumerate((wk_ref, wq_ref, wv_ref))
    ]
    vector_loads = [
        pltpu.make_async_copy(src, dst, load_sem.at[4 + i])
        for i, (src, dst) in enumerate(
            ((gain_ref, gain), (shift_ref, shift), (bq_ref, b_query), (bv_ref, b_value))
        )
    ]
    for load in vector_loads + weight_loads:
        load.start()
    all_here = greet([(scene, devices[s]) for s in range(1, n)])

    def gather_copy(slot, over, part):
        piece = slice(part * half_rows, (part + 1) * half_rows)
        there = slot ^ over
        return remote(
            land.at[slot, piece, :],
            land.at[there, piece, :],
            gather_send.at[there, part],
            gather_recv.at[there, part],
            (scene, devices[over]),
        )

    routes = {0: (4, 2, 8, 1), 8: (4, 2, 1), 4: (2, 1), 12: (2, 1), 2: (1,), 6: (1,), 10: (1,), 14: (1,)}

    def routes_of(slot, part):
        if part == 1 and slot == 12:
            return (1,)
        if part == 1 and slot == 10:
            return (4, 1)
        return routes.get(slot, ())

    def came_over(slot, part):
        for source in range(n):
            for over in routes_of(source, part):
                if source ^ over == slot:
                    return over

    sent = []
    saves = []

    def forward(slot, part):
        for over in routes_of(slot, part):
            copy = gather_copy(slot, over, part)
            copy.start()
            sent.append(copy)

    def arrive(slot, part):
        over = came_over(slot, part)
        gather_copy(slot ^ over, over, part).wait_recv()
        forward(slot, part)

    for load in [tokens_load] + vector_loads:
        load.wait()
    for part in range(2):
        piece = slice(part * half_rows, (part + 1) * half_rows)
        scaled, _ = normalise(rows_in[piece, :].astype(f32))
        land[0, piece, :] = (scaled * gain[...] + shift[...]).astype(bf16)
        if part == 0:
            all_here()
        forward(0, part)

    odd = core == 1
    for i, load in enumerate(weight_loads):
        load.wait()
        pair = w_pair[i].astype(f32)
        w_head[:, HEAD_DIM * i : HEAD_DIM * i + HEAD_DIM] = jnp.where(
            odd, pair[:, HEAD_DIM:], pair[:, :HEAD_DIM]
        ).astype(bf16)
    for i, ref in ((1, b_query), (2, b_value)):
        pair = ref[0:1, lanes(me // 2, 128)]
        bias[0:1, HEAD_DIM * i : HEAD_DIM * i + HEAD_DIM] = jnp.where(
            odd, pair[:, HEAD_DIM:], pair[:, :HEAD_DIM]
        )
    bias[0:1, :HEAD_DIM] = jnp.zeros((1, HEAD_DIM), f32)

    def project(slot):
        made = contract(land[slot], w_head[...], 1, 0) + bias[0:1, :]
        low = made.astype(bf16)
        turned = low.T
        span = slice(slot * tok, (slot + 1) * tok)
        k_nat[span, :] = low[:, :HEAD_DIM]
        k_all[:, span] = turned[:HEAD_DIM]
        q_all[:, span] = turned[HEAD_DIM : 2 * HEAD_DIM] * jnp.asarray(score_scale, bf16)
        v_all[:, span] = turned[2 * HEAD_DIM :]
        save = pltpu.make_async_copy(land.at[slot], normed_out.at[span, :], save_sem.at[slot])
        save.start()
        saves.append(save)

    def attend(span, first, state):
        top, total, acc = state
        keys = slice(first, first + chips // 2 * wide)
        scores = contract(k_nat[keys, :], q_all[:, span], 1, 0)
        here = jnp.max(scores, axis=0, keepdims=True)
        new_top = here if top is None else jnp.maximum(top, here)
        shifted = jnp.exp(scores - new_top)
        part_sum = jnp.sum(shifted, axis=0, keepdims=True)
        part = contract(v_all[:, keys], shifted.astype(bf16), 1, 0)
        if top is None:
            return new_top, part_sum, part
        fade = jnp.exp(top - new_top)
        return new_top, total * fade + part_sum, acc * fade + part

    middle = chips // 2 * wide

    def early(i):
        span = slice(i * wide, (i + 1) * wide)
        top, total, acc = attend(span, 0, (None, None, None))
        stats[0:1, span] = top
        stats[1:2, span] = total
        o_all[:, span] = acc

    def close(i, span, state):
        top, total, acc = state
        out = acc / total
        o_all[:, span] = out
        lse_all[:, span] = jnp.broadcast_to(top + jnp.log(total), (8, wide))
        low = out.astype(bf16)
        att_send[i, 0] = low[:, :tok]
        att_send[i, 1] = low[:, tok:]

    def out_copy(i, flip):
        return remote(
            att_send.at[i, flip],
            att_ref.at[rows(me), :],
            out_send.at[i, flip],
            out_recv.at[i, flip],
            (scene, flipped(me, 2 * i + flip)),
        )

    project(0)
    for part in range(2):
        arrive(1, part)
    project(1)
    for part in range(2):
        arrive(2, part)
        arrive(4, part)
    project(2)
    for slot in (3, 5):
        for part in range(2):
            arrive(slot, part)
    project(3)
    project(4)
    project(5)
    for part in range(2):
        arrive(8, part)
    for slot in (6, 7):
        for part in range(2):
            arrive(slot, part)
    project(6)
    project(7)
    early(0)
    early(1)
    arrive(9, 0)
    arrive(9, 1)
    project(8)
    project(9)
    for part in range(2):
        arrive(12, part)
        arrive(10, part)
    early(2)
    for slot in (11, 13):
        for part in range(2):
            arrive(slot, part)
    project(10)
    project(11)
    early(3)
    project(12)
    project(13)
    arrive(14, 0)
    arrive(14, 1)
    project(14)
    arrive(15, 0)
    arrive(15, 1)
    project(15)
    for i, (src, dst) in enumerate(((q_all, q_out), (k_all, k_out), (v_all, v_out))):
        save = pltpu.make_async_copy(src, dst, last_sem.at[i])
        save.start()
        saves.append(save)

    def late_body(j, carry):
        i = chips - 1 - j
        span = lanes(i, wide)
        close(i, span, attend(span, middle, attend(span, 0, (None, None, None))))
        out_copy(i, 0).start()
        out_copy(i, 1).start()
        return carry

    lax.fori_loop(0, chips // 2, late_body, 0)

    def rest(i, span):
        state = (stats[0:1, span], stats[1:2, span], o_all[:, span])
        close(i, span, attend(span, middle, state))

    def rest_body(j, carry):
        i = chips // 2 - 1 - j
        rest(i, lanes(i, wide))
        out_copy(i, 0).start()
        out_copy(i, 1).start()
        return carry

    lax.fori_loop(0, chips // 2 - 1, rest_body, 0)
    rest(0, slice(0, wide))
    mine = pltpu.make_async_copy(att_send.at[0, 0], att_ref.at[rows(me), :], out_local)
    mine.start()
    out_copy(0, 1).start()
    for i, (src, dst) in enumerate(((o_all, o_out), (lse_all, lse_out))):
        save = pltpu.make_async_copy(src, dst, last_sem.at[3 + i])
        save.start()
        saves.append(save)
    for copy in sent:
        copy.wait_send()
    mine.wait()
    out_copy(0, 1).wait()

    def drain(i, carry):
        out_copy(i, 0).wait()
        out_copy(i, 1).wait()
        return carry

    lax.fori_loop(1, chips, drain, 0)
    for save in saves:
        save.wait()


def attention_forward(n, tokens, gain, shift, w_query, w_key, w_value, b_query, b_value):
    tok, width = tokens.shape
    length = n * tok
    any_spec = pl.BlockSpec(memory_space=pl.ANY)
    head_all = jax.ShapeDtypeStruct((HEAD_DIM, length), bf16)
    dma = pltpu.SemaphoreType.DMA
    return pl.pallas_call(
        functools.partial(forward_kernel, n, tok),
        out_shape=(
            jax.ShapeDtypeStruct((width, tok), bf16),
            jax.ShapeDtypeStruct((length, width), bf16),
            head_all,
            head_all,
            head_all,
            jax.ShapeDtypeStruct((HEAD_DIM, length), f32),
            jax.ShapeDtypeStruct((8, length), f32),
        ),
        in_specs=[any_spec] * 8,
        out_specs=[any_spec] * 7,
        scratch_shapes=[
            pltpu.VMEM((tok, width), bf16),
            pltpu.VMEM((1, width), f32),
            pltpu.VMEM((1, width), f32),
            pltpu.VMEM((1, width), f32),
            pltpu.VMEM((1, width), f32),
            pltpu.VMEM((n, tok, width), bf16),
            pltpu.VMEM((3, width, 2 * HEAD_DIM), bf16),
            pltpu.VMEM((width, 3 * HEAD_DIM), bf16),
            pltpu.VMEM((8, 3 * HEAD_DIM), f32),
            pltpu.VMEM((HEAD_DIM, length), bf16),
            pltpu.VMEM((HEAD_DIM, length), bf16),
            pltpu.VMEM((HEAD_DIM, length), bf16),
            pltpu.VMEM((length, HEAD_DIM), bf16),
            pltpu.VMEM((HEAD_DIM, length), f32),
            pltpu.VMEM((8, length), f32),
            pltpu.VMEM((8, length), f32),
            pltpu.VMEM((n // 2, 2, HEAD_DIM, tok), bf16),
            dma((8,)),
            dma((n, 2)),
            dma((n, 2)),
            dma((n,)),
            dma((n // 2, 2)),
            dma((n // 2, 2)),
            dma,
            dma((5,)),
        ],
        compiler_params=pltpu.CompilerParams(
            collective_id=0, has_side_effects=True, vmem_limit_bytes=FORWARD_LIMIT
        ),
        name="attention_forward",
    )(
        tokens,
        gain[None],
        shift[None],
        w_query,
        w_key,
        w_value,
        b_query[None],
        b_value[None],
    )


CHUNKS = 9
TICKS = CHUNKS + 4
SLOTS = 3


def halving_plan(full, got0, got1a, got1b, got2a, got2b, got3, got4, total, send_sem, recv_sem):
    me = lax.axis_index("seq")
    x = lax.axis_index("scene")
    core = lax.rem(me, 2)
    y = lax.rem(me // 2, 2)
    z0 = lax.rem(me // 4, 2)
    z1 = me // 8
    at_core = (x, me + 1 - 2 * core)
    at_x = (1 - x, me)
    at_y = (x, me + 2 - 4 * y)
    at_z0 = (x, me + 4 - 8 * z0)
    at_z1 = (x, me + 8 - 16 * z1)
    up, low = slice(0, 64), slice(64, 128)

    def copy_of(slot, c):
        src, dst, device = (
            lambda: (full.at[lax.rem(c, SLOTS), :, :, :, :, 1 - core], got0.at[c], at_core),
            lambda: (got0.at[c, 1 - x, :, :, :, up, :], got1a.at[c], at_x),
            lambda: (got0.at[c, :, :, :, 1 - y, low, :], got1b.at[c], at_y),
            lambda: (got1a.at[c, :, 1 - z0], got2a.at[c], at_z0),
            lambda: (got1b.at[c, 1 - x], got2b.at[c], at_x),
            lambda: (got2a.at[c, :, 1 - y], got3.at[c, :, up, :], at_y),
            lambda: (got2b.at[c, :, 1 - z0], got3.at[c, :, low, :], at_z0),
            lambda: (got3.at[c, 1 - z1], got4.at[c], at_z1),
        )[slot]()
        going = send_sem.at[c] if slot == 0 else send_sem.at[CHUNKS + slot]
        return remote(src, dst, going, recv_sem.at[c, slot], device)

    def sum1(c):
        copy_of(0, c).wait_recv()
        got0[c] = got0[c] + full[lax.rem(c, SLOTS), :, :, :, :, core]

    def start1(c):
        copy_of(1, c).start()
        copy_of(2, c).start()

    def stage2(c):
        copy_of(1, c).wait_recv()
        got1a[c] = got1a[c] + got0[c, x, :, :, :, up, :]
        copy_of(3, c).start()
        copy_of(2, c).wait_recv()
        got1b[c] = got1b[c] + got0[c, :, :, :, y, low, :]
        copy_of(4, c).start()

    def stage3(c):
        copy_of(3, c).wait_recv()
        got2a[c] = got2a[c] + got1a[c, :, z0]
        copy_of(5, c).start()
        copy_of(4, c).wait_recv()
        got2b[c] = got2b[c] + got1b[c, x]
        copy_of(6, c).start()

    def stage4(c):
        copy_of(5, c).wait_recv()
        got3[c, :, up, :] = got3[c, :, up, :] + got2a[c, :, y]
        copy_of(6, c).wait_recv()
        got3[c, :, low, :] = got3[c, :, low, :] + got2b[c, :, z0]
        copy_of(7, c).start()

    def stage5(c):
        copy_of(7, c).wait_recv()
        total[c] = got3[c, z1].astype(f32) + got4[c].astype(f32)

    def tick(when):
        for stage, c in (
            (stage5, when - 4),
            (stage4, when - 3),
            (stage3, when - 2),
            (stage2, when - 1),
            (start1, when + 1),
        ):

            @pl.when((c >= 0) & (c < CHUNKS))
            def _(stage=stage, c=c):
                stage(c)

    def settle():
        for slot, src in enumerate((got1a, got1a, got1b, got2a, got2b, got3, got3, got4)):
            if slot:
                everything = src.at[:, :, up, :] if slot in (5, 6) else src
                pltpu.make_async_copy(everything, everything, send_sem.at[CHUNKS + slot]).wait()

    return copy_of, sum1, start1, tick, settle


def tail_kernel(n, tok, *refs):
    (
        q_ref,
        k_ref,
        v_ref,
        o_ref,
        lse_ref,
        act_ref,
        slope_ref,
        masked_ref,
        two_ref,
        residual_ref,
        att_ref,
        normed_ref,
        wd_ref,
        wu_ref,
        wo_ref,
        wq_ref,
        wk_ref,
        wv_ref,
        tokens_ref,
        gain_ref,
        gain_two_ref,
        b_down_ref,
        block_out,
        tokens_out,
        total,
        pack_got,
        small_got,
        early_got,
        q_all,
        k_all,
        v_all,
        d_all,
        d_send,
        o_all,
        lse_all,
        low,
        act,
        masked,
        two,
        hidden,
        att,
        resid_low,
        act_t,
        two_t,
        full,
        got0,
        got1a,
        got1b,
        got2a,
        got2b,
        got3,
        got4,
        land,
        rows_in,
        resid,
        gain_one,
        gain_two,
        b_down,
        pack,
        small,
        early,
        load_sem,
        ring_sem,
        weight_sem,
        normed_sem,
        in_send,
        in_recv,
        in_local,
        kv_send,
        kv_recv,
        kv_local,
        q_send,
        q_recv,
        q_local,
        half_send,
        half_recv,
        last_send,
        last_recv,
        last_local,
    ) = refs
    me = lax.axis_index("seq")
    scene = lax.axis_index("scene")
    chips = n // 2
    length = n * tok
    wide = 2 * tok
    devices = 2 * n
    width = masked.shape[1]
    mine = scene * n + me

    def rows(head):
        return pl.ds(pl.multiple_of(head * HEAD_DIM, HEAD_DIM), HEAD_DIM)

    def lanes(block, width=tok):
        return pl.ds(pl.multiple_of(block * width, width), width)

    def by_block(ref, block):
        return ref.at[:, 1024 * block : 1024 * block + 1024]

    loads = [
        pltpu.make_async_copy(src, dst, load_sem.at[i])
        for i, (src, dst) in enumerate(
            [(by_block(act_ref, i), act.at[tok * i : tok * i + tok, :]) for i in range(4)]
            + [
                (masked_ref, masked),
                (q_ref, q_all),
                (k_ref, k_all),
                (v_ref, v_all),
                (o_ref, o_all),
                (lse_ref, lse_all),
                (two_ref, two),
                (att_ref, att),
                (residual_ref, resid),
                (tokens_ref, rows_in),
                (gain_ref, gain_one),
                (gain_two_ref, gain_two),
                (b_down_ref, b_down),
            ]
        )
    ]
    for load in loads:
        load.start()

    def peer(j):
        index = lax.rem(mine + j, devices)
        return index, (index // n, lax.rem(index, n))

    all_here = greet([peer(j)[1] for j in range(1, devices)])

    half, sum1, start1, tick, settle = halving_plan(
        full, got0, got1a, got1b, got2a, got2b, got3, got4, total, half_send, half_recv
    )

    def chunk_begin(c):
        @pl.when(c >= SLOTS)
        def _():
            half(0, c - SLOTS).wait_send()

        return lax.rem(c, SLOTS)

    def chunk_end(c):
        half(0, c).start()

        @pl.when((c >= 1) & (c != 4))
        def _():
            sum1(c - 1)

    def down_chunk(c):
        slot = chunk_begin(c)
        columns = masked[:, lanes(c, 256)]
        for block in range(4):
            part = contract(act_t[1024 * block : 1024 * block + 1024, :], columns, 1, 0)
            full[slot, block // 2, block % 2] = part.astype(bf16).reshape(2, 2, 2, 128, 256)
        chunk_end(c)

    def narrow_chunk(c, left, right):
        slot = chunk_begin(c)
        for block in range(4):
            part = contract(left, right[:, 256 * block : 256 * block + 256], 1, 0)
            full[slot, :, :, :, :, :, 32 * block : 32 * block + 32, :] = part.astype(bf16).reshape(
                2, 2, 2, 2, 2, 32, 256
            )
        chunk_end(c)

    for block in range(4):
        loads[block].wait()
        act_t[1024 * block : 1024 * block + 1024, :] = act[tok * block : tok * block + tok, :].T
    loads[4].wait()
    all_here()

    def first_chunk(c, carry):
        down_chunk(c)

        @pl.when((c >= 1) & (c <= 2))
        def _():
            start1(c - 1)

        return carry

    lax.fori_loop(0, 4, first_chunk, 0)

    def feed_forward(ring, slope, out_acc, two_acc):
        def weight_load(i):
            if i < 4:
                src = wd_ref.at[1024 * i : 1024 * i + 1024, :]
            elif i < 8:
                src = wu_ref.at[:, 1024 * (i - 4) : 1024 * (i - 4) + 1024]
            else:
                src = wo_ref
            return pltpu.make_async_copy(src, ring.at[i % 2], ring_sem.at[i % 2])

        def slope_load(i):
            return pltpu.make_async_copy(by_block(slope_ref, i), slope.at[i % 2], ring_sem.at[2 + i % 2])

        for i in range(2):
            weight_load(i).start()
            slope_load(i).start()
        for load in loads[10:]:
            load.wait()
        masked_sum = jnp.sum(masked[...].astype(f32), axis=0, keepdims=True)
        for i in range(4):
            weight_load(i).wait()
            slope_load(i).wait()
            there = slice(tok * i, tok * i + tok)
            part = contract(act[there, :], ring[i % 2], 1, 0)
            out_acc[...] = resid[...] + b_down[...] + part if i == 0 else out_acc[...] + part
            grown = contract(masked[...], ring[i % 2], 1, 1) * slope[i % 2]
            weight_load(i + 2).start()
            if i < 2:
                slope_load(i + 2).start()
            grown = grown.astype(bf16)
            hidden[there, :] = grown
            sums = jnp.sum(grown.astype(f32), axis=0, keepdims=True)
            for j in range(8):
                early[8 * i + j, 4:5, :] = sums[:, 128 * j : 128 * j + 128]
            if i == 1:
                tick(1)
        block_out[...] = out_acc[...].astype(bf16)
        sum1(3)
        for i in range(4):
            weight_load(4 + i).wait()
            part = contract(hidden[tok * i : tok * i + tok, :], ring[i % 2], 1, 1)
            two_acc[...] = part if i == 0 else two_acc[...] + part
            if i < 3:
                weight_load(6 + i).start()
            if i == 1:
                tick(2)
        scaled, inverse = normalise(resid[...])
        part, gain_grad, shift_grad = norm_back(two_acc[...], scaled, inverse, gain_two[...])
        resid[...] = masked[...].astype(f32) + part
        resid_low[...] = resid[...].astype(bf16)
        low_sum = jnp.sum(resid_low[...].astype(f32), axis=0, keepdims=True)
        for row, vector in enumerate((low_sum, masked_sum, gain_grad[None], shift_grad[None])):
            for d in range(devices):
                start = 128 * (d // 4)
                early[d, row : row + 1, :] = vector[:, start : start + 128]
        weight_load(8).wait()
        d_send[...] = contract(ring[0], resid_low[...], 1, 1).astype(bf16)

    pl.run_scoped(
        feed_forward,
        pltpu.VMEM((2, 1024, 1024), bf16),
        pltpu.VMEM((2, tok, 1024), f32),
        pltpu.VMEM((tok, width), f32),
        pltpu.VMEM((tok, width), f32),
    )

    copies = []
    for s in reversed(range(1, n)):
        head = flipped(me, s)
        copies.append(
            remote(
                d_send.at[rows(head), :],
                d_all.at[:, s * tok : s * tok + tok],
                in_send,
                in_recv,
                (scene, head),
            )
        )
        copies[-1].start()
    local = pltpu.make_async_copy(d_send.at[rows(me), :], d_all.at[:, :tok], in_local)
    local.start()

    def pack_copy(j):
        index, device = peer(j)
        return remote(pack.at[index], pack_got.at[mine], last_send.at[0], last_recv.at[0], device)

    def small_copy(j):
        index, device = peer(j)
        return remote(
            small.at[0:4, lanes(index // 4, 128)],
            small_got.at[mine, 0:4, :],
            last_send.at[1],
            last_recv.at[1],
            device,
        )

    def early_copy(j):
        index, device = peer(j)
        return remote(
            early.at[index, 0:5, :],
            early_got.at[mine, 0:5, :],
            last_send.at[2],
            last_recv.at[2],
            device,
        )

    kept = [
        pltpu.make_async_copy(pack.at[mine], pack_got.at[mine], last_local.at[0]),
        pltpu.make_async_copy(
            small.at[0:4, lanes(mine // 4, 128)], small_got.at[mine, 0:4, :], last_local.at[1]
        ),
        pltpu.make_async_copy(
            early.at[mine, 0:5, :], early_got.at[mine, 0:5, :], last_local.at[2]
        ),
    ]
    kept[2].start()

    def early_body(j, carry):
        early_copy(j).start()
        return carry

    lax.fori_loop(1, devices, early_body, 0)
    two_t[...] = two[...].T
    for load in loads[5:10]:
        load.wait()

    def chunk(step):
        @pl.when(step == 0)
        def _():
            narrow_chunk(step + 7, two_t[...], hidden[3 * tok :, :])
            normed_load(0).start()

        @pl.when(step == 1)
        def _():
            narrow_chunk(step + 7, att[...], resid_low[...])
            normed_load(1).start()

        @pl.when(step == 2)
        def _():
            sum1(CHUNKS - 1)

    def normed_load(i):
        return pltpu.make_async_copy(
            normed_ref.at[1024 * i : 1024 * i + 1024, :],
            (act, hidden)[i % 2],
            normed_sem.at[i % 2],
        )

    def q_copy(step, flip):
        slot = 2 * step + flip
        return remote(
            low.at[0, :, lanes(slot)],
            land.at[0, rows(me), :],
            q_send,
            q_recv,
            (scene, flipped(me, slot)),
        )

    def kv_copy(step, flip):
        slot = 2 * step + flip
        return remote(
            low.at[1:3, :, lanes(slot)],
            land.at[1:3, rows(me), :],
            kv_send,
            kv_recv,
            (scene, flipped(me, slot)),
        )

    own = [
        pltpu.make_async_copy(low.at[0, :, :tok], land.at[0, rows(me), :], q_local),
        pltpu.make_async_copy(low.at[1:3, :, :tok], land.at[1:3, rows(me), :], kv_local),
    ]

    weight_loads = [
        pltpu.make_async_copy(
            ref.at[:, :, :, :, 256 * block : 256 * block + 256],
            full.at[a, block // 2, block % 2],
            weight_sem.at[a, block],
        )
        for a, ref in enumerate((wq_ref, wk_ref, wv_ref))
        for block in range(4)
    ]

    def load_weights():
        for c in range(CHUNKS - SLOTS, CHUNKS):
            half(0, c).wait_send()
        for load in weight_loads:
            load.start()

    def attention(q_nat, k_nat, v_nat, d_nat, delta, dq_acc):
        q_nat[...] = q_all[...].T
        k_nat[...] = k_all[...].T
        v_nat[...] = v_all[...].T
        dq_acc[...] = jnp.zeros_like(dq_acc)

        def middle_chunk(i, carry):
            there = pl.ds(pl.multiple_of(i * tok, tok), tok)
            narrow_chunk(4 + i, two_t[...], hidden[there, :])

            @pl.when(i == 1)
            def _():
                tick(3)

            return carry

        lax.fori_loop(0, 3, middle_chunk, 0)
        local.wait()
        pltpu.make_async_copy(d_all.at[:, tok:], d_all.at[:, tok:], in_recv).wait()
        d_nat[...] = d_all[...].T
        delta[...] = jnp.broadcast_to(
            jnp.sum(d_all[...].astype(f32) * o_all[...], axis=0, keepdims=True), delta.shape
        )

        def keys(step, last):
            span = lanes(step, wide)
            k_here, v_here, kt_here = k_nat[span, :], v_nat[span, :], k_all[:, span]
            dk = dv = None
            for i in reversed(range(chips)):
                there = slice(i * wide, (i + 1) * wide)
                scores = contract(k_here, q_all[:, there], 1, 0)
                prob = jnp.exp(scores - lse_all[0:1, there])
                dprob = contract(v_here, d_all[:, there], 1, 0)
                dscore = (prob * (dprob - delta[0:1, there])).astype(bf16)
                v_part = contract(prob.astype(bf16), d_nat[there, :], 1, 0)
                k_part = contract(dscore, q_nat[there, :], 1, 0)
                dk = k_part if dk is None else dk + k_part
                dv = v_part if dv is None else dv + v_part
                dq = dq_acc[:, there] + contract(kt_here, dscore, 1, 0)
                if last:
                    low[0, :, there] = (dq * score_scale).astype(bf16)
                    if i == 0:
                        own[0].start()
                    else:
                        q_copy(i, 0).start()
                    q_copy(i, 1).start()
                else:
                    dq_acc[:, there] = dq
            low[1, :, span] = dk.astype(bf16).T
            low[2, :, span] = dv.astype(bf16).T

        def step_body(step, carry):
            tick(step + 4)
            chunk(step)
            keys(chips - 1 - step, False)

            kv_copy(chips - 1 - step, 0).start()
            kv_copy(chips - 1 - step, 1).start()
            return carry

        lax.fori_loop(0, chips - 1, step_body, 0)
        load_weights()
        tick(11)
        keys(0, True)
        own[1].start()
        kv_copy(0, 1).start()

    pl.run_scoped(
        attention,
        *(pltpu.VMEM((length, HEAD_DIM), bf16) for _ in range(4)),
        pltpu.VMEM((8, length), f32),
        pltpu.VMEM((HEAD_DIM, length), f32),
    )

    head_acc = None
    for i in range(length // 1024):
        normed_load(i).wait()
        left = low[:, :, 1024 * i : 1024 * i + 1024].reshape(3 * HEAD_DIM, 1024)
        part = contract(left, (act, hidden)[i % 2][...], 1, 0)
        head_acc = part if head_acc is None else head_acc + part
        if i + 2 < length // 1024:
            normed_load(i + 2).start()
    by_row = head_acc.T
    share = width // devices
    pack[:, :share, :] = by_row[:, : 2 * HEAD_DIM].astype(bf16).reshape(devices, share, 2 * HEAD_DIM)
    third = by_row[:, 2 * HEAD_DIM :].astype(bf16).reshape(devices, 2, share // 2, HEAD_DIM)
    pack[:, share:, :] = jnp.concatenate([third[:, 0], third[:, 1]], axis=-1)

    kept[0].start()

    def pack_body(j, carry):
        pack_copy(j).start()
        return carry

    lax.fori_loop(1, devices, pack_body, 0)

    for copy in own:
        copy.wait()
    for sem, others in ((q_recv, land.at[0, HEAD_DIM:, :]), (kv_recv, land.at[1:3, HEAD_DIM:, :])):
        pltpu.make_async_copy(others, others, sem).wait()
    for load in weight_loads:
        load.wait()
    def first_norm(back_in):
        for i in range(4):
            part = None
            for a in range(3):
                left = jnp.concatenate(
                    [full[a, b // 2, b % 2, i // 2, i % 2].reshape(256, 256) for b in range(4)],
                    axis=1,
                )
                here = contract(left, land[a], 1, 0)
                part = here if part is None else part + here
            back_in[:, 256 * i : 256 * i + 256] = part.T
        scaled, inverse = normalise(rows_in[...].astype(f32))
        token_part, gain_grad, shift_grad = norm_back(back_in[...], scaled, inverse, gain_one[...])
        tokens_out[...] = (resid[...] + token_part).astype(bf16)
        small[2:3, :] = gain_grad[None]
        small[3:4, :] = shift_grad[None]

    pl.run_scoped(first_norm, pltpu.VMEM((tok, width), f32))
    ones = jnp.ones((8, tok), bf16)
    small[0:1, :] = contract(ones, land[0], 1, 1)[0:1]
    small[1:2, :] = contract(ones, land[2], 1, 1)[0:1]
    kept[1].start()

    def small_body(j, carry):
        small_copy(j).start()
        return carry

    lax.fori_loop(1, devices, small_body, 0)

    tick(12)
    for copy in kept:
        copy.wait()
    for i, src in enumerate(
        (pack.at[1:], small_got.at[1:, 0:4, :], early_got.at[1:, 0:5, :])
    ):
        pltpu.make_async_copy(src, src, last_recv.at[i]).wait()
        pltpu.make_async_copy(src, src, last_send.at[i]).wait()
    for sem, others in (
        (in_send, low.at[0, :, tok:]),
        (q_send, low.at[0, :, tok:]),
        (kv_send, low.at[1:3, :, tok:]),
    ):
        pltpu.make_async_copy(others, others, sem).wait()

    settle()


def tail(n, tok, width, hidden_width, *arrays):
    length = n * tok
    chips = n // 2
    devices = 2 * n
    share = width // devices
    any_spec = pl.BlockSpec(memory_space=pl.ANY)
    vmem = pl.BlockSpec(memory_space=pltpu.VMEM)
    dma = pltpu.SemaphoreType.DMA

    def space(*shape, kind=bf16):
        return pltpu.VMEM(shape, kind)

    def out(*shape, kind=f32):
        return jax.ShapeDtypeStruct(shape, kind)

    pieces = CHUNKS
    scratch = (
        [space(HEAD_DIM, length)] * 4
        + [
            space(width, tok),
            space(HEAD_DIM, length, kind=f32),
            space(8, length, kind=f32),
            space(3, HEAD_DIM, length),
            space(hidden_width // 1024 * tok, 1024),
            space(tok, width),
            space(tok, width),
            space(hidden_width // 1024 * tok, 1024),
            space(width, tok),
            space(tok, width),
            space(hidden_width, tok),
            space(width, tok),
            space(SLOTS, 2, 2, 2, 2, 2, 128, 256),
            space(pieces, 2, 2, 2, 2, 128, 256),
            space(pieces, 2, 2, 2, 64, 256),
            space(pieces, 2, 2, 2, 64, 256),
            space(pieces, 2, 2, 64, 256),
            space(pieces, 2, 2, 64, 256),
            space(pieces, 2, 128, 256),
            space(pieces, 128, 256),
            space(3, width, tok),
            space(tok, width),
            space(tok, width, kind=f32),
            space(1, width, kind=f32),
            space(1, width, kind=f32),
            space(1, width, kind=f32),
            space(devices, share + share // 2, 128),
            space(8, width, kind=f32),
            space(devices, 8, 128, kind=f32),
            dma((17,)),
            dma((4,)),
            dma((3, 4)),
            dma((2,)),
            dma,
            dma,
            dma,
            dma,
            dma,
            dma,
            dma,
            dma,
            dma,
            dma((pieces + 8,)),
            dma((pieces, 8)),
        ]
        + [dma((3,))] * 3
    )
    return pl.pallas_call(
        functools.partial(tail_kernel, n, tok),
        out_shape=(
            out(tok, width, kind=bf16),
            out(tok, width, kind=bf16),
            out(pieces, 128, 256),
            out(devices, share + share // 2, 128, kind=bf16),
            out(devices, 8, 128),
            out(devices, 8, 128),
        ),
        in_specs=[any_spec] * 22,
        out_specs=[vmem] * 6,
        scratch_shapes=scratch,
        compiler_params=pltpu.CompilerParams(
            collective_id=1, has_side_effects=True, vmem_limit_bytes=63 << 20
        ),
        name="tail",
    )(*arrays)


def finish_kernel(n, *refs):
    block_in, tokens_in, total, pack_got, small_got, early_got = refs[:6]
    block_out, tokens_out, query_out, key_out, value_out, out_out, up_out, down_out = refs[6:14]
    vectors, up_vector = refs[14:22], refs[22]
    block_out[...] = block_in[...]
    tokens_out[...] = tokens_in[...]
    mine = lax.axis_index("scene") * n + lax.axis_index("seq")
    share = query_out.shape[0]
    for head in range(0, n, 2):
        pair = [
            pack_got[head + i].astype(f32) + pack_got[n + head + i].astype(f32) for i in range(2)
        ]
        columns = slice(head * HEAD_DIM, head * HEAD_DIM + 2 * HEAD_DIM)

        def joined(first, last, start):
            return jnp.concatenate(
                [part[first:last, start : start + HEAD_DIM] for part in pair], axis=1
            )

        query_out[:, columns] = joined(0, share, 0)
        key_out[:, columns] = joined(0, share, HEAD_DIM)
        value_out[: share // 2, columns] = joined(share, share + share // 2, 0)
        value_out[share // 2 :, columns] = joined(share, share + share // 2, HEAD_DIM)
    for i in range(4):
        down_out[:, 256 * i : 256 * i + 256] = total[i]
        out_out[:, 256 * i : 256 * i + 256] = total[8, 32 * i : 32 * i + 32, :]
    for i in range(16):
        up_out[:, 256 * i : 256 * i + 256] = total[4 + i // 4, 32 * (i % 4) : 32 * (i % 4) + 32, :]
    turn = lax.rem(128 - 32 * lax.rem(mine, 4), 128)
    late = pltpu.roll(jnp.sum(small_got[...], axis=0), turn, 1)
    early = jnp.sum(early_got[...], axis=0)
    up_vector[...] = early[4]
    early = pltpu.roll(early, turn, 1)
    for i in range(4):
        vectors[i][...] = late[i, :share]
        vectors[4 + i][...] = early[i, :share]


def finish(n, block_rows, tokens_grad, total, pack_got, small_got, early_got):
    tok, width = tokens_grad.shape
    devices = 2 * n
    share = width // devices
    vmem = pl.BlockSpec(memory_space=pltpu.VMEM)

    def out(*shape):
        return jax.ShapeDtypeStruct(shape, f32)

    return pl.pallas_call(
        functools.partial(finish_kernel, n),
        out_shape=(
            jax.ShapeDtypeStruct((tok, width), bf16),
            jax.ShapeDtypeStruct((tok, width), bf16),
            out(share, width),
            out(share, width),
            out(share, width),
            out(share, width),
            out(share, 4 * width),
            out(4 * share, width),
        )
        + (out(share),) * 8
        + (out(4 * share),),
        in_specs=[vmem] * 6,
        out_specs=[vmem] * 17,
        compiler_params=pltpu.CompilerParams(vmem_limit_bytes=60 << 20),
        name="finish",
    )(block_rows, tokens_grad, total, pack_got, small_got, early_got)


def gelu_both(values):
    cubic = gelu_coef * (values + 0.044715 * values * values * values)
    bend = jnp.tanh(cubic)
    slope = gelu_coef * (1.0 + 3.0 * 0.044715 * values * values)
    grad = 0.5 * (1.0 + bend) + 0.5 * values * (1.0 - bend * bend) * slope
    return 0.5 * values * (1.0 + bend), grad


def layer_on_device(
    scenes,
    n,
    tokens,
    surface_mask,
    out_grad,
    w_query,
    w_key,
    w_value,
    w_out,
    w_up,
    w_down,
    b_query,
    b_value,
    b_out,
    b_up,
    b_down,
    gain_one,
    shift_one,
    gain_two,
    shift_two,
):
    _, tok, width = tokens.shape
    rows = tokens[0].astype(f32)
    att_t, normed_all, q_all, k_all, v_all, o_all, lse_all = attention_forward(
        n, tokens[0], gain_one, shift_one, w_query, w_key, w_value, b_query, b_value
    )

    att_t, out_grad, surface_mask = lax.optimization_barrier((att_t, out_grad, surface_mask))
    residual = rows + matmul_tn(att_t, w_out) + b_out
    scaled_two, _ = normalise(residual)
    normed_two = (scaled_two * gain_two + shift_two).astype(bf16)
    activated, slope = gelu_both(matmul(normed_two, w_up) + b_up)
    activated = activated.astype(bf16)
    masked = out_grad[0] * surface_mask[0].astype(bf16)[:, None]
    arrived = tail(
        n,
        tok,
        width,
        w_up.shape[1],
        q_all,
        k_all,
        v_all,
        o_all,
        lse_all,
        activated,
        slope,
        masked,
        normed_two,
        residual,
        att_t,
        normed_all,
        w_down,
        w_up,
        w_out,
        *(w.reshape(2, 2, 2, 128, width) for w in (w_query, w_key, w_value)),
        tokens[0],
        gain_one[None],
        gain_two[None],
        b_down[None],
    )
    block_out, tokens_grad, *sums = finish(n, *arrived)
    bquery, bvalue, gone, sone, bout, bdown, gtwo, stwo, bup = sums[6:]
    return (
        block_out[None],
        tokens_grad[None],
        *sums[:6],
        bquery,
        bvalue,
        bout,
        bup,
        bdown,
        gone,
        sone,
        gtwo,
        stwo,
    )


def norm_rows(values, gain, shift):
    row_mean = jnp.mean(values, axis=-1, keepdims=True)
    centred = values - row_mean
    row_var = jnp.mean(centred * centred, axis=-1, keepdims=True)
    return centred * lax.rsqrt(row_var + norm_eps) * gain + shift


def gelu_tanh(values):
    return (
        0.5 * values * (1.0 + jnp.tanh(gelu_coef * (values + 0.044715 * values * values * values)))
    )


def take_pair(array_in, pair_index):
    pair_width = 2 * HEAD_DIM
    sliced = lax.dynamic_slice_in_dim(array_in, pair_index * pair_width, pair_width, 2)
    return sliced.reshape(sliced.shape[:2] + (2, HEAD_DIM))


def take_stats(array_in, pair_index):
    return lax.dynamic_slice_in_dim(array_in, pair_index * 2, 2, 1)


def join_pairs(stacked):
    moved = jnp.moveaxis(stacked, 0, 2)
    return moved.reshape(moved.shape[:2] + (moved.shape[2] * moved.shape[3],))


def join_stats(stacked):
    moved = jnp.moveaxis(stacked, 0, 1)
    return moved.reshape((moved.shape[0], moved.shape[1] * moved.shape[2], moved.shape[3]))


def merge_heads(pair_part):
    return pair_part.reshape(pair_part.shape[:2] + (2 * HEAD_DIM,))


def attend(q_scene, k_gathered, v_gathered):

    def attend_pair_step(unused, pair_index):
        q_pair = take_pair(q_scene, pair_index)
        k_pair = take_pair(k_gathered, pair_index)
        v_pair = take_pair(v_gathered, pair_index)
        scores = (
            jnp.einsum("sqhe,skhe->shqk", q_pair, k_pair, preferred_element_type=jnp.float32)
            * score_scale
        )
        row_max = jnp.max(scores, axis=-1, keepdims=True)
        shifted = jnp.exp(scores - row_max)
        row_sum = jnp.sum(shifted, axis=-1, keepdims=True)
        prob_low = (shifted / row_sum).astype(jnp.bfloat16)
        pair_out = jnp.einsum(
            "shqk,skhe->sqhe", prob_low, v_pair, preferred_element_type=jnp.float32
        )
        pair_lse = (row_max + jnp.log(row_sum))[..., 0]
        return (unused, (merge_heads(pair_out), pair_lse))

    pair_count = HEADS // 2
    _, (pair_outs, pair_lses) = lax.scan(
        attend_pair_step, jnp.zeros((), jnp.float32), jnp.arange(pair_count, dtype=jnp.int32)
    )
    return (join_pairs(pair_outs), join_stats(pair_lses))


def query_side(q_scene, k_gathered, v_gathered, row_lse, att_grad):

    def query_pair_step(unused, pair_index):
        q_pair = take_pair(q_scene, pair_index)
        k_pair = take_pair(k_gathered, pair_index)
        v_pair = take_pair(v_gathered, pair_index)
        d_pair = take_pair(att_grad, pair_index)
        l_pair = take_stats(row_lse, pair_index)
        scores = (
            jnp.einsum("sqhe,skhe->shqk", q_pair, k_pair, preferred_element_type=jnp.float32)
            * score_scale
        )
        attn_prob = jnp.exp(scores - l_pair[..., None])
        dprob = jnp.einsum("sqhe,skhe->shqk", d_pair, v_pair, preferred_element_type=jnp.float32)
        row_delta = jnp.sum(attn_prob * dprob, axis=-1)
        dscore = (attn_prob * (dprob - row_delta[..., None])).astype(jnp.bfloat16)
        q_part = (
            jnp.einsum("shqk,skhe->sqhe", dscore, k_pair, preferred_element_type=jnp.float32)
            * score_scale
        )
        results = (merge_heads(q_part), row_delta)
        prob_low = attn_prob.astype(jnp.bfloat16)
        k_part = (
            jnp.einsum("shqk,sqhe->skhe", dscore, q_pair, preferred_element_type=jnp.float32)
            * score_scale
        )
        v_part = jnp.einsum("shqk,sqhe->skhe", prob_low, d_pair, preferred_element_type=jnp.float32)
        results = results + (merge_heads(k_part), merge_heads(v_part))
        return (unused, results)

    pair_count = HEADS // 2
    _, results = lax.scan(
        query_pair_step, jnp.zeros((), jnp.float32), jnp.arange(pair_count, dtype=jnp.int32)
    )
    return results


def on_any_device(
    tokens,
    surface_mask,
    out_grad,
    w_query,
    w_key,
    w_value,
    w_out,
    w_up,
    w_down,
    b_query,
    b_value,
    b_out,
    b_up,
    b_down,
    gain_one,
    shift_one,
    gain_two,
    shift_two,
):
    scenes, local_len, model_width = tokens.shape
    row_count = scenes * local_len
    flat_rows = tokens.astype(jnp.float32).reshape(row_count, model_width)
    normed, norm_one_pull = jax.vjp(norm_rows, flat_rows, gain_one, shift_one)
    normed_low = normed.astype(jnp.bfloat16)
    q_low = (matmul(normed_low, w_query) + b_query).astype(jnp.bfloat16)
    k_low = matmul(normed_low, w_key).astype(jnp.bfloat16)
    v_low = (matmul(normed_low, w_value) + b_value).astype(jnp.bfloat16)
    q_scene = q_low.reshape(scenes, local_len, model_width)
    k_scene = k_low.reshape(scenes, local_len, model_width)
    v_scene = v_low.reshape(scenes, local_len, model_width)
    k_gathered, v_gathered = (
        lax.all_gather(k_scene, "seq", axis=1, tiled=True),
        lax.all_gather(v_scene, "seq", axis=1, tiled=True),
    )
    attended, row_lse = attend(q_scene, k_gathered, v_gathered)
    att_low = attended.reshape(row_count, model_width).astype(jnp.bfloat16)
    residual = flat_rows + matmul(att_low, w_out) + b_out
    normed_two, norm_two_pull = jax.vjp(norm_rows, residual, gain_two, shift_two)
    normed_two_low = normed_two.astype(jnp.bfloat16)
    hidden = matmul(normed_two_low, w_up) + b_up
    activated, gelu_pull = jax.vjp(gelu_tanh, hidden)
    act_low = activated.astype(jnp.bfloat16)
    block_rows = residual + matmul(act_low, w_down) + b_down
    block_out = block_rows.reshape(scenes, local_len, model_width).astype(jnp.bfloat16)
    masked_f = out_grad.astype(jnp.float32) * surface_mask.astype(jnp.float32)[..., None]
    masked_rows = masked_f.reshape(row_count, model_width)
    masked_low = masked_rows.astype(jnp.bfloat16)
    grad_down = matmul_tn(act_low, masked_low)
    grad_bdown = jnp.sum(masked_rows, axis=0)
    act_grad = matmul_nt(masked_low, w_down)
    hidden_low = gelu_pull(act_grad)[0].astype(jnp.bfloat16)
    grad_up = matmul_tn(normed_two_low, hidden_low)
    grad_bup = jnp.sum(hidden_low.astype(jnp.float32), axis=0)
    norm_two_in = matmul_nt(hidden_low, w_up)
    resid_part, grad_gain_two, grad_shift_two = norm_two_pull(norm_two_in)
    resid_grad = masked_rows + resid_part
    resid_low = resid_grad.astype(jnp.bfloat16)
    grad_out = matmul_tn(att_low, resid_low)
    grad_bout = jnp.sum(resid_low.astype(jnp.float32), axis=0)
    att_grad = (
        matmul_nt(resid_low, w_out).astype(jnp.bfloat16).reshape(scenes, local_len, model_width)
    )
    q_parts, delta_parts, k_parts, v_parts = query_side(
        q_scene, k_gathered, v_gathered, row_lse, att_grad
    )
    k_summed, v_summed = (
        lax.psum_scatter(
            k_parts.astype(jnp.bfloat16), "seq", scatter_dimension=2, tiled=True
        ).astype(jnp.float32),
        lax.psum_scatter(
            v_parts.astype(jnp.bfloat16), "seq", scatter_dimension=2, tiled=True
        ).astype(jnp.float32),
    )
    k_grad = join_pairs(k_summed)
    v_grad = join_pairs(v_summed)
    q_grad = join_pairs(q_parts)
    q_grad_low = q_grad.reshape(row_count, model_width).astype(jnp.bfloat16)
    k_grad_low = k_grad.reshape(row_count, model_width).astype(jnp.bfloat16)
    v_grad_low = v_grad.reshape(row_count, model_width).astype(jnp.bfloat16)
    grad_query = matmul_tn(normed_low, q_grad_low)
    grad_key = matmul_tn(normed_low, k_grad_low)
    grad_value = matmul_tn(normed_low, v_grad_low)
    grad_bquery = jnp.sum(q_grad_low.astype(jnp.float32), axis=0)
    grad_bvalue = jnp.sum(v_grad_low.astype(jnp.float32), axis=0)
    norm_one_in = (
        matmul_nt(q_grad_low, w_query)
        + matmul_nt(k_grad_low, w_key)
        + matmul_nt(v_grad_low, w_value)
    )
    token_part, grad_gain_one, grad_shift_one = norm_one_pull(norm_one_in)
    tokens_grad = (
        (resid_grad + token_part).reshape(scenes, local_len, model_width).astype(jnp.bfloat16)
    )
    (
        sum_query,
        sum_key,
        sum_value,
        sum_out,
        sum_bquery,
        sum_bvalue,
        sum_bout,
        sum_gain_one,
        sum_shift_one,
        sum_up,
        sum_down,
        sum_bup,
        sum_bdown,
        sum_gain_two,
        sum_shift_two,
    ) = (
        lax.psum_scatter(grad_query, ("scene", "seq"), scatter_dimension=0, tiled=True),
        lax.psum_scatter(grad_key, ("scene", "seq"), scatter_dimension=0, tiled=True),
        lax.psum_scatter(grad_value, ("scene", "seq"), scatter_dimension=0, tiled=True),
        lax.psum_scatter(grad_out, ("scene", "seq"), scatter_dimension=0, tiled=True),
        lax.psum_scatter(grad_bquery, ("scene", "seq"), scatter_dimension=0, tiled=True),
        lax.psum_scatter(grad_bvalue, ("scene", "seq"), scatter_dimension=0, tiled=True),
        lax.psum_scatter(grad_bout, ("scene", "seq"), scatter_dimension=0, tiled=True),
        lax.psum_scatter(grad_gain_one, ("scene", "seq"), scatter_dimension=0, tiled=True),
        lax.psum_scatter(grad_shift_one, ("scene", "seq"), scatter_dimension=0, tiled=True),
        lax.psum_scatter(grad_up, ("scene", "seq"), scatter_dimension=0, tiled=True),
        lax.psum_scatter(grad_down, ("scene", "seq"), scatter_dimension=0, tiled=True),
        lax.psum_scatter(grad_bup, ("scene", "seq"), scatter_dimension=0, tiled=True),
        lax.psum_scatter(grad_bdown, ("scene", "seq"), scatter_dimension=0, tiled=True),
        lax.psum_scatter(grad_gain_two, ("scene", "seq"), scatter_dimension=0, tiled=True),
        lax.psum_scatter(grad_shift_two, ("scene", "seq"), scatter_dimension=0, tiled=True),
    )
    return (
        block_out,
        tokens_grad,
        sum_query,
        sum_key,
        sum_value,
        sum_out,
        sum_up,
        sum_down,
        sum_bquery,
        sum_bvalue,
        sum_bout,
        sum_bup,
        sum_bdown,
        sum_gain_one,
        sum_shift_one,
        sum_gain_two,
        sum_shift_two,
    )


def solution(mesh):
    placed = (
        P("scene", "seq", None),
        P("scene", "seq"),
        P("scene", "seq", None),
        P(),
        P(),
        P(),
        P(),
        P(),
        P(),
        P(),
        P(),
        P(),
        P(),
        P(),
        P(),
        P(),
        P(),
        P(),
    )
    scenes, n = mesh.shape["scene"], mesh.shape["seq"]
    if (scenes, n) == (2, HEADS):
        on_device = functools.partial(layer_on_device, scenes, n)
    else:
        on_device = on_any_device
    return jax.shard_map(
        on_device,
        mesh=mesh,
        in_specs=placed,
        out_specs=(
            P("scene", "seq", None),
            P("scene", "seq", None),
            P(("scene", "seq"), None),
            P(("scene", "seq"), None),
            P(("scene", "seq"), None),
            P(("scene", "seq"), None),
            P(("scene", "seq"), None),
            P(("scene", "seq"), None),
            P(("scene", "seq")),
            P(("scene", "seq")),
            P(("scene", "seq")),
            P(("scene", "seq")),
            P(("scene", "seq")),
            P(("scene", "seq")),
            P(("scene", "seq")),
            P(("scene", "seq")),
            P(("scene", "seq")),
        ),
        check_vma=False,
    )
```

```python
import functools

import jax
import jax.numpy as jnp
from jax import lax
from jax.experimental import pallas as pl
from jax.experimental.pallas import tpu as pltpu
from jax.sharding import PartitionSpec as P

HEADS = 16
HEAD_DIM = 64
MESH = pl.DeviceIdType.MESH
f32 = jnp.float32
bf16 = jnp.bfloat16

norm_eps = 1e-05
score_scale = 0.125
FORWARD_LIMIT = 60 << 20
gelu_coef = 0.7978845608028654


def matmul(left, right):
    return jnp.dot(left, right, preferred_element_type=jnp.float32)


def contract(left, right, left_dim, right_dim):
    return lax.dot_general(
        left, right, (((left_dim,), (right_dim,)), ((), ())), preferred_element_type=jnp.float32
    )


def matmul_tn(left, right):
    return contract(left, right, 0, 0)


def matmul_nt(left, right):
    return contract(left, right, 1, 1)


def normalise(values):
    row_mean = jnp.mean(values, axis=-1, keepdims=True)
    centred = values - row_mean
    row_var = jnp.mean(centred * centred, axis=-1, keepdims=True)
    inverse = lax.rsqrt(row_var + norm_eps)
    return centred * inverse, inverse


def norm_back(grad, scaled, inverse, gain):
    weighted = grad * gain
    back = inverse * (
        weighted
        - jnp.mean(weighted, axis=-1, keepdims=True)
        - scaled * jnp.mean(weighted * scaled, axis=-1, keepdims=True)
    )
    return back, jnp.sum(grad * scaled, axis=0), jnp.sum(grad, axis=0)


def greet(partners):
    barrier = pltpu.get_barrier_semaphore()
    for partner in partners:
        pl.semaphore_signal(barrier, inc=1, device_id=partner, device_id_type=MESH)
    return lambda: pl.semaphore_wait(barrier, len(partners))


def remote(src, dst, send_sem, recv_sem, device):
    return pltpu.make_async_remote_copy(
        src_ref=src,
        dst_ref=dst,
        send_sem=send_sem,
        recv_sem=recv_sem,
        device_id=device,
        device_id_type=MESH,
    )


def flipped(index, other):
    out = 0
    for weight in (1, 2, 4, 8):
        bit, turn = lax.rem(index // weight, 2), lax.rem(other // weight, 2)
        out = out + weight * (bit + turn - 2 * bit * turn)
    return out


def forward_kernel(n, tok, *refs):
    (
        tokens_ref,
        gain_ref,
        shift_ref,
        wq_ref,
        wk_ref,
        wv_ref,
        bq_ref,
        bv_ref,
        att_ref,
        normed_out,
        q_out,
        k_out,
        v_out,
        o_out,
        lse_out,
        rows_in,
        gain,
        shift,
        b_query,
        b_value,
        land,
        w_pair,
        w_head,
        bias,
        q_all,
        k_all,
        v_all,
        k_nat,
        o_all,
        lse_all,
        stats,
        att_send,
        load_sem,
        gather_send,
        gather_recv,
        save_sem,
        out_send,
        out_recv,
        out_local,
        last_sem,
    ) = refs
    me = lax.axis_index("seq")
    scene = lax.axis_index("scene")
    core = lax.rem(me, 2)
    chips = n // 2
    wide = 2 * tok
    half_rows = tok // 2
    devices = [flipped(me, s) for s in range(n)]

    def rows(head):
        return pl.ds(pl.multiple_of(head * HEAD_DIM, HEAD_DIM), HEAD_DIM)

    def lanes(block, width=tok):
        return pl.ds(pl.multiple_of(block * width, width), width)

    tokens_load = pltpu.make_async_copy(tokens_ref, rows_in, load_sem.at[0])
    tokens_load.start()
    weight_loads = [
        pltpu.make_async_copy(ref.at[:, lanes(me // 2, 128)], w_pair.at[i], load_sem.at[1 + i])
        for i, ref in enumerate((wk_ref, wq_ref, wv_ref))
    ]
    vector_loads = [
        pltpu.make_async_copy(src, dst, load_sem.at[4 + i])
        for i, (src, dst) in enumerate(
            ((gain_ref, gain), (shift_ref, shift), (bq_ref, b_query), (bv_ref, b_value))
        )
    ]
    for load in vector_loads + weight_loads:
        load.start()
    all_here = greet([(scene, devices[s]) for s in range(1, n)])

    def gather_copy(slot, over, part):
        piece = slice(part * half_rows, (part + 1) * half_rows)
        there = slot ^ over
        return remote(
            land.at[slot, piece, :],
            land.at[there, piece, :],
            gather_send.at[there, part],
            gather_recv.at[there, part],
            (scene, devices[over]),
        )

    routes = {0: (4, 2, 8, 1), 8: (4, 2, 1), 4: (2, 1), 12: (2, 1), 2: (1,), 6: (1,), 10: (1,), 14: (1,)}

    def routes_of(slot, part):
        if part == 1 and slot == 12:
            return (1,)
        if part == 1 and slot == 10:
            return (4, 1)
        return routes.get(slot, ())

    def came_over(slot, part):
        for source in range(n):
            for over in routes_of(source, part):
                if source ^ over == slot:
                    return over

    sent = []
    saves = []

    def forward(slot, part):
        for over in routes_of(slot, part):
            copy = gather_copy(slot, over, part)
            copy.start()
            sent.append(copy)

    def arrive(slot, part):
        over = came_over(slot, part)
        gather_copy(slot ^ over, over, part).wait_recv()
        forward(slot, part)

    for load in [tokens_load] + vector_loads:
        load.wait()
    for part in range(2):
        piece = slice(part * half_rows, (part + 1) * half_rows)
        scaled, _ = normalise(rows_in[piece, :].astype(f32))
        land[0, piece, :] = (scaled * gain[...] + shift[...]).astype(bf16)
        if part == 0:
            all_here()
        forward(0, part)

    odd = core == 1
    for i, load in enumerate(weight_loads):
        load.wait()
        pair = w_pair[i].astype(f32)
        w_head[:, HEAD_DIM * i : HEAD_DIM * i + HEAD_DIM] = jnp.where(
            odd, pair[:, HEAD_DIM:], pair[:, :HEAD_DIM]
        ).astype(bf16)
    for i, ref in ((1, b_query), (2, b_value)):
        pair = ref[0:1, lanes(me // 2, 128)]
        bias[0:1, HEAD_DIM * i : HEAD_DIM * i + HEAD_DIM] = jnp.where(
            odd, pair[:, HEAD_DIM:], pair[:, :HEAD_DIM]
        )
    bias[0:1, :HEAD_DIM] = jnp.zeros((1, HEAD_DIM), f32)

    def project(slot):
        made = contract(land[slot], w_head[...], 1, 0) + bias[0:1, :]
        low = made.astype(bf16)
        turned = low.T
        span = slice(slot * tok, (slot + 1) * tok)
        k_nat[span, :] = low[:, :HEAD_DIM]
        k_all[:, span] = turned[:HEAD_DIM]
        q_all[:, span] = turned[HEAD_DIM : 2 * HEAD_DIM] * jnp.asarray(score_scale, bf16)
        v_all[:, span] = turned[2 * HEAD_DIM :]
        save = pltpu.make_async_copy(land.at[slot], normed_out.at[span, :], save_sem.at[slot])
        save.start()
        saves.append(save)

    def attend(span, first, state):
        top, total, acc = state
        keys = slice(first, first + chips // 2 * wide)
        scores = contract(k_nat[keys, :], q_all[:, span], 1, 0)
        here = jnp.max(scores, axis=0, keepdims=True)
        new_top = here if top is None else jnp.maximum(top, here)
        shifted = jnp.exp(scores - new_top)
        part_sum = jnp.sum(shifted, axis=0, keepdims=True)
        part = contract(v_all[:, keys], shifted.astype(bf16), 1, 0)
        if top is None:
            return new_top, part_sum, part
        fade = jnp.exp(top - new_top)
        return new_top, total * fade + part_sum, acc * fade + part

    middle = chips // 2 * wide

    def early(i):
        span = slice(i * wide, (i + 1) * wide)
        top, total, acc = attend(span, 0, (None, None, None))
        stats[0:1, span] = top
        stats[1:2, span] = total
        o_all[:, span] = acc

    def close(i, span, state):
        top, total, acc = state
        out = acc / total
        o_all[:, span] = out
        lse_all[:, span] = jnp.broadcast_to(top + jnp.log(total), (8, wide))
        low = out.astype(bf16)
        att_send[i, 0] = low[:, :tok]
        att_send[i, 1] = low[:, tok:]

    def out_copy(i, flip):
        return remote(
            att_send.at[i, flip],
            att_ref.at[rows(me), :],
            out_send.at[i, flip],
            out_recv.at[i, flip],
            (scene, flipped(me, 2 * i + flip)),
        )

    project(0)
    for part in range(2):
        arrive(1, part)
    project(1)
    for part in range(2):
        arrive(2, part)
        arrive(4, part)
    project(2)
    for slot in (3, 5):
        for part in range(2):
            arrive(slot, part)
    project(3)
    project(4)
    project(5)
    for part in range(2):
        arrive(8, part)
    for slot in (6, 7):
        for part in range(2):
            arrive(slot, part)
    project(6)
    project(7)
    early(0)
    early(1)
    arrive(9, 0)
    arrive(9, 1)
    project(8)
    project(9)
    for part in range(2):
        arrive(12, part)
        arrive(10, part)
    early(2)
    for slot in (11, 13):
        for part in range(2):
            arrive(slot, part)
    project(10)
    project(11)
    early(3)
    project(12)
    project(13)
    arrive(14, 0)
    arrive(14, 1)
    project(14)
    arrive(15, 0)
    arrive(15, 1)
    project(15)
    for i, (src, dst) in enumerate(((q_all, q_out), (k_all, k_out), (v_all, v_out))):
        save = pltpu.make_async_copy(src, dst, last_sem.at[i])
        save.start()
        saves.append(save)

    def late_body(j, carry):
        i = chips - 1 - j
        span = lanes(i, wide)
        close(i, span, attend(span, middle, attend(span, 0, (None, None, None))))
        out_copy(i, 0).start()
        out_copy(i, 1).start()
        return carry

    lax.fori_loop(0, chips // 2, late_body, 0)

    def rest(i, span):
        state = (stats[0:1, span], stats[1:2, span], o_all[:, span])
        close(i, span, attend(span, middle, state))

    def rest_body(j, carry):
        i = chips // 2 - 1 - j
        rest(i, lanes(i, wide))
        out_copy(i, 0).start()
        out_copy(i, 1).start()
        return carry

    lax.fori_loop(0, chips // 2 - 1, rest_body, 0)
    rest(0, slice(0, wide))
    mine = pltpu.make_async_copy(att_send.at[0, 0], att_ref.at[rows(me), :], out_local)
    mine.start()
    out_copy(0, 1).start()
    for i, (src, dst) in enumerate(((o_all, o_out), (lse_all, lse_out))):
        save = pltpu.make_async_copy(src, dst, last_sem.at[3 + i])
        save.start()
        saves.append(save)
    for copy in sent:
        copy.wait_send()
    mine.wait()
    out_copy(0, 1).wait()

    def drain(i, carry):
        out_copy(i, 0).wait()
        out_copy(i, 1).wait()
        return carry

    lax.fori_loop(1, chips, drain, 0)
    for save in saves:
        save.wait()


def attention_forward(n, tokens, gain, shift, w_query, w_key, w_value, b_query, b_value):
    tok, width = tokens.shape
    length = n * tok
    any_spec = pl.BlockSpec(memory_space=pl.ANY)
    head_all = jax.ShapeDtypeStruct((HEAD_DIM, length), bf16)
    dma = pltpu.SemaphoreType.DMA
    return pl.pallas_call(
        functools.partial(forward_kernel, n, tok),
        out_shape=(
            jax.ShapeDtypeStruct((width, tok), bf16),
            jax.ShapeDtypeStruct((length, width), bf16),
            head_all,
            head_all,
            head_all,
            jax.ShapeDtypeStruct((HEAD_DIM, length), f32),
            jax.ShapeDtypeStruct((8, length), f32),
        ),
        in_specs=[any_spec] * 8,
        out_specs=[any_spec] * 7,
        scratch_shapes=[
            pltpu.VMEM((tok, width), bf16),
            pltpu.VMEM((1, width), f32),
            pltpu.VMEM((1, width), f32),
            pltpu.VMEM((1, width), f32),
            pltpu.VMEM((1, width), f32),
            pltpu.VMEM((n, tok, width), bf16),
            pltpu.VMEM((3, width, 2 * HEAD_DIM), bf16),
            pltpu.VMEM((width, 3 * HEAD_DIM), bf16),
            pltpu.VMEM((8, 3 * HEAD_DIM), f32),
            pltpu.VMEM((HEAD_DIM, length), bf16),
            pltpu.VMEM((HEAD_DIM, length), bf16),
            pltpu.VMEM((HEAD_DIM, length), bf16),
            pltpu.VMEM((length, HEAD_DIM), bf16),
            pltpu.VMEM((HEAD_DIM, length), f32),
            pltpu.VMEM((8, length), f32),
            pltpu.VMEM((8, length), f32),
            pltpu.VMEM((n // 2, 2, HEAD_DIM, tok), bf16),
            dma((8,)),
            dma((n, 2)),
            dma((n, 2)),
            dma((n,)),
            dma((n // 2, 2)),
            dma((n // 2, 2)),
            dma,
            dma((5,)),
        ],
        compiler_params=pltpu.CompilerParams(
            collective_id=0, has_side_effects=True, vmem_limit_bytes=FORWARD_LIMIT
        ),
        name="attention_forward",
    )(
        tokens,
        gain[None],
        shift[None],
        w_query,
        w_key,
        w_value,
        b_query[None],
        b_value[None],
    )


CHUNKS = 9
TICKS = CHUNKS + 4
SLOTS = 3


def halving_plan(full, got0, got1a, got1b, got2a, got2b, got3, got4, total, send_sem, recv_sem):
    me = lax.axis_index("seq")
    x = lax.axis_index("scene")
    core = lax.rem(me, 2)
    y = lax.rem(me // 2, 2)
    z0 = lax.rem(me // 4, 2)
    z1 = me // 8
    at_core = (x, me + 1 - 2 * core)
    at_x = (1 - x, me)
    at_y = (x, me + 2 - 4 * y)
    at_z0 = (x, me + 4 - 8 * z0)
    at_z1 = (x, me + 8 - 16 * z1)
    up, low = slice(0, 64), slice(64, 128)

    def copy_of(slot, c):
        src, dst, device = (
            lambda: (full.at[lax.rem(c, SLOTS), :, :, :, :, 1 - core], got0.at[c], at_core),
            lambda: (got0.at[c, 1 - x, :, :, :, up, :], got1a.at[c], at_x),
            lambda: (got0.at[c, :, :, :, 1 - y, low, :], got1b.at[c], at_y),
            lambda: (got1a.at[c, :, 1 - z0], got2a.at[c], at_z0),
            lambda: (got1b.at[c, 1 - x], got2b.at[c], at_x),
            lambda: (got2a.at[c, :, 1 - y], got3.at[c, :, up, :], at_y),
            lambda: (got2b.at[c, :, 1 - z0], got3.at[c, :, low, :], at_z0),
            lambda: (got3.at[c, 1 - z1], got4.at[c], at_z1),
        )[slot]()
        going = send_sem.at[c] if slot == 0 else send_sem.at[CHUNKS + slot]
        return remote(src, dst, going, recv_sem.at[c, slot], device)

    def sum1(c):
        copy_of(0, c).wait_recv()
        got0[c] = got0[c] + full[lax.rem(c, SLOTS), :, :, :, :, core]

    def start1(c):
        copy_of(1, c).start()
        copy_of(2, c).start()

    def stage2(c):
        copy_of(1, c).wait_recv()
        got1a[c] = got1a[c] + got0[c, x, :, :, :, up, :]
        copy_of(3, c).start()
        copy_of(2, c).wait_recv()
        got1b[c] = got1b[c] + got0[c, :, :, :, y, low, :]
        copy_of(4, c).start()

    def stage3(c):
        copy_of(3, c).wait_recv()
        got2a[c] = got2a[c] + got1a[c, :, z0]
        copy_of(5, c).start()
        copy_of(4, c).wait_recv()
        got2b[c] = got2b[c] + got1b[c, x]
        copy_of(6, c).start()

    def stage4(c):
        copy_of(5, c).wait_recv()
        got3[c, :, up, :] = got3[c, :, up, :] + got2a[c, :, y]
        copy_of(6, c).wait_recv()
        got3[c, :, low, :] = got3[c, :, low, :] + got2b[c, :, z0]
        copy_of(7, c).start()

    def stage5(c):
        copy_of(7, c).wait_recv()
        total[c] = got3[c, z1].astype(f32) + got4[c].astype(f32)

    def tick(when):
        for stage, c in (
            (stage5, when - 4),
            (stage4, when - 3),
            (stage3, when - 2),
            (stage2, when - 1),
            (start1, when + 1),
        ):

            @pl.when((c >= 0) & (c < CHUNKS))
            def _(stage=stage, c=c):
                stage(c)

    def settle():
        for slot, src in enumerate((got1a, got1a, got1b, got2a, got2b, got3, got3, got4)):
            if slot:
                everything = src.at[:, :, up, :] if slot in (5, 6) else src
                pltpu.make_async_copy(everything, everything, send_sem.at[CHUNKS + slot]).wait()

    return copy_of, sum1, start1, tick, settle


def tail_kernel(n, tok, *refs):
    (
        q_ref,
        k_ref,
        v_ref,
        o_ref,
        lse_ref,
        masked_ref,
        two_ref,
        residual_ref,
        att_ref,
        normed_ref,
        wd_ref,
        wu_ref,
        wo_ref,
        wq_ref,
        wk_ref,
        wv_ref,
        tokens_ref,
        gain_ref,
        gain_two_ref,
        b_down_ref,
        b_up_ref,
        block_out,
        tokens_out,
        total,
        pack_got,
        small_got,
        early_got,
        q_all,
        k_all,
        v_all,
        d_all,
        d_send,
        o_all,
        lse_all,
        low,
        act,
        masked,
        two,
        hidden,
        att,
        resid_low,
        act_t,
        two_t,
        full,
        got0,
        got1a,
        got1b,
        got2a,
        got2b,
        got3,
        got4,
        land,
        rows_in,
        resid,
        gain_one,
        gain_two,
        b_down,
        b_up,
        pack,
        small,
        early,
        load_sem,
        ring_sem,
        weight_sem,
        normed_sem,
        in_send,
        in_recv,
        in_local,
        kv_send,
        kv_recv,
        kv_local,
        q_send,
        q_recv,
        q_local,
        half_send,
        half_recv,
        last_send,
        last_recv,
        last_local,
    ) = refs
    me = lax.axis_index("seq")
    scene = lax.axis_index("scene")
    chips = n // 2
    length = n * tok
    wide = 2 * tok
    devices = 2 * n
    width = masked.shape[1]
    mine = scene * n + me

    def rows(head):
        return pl.ds(pl.multiple_of(head * HEAD_DIM, HEAD_DIM), HEAD_DIM)

    def lanes(block, width=tok):
        return pl.ds(pl.multiple_of(block * width, width), width)

    loads = [
        pltpu.make_async_copy(src, dst, load_sem.at[i])
        for i, (src, dst) in enumerate(
            (
                (two_ref, two),
                (b_up_ref, b_up),
                (masked_ref, masked),
                (q_ref, q_all),
                (k_ref, k_all),
                (v_ref, v_all),
                (o_ref, o_all),
                (lse_ref, lse_all),
                (att_ref, att),
                (residual_ref, resid),
                (tokens_ref, rows_in),
                (gain_ref, gain_one),
                (gain_two_ref, gain_two),
                (b_down_ref, b_down),
            )
        )
    ]
    for load in loads:
        load.start()

    def peer(j):
        index = lax.rem(mine + j, devices)
        return index, (index // n, lax.rem(index, n))

    all_here = greet([peer(j)[1] for j in range(1, devices)])

    half, sum1, start1, tick, settle = halving_plan(
        full, got0, got1a, got1b, got2a, got2b, got3, got4, total, half_send, half_recv
    )

    def chunk_begin(c):
        @pl.when(c >= SLOTS)
        def _():
            half(0, c - SLOTS).wait_send()

        return lax.rem(c, SLOTS)

    def chunk_end(c):
        half(0, c).start()

        @pl.when((c >= 1) & (c != 4))
        def _():
            sum1(c - 1)

    def down_chunk(c):
        slot = chunk_begin(c)
        columns = masked[:, lanes(c, 256)]
        for block in range(4):
            part = contract(act_t[1024 * block : 1024 * block + 1024, :], columns, 1, 0)
            full[slot, block // 2, block % 2] = part.astype(bf16).reshape(2, 2, 2, 128, 256)
        chunk_end(c)

    def narrow_chunk(c, left, right):
        slot = chunk_begin(c)
        for block in range(4):
            part = contract(left, right[:, 256 * block : 256 * block + 256], 1, 0)
            full[slot, :, :, :, :, :, 32 * block : 32 * block + 32, :] = part.astype(bf16).reshape(
                2, 2, 2, 2, 2, 32, 256
            )
        chunk_end(c)

    def first_chunk(c, carry):
        down_chunk(c)

        @pl.when((c >= 1) & (c <= 2))
        def _():
            start1(c - 1)

        return carry

    def feed_forward(ring, slope, out_acc, two_acc):
        def weight_load(i):
            if i == 12:
                src = wo_ref
            elif 4 <= i < 8:
                src = wd_ref.at[1024 * (i - 4) : 1024 * (i - 4) + 1024, :]
            else:
                src = wu_ref.at[:, 1024 * (i % 4) : 1024 * (i % 4) + 1024]
            return pltpu.make_async_copy(src, ring.at[i % 2], ring_sem.at[i % 2])

        for i in range(2):
            weight_load(i).start()
        loads[0].wait()
        loads[1].wait()
        for i in range(4):
            weight_load(i).wait()
            grown = contract(two[...], ring[i % 2], 1, 0) + b_up[:, 1024 * i : 1024 * i + 1024]
            weight_load(i + 2).start()
            value, slope[i] = gelu_both(grown)
            value = value.astype(bf16)
            act[tok * i : tok * i + tok, :] = value
            act_t[1024 * i : 1024 * i + 1024, :] = value.T
        loads[2].wait()
        all_here()
        lax.fori_loop(0, 4, first_chunk, 0)
        for load in loads[8:]:
            load.wait()
        masked_sum = jnp.sum(masked[...].astype(f32), axis=0, keepdims=True)
        for i in range(4):
            weight_load(4 + i).wait()
            there = slice(tok * i, tok * i + tok)
            part = contract(act[there, :], ring[i % 2], 1, 0)
            out_acc[...] = resid[...] + b_down[...] + part if i == 0 else out_acc[...] + part
            grown = contract(masked[...], ring[i % 2], 1, 1) * slope[i]
            weight_load(6 + i).start()
            grown = grown.astype(bf16)
            hidden[there, :] = grown
            sums = jnp.sum(grown.astype(f32), axis=0, keepdims=True)
            for j in range(8):
                early[8 * i + j, 4:5, :] = sums[:, 128 * j : 128 * j + 128]
            if i == 1:
                tick(1)
        block_out[...] = out_acc[...].astype(bf16)
        sum1(3)
        for i in range(4):
            weight_load(8 + i).wait()
            part = contract(hidden[tok * i : tok * i + tok, :], ring[i % 2], 1, 1)
            two_acc[...] = part if i == 0 else two_acc[...] + part
            if i < 3:
                weight_load(10 + i).start()
            if i == 1:
                tick(2)
        scaled, inverse = normalise(resid[...])
        part, gain_grad, shift_grad = norm_back(two_acc[...], scaled, inverse, gain_two[...])
        resid[...] = masked[...].astype(f32) + part
        resid_low[...] = resid[...].astype(bf16)
        low_sum = jnp.sum(resid_low[...].astype(f32), axis=0, keepdims=True)
        for row, vector in enumerate((low_sum, masked_sum, gain_grad[None], shift_grad[None])):
            for d in range(devices):
                start = 128 * (d // 4)
                early[d, row : row + 1, :] = vector[:, start : start + 128]
        weight_load(12).wait()
        d_send[...] = contract(ring[0], resid_low[...], 1, 1).astype(bf16)

    pl.run_scoped(
        feed_forward,
        pltpu.VMEM((2, 1024, 1024), bf16),
        pltpu.VMEM((4, tok, 1024), f32),
        pltpu.VMEM((tok, width), f32),
        pltpu.VMEM((tok, width), f32),
    )

    copies = []
    for s in reversed(range(1, n)):
        head = flipped(me, s)
        copies.append(
            remote(
                d_send.at[rows(head), :],
                d_all.at[:, s * tok : s * tok + tok],
                in_send,
                in_recv,
                (scene, head),
            )
        )
        copies[-1].start()
    local = pltpu.make_async_copy(d_send.at[rows(me), :], d_all.at[:, :tok], in_local)
    local.start()

    def pack_copy(j):
        index, device = peer(j)
        return remote(pack.at[index], pack_got.at[mine], last_send.at[0], last_recv.at[0], device)

    def small_copy(j):
        index, device = peer(j)
        return remote(
            small.at[0:4, lanes(index // 4, 128)],
            small_got.at[mine, 0:4, :],
            last_send.at[1],
            last_recv.at[1],
            device,
        )

    def early_copy(j):
        index, device = peer(j)
        return remote(
            early.at[index, 0:5, :],
            early_got.at[mine, 0:5, :],
            last_send.at[2],
            last_recv.at[2],
            device,
        )

    kept = [
        pltpu.make_async_copy(pack.at[mine], pack_got.at[mine], last_local.at[0]),
        pltpu.make_async_copy(
            small.at[0:4, lanes(mine // 4, 128)], small_got.at[mine, 0:4, :], last_local.at[1]
        ),
        pltpu.make_async_copy(
            early.at[mine, 0:5, :], early_got.at[mine, 0:5, :], last_local.at[2]
        ),
    ]
    kept[2].start()

    def early_body(j, carry):
        early_copy(j).start()
        return carry

    lax.fori_loop(1, devices, early_body, 0)
    two_t[...] = two[...].T
    for load in loads[3:8]:
        load.wait()

    def chunk(step):
        @pl.when(step == 0)
        def _():
            narrow_chunk(step + 7, two_t[...], hidden[3 * tok :, :])
            normed_load(0).start()

        @pl.when(step == 1)
        def _():
            narrow_chunk(step + 7, att[...], resid_low[...])
            normed_load(1).start()

        @pl.when(step == 2)
        def _():
            sum1(CHUNKS - 1)

    def normed_load(i):
        return pltpu.make_async_copy(
            normed_ref.at[1024 * i : 1024 * i + 1024, :],
            (act, hidden)[i % 2],
            normed_sem.at[i % 2],
        )

    def q_copy(step, flip):
        slot = 2 * step + flip
        return remote(
            low.at[0, :, lanes(slot)],
            land.at[0, rows(me), :],
            q_send,
            q_recv,
            (scene, flipped(me, slot)),
        )

    def kv_copy(step, flip):
        slot = 2 * step + flip
        return remote(
            low.at[1:3, :, lanes(slot)],
            land.at[1:3, rows(me), :],
            kv_send,
            kv_recv,
            (scene, flipped(me, slot)),
        )

    own = [
        pltpu.make_async_copy(low.at[0, :, :tok], land.at[0, rows(me), :], q_local),
        pltpu.make_async_copy(low.at[1:3, :, :tok], land.at[1:3, rows(me), :], kv_local),
    ]

    weight_loads = [
        pltpu.make_async_copy(
            ref.at[:, :, :, :, 256 * block : 256 * block + 256],
            full.at[a, block // 2, block % 2],
            weight_sem.at[a, block],
        )
        for a, ref in enumerate((wq_ref, wk_ref, wv_ref))
        for block in range(4)
    ]

    def load_weights():
        for c in range(CHUNKS - SLOTS, CHUNKS):
            half(0, c).wait_send()
        for load in weight_loads:
            load.start()

    def attention(q_nat, k_nat, v_nat, d_nat, delta, dq_acc):
        q_nat[...] = q_all[...].T
        k_nat[...] = k_all[...].T
        v_nat[...] = v_all[...].T
        dq_acc[...] = jnp.zeros_like(dq_acc)

        def middle_chunk(i, carry):
            there = pl.ds(pl.multiple_of(i * tok, tok), tok)
            narrow_chunk(4 + i, two_t[...], hidden[there, :])

            @pl.when(i == 1)
            def _():
                tick(3)

            return carry

        lax.fori_loop(0, 3, middle_chunk, 0)
        local.wait()
        pltpu.make_async_copy(d_all.at[:, tok:], d_all.at[:, tok:], in_recv).wait()
        d_nat[...] = d_all[...].T
        delta[...] = jnp.broadcast_to(
            jnp.sum(d_all[...].astype(f32) * o_all[...], axis=0, keepdims=True), delta.shape
        )

        def keys(step, last):
            span = lanes(step, wide)
            k_here, v_here, kt_here = k_nat[span, :], v_nat[span, :], k_all[:, span]
            dk = dv = None
            for i in reversed(range(chips)):
                there = slice(i * wide, (i + 1) * wide)
                scores = contract(k_here, q_all[:, there], 1, 0)
                prob = jnp.exp(scores - lse_all[0:1, there])
                dprob = contract(v_here, d_all[:, there], 1, 0)
                dscore = (prob * (dprob - delta[0:1, there])).astype(bf16)
                v_part = contract(prob.astype(bf16), d_nat[there, :], 1, 0)
                k_part = contract(dscore, q_nat[there, :], 1, 0)
                dk = k_part if dk is None else dk + k_part
                dv = v_part if dv is None else dv + v_part
                dq = dq_acc[:, there] + contract(kt_here, dscore, 1, 0)
                if last:
                    low[0, :, there] = (dq * score_scale).astype(bf16)
                    if i == 0:
                        own[0].start()
                    else:
                        q_copy(i, 0).start()
                    q_copy(i, 1).start()
                else:
                    dq_acc[:, there] = dq
            low[1, :, span] = dk.astype(bf16).T
            low[2, :, span] = dv.astype(bf16).T

        def step_body(step, carry):
            tick(step + 4)
            chunk(step)
            keys(chips - 1 - step, False)

            kv_copy(chips - 1 - step, 0).start()
            kv_copy(chips - 1 - step, 1).start()
            return carry

        lax.fori_loop(0, chips - 1, step_body, 0)
        load_weights()
        tick(11)
        keys(0, True)
        own[1].start()
        kv_copy(0, 1).start()

    pl.run_scoped(
        attention,
        *(pltpu.VMEM((length, HEAD_DIM), bf16) for _ in range(4)),
        pltpu.VMEM((8, length), f32),
        pltpu.VMEM((HEAD_DIM, length), f32),
    )

    head_acc = None
    for i in range(length // 1024):
        normed_load(i).wait()
        left = low[:, :, 1024 * i : 1024 * i + 1024].reshape(3 * HEAD_DIM, 1024)
        part = contract(left, (act, hidden)[i % 2][...], 1, 0)
        head_acc = part if head_acc is None else head_acc + part
        if i + 2 < length // 1024:
            normed_load(i + 2).start()
    by_row = head_acc.T
    share = width // devices
    pack[:, :share, :] = by_row[:, : 2 * HEAD_DIM].astype(bf16).reshape(devices, share, 2 * HEAD_DIM)
    third = by_row[:, 2 * HEAD_DIM :].astype(bf16).reshape(devices, 2, share // 2, HEAD_DIM)
    pack[:, share:, :] = jnp.concatenate([third[:, 0], third[:, 1]], axis=-1)

    kept[0].start()

    def pack_body(j, carry):
        pack_copy(j).start()
        return carry

    lax.fori_loop(1, devices, pack_body, 0)

    for copy in own:
        copy.wait()
    for sem, others in ((q_recv, land.at[0, HEAD_DIM:, :]), (kv_recv, land.at[1:3, HEAD_DIM:, :])):
        pltpu.make_async_copy(others, others, sem).wait()
    for load in weight_loads:
        load.wait()
    def first_norm(back_in):
        for i in range(4):
            part = None
            for a in range(3):
                left = jnp.concatenate(
                    [full[a, b // 2, b % 2, i // 2, i % 2].reshape(256, 256) for b in range(4)],
                    axis=1,
                )
                here = contract(left, land[a], 1, 0)
                part = here if part is None else part + here
            back_in[:, 256 * i : 256 * i + 256] = part.T
        scaled, inverse = normalise(rows_in[...].astype(f32))
        token_part, gain_grad, shift_grad = norm_back(back_in[...], scaled, inverse, gain_one[...])
        tokens_out[...] = (resid[...] + token_part).astype(bf16)
        small[2:3, :] = gain_grad[None]
        small[3:4, :] = shift_grad[None]

    pl.run_scoped(first_norm, pltpu.VMEM((tok, width), f32))
    ones = jnp.ones((8, tok), bf16)
    small[0:1, :] = contract(ones, land[0], 1, 1)[0:1]
    small[1:2, :] = contract(ones, land[2], 1, 1)[0:1]
    kept[1].start()

    def small_body(j, carry):
        small_copy(j).start()
        return carry

    lax.fori_loop(1, devices, small_body, 0)

    tick(12)
    for copy in kept:
        copy.wait()
    for i, src in enumerate(
        (pack.at[1:], small_got.at[1:, 0:4, :], early_got.at[1:, 0:5, :])
    ):
        pltpu.make_async_copy(src, src, last_recv.at[i]).wait()
        pltpu.make_async_copy(src, src, last_send.at[i]).wait()
    for sem, others in (
        (in_send, low.at[0, :, tok:]),
        (q_send, low.at[0, :, tok:]),
        (kv_send, low.at[1:3, :, tok:]),
    ):
        pltpu.make_async_copy(others, others, sem).wait()

    settle()


def tail(n, tok, width, hidden_width, *arrays):
    length = n * tok
    chips = n // 2
    devices = 2 * n
    share = width // devices
    any_spec = pl.BlockSpec(memory_space=pl.ANY)
    vmem = pl.BlockSpec(memory_space=pltpu.VMEM)
    dma = pltpu.SemaphoreType.DMA

    def space(*shape, kind=bf16):
        return pltpu.VMEM(shape, kind)

    def out(*shape, kind=f32):
        return jax.ShapeDtypeStruct(shape, kind)

    pieces = CHUNKS
    scratch = (
        [space(HEAD_DIM, length)] * 4
        + [
            space(width, tok),
            space(HEAD_DIM, length, kind=f32),
            space(8, length, kind=f32),
            space(3, HEAD_DIM, length),
            space(hidden_width // 1024 * tok, 1024),
            space(tok, width),
            space(tok, width),
            space(hidden_width // 1024 * tok, 1024),
            space(width, tok),
            space(tok, width),
            space(hidden_width, tok),
            space(width, tok),
            space(SLOTS, 2, 2, 2, 2, 2, 128, 256),
            space(pieces, 2, 2, 2, 2, 128, 256),
            space(pieces, 2, 2, 2, 64, 256),
            space(pieces, 2, 2, 2, 64, 256),
            space(pieces, 2, 2, 64, 256),
            space(pieces, 2, 2, 64, 256),
            space(pieces, 2, 128, 256),
            space(pieces, 128, 256),
            space(3, width, tok),
            space(tok, width),
            space(tok, width, kind=f32),
            space(1, width, kind=f32),
            space(1, width, kind=f32),
            space(1, width, kind=f32),
            space(1, hidden_width, kind=f32),
            space(devices, share + share // 2, 128),
            space(8, width, kind=f32),
            space(devices, 8, 128, kind=f32),
            dma((14,)),
            dma((2,)),
            dma((3, 4)),
            dma((2,)),
            dma,
            dma,
            dma,
            dma,
            dma,
            dma,
            dma,
            dma,
            dma,
            dma((pieces + 8,)),
            dma((pieces, 8)),
        ]
        + [dma((3,))] * 3
    )
    return pl.pallas_call(
        functools.partial(tail_kernel, n, tok),
        out_shape=(
            out(tok, width, kind=bf16),
            out(tok, width, kind=bf16),
            out(pieces, 128, 256),
            out(devices, share + share // 2, 128, kind=bf16),
            out(devices, 8, 128),
            out(devices, 8, 128),
        ),
        in_specs=[any_spec] * 21,
        out_specs=[vmem] * 6,
        scratch_shapes=scratch,
        compiler_params=pltpu.CompilerParams(
            collective_id=1, has_side_effects=True, vmem_limit_bytes=63 << 20
        ),
        name="tail",
    )(*arrays)


def finish_kernel(n, *refs):
    block_in, tokens_in, total, pack_got, small_got, early_got = refs[:6]
    block_out, tokens_out, query_out, key_out, value_out, out_out, up_out, down_out = refs[6:14]
    vectors, up_vector = refs[14:22], refs[22]
    block_out[...] = block_in[...]
    tokens_out[...] = tokens_in[...]
    mine = lax.axis_index("scene") * n + lax.axis_index("seq")
    share = query_out.shape[0]
    for head in range(0, n, 2):
        pair = [
            pack_got[head + i].astype(f32) + pack_got[n + head + i].astype(f32) for i in range(2)
        ]
        columns = slice(head * HEAD_DIM, head * HEAD_DIM + 2 * HEAD_DIM)

        def joined(first, last, start):
            return jnp.concatenate(
                [part[first:last, start : start + HEAD_DIM] for part in pair], axis=1
            )

        query_out[:, columns] = joined(0, share, 0)
        key_out[:, columns] = joined(0, share, HEAD_DIM)
        value_out[: share // 2, columns] = joined(share, share + share // 2, 0)
        value_out[share // 2 :, columns] = joined(share, share + share // 2, HEAD_DIM)
    for i in range(4):
        down_out[:, 256 * i : 256 * i + 256] = total[i]
        out_out[:, 256 * i : 256 * i + 256] = total[8, 32 * i : 32 * i + 32, :]
    for i in range(16):
        up_out[:, 256 * i : 256 * i + 256] = total[4 + i // 4, 32 * (i % 4) : 32 * (i % 4) + 32, :]
    turn = lax.rem(128 - 32 * lax.rem(mine, 4), 128)
    late = pltpu.roll(jnp.sum(small_got[...], axis=0), turn, 1)
    early = jnp.sum(early_got[...], axis=0)
    up_vector[...] = early[4]
    early = pltpu.roll(early, turn, 1)
    for i in range(4):
        vectors[i][...] = late[i, :share]
        vectors[4 + i][...] = early[i, :share]


def finish(n, block_rows, tokens_grad, total, pack_got, small_got, early_got):
    tok, width = tokens_grad.shape
    devices = 2 * n
    share = width // devices
    vmem = pl.BlockSpec(memory_space=pltpu.VMEM)

    def out(*shape):
        return jax.ShapeDtypeStruct(shape, f32)

    return pl.pallas_call(
        functools.partial(finish_kernel, n),
        out_shape=(
            jax.ShapeDtypeStruct((tok, width), bf16),
            jax.ShapeDtypeStruct((tok, width), bf16),
            out(share, width),
            out(share, width),
            out(share, width),
            out(share, width),
            out(share, 4 * width),
            out(4 * share, width),
        )
        + (out(share),) * 8
        + (out(4 * share),),
        in_specs=[vmem] * 6,
        out_specs=[vmem] * 17,
        compiler_params=pltpu.CompilerParams(vmem_limit_bytes=60 << 20),
        name="finish",
    )(block_rows, tokens_grad, total, pack_got, small_got, early_got)


def gelu_both(values):
    cubic = gelu_coef * (values + 0.044715 * values * values * values)
    bend = jnp.tanh(cubic)
    slope = gelu_coef * (1.0 + 3.0 * 0.044715 * values * values)
    grad = 0.5 * (1.0 + bend) + 0.5 * values * (1.0 - bend * bend) * slope
    return 0.5 * values * (1.0 + bend), grad


def layer_on_device(
    scenes,
    n,
    tokens,
    surface_mask,
    out_grad,
    w_query,
    w_key,
    w_value,
    w_out,
    w_up,
    w_down,
    b_query,
    b_value,
    b_out,
    b_up,
    b_down,
    gain_one,
    shift_one,
    gain_two,
    shift_two,
):
    _, tok, width = tokens.shape
    rows = tokens[0].astype(f32)
    att_t, normed_all, q_all, k_all, v_all, o_all, lse_all = attention_forward(
        n, tokens[0], gain_one, shift_one, w_query, w_key, w_value, b_query, b_value
    )

    att_t, out_grad, surface_mask = lax.optimization_barrier((att_t, out_grad, surface_mask))
    residual = rows + matmul_tn(att_t, w_out) + b_out
    scaled_two, _ = normalise(residual)
    normed_two = (scaled_two * gain_two + shift_two).astype(bf16)
    masked = out_grad[0] * surface_mask[0].astype(bf16)[:, None]
    arrived = tail(
        n,
        tok,
        width,
        w_up.shape[1],
        q_all,
        k_all,
        v_all,
        o_all,
        lse_all,
        masked,
        normed_two,
        residual,
        att_t,
        normed_all,
        w_down,
        w_up,
        w_out,
        *(w.reshape(2, 2, 2, 128, width) for w in (w_query, w_key, w_value)),
        tokens[0],
        gain_one[None],
        gain_two[None],
        b_down[None],
        b_up[None],
    )
    block_out, tokens_grad, *sums = finish(n, *arrived)
    bquery, bvalue, gone, sone, bout, bdown, gtwo, stwo, bup = sums[6:]
    return (
        block_out[None],
        tokens_grad[None],
        *sums[:6],
        bquery,
        bvalue,
        bout,
        bup,
        bdown,
        gone,
        sone,
        gtwo,
        stwo,
    )


def norm_rows(values, gain, shift):
    row_mean = jnp.mean(values, axis=-1, keepdims=True)
    centred = values - row_mean
    row_var = jnp.mean(centred * centred, axis=-1, keepdims=True)
    return centred * lax.rsqrt(row_var + norm_eps) * gain + shift


def gelu_tanh(values):
    return (
        0.5 * values * (1.0 + jnp.tanh(gelu_coef * (values + 0.044715 * values * values * values)))
    )


def take_pair(array_in, pair_index):
    pair_width = 2 * HEAD_DIM
    sliced = lax.dynamic_slice_in_dim(array_in, pair_index * pair_width, pair_width, 2)
    return sliced.reshape(sliced.shape[:2] + (2, HEAD_DIM))


def take_stats(array_in, pair_index):
    return lax.dynamic_slice_in_dim(array_in, pair_index * 2, 2, 1)


def join_pairs(stacked):
    moved = jnp.moveaxis(stacked, 0, 2)
    return moved.reshape(moved.shape[:2] + (moved.shape[2] * moved.shape[3],))


def join_stats(stacked):
    moved = jnp.moveaxis(stacked, 0, 1)
    return moved.reshape((moved.shape[0], moved.shape[1] * moved.shape[2], moved.shape[3]))


def merge_heads(pair_part):
    return pair_part.reshape(pair_part.shape[:2] + (2 * HEAD_DIM,))


def attend(q_scene, k_gathered, v_gathered):

    def attend_pair_step(unused, pair_index):
        q_pair = take_pair(q_scene, pair_index)
        k_pair = take_pair(k_gathered, pair_index)
        v_pair = take_pair(v_gathered, pair_index)
        scores = (
            jnp.einsum("sqhe,skhe->shqk", q_pair, k_pair, preferred_element_type=jnp.float32)
            * score_scale
        )
        row_max = jnp.max(scores, axis=-1, keepdims=True)
        shifted = jnp.exp(scores - row_max)
        row_sum = jnp.sum(shifted, axis=-1, keepdims=True)
        prob_low = (shifted / row_sum).astype(jnp.bfloat16)
        pair_out = jnp.einsum(
            "shqk,skhe->sqhe", prob_low, v_pair, preferred_element_type=jnp.float32
        )
        pair_lse = (row_max + jnp.log(row_sum))[..., 0]
        return (unused, (merge_heads(pair_out), pair_lse))

    pair_count = HEADS // 2
    _, (pair_outs, pair_lses) = lax.scan(
        attend_pair_step, jnp.zeros((), jnp.float32), jnp.arange(pair_count, dtype=jnp.int32)
    )
    return (join_pairs(pair_outs), join_stats(pair_lses))


def query_side(q_scene, k_gathered, v_gathered, row_lse, att_grad):

    def query_pair_step(unused, pair_index):
        q_pair = take_pair(q_scene, pair_index)
        k_pair = take_pair(k_gathered, pair_index)
        v_pair = take_pair(v_gathered, pair_index)
        d_pair = take_pair(att_grad, pair_index)
        l_pair = take_stats(row_lse, pair_index)
        scores = (
            jnp.einsum("sqhe,skhe->shqk", q_pair, k_pair, preferred_element_type=jnp.float32)
            * score_scale
        )
        attn_prob = jnp.exp(scores - l_pair[..., None])
        dprob = jnp.einsum("sqhe,skhe->shqk", d_pair, v_pair, preferred_element_type=jnp.float32)
        row_delta = jnp.sum(attn_prob * dprob, axis=-1)
        dscore = (attn_prob * (dprob - row_delta[..., None])).astype(jnp.bfloat16)
        q_part = (
            jnp.einsum("shqk,skhe->sqhe", dscore, k_pair, preferred_element_type=jnp.float32)
            * score_scale
        )
        results = (merge_heads(q_part), row_delta)
        prob_low = attn_prob.astype(jnp.bfloat16)
        k_part = (
            jnp.einsum("shqk,sqhe->skhe", dscore, q_pair, preferred_element_type=jnp.float32)
            * score_scale
        )
        v_part = jnp.einsum("shqk,sqhe->skhe", prob_low, d_pair, preferred_element_type=jnp.float32)
        results = results + (merge_heads(k_part), merge_heads(v_part))
        return (unused, results)

    pair_count = HEADS // 2
    _, results = lax.scan(
        query_pair_step, jnp.zeros((), jnp.float32), jnp.arange(pair_count, dtype=jnp.int32)
    )
    return results


def on_any_device(
    tokens,
    surface_mask,
    out_grad,
    w_query,
    w_key,
    w_value,
    w_out,
    w_up,
    w_down,
    b_query,
    b_value,
    b_out,
    b_up,
    b_down,
    gain_one,
    shift_one,
    gain_two,
    shift_two,
):
    scenes, local_len, model_width = tokens.shape
    row_count = scenes * local_len
    flat_rows = tokens.astype(jnp.float32).reshape(row_count, model_width)
    normed, norm_one_pull = jax.vjp(norm_rows, flat_rows, gain_one, shift_one)
    normed_low = normed.astype(jnp.bfloat16)
    q_low = (matmul(normed_low, w_query) + b_query).astype(jnp.bfloat16)
    k_low = matmul(normed_low, w_key).astype(jnp.bfloat16)
    v_low = (matmul(normed_low, w_value) + b_value).astype(jnp.bfloat16)
    q_scene = q_low.reshape(scenes, local_len, model_width)
    k_scene = k_low.reshape(scenes, local_len, model_width)
    v_scene = v_low.reshape(scenes, local_len, model_width)
    k_gathered, v_gathered = (
        lax.all_gather(k_scene, "seq", axis=1, tiled=True),
        lax.all_gather(v_scene, "seq", axis=1, tiled=True),
    )
    attended, row_lse = attend(q_scene, k_gathered, v_gathered)
    att_low = attended.reshape(row_count, model_width).astype(jnp.bfloat16)
    residual = flat_rows + matmul(att_low, w_out) + b_out
    normed_two, norm_two_pull = jax.vjp(norm_rows, residual, gain_two, shift_two)
    normed_two_low = normed_two.astype(jnp.bfloat16)
    hidden = matmul(normed_two_low, w_up) + b_up
    activated, gelu_pull = jax.vjp(gelu_tanh, hidden)
    act_low = activated.astype(jnp.bfloat16)
    block_rows = residual + matmul(act_low, w_down) + b_down
    block_out = block_rows.reshape(scenes, local_len, model_width).astype(jnp.bfloat16)
    masked_f = out_grad.astype(jnp.float32) * surface_mask.astype(jnp.float32)[..., None]
    masked_rows = masked_f.reshape(row_count, model_width)
    masked_low = masked_rows.astype(jnp.bfloat16)
    grad_down = matmul_tn(act_low, masked_low)
    grad_bdown = jnp.sum(masked_rows, axis=0)
    act_grad = matmul_nt(masked_low, w_down)
    hidden_low = gelu_pull(act_grad)[0].astype(jnp.bfloat16)
    grad_up = matmul_tn(normed_two_low, hidden_low)
    grad_bup = jnp.sum(hidden_low.astype(jnp.float32), axis=0)
    norm_two_in = matmul_nt(hidden_low, w_up)
    resid_part, grad_gain_two, grad_shift_two = norm_two_pull(norm_two_in)
    resid_grad = masked_rows + resid_part
    resid_low = resid_grad.astype(jnp.bfloat16)
    grad_out = matmul_tn(att_low, resid_low)
    grad_bout = jnp.sum(resid_low.astype(jnp.float32), axis=0)
    att_grad = (
        matmul_nt(resid_low, w_out).astype(jnp.bfloat16).reshape(scenes, local_len, model_width)
    )
    q_parts, delta_parts, k_parts, v_parts = query_side(
        q_scene, k_gathered, v_gathered, row_lse, att_grad
    )
    k_summed, v_summed = (
        lax.psum_scatter(
            k_parts.astype(jnp.bfloat16), "seq", scatter_dimension=2, tiled=True
        ).astype(jnp.float32),
        lax.psum_scatter(
            v_parts.astype(jnp.bfloat16), "seq", scatter_dimension=2, tiled=True
        ).astype(jnp.float32),
    )
    k_grad = join_pairs(k_summed)
    v_grad = join_pairs(v_summed)
    q_grad = join_pairs(q_parts)
    q_grad_low = q_grad.reshape(row_count, model_width).astype(jnp.bfloat16)
    k_grad_low = k_grad.reshape(row_count, model_width).astype(jnp.bfloat16)
    v_grad_low = v_grad.reshape(row_count, model_width).astype(jnp.bfloat16)
    grad_query = matmul_tn(normed_low, q_grad_low)
    grad_key = matmul_tn(normed_low, k_grad_low)
    grad_value = matmul_tn(normed_low, v_grad_low)
    grad_bquery = jnp.sum(q_grad_low.astype(jnp.float32), axis=0)
    grad_bvalue = jnp.sum(v_grad_low.astype(jnp.float32), axis=0)
    norm_one_in = (
        matmul_nt(q_grad_low, w_query)
        + matmul_nt(k_grad_low, w_key)
        + matmul_nt(v_grad_low, w_value)
    )
    token_part, grad_gain_one, grad_shift_one = norm_one_pull(norm_one_in)
    tokens_grad = (
        (resid_grad + token_part).reshape(scenes, local_len, model_width).astype(jnp.bfloat16)
    )
    (
        sum_query,
        sum_key,
        sum_value,
        sum_out,
        sum_bquery,
        sum_bvalue,
        sum_bout,
        sum_gain_one,
        sum_shift_one,
        sum_up,
        sum_down,
        sum_bup,
        sum_bdown,
        sum_gain_two,
        sum_shift_two,
    ) = (
        lax.psum_scatter(grad_query, ("scene", "seq"), scatter_dimension=0, tiled=True),
        lax.psum_scatter(grad_key, ("scene", "seq"), scatter_dimension=0, tiled=True),
        lax.psum_scatter(grad_value, ("scene", "seq"), scatter_dimension=0, tiled=True),
        lax.psum_scatter(grad_out, ("scene", "seq"), scatter_dimension=0, tiled=True),
        lax.psum_scatter(grad_bquery, ("scene", "seq"), scatter_dimension=0, tiled=True),
        lax.psum_scatter(grad_bvalue, ("scene", "seq"), scatter_dimension=0, tiled=True),
        lax.psum_scatter(grad_bout, ("scene", "seq"), scatter_dimension=0, tiled=True),
        lax.psum_scatter(grad_gain_one, ("scene", "seq"), scatter_dimension=0, tiled=True),
        lax.psum_scatter(grad_shift_one, ("scene", "seq"), scatter_dimension=0, tiled=True),
        lax.psum_scatter(grad_up, ("scene", "seq"), scatter_dimension=0, tiled=True),
        lax.psum_scatter(grad_down, ("scene", "seq"), scatter_dimension=0, tiled=True),
        lax.psum_scatter(grad_bup, ("scene", "seq"), scatter_dimension=0, tiled=True),
        lax.psum_scatter(grad_bdown, ("scene", "seq"), scatter_dimension=0, tiled=True),
        lax.psum_scatter(grad_gain_two, ("scene", "seq"), scatter_dimension=0, tiled=True),
        lax.psum_scatter(grad_shift_two, ("scene", "seq"), scatter_dimension=0, tiled=True),
    )
    return (
        block_out,
        tokens_grad,
        sum_query,
        sum_key,
        sum_value,
        sum_out,
        sum_up,
        sum_down,
        sum_bquery,
        sum_bvalue,
        sum_bout,
        sum_bup,
        sum_bdown,
        sum_gain_one,
        sum_shift_one,
        sum_gain_two,
        sum_shift_two,
    )


def solution(mesh):
    placed = (
        P("scene", "seq", None),
        P("scene", "seq"),
        P("scene", "seq", None),
        P(),
        P(),
        P(),
        P(),
        P(),
        P(),
        P(),
        P(),
        P(),
        P(),
        P(),
        P(),
        P(),
        P(),
        P(),
    )
    scenes, n = mesh.shape["scene"], mesh.shape["seq"]
    if (scenes, n) == (2, HEADS):
        on_device = functools.partial(layer_on_device, scenes, n)
    else:
        on_device = on_any_device
    return jax.shard_map(
        on_device,
        mesh=mesh,
        in_specs=placed,
        out_specs=(
            P("scene", "seq", None),
            P("scene", "seq", None),
            P(("scene", "seq"), None),
            P(("scene", "seq"), None),
            P(("scene", "seq"), None),
            P(("scene", "seq"), None),
            P(("scene", "seq"), None),
            P(("scene", "seq"), None),
            P(("scene", "seq")),
            P(("scene", "seq")),
            P(("scene", "seq")),
            P(("scene", "seq")),
            P(("scene", "seq")),
            P(("scene", "seq")),
            P(("scene", "seq")),
            P(("scene", "seq")),
            P(("scene", "seq")),
        ),
        check_vma=False,
    )
```

```python
import functools

import jax
import jax.numpy as jnp
from jax import lax
from jax.experimental import pallas as pl
from jax.experimental.pallas import tpu as pltpu
from jax.sharding import PartitionSpec as P

HEADS = 16
HEAD_DIM = 64
MESH = pl.DeviceIdType.MESH
f32 = jnp.float32
bf16 = jnp.bfloat16

norm_eps = 1e-05
score_scale = 0.125
FORWARD_LIMIT = 60 << 20
gelu_coef = 0.7978845608028654


def matmul(left, right):
    return jnp.dot(left, right, preferred_element_type=jnp.float32)


def contract(left, right, left_dim, right_dim):
    return lax.dot_general(
        left, right, (((left_dim,), (right_dim,)), ((), ())), preferred_element_type=jnp.float32
    )


def matmul_tn(left, right):
    return contract(left, right, 0, 0)


def matmul_nt(left, right):
    return contract(left, right, 1, 1)


def normalise(values):
    row_mean = jnp.mean(values, axis=-1, keepdims=True)
    centred = values - row_mean
    row_var = jnp.mean(centred * centred, axis=-1, keepdims=True)
    inverse = lax.rsqrt(row_var + norm_eps)
    return centred * inverse, inverse


def norm_back(grad, scaled, inverse, gain):
    weighted = grad * gain
    back = inverse * (
        weighted
        - jnp.mean(weighted, axis=-1, keepdims=True)
        - scaled * jnp.mean(weighted * scaled, axis=-1, keepdims=True)
    )
    return back, jnp.sum(grad * scaled, axis=0), jnp.sum(grad, axis=0)


def greet(partners):
    barrier = pltpu.get_barrier_semaphore()
    for partner in partners:
        pl.semaphore_signal(barrier, inc=1, device_id=partner, device_id_type=MESH)
    return lambda: pl.semaphore_wait(barrier, len(partners))


def remote(src, dst, send_sem, recv_sem, device):
    return pltpu.make_async_remote_copy(
        src_ref=src,
        dst_ref=dst,
        send_sem=send_sem,
        recv_sem=recv_sem,
        device_id=device,
        device_id_type=MESH,
    )


def flipped(index, other):
    out = 0
    for weight in (1, 2, 4, 8):
        bit, turn = lax.rem(index // weight, 2), lax.rem(other // weight, 2)
        out = out + weight * (bit + turn - 2 * bit * turn)
    return out


def forward_kernel(n, tok, *refs):
    (
        tokens_ref,
        gain_ref,
        shift_ref,
        wq_ref,
        wk_ref,
        wv_ref,
        bq_ref,
        bv_ref,
        att_ref,
        normed_out,
        q_out,
        k_out,
        v_out,
        o_out,
        lse_out,
        rows_in,
        gain,
        shift,
        b_query,
        b_value,
        land,
        w_pair,
        w_head,
        bias,
        q_all,
        k_all,
        v_all,
        k_nat,
        o_all,
        lse_all,
        stats,
        att_send,
        load_sem,
        gather_send,
        gather_recv,
        save_sem,
        out_send,
        out_recv,
        out_local,
        last_sem,
    ) = refs
    me = lax.axis_index("seq")
    scene = lax.axis_index("scene")
    core = lax.rem(me, 2)
    chips = n // 2
    wide = 2 * tok
    half_rows = tok // 2
    devices = [flipped(me, s) for s in range(n)]

    def rows(head):
        return pl.ds(pl.multiple_of(head * HEAD_DIM, HEAD_DIM), HEAD_DIM)

    def lanes(block, width=tok):
        return pl.ds(pl.multiple_of(block * width, width), width)

    tokens_load = pltpu.make_async_copy(tokens_ref, rows_in, load_sem.at[0])
    tokens_load.start()
    weight_loads = [
        pltpu.make_async_copy(ref.at[:, lanes(me // 2, 128)], w_pair.at[i], load_sem.at[1 + i])
        for i, ref in enumerate((wk_ref, wq_ref, wv_ref))
    ]
    vector_loads = [
        pltpu.make_async_copy(src, dst, load_sem.at[4 + i])
        for i, (src, dst) in enumerate(
            ((gain_ref, gain), (shift_ref, shift), (bq_ref, b_query), (bv_ref, b_value))
        )
    ]
    for load in vector_loads + weight_loads:
        load.start()
    all_here = greet([(scene, devices[s]) for s in range(1, n)])

    def gather_copy(slot, over, part):
        piece = slice(part * half_rows, (part + 1) * half_rows)
        there = slot ^ over
        return remote(
            land.at[slot, piece, :],
            land.at[there, piece, :],
            gather_send.at[there, part],
            gather_recv.at[there, part],
            (scene, devices[over]),
        )

    routes = {0: (4, 2, 8, 1), 8: (4, 2, 1), 4: (2, 1), 12: (2, 1), 2: (1,), 6: (1,), 10: (1,), 14: (1,)}

    def routes_of(slot, part):
        if part == 1 and slot == 12:
            return (1,)
        if part == 1 and slot == 10:
            return (4, 1)
        return routes.get(slot, ())

    def came_over(slot, part):
        for source in range(n):
            for over in routes_of(source, part):
                if source ^ over == slot:
                    return over

    sent = []
    saves = []

    def forward(slot, part):
        for over in routes_of(slot, part):
            copy = gather_copy(slot, over, part)
            copy.start()
            sent.append(copy)

    def arrive(slot, part):
        over = came_over(slot, part)
        gather_copy(slot ^ over, over, part).wait_recv()
        forward(slot, part)

    for load in [tokens_load] + vector_loads:
        load.wait()
    for part in range(2):
        piece = slice(part * half_rows, (part + 1) * half_rows)
        scaled, _ = normalise(rows_in[piece, :].astype(f32))
        land[0, piece, :] = (scaled * gain[...] + shift[...]).astype(bf16)
        if part == 0:
            all_here()
        forward(0, part)

    odd = core == 1
    for i, load in enumerate(weight_loads):
        load.wait()
        pair = w_pair[i].astype(f32)
        w_head[:, HEAD_DIM * i : HEAD_DIM * i + HEAD_DIM] = jnp.where(
            odd, pair[:, HEAD_DIM:], pair[:, :HEAD_DIM]
        ).astype(bf16)
    for i, ref in ((1, b_query), (2, b_value)):
        pair = ref[0:1, lanes(me // 2, 128)]
        bias[0:1, HEAD_DIM * i : HEAD_DIM * i + HEAD_DIM] = jnp.where(
            odd, pair[:, HEAD_DIM:], pair[:, :HEAD_DIM]
        )
    bias[0:1, :HEAD_DIM] = jnp.zeros((1, HEAD_DIM), f32)

    def project(slot):
        made = contract(land[slot], w_head[...], 1, 0) + bias[0:1, :]
        low = made.astype(bf16)
        turned = low.T
        span = slice(slot * tok, (slot + 1) * tok)
        k_nat[span, :] = low[:, :HEAD_DIM]
        k_all[:, span] = turned[:HEAD_DIM]
        q_all[:, span] = turned[HEAD_DIM : 2 * HEAD_DIM] * jnp.asarray(score_scale, bf16)
        v_all[:, span] = turned[2 * HEAD_DIM :]
        save = pltpu.make_async_copy(land.at[slot], normed_out.at[span, :], save_sem.at[slot])
        save.start()
        saves.append(save)

    def attend(span, first, state):
        top, total, acc = state
        keys = slice(first, first + chips // 2 * wide)
        scores = contract(k_nat[keys, :], q_all[:, span], 1, 0)
        here = jnp.max(scores, axis=0, keepdims=True)
        new_top = here if top is None else jnp.maximum(top, here)
        shifted = jnp.exp(scores - new_top)
        part_sum = jnp.sum(shifted, axis=0, keepdims=True)
        part = contract(v_all[:, keys], shifted.astype(bf16), 1, 0)
        if top is None:
            return new_top, part_sum, part
        fade = jnp.exp(top - new_top)
        return new_top, total * fade + part_sum, acc * fade + part

    middle = chips // 2 * wide

    def early(i):
        span = slice(i * wide, (i + 1) * wide)
        top, total, acc = attend(span, 0, (None, None, None))
        stats[0:1, span] = top
        stats[1:2, span] = total
        o_all[:, span] = acc

    def close(i, span, state):
        top, total, acc = state
        out = acc / total
        o_all[:, span] = out
        lse_all[:, span] = jnp.broadcast_to(top + jnp.log(total), (8, wide))
        low = out.astype(bf16)
        att_send[i, 0] = low[:, :tok]
        att_send[i, 1] = low[:, tok:]

    def out_copy(i, flip):
        return remote(
            att_send.at[i, flip],
            att_ref.at[rows(me), :],
            out_send.at[i, flip],
            out_recv.at[i, flip],
            (scene, flipped(me, 2 * i + flip)),
        )

    project(0)
    for part in range(2):
        arrive(1, part)
    project(1)
    for part in range(2):
        arrive(2, part)
        arrive(4, part)
    project(2)
    for slot in (3, 5):
        for part in range(2):
            arrive(slot, part)
    project(3)
    project(4)
    project(5)
    for part in range(2):
        arrive(8, part)
    for slot in (6, 7):
        for part in range(2):
            arrive(slot, part)
    project(6)
    project(7)
    early(0)
    early(1)
    arrive(9, 0)
    arrive(9, 1)
    project(8)
    project(9)
    for part in range(2):
        arrive(12, part)
        arrive(10, part)
    early(2)
    for slot in (11, 13):
        for part in range(2):
            arrive(slot, part)
    project(10)
    project(11)
    early(3)
    project(12)
    project(13)
    arrive(14, 0)
    arrive(14, 1)
    project(14)
    arrive(15, 0)
    arrive(15, 1)
    project(15)
    for i, (src, dst) in enumerate(((q_all, q_out), (k_all, k_out), (v_all, v_out))):
        save = pltpu.make_async_copy(src, dst, last_sem.at[i])
        save.start()
        saves.append(save)

    def late_body(j, carry):
        i = chips - 1 - j
        span = lanes(i, wide)
        close(i, span, attend(span, middle, attend(span, 0, (None, None, None))))
        out_copy(i, 0).start()
        out_copy(i, 1).start()
        return carry

    lax.fori_loop(0, chips // 2, late_body, 0)

    def rest(i, span):
        state = (stats[0:1, span], stats[1:2, span], o_all[:, span])
        close(i, span, attend(span, middle, state))

    def rest_body(j, carry):
        i = chips // 2 - 1 - j
        rest(i, lanes(i, wide))
        out_copy(i, 0).start()
        out_copy(i, 1).start()
        return carry

    lax.fori_loop(0, chips // 2 - 1, rest_body, 0)
    rest(0, slice(0, wide))
    mine = pltpu.make_async_copy(att_send.at[0, 0], att_ref.at[rows(me), :], out_local)
    mine.start()
    out_copy(0, 1).start()
    for i, (src, dst) in enumerate(((o_all, o_out), (lse_all, lse_out))):
        save = pltpu.make_async_copy(src, dst, last_sem.at[3 + i])
        save.start()
        saves.append(save)
    for copy in sent:
        copy.wait_send()
    mine.wait()
    out_copy(0, 1).wait()

    def drain(i, carry):
        out_copy(i, 0).wait()
        out_copy(i, 1).wait()
        return carry

    lax.fori_loop(1, chips, drain, 0)
    for save in saves:
        save.wait()


def attention_forward(n, tokens, gain, shift, w_query, w_key, w_value, b_query, b_value):
    tok, width = tokens.shape
    length = n * tok
    any_spec = pl.BlockSpec(memory_space=pl.ANY)
    head_all = jax.ShapeDtypeStruct((HEAD_DIM, length), bf16)
    dma = pltpu.SemaphoreType.DMA
    return pl.pallas_call(
        functools.partial(forward_kernel, n, tok),
        out_shape=(
            jax.ShapeDtypeStruct((width, tok), bf16),
            jax.ShapeDtypeStruct((length, width), bf16),
            head_all,
            head_all,
            head_all,
            jax.ShapeDtypeStruct((HEAD_DIM, length), f32),
            jax.ShapeDtypeStruct((8, length), f32),
        ),
        in_specs=[any_spec] * 8,
        out_specs=[any_spec] * 7,
        scratch_shapes=[
            pltpu.VMEM((tok, width), bf16),
            pltpu.VMEM((1, width), f32),
            pltpu.VMEM((1, width), f32),
            pltpu.VMEM((1, width), f32),
            pltpu.VMEM((1, width), f32),
            pltpu.VMEM((n, tok, width), bf16),
            pltpu.VMEM((3, width, 2 * HEAD_DIM), bf16),
            pltpu.VMEM((width, 3 * HEAD_DIM), bf16),
            pltpu.VMEM((8, 3 * HEAD_DIM), f32),
            pltpu.VMEM((HEAD_DIM, length), bf16),
            pltpu.VMEM((HEAD_DIM, length), bf16),
            pltpu.VMEM((HEAD_DIM, length), bf16),
            pltpu.VMEM((length, HEAD_DIM), bf16),
            pltpu.VMEM((HEAD_DIM, length), f32),
            pltpu.VMEM((8, length), f32),
            pltpu.VMEM((8, length), f32),
            pltpu.VMEM((n // 2, 2, HEAD_DIM, tok), bf16),
            dma((8,)),
            dma((n, 2)),
            dma((n, 2)),
            dma((n,)),
            dma((n // 2, 2)),
            dma((n // 2, 2)),
            dma,
            dma((5,)),
        ],
        compiler_params=pltpu.CompilerParams(
            collective_id=0, has_side_effects=True, vmem_limit_bytes=FORWARD_LIMIT
        ),
        name="attention_forward",
    )(
        tokens,
        gain[None],
        shift[None],
        w_query,
        w_key,
        w_value,
        b_query[None],
        b_value[None],
    )


CHUNKS = 9
TICKS = CHUNKS + 4
SLOTS = 3


def halving_plan(full, got0, got1a, got1b, got2a, got2b, got3, got4, total, send_sem, recv_sem):
    me = lax.axis_index("seq")
    x = lax.axis_index("scene")
    core = lax.rem(me, 2)
    y = lax.rem(me // 2, 2)
    z0 = lax.rem(me // 4, 2)
    z1 = me // 8
    at_core = (x, me + 1 - 2 * core)
    at_x = (1 - x, me)
    at_y = (x, me + 2 - 4 * y)
    at_z0 = (x, me + 4 - 8 * z0)
    at_z1 = (x, me + 8 - 16 * z1)
    up, low = slice(0, 64), slice(64, 128)

    def copy_of(slot, c):
        src, dst, device = (
            lambda: (full.at[lax.rem(c, SLOTS), :, :, :, :, 1 - core], got0.at[c], at_core),
            lambda: (got0.at[c, 1 - x, :, :, :, up, :], got1a.at[c], at_x),
            lambda: (got0.at[c, :, :, :, 1 - y, low, :], got1b.at[c], at_y),
            lambda: (got1a.at[c, :, 1 - z0], got2a.at[c], at_z0),
            lambda: (got1b.at[c, 1 - x], got2b.at[c], at_x),
            lambda: (got2a.at[c, :, 1 - y], got3.at[c, :, up, :], at_y),
            lambda: (got2b.at[c, :, 1 - z0], got3.at[c, :, low, :], at_z0),
            lambda: (got3.at[c, 1 - z1], got4.at[c], at_z1),
        )[slot]()
        going = send_sem.at[c] if slot == 0 else send_sem.at[CHUNKS + slot]
        return remote(src, dst, going, recv_sem.at[c, slot], device)

    def sum1(c):
        copy_of(0, c).wait_recv()
        got0[c] = got0[c] + full[lax.rem(c, SLOTS), :, :, :, :, core]

    def start1(c):
        copy_of(1, c).start()
        copy_of(2, c).start()

    def stage2(c):
        copy_of(1, c).wait_recv()
        got1a[c] = got1a[c] + got0[c, x, :, :, :, up, :]
        copy_of(3, c).start()
        copy_of(2, c).wait_recv()
        got1b[c] = got1b[c] + got0[c, :, :, :, y, low, :]
        copy_of(4, c).start()

    def stage3(c):
        copy_of(3, c).wait_recv()
        got2a[c] = got2a[c] + got1a[c, :, z0]
        copy_of(5, c).start()
        copy_of(4, c).wait_recv()
        got2b[c] = got2b[c] + got1b[c, x]
        copy_of(6, c).start()

    def stage4(c):
        copy_of(5, c).wait_recv()
        got3[c, :, up, :] = got3[c, :, up, :] + got2a[c, :, y]
        copy_of(6, c).wait_recv()
        got3[c, :, low, :] = got3[c, :, low, :] + got2b[c, :, z0]
        copy_of(7, c).start()

    def stage5(c):
        copy_of(7, c).wait_recv()
        total[c] = got3[c, z1].astype(f32) + got4[c].astype(f32)

    def tick(when):
        for stage, c in (
            (stage5, when - 4),
            (stage4, when - 3),
            (stage3, when - 2),
            (stage2, when - 1),
            (start1, when + 1),
        ):

            @pl.when((c >= 0) & (c < CHUNKS))
            def _(stage=stage, c=c):
                stage(c)

    def settle():
        for slot, src in enumerate((got1a, got1a, got1b, got2a, got2b, got3, got3, got4)):
            if slot:
                everything = src.at[:, :, up, :] if slot in (5, 6) else src
                pltpu.make_async_copy(everything, everything, send_sem.at[CHUNKS + slot]).wait()

    return copy_of, sum1, start1, tick, settle


def tail_kernel(n, tok, *refs):
    (
        q_ref,
        k_ref,
        v_ref,
        o_ref,
        lse_ref,
        masked_ref,
        att_ref,
        normed_ref,
        wd_ref,
        wu_ref,
        wo_ref,
        wq_ref,
        wk_ref,
        wv_ref,
        tokens_ref,
        gain_ref,
        gain_two_ref,
        b_down_ref,
        b_up_ref,
        b_out_ref,
        shift_two_ref,
        block_out,
        tokens_out,
        total,
        pack_got,
        small_got,
        early_got,
        q_all,
        k_all,
        v_all,
        d_all,
        d_send,
        o_all,
        lse_all,
        low,
        act,
        masked,
        two,
        hidden,
        att,
        resid_low,
        act_t,
        two_t,
        full,
        got0,
        got1a,
        got1b,
        got2a,
        got2b,
        got3,
        got4,
        land,
        rows_in,
        resid,
        gain_one,
        gain_two,
        b_down,
        b_up,
        b_out,
        shift_two,
        pack,
        small,
        early,
        load_sem,
        ring_sem,
        weight_sem,
        normed_sem,
        in_send,
        in_recv,
        in_local,
        kv_send,
        kv_recv,
        kv_local,
        q_send,
        q_recv,
        q_local,
        half_send,
        half_recv,
        last_send,
        last_recv,
        last_local,
    ) = refs
    me = lax.axis_index("seq")
    scene = lax.axis_index("scene")
    chips = n // 2
    length = n * tok
    wide = 2 * tok
    devices = 2 * n
    width = masked.shape[1]
    mine = scene * n + me

    def rows(head):
        return pl.ds(pl.multiple_of(head * HEAD_DIM, HEAD_DIM), HEAD_DIM)

    def lanes(block, width=tok):
        return pl.ds(pl.multiple_of(block * width, width), width)

    loads = [
        pltpu.make_async_copy(src, dst, load_sem.at[i])
        for i, (src, dst) in enumerate(
            (
                (att_ref, att),
                (b_up_ref, b_up),
                (masked_ref, masked),
                (q_ref, q_all),
                (k_ref, k_all),
                (v_ref, v_all),
                (o_ref, o_all),
                (lse_ref, lse_all),
                (b_out_ref, b_out),
                (shift_two_ref, shift_two),
                (tokens_ref, rows_in),
                (gain_ref, gain_one),
                (gain_two_ref, gain_two),
                (b_down_ref, b_down),
            )
        )
    ]
    for load in loads:
        load.start()

    def peer(j):
        index = lax.rem(mine + j, devices)
        return index, (index // n, lax.rem(index, n))

    all_here = greet([peer(j)[1] for j in range(1, devices)])

    half, sum1, start1, tick, settle = halving_plan(
        full, got0, got1a, got1b, got2a, got2b, got3, got4, total, half_send, half_recv
    )

    def chunk_begin(c):
        @pl.when(c >= SLOTS)
        def _():
            half(0, c - SLOTS).wait_send()

        return lax.rem(c, SLOTS)

    def chunk_end(c):
        half(0, c).start()

        @pl.when((c >= 1) & (c != 4))
        def _():
            sum1(c - 1)

    def down_chunk(c):
        slot = chunk_begin(c)
        columns = masked[:, lanes(c, 256)]
        for block in range(4):
            part = contract(act_t[1024 * block : 1024 * block + 1024, :], columns, 1, 0)
            full[slot, block // 2, block % 2] = part.astype(bf16).reshape(2, 2, 2, 128, 256)
        chunk_end(c)

    def narrow_chunk(c, left, right):
        slot = chunk_begin(c)
        for block in range(4):
            part = contract(left, right[:, 256 * block : 256 * block + 256], 1, 0)
            full[slot, :, :, :, :, :, 32 * block : 32 * block + 32, :] = part.astype(bf16).reshape(
                2, 2, 2, 2, 2, 32, 256
            )
        chunk_end(c)

    def first_chunk(c, carry):
        down_chunk(c)

        @pl.when((c >= 1) & (c <= 2))
        def _():
            start1(c - 1)

        return carry

    def feed_forward(ring, slope, out_acc, two_acc):
        def weight_load(i):
            if i in (-1, 12):
                src = wo_ref
            elif 4 <= i < 8:
                src = wd_ref.at[1024 * (i - 4) : 1024 * (i - 4) + 1024, :]
            else:
                src = wu_ref.at[:, 1024 * (i % 4) : 1024 * (i % 4) + 1024]
            return pltpu.make_async_copy(src, ring.at[i % 2], ring_sem.at[i % 2])

        for i in (-1, 0):
            weight_load(i).start()
        for i in (0, 1, *range(8, 14)):
            loads[i].wait()
        turned = att[...].T
        weight_load(-1).wait()
        resid[...] = rows_in[...].astype(f32) + contract(turned, ring[1], 1, 0) + b_out[...]
        weight_load(1).start()
        scaled, _ = normalise(resid[...])
        two[...] = (scaled * gain_two[...] + shift_two[...]).astype(bf16)
        for i in range(4):
            weight_load(i).wait()
            grown = contract(two[...], ring[i % 2], 1, 0) + b_up[:, 1024 * i : 1024 * i + 1024]
            weight_load(i + 2).start()
            value, slope[i] = gelu_both(grown)
            value = value.astype(bf16)
            act[tok * i : tok * i + tok, :] = value
            act_t[1024 * i : 1024 * i + 1024, :] = value.T
        loads[2].wait()
        all_here()
        lax.fori_loop(0, 4, first_chunk, 0)
        masked_sum = jnp.sum(masked[...].astype(f32), axis=0, keepdims=True)
        for i in range(4):
            weight_load(4 + i).wait()
            there = slice(tok * i, tok * i + tok)
            part = contract(act[there, :], ring[i % 2], 1, 0)
            out_acc[...] = resid[...] + b_down[...] + part if i == 0 else out_acc[...] + part
            grown = contract(masked[...], ring[i % 2], 1, 1) * slope[i]
            weight_load(6 + i).start()
            grown = grown.astype(bf16)
            hidden[there, :] = grown
            sums = jnp.sum(grown.astype(f32), axis=0, keepdims=True)
            for j in range(8):
                early[8 * i + j, 4:5, :] = sums[:, 128 * j : 128 * j + 128]
            if i == 1:
                tick(1)
        block_out[...] = out_acc[...].astype(bf16)
        sum1(3)
        for i in range(4):
            weight_load(8 + i).wait()
            part = contract(hidden[tok * i : tok * i + tok, :], ring[i % 2], 1, 1)
            two_acc[...] = part if i == 0 else two_acc[...] + part
            if i < 3:
                weight_load(10 + i).start()
            if i == 1:
                tick(2)
        scaled, inverse = normalise(resid[...])
        part, gain_grad, shift_grad = norm_back(two_acc[...], scaled, inverse, gain_two[...])
        resid[...] = masked[...].astype(f32) + part
        resid_low[...] = resid[...].astype(bf16)
        low_sum = jnp.sum(resid_low[...].astype(f32), axis=0, keepdims=True)
        for row, vector in enumerate((low_sum, masked_sum, gain_grad[None], shift_grad[None])):
            for d in range(devices):
                start = 128 * (d // 4)
                early[d, row : row + 1, :] = vector[:, start : start + 128]
        weight_load(12).wait()
        d_send[...] = contract(ring[0], resid_low[...], 1, 1).astype(bf16)

    pl.run_scoped(
        feed_forward,
        pltpu.VMEM((2, 1024, 1024), bf16),
        pltpu.VMEM((4, tok, 1024), f32),
        pltpu.VMEM((tok, width), f32),
        pltpu.VMEM((tok, width), f32),
    )

    copies = []
    for s in reversed(range(1, n)):
        head = flipped(me, s)
        copies.append(
            remote(
                d_send.at[rows(head), :],
                d_all.at[:, s * tok : s * tok + tok],
                in_send,
                in_recv,
                (scene, head),
            )
        )
        copies[-1].start()
    local = pltpu.make_async_copy(d_send.at[rows(me), :], d_all.at[:, :tok], in_local)
    local.start()

    def pack_copy(j):
        index, device = peer(j)
        return remote(pack.at[index], pack_got.at[mine], last_send.at[0], last_recv.at[0], device)

    def small_copy(j):
        index, device = peer(j)
        return remote(
            small.at[0:4, lanes(index // 4, 128)],
            small_got.at[mine, 0:4, :],
            last_send.at[1],
            last_recv.at[1],
            device,
        )

    def early_copy(j):
        index, device = peer(j)
        return remote(
            early.at[index, 0:5, :],
            early_got.at[mine, 0:5, :],
            last_send.at[2],
            last_recv.at[2],
            device,
        )

    kept = [
        pltpu.make_async_copy(pack.at[mine], pack_got.at[mine], last_local.at[0]),
        pltpu.make_async_copy(
            small.at[0:4, lanes(mine // 4, 128)], small_got.at[mine, 0:4, :], last_local.at[1]
        ),
        pltpu.make_async_copy(
            early.at[mine, 0:5, :], early_got.at[mine, 0:5, :], last_local.at[2]
        ),
    ]
    kept[2].start()

    def early_body(j, carry):
        early_copy(j).start()
        return carry

    lax.fori_loop(1, devices, early_body, 0)
    two_t[...] = two[...].T
    for load in loads[3:8]:
        load.wait()

    def chunk(step):
        @pl.when(step == 0)
        def _():
            narrow_chunk(step + 7, two_t[...], hidden[3 * tok :, :])
            normed_load(0).start()

        @pl.when(step == 1)
        def _():
            narrow_chunk(step + 7, att[...], resid_low[...])
            normed_load(1).start()

        @pl.when(step == 2)
        def _():
            sum1(CHUNKS - 1)

    def normed_load(i):
        return pltpu.make_async_copy(
            normed_ref.at[1024 * i : 1024 * i + 1024, :],
            (act, hidden)[i % 2],
            normed_sem.at[i % 2],
        )

    def q_copy(step, flip):
        slot = 2 * step + flip
        return remote(
            low.at[0, :, lanes(slot)],
            land.at[0, rows(me), :],
            q_send,
            q_recv,
            (scene, flipped(me, slot)),
        )

    def kv_copy(step, flip):
        slot = 2 * step + flip
        return remote(
            low.at[1:3, :, lanes(slot)],
            land.at[1:3, rows(me), :],
            kv_send,
            kv_recv,
            (scene, flipped(me, slot)),
        )

    own = [
        pltpu.make_async_copy(low.at[0, :, :tok], land.at[0, rows(me), :], q_local),
        pltpu.make_async_copy(low.at[1:3, :, :tok], land.at[1:3, rows(me), :], kv_local),
    ]

    weight_loads = [
        pltpu.make_async_copy(
            ref.at[:, :, :, :, 256 * block : 256 * block + 256],
            full.at[a, block // 2, block % 2],
            weight_sem.at[a, block],
        )
        for a, ref in enumerate((wq_ref, wk_ref, wv_ref))
        for block in range(4)
    ]

    def load_weights():
        for c in range(CHUNKS - SLOTS, CHUNKS):
            half(0, c).wait_send()
        for load in weight_loads:
            load.start()

    def attention(q_nat, k_nat, v_nat, d_nat, delta, dq_acc):
        q_nat[...] = q_all[...].T
        k_nat[...] = k_all[...].T
        v_nat[...] = v_all[...].T
        dq_acc[...] = jnp.zeros_like(dq_acc)

        def middle_chunk(i, carry):
            there = pl.ds(pl.multiple_of(i * tok, tok), tok)
            narrow_chunk(4 + i, two_t[...], hidden[there, :])

            @pl.when(i == 1)
            def _():
                tick(3)

            return carry

        lax.fori_loop(0, 3, middle_chunk, 0)
        local.wait()
        pltpu.make_async_copy(d_all.at[:, tok:], d_all.at[:, tok:], in_recv).wait()
        d_nat[...] = d_all[...].T
        delta[...] = jnp.broadcast_to(
            jnp.sum(d_all[...].astype(f32) * o_all[...], axis=0, keepdims=True), delta.shape
        )

        def keys(step, last):
            span = lanes(step, wide)
            k_here, v_here, kt_here = k_nat[span, :], v_nat[span, :], k_all[:, span]
            dk = dv = None
            for i in reversed(range(chips)):
                there = slice(i * wide, (i + 1) * wide)
                scores = contract(k_here, q_all[:, there], 1, 0)
                prob = jnp.exp(scores - lse_all[0:1, there])
                dprob = contract(v_here, d_all[:, there], 1, 0)
                dscore = (prob * (dprob - delta[0:1, there])).astype(bf16)
                v_part = contract(prob.astype(bf16), d_nat[there, :], 1, 0)
                k_part = contract(dscore, q_nat[there, :], 1, 0)
                dk = k_part if dk is None else dk + k_part
                dv = v_part if dv is None else dv + v_part
                dq = dq_acc[:, there] + contract(kt_here, dscore, 1, 0)
                if last:
                    low[0, :, there] = (dq * score_scale).astype(bf16)
                    if i == 0:
                        own[0].start()
                    else:
                        q_copy(i, 0).start()
                    q_copy(i, 1).start()
                else:
                    dq_acc[:, there] = dq
            low[1, :, span] = dk.astype(bf16).T
            low[2, :, span] = dv.astype(bf16).T

        def step_body(step, carry):
            tick(step + 4)
            chunk(step)
            keys(chips - 1 - step, False)

            kv_copy(chips - 1 - step, 0).start()
            kv_copy(chips - 1 - step, 1).start()
            return carry

        lax.fori_loop(0, chips - 1, step_body, 0)
        load_weights()
        tick(11)
        keys(0, True)
        own[1].start()
        kv_copy(0, 1).start()

    pl.run_scoped(
        attention,
        *(pltpu.VMEM((length, HEAD_DIM), bf16) for _ in range(4)),
        pltpu.VMEM((8, length), f32),
        pltpu.VMEM((HEAD_DIM, length), f32),
    )

    head_acc = None
    for i in range(length // 1024):
        normed_load(i).wait()
        left = low[:, :, 1024 * i : 1024 * i + 1024].reshape(3 * HEAD_DIM, 1024)
        part = contract(left, (act, hidden)[i % 2][...], 1, 0)
        head_acc = part if head_acc is None else head_acc + part
        if i + 2 < length // 1024:
            normed_load(i + 2).start()
    by_row = head_acc.T
    share = width // devices
    pack[:, :share, :] = by_row[:, : 2 * HEAD_DIM].astype(bf16).reshape(devices, share, 2 * HEAD_DIM)
    third = by_row[:, 2 * HEAD_DIM :].astype(bf16).reshape(devices, 2, share // 2, HEAD_DIM)
    pack[:, share:, :] = jnp.concatenate([third[:, 0], third[:, 1]], axis=-1)

    kept[0].start()

    def pack_body(j, carry):
        pack_copy(j).start()
        return carry

    lax.fori_loop(1, devices, pack_body, 0)

    for copy in own:
        copy.wait()
    for sem, others in ((q_recv, land.at[0, HEAD_DIM:, :]), (kv_recv, land.at[1:3, HEAD_DIM:, :])):
        pltpu.make_async_copy(others, others, sem).wait()
    for load in weight_loads:
        load.wait()
    def first_norm(back_in):
        for i in range(4):
            part = None
            for a in range(3):
                left = jnp.concatenate(
                    [full[a, b // 2, b % 2, i // 2, i % 2].reshape(256, 256) for b in range(4)],
                    axis=1,
                )
                here = contract(left, land[a], 1, 0)
                part = here if part is None else part + here
            back_in[:, 256 * i : 256 * i + 256] = part.T
        scaled, inverse = normalise(rows_in[...].astype(f32))
        token_part, gain_grad, shift_grad = norm_back(back_in[...], scaled, inverse, gain_one[...])
        tokens_out[...] = (resid[...] + token_part).astype(bf16)
        small[2:3, :] = gain_grad[None]
        small[3:4, :] = shift_grad[None]

    pl.run_scoped(first_norm, pltpu.VMEM((tok, width), f32))
    ones = jnp.ones((8, tok), bf16)
    small[0:1, :] = contract(ones, land[0], 1, 1)[0:1]
    small[1:2, :] = contract(ones, land[2], 1, 1)[0:1]
    kept[1].start()

    def small_body(j, carry):
        small_copy(j).start()
        return carry

    lax.fori_loop(1, devices, small_body, 0)

    tick(12)
    for copy in kept:
        copy.wait()
    for i, src in enumerate(
        (pack.at[1:], small_got.at[1:, 0:4, :], early_got.at[1:, 0:5, :])
    ):
        pltpu.make_async_copy(src, src, last_recv.at[i]).wait()
        pltpu.make_async_copy(src, src, last_send.at[i]).wait()
    for sem, others in (
        (in_send, low.at[0, :, tok:]),
        (q_send, low.at[0, :, tok:]),
        (kv_send, low.at[1:3, :, tok:]),
    ):
        pltpu.make_async_copy(others, others, sem).wait()

    settle()


def tail(n, tok, width, hidden_width, *arrays):
    length = n * tok
    chips = n // 2
    devices = 2 * n
    share = width // devices
    any_spec = pl.BlockSpec(memory_space=pl.ANY)
    vmem = pl.BlockSpec(memory_space=pltpu.VMEM)
    dma = pltpu.SemaphoreType.DMA

    def space(*shape, kind=bf16):
        return pltpu.VMEM(shape, kind)

    def out(*shape, kind=f32):
        return jax.ShapeDtypeStruct(shape, kind)

    pieces = CHUNKS
    scratch = (
        [space(HEAD_DIM, length)] * 4
        + [
            space(width, tok),
            space(HEAD_DIM, length, kind=f32),
            space(8, length, kind=f32),
            space(3, HEAD_DIM, length),
            space(hidden_width // 1024 * tok, 1024),
            space(tok, width),
            space(tok, width),
            space(hidden_width // 1024 * tok, 1024),
            space(width, tok),
            space(tok, width),
            space(hidden_width, tok),
            space(width, tok),
            space(SLOTS, 2, 2, 2, 2, 2, 128, 256),
            space(pieces, 2, 2, 2, 2, 128, 256),
            space(pieces, 2, 2, 2, 64, 256),
            space(pieces, 2, 2, 2, 64, 256),
            space(pieces, 2, 2, 64, 256),
            space(pieces, 2, 2, 64, 256),
            space(pieces, 2, 128, 256),
            space(pieces, 128, 256),
            space(3, width, tok),
            space(tok, width),
            space(tok, width, kind=f32),
            space(1, width, kind=f32),
            space(1, width, kind=f32),
            space(1, width, kind=f32),
            space(1, hidden_width, kind=f32),
            space(1, width, kind=f32),
            space(1, width, kind=f32),
            space(devices, share + share // 2, 128),
            space(8, width, kind=f32),
            space(devices, 8, 128, kind=f32),
            dma((14,)),
            dma((2,)),
            dma((3, 4)),
            dma((2,)),
            dma,
            dma,
            dma,
            dma,
            dma,
            dma,
            dma,
            dma,
            dma,
            dma((pieces + 8,)),
            dma((pieces, 8)),
        ]
        + [dma((3,))] * 3
    )
    return pl.pallas_call(
        functools.partial(tail_kernel, n, tok),
        out_shape=(
            out(tok, width, kind=bf16),
            out(tok, width, kind=bf16),
            out(pieces, 128, 256),
            out(devices, share + share // 2, 128, kind=bf16),
            out(devices, 8, 128),
            out(devices, 8, 128),
        ),
        in_specs=[any_spec] * 21,
        out_specs=[vmem] * 6,
        scratch_shapes=scratch,
        compiler_params=pltpu.CompilerParams(
            collective_id=1, has_side_effects=True, vmem_limit_bytes=63 << 20
        ),
        name="tail",
    )(*arrays)


def finish_kernel(n, *refs):
    block_in, tokens_in, total, pack_got, small_got, early_got = refs[:6]
    block_out, tokens_out, query_out, key_out, value_out, out_out, up_out, down_out = refs[6:14]
    vectors, up_vector = refs[14:22], refs[22]
    block_out[...] = block_in[...]
    tokens_out[...] = tokens_in[...]
    mine = lax.axis_index("scene") * n + lax.axis_index("seq")
    share = query_out.shape[0]
    for head in range(0, n, 2):
        pair = [
            pack_got[head + i].astype(f32) + pack_got[n + head + i].astype(f32) for i in range(2)
        ]
        columns = slice(head * HEAD_DIM, head * HEAD_DIM + 2 * HEAD_DIM)

        def joined(first, last, start):
            return jnp.concatenate(
                [part[first:last, start : start + HEAD_DIM] for part in pair], axis=1
            )

        query_out[:, columns] = joined(0, share, 0)
        key_out[:, columns] = joined(0, share, HEAD_DIM)
        value_out[: share // 2, columns] = joined(share, share + share // 2, 0)
        value_out[share // 2 :, columns] = joined(share, share + share // 2, HEAD_DIM)
    for i in range(4):
        down_out[:, 256 * i : 256 * i + 256] = total[i]
        out_out[:, 256 * i : 256 * i + 256] = total[8, 32 * i : 32 * i + 32, :]
    for i in range(16):
        up_out[:, 256 * i : 256 * i + 256] = total[4 + i // 4, 32 * (i % 4) : 32 * (i % 4) + 32, :]
    turn = lax.rem(128 - 32 * lax.rem(mine, 4), 128)
    late = pltpu.roll(jnp.sum(small_got[...], axis=0), turn, 1)
    early = jnp.sum(early_got[...], axis=0)
    up_vector[...] = early[4]
    early = pltpu.roll(early, turn, 1)
    for i in range(4):
        vectors[i][...] = late[i, :share]
        vectors[4 + i][...] = early[i, :share]


def finish(n, block_rows, tokens_grad, total, pack_got, small_got, early_got):
    tok, width = tokens_grad.shape
    devices = 2 * n
    share = width // devices
    vmem = pl.BlockSpec(memory_space=pltpu.VMEM)

    def out(*shape):
        return jax.ShapeDtypeStruct(shape, f32)

    return pl.pallas_call(
        functools.partial(finish_kernel, n),
        out_shape=(
            jax.ShapeDtypeStruct((tok, width), bf16),
            jax.ShapeDtypeStruct((tok, width), bf16),
            out(share, width),
            out(share, width),
            out(share, width),
            out(share, width),
            out(share, 4 * width),
            out(4 * share, width),
        )
        + (out(share),) * 8
        + (out(4 * share),),
        in_specs=[vmem] * 6,
        out_specs=[vmem] * 17,
        compiler_params=pltpu.CompilerParams(vmem_limit_bytes=60 << 20),
        name="finish",
    )(block_rows, tokens_grad, total, pack_got, small_got, early_got)


def gelu_both(values):
    cubic = gelu_coef * (values + 0.044715 * values * values * values)
    bend = jnp.tanh(cubic)
    slope = gelu_coef * (1.0 + 3.0 * 0.044715 * values * values)
    grad = 0.5 * (1.0 + bend) + 0.5 * values * (1.0 - bend * bend) * slope
    return 0.5 * values * (1.0 + bend), grad


def layer_on_device(
    scenes,
    n,
    tokens,
    surface_mask,
    out_grad,
    w_query,
    w_key,
    w_value,
    w_out,
    w_up,
    w_down,
    b_query,
    b_value,
    b_out,
    b_up,
    b_down,
    gain_one,
    shift_one,
    gain_two,
    shift_two,
):
    _, tok, width = tokens.shape
    att_t, normed_all, q_all, k_all, v_all, o_all, lse_all = attention_forward(
        n, tokens[0], gain_one, shift_one, w_query, w_key, w_value, b_query, b_value
    )

    att_t, out_grad, surface_mask = lax.optimization_barrier((att_t, out_grad, surface_mask))
    masked = out_grad[0] * surface_mask[0].astype(bf16)[:, None]
    arrived = tail(
        n,
        tok,
        width,
        w_up.shape[1],
        q_all,
        k_all,
        v_all,
        o_all,
        lse_all,
        masked,
        att_t,
        normed_all,
        w_down,
        w_up,
        w_out,
        *(w.reshape(2, 2, 2, 128, width) for w in (w_query, w_key, w_value)),
        tokens[0],
        gain_one[None],
        gain_two[None],
        b_down[None],
        b_up[None],
        b_out[None],
        shift_two[None],
    )
    block_out, tokens_grad, *sums = finish(n, *arrived)
    bquery, bvalue, gone, sone, bout, bdown, gtwo, stwo, bup = sums[6:]
    return (
        block_out[None],
        tokens_grad[None],
        *sums[:6],
        bquery,
        bvalue,
        bout,
        bup,
        bdown,
        gone,
        sone,
        gtwo,
        stwo,
    )


def norm_rows(values, gain, shift):
    row_mean = jnp.mean(values, axis=-1, keepdims=True)
    centred = values - row_mean
    row_var = jnp.mean(centred * centred, axis=-1, keepdims=True)
    return centred * lax.rsqrt(row_var + norm_eps) * gain + shift


def gelu_tanh(values):
    return (
        0.5 * values * (1.0 + jnp.tanh(gelu_coef * (values + 0.044715 * values * values * values)))
    )


def take_pair(array_in, pair_index):
    pair_width = 2 * HEAD_DIM
    sliced = lax.dynamic_slice_in_dim(array_in, pair_index * pair_width, pair_width, 2)
    return sliced.reshape(sliced.shape[:2] + (2, HEAD_DIM))


def take_stats(array_in, pair_index):
    return lax.dynamic_slice_in_dim(array_in, pair_index * 2, 2, 1)


def join_pairs(stacked):
    moved = jnp.moveaxis(stacked, 0, 2)
    return moved.reshape(moved.shape[:2] + (moved.shape[2] * moved.shape[3],))


def join_stats(stacked):
    moved = jnp.moveaxis(stacked, 0, 1)
    return moved.reshape((moved.shape[0], moved.shape[1] * moved.shape[2], moved.shape[3]))


def merge_heads(pair_part):
    return pair_part.reshape(pair_part.shape[:2] + (2 * HEAD_DIM,))


def attend(q_scene, k_gathered, v_gathered):

    def attend_pair_step(unused, pair_index):
        q_pair = take_pair(q_scene, pair_index)
        k_pair = take_pair(k_gathered, pair_index)
        v_pair = take_pair(v_gathered, pair_index)
        scores = (
            jnp.einsum("sqhe,skhe->shqk", q_pair, k_pair, preferred_element_type=jnp.float32)
            * score_scale
        )
        row_max = jnp.max(scores, axis=-1, keepdims=True)
        shifted = jnp.exp(scores - row_max)
        row_sum = jnp.sum(shifted, axis=-1, keepdims=True)
        prob_low = (shifted / row_sum).astype(jnp.bfloat16)
        pair_out = jnp.einsum(
            "shqk,skhe->sqhe", prob_low, v_pair, preferred_element_type=jnp.float32
        )
        pair_lse = (row_max + jnp.log(row_sum))[..., 0]
        return (unused, (merge_heads(pair_out), pair_lse))

    pair_count = HEADS // 2
    _, (pair_outs, pair_lses) = lax.scan(
        attend_pair_step, jnp.zeros((), jnp.float32), jnp.arange(pair_count, dtype=jnp.int32)
    )
    return (join_pairs(pair_outs), join_stats(pair_lses))


def query_side(q_scene, k_gathered, v_gathered, row_lse, att_grad):

    def query_pair_step(unused, pair_index):
        q_pair = take_pair(q_scene, pair_index)
        k_pair = take_pair(k_gathered, pair_index)
        v_pair = take_pair(v_gathered, pair_index)
        d_pair = take_pair(att_grad, pair_index)
        l_pair = take_stats(row_lse, pair_index)
        scores = (
            jnp.einsum("sqhe,skhe->shqk", q_pair, k_pair, preferred_element_type=jnp.float32)
            * score_scale
        )
        attn_prob = jnp.exp(scores - l_pair[..., None])
        dprob = jnp.einsum("sqhe,skhe->shqk", d_pair, v_pair, preferred_element_type=jnp.float32)
        row_delta = jnp.sum(attn_prob * dprob, axis=-1)
        dscore = (attn_prob * (dprob - row_delta[..., None])).astype(jnp.bfloat16)
        q_part = (
            jnp.einsum("shqk,skhe->sqhe", dscore, k_pair, preferred_element_type=jnp.float32)
            * score_scale
        )
        results = (merge_heads(q_part), row_delta)
        prob_low = attn_prob.astype(jnp.bfloat16)
        k_part = (
            jnp.einsum("shqk,sqhe->skhe", dscore, q_pair, preferred_element_type=jnp.float32)
            * score_scale
        )
        v_part = jnp.einsum("shqk,sqhe->skhe", prob_low, d_pair, preferred_element_type=jnp.float32)
        results = results + (merge_heads(k_part), merge_heads(v_part))
        return (unused, results)

    pair_count = HEADS // 2
    _, results = lax.scan(
        query_pair_step, jnp.zeros((), jnp.float32), jnp.arange(pair_count, dtype=jnp.int32)
    )
    return results


def on_any_device(
    tokens,
    surface_mask,
    out_grad,
    w_query,
    w_key,
    w_value,
    w_out,
    w_up,
    w_down,
    b_query,
    b_value,
    b_out,
    b_up,
    b_down,
    gain_one,
    shift_one,
    gain_two,
    shift_two,
):
    scenes, local_len, model_width = tokens.shape
    row_count = scenes * local_len
    flat_rows = tokens.astype(jnp.float32).reshape(row_count, model_width)
    normed, norm_one_pull = jax.vjp(norm_rows, flat_rows, gain_one, shift_one)
    normed_low = normed.astype(jnp.bfloat16)
    q_low = (matmul(normed_low, w_query) + b_query).astype(jnp.bfloat16)
    k_low = matmul(normed_low, w_key).astype(jnp.bfloat16)
    v_low = (matmul(normed_low, w_value) + b_value).astype(jnp.bfloat16)
    q_scene = q_low.reshape(scenes, local_len, model_width)
    k_scene = k_low.reshape(scenes, local_len, model_width)
    v_scene = v_low.reshape(scenes, local_len, model_width)
    k_gathered, v_gathered = (
        lax.all_gather(k_scene, "seq", axis=1, tiled=True),
        lax.all_gather(v_scene, "seq", axis=1, tiled=True),
    )
    attended, row_lse = attend(q_scene, k_gathered, v_gathered)
    att_low = attended.reshape(row_count, model_width).astype(jnp.bfloat16)
    residual = flat_rows + matmul(att_low, w_out) + b_out
    normed_two, norm_two_pull = jax.vjp(norm_rows, residual, gain_two, shift_two)
    normed_two_low = normed_two.astype(jnp.bfloat16)
    hidden = matmul(normed_two_low, w_up) + b_up
    activated, gelu_pull = jax.vjp(gelu_tanh, hidden)
    act_low = activated.astype(jnp.bfloat16)
    block_rows = residual + matmul(act_low, w_down) + b_down
    block_out = block_rows.reshape(scenes, local_len, model_width).astype(jnp.bfloat16)
    masked_f = out_grad.astype(jnp.float32) * surface_mask.astype(jnp.float32)[..., None]
    masked_rows = masked_f.reshape(row_count, model_width)
    masked_low = masked_rows.astype(jnp.bfloat16)
    grad_down = matmul_tn(act_low, masked_low)
    grad_bdown = jnp.sum(masked_rows, axis=0)
    act_grad = matmul_nt(masked_low, w_down)
    hidden_low = gelu_pull(act_grad)[0].astype(jnp.bfloat16)
    grad_up = matmul_tn(normed_two_low, hidden_low)
    grad_bup = jnp.sum(hidden_low.astype(jnp.float32), axis=0)
    norm_two_in = matmul_nt(hidden_low, w_up)
    resid_part, grad_gain_two, grad_shift_two = norm_two_pull(norm_two_in)
    resid_grad = masked_rows + resid_part
    resid_low = resid_grad.astype(jnp.bfloat16)
    grad_out = matmul_tn(att_low, resid_low)
    grad_bout = jnp.sum(resid_low.astype(jnp.float32), axis=0)
    att_grad = (
        matmul_nt(resid_low, w_out).astype(jnp.bfloat16).reshape(scenes, local_len, model_width)
    )
    q_parts, delta_parts, k_parts, v_parts = query_side(
        q_scene, k_gathered, v_gathered, row_lse, att_grad
    )
    k_summed, v_summed = (
        lax.psum_scatter(
            k_parts.astype(jnp.bfloat16), "seq", scatter_dimension=2, tiled=True
        ).astype(jnp.float32),
        lax.psum_scatter(
            v_parts.astype(jnp.bfloat16), "seq", scatter_dimension=2, tiled=True
        ).astype(jnp.float32),
    )
    k_grad = join_pairs(k_summed)
    v_grad = join_pairs(v_summed)
    q_grad = join_pairs(q_parts)
    q_grad_low = q_grad.reshape(row_count, model_width).astype(jnp.bfloat16)
    k_grad_low = k_grad.reshape(row_count, model_width).astype(jnp.bfloat16)
    v_grad_low = v_grad.reshape(row_count, model_width).astype(jnp.bfloat16)
    grad_query = matmul_tn(normed_low, q_grad_low)
    grad_key = matmul_tn(normed_low, k_grad_low)
    grad_value = matmul_tn(normed_low, v_grad_low)
    grad_bquery = jnp.sum(q_grad_low.astype(jnp.float32), axis=0)
    grad_bvalue = jnp.sum(v_grad_low.astype(jnp.float32), axis=0)
    norm_one_in = (
        matmul_nt(q_grad_low, w_query)
        + matmul_nt(k_grad_low, w_key)
        + matmul_nt(v_grad_low, w_value)
    )
    token_part, grad_gain_one, grad_shift_one = norm_one_pull(norm_one_in)
    tokens_grad = (
        (resid_grad + token_part).reshape(scenes, local_len, model_width).astype(jnp.bfloat16)
    )
    (
        sum_query,
        sum_key,
        sum_value,
        sum_out,
        sum_bquery,
        sum_bvalue,
        sum_bout,
        sum_gain_one,
        sum_shift_one,
        sum_up,
        sum_down,
        sum_bup,
        sum_bdown,
        sum_gain_two,
        sum_shift_two,
    ) = (
        lax.psum_scatter(grad_query, ("scene", "seq"), scatter_dimension=0, tiled=True),
        lax.psum_scatter(grad_key, ("scene", "seq"), scatter_dimension=0, tiled=True),
        lax.psum_scatter(grad_value, ("scene", "seq"), scatter_dimension=0, tiled=True),
        lax.psum_scatter(grad_out, ("scene", "seq"), scatter_dimension=0, tiled=True),
        lax.psum_scatter(grad_bquery, ("scene", "seq"), scatter_dimension=0, tiled=True),
        lax.psum_scatter(grad_bvalue, ("scene", "seq"), scatter_dimension=0, tiled=True),
        lax.psum_scatter(grad_bout, ("scene", "seq"), scatter_dimension=0, tiled=True),
        lax.psum_scatter(grad_gain_one, ("scene", "seq"), scatter_dimension=0, tiled=True),
        lax.psum_scatter(grad_shift_one, ("scene", "seq"), scatter_dimension=0, tiled=True),
        lax.psum_scatter(grad_up, ("scene", "seq"), scatter_dimension=0, tiled=True),
        lax.psum_scatter(grad_down, ("scene", "seq"), scatter_dimension=0, tiled=True),
        lax.psum_scatter(grad_bup, ("scene", "seq"), scatter_dimension=0, tiled=True),
        lax.psum_scatter(grad_bdown, ("scene", "seq"), scatter_dimension=0, tiled=True),
        lax.psum_scatter(grad_gain_two, ("scene", "seq"), scatter_dimension=0, tiled=True),
        lax.psum_scatter(grad_shift_two, ("scene", "seq"), scatter_dimension=0, tiled=True),
    )
    return (
        block_out,
        tokens_grad,
        sum_query,
        sum_key,
        sum_value,
        sum_out,
        sum_up,
        sum_down,
        sum_bquery,
        sum_bvalue,
        sum_bout,
        sum_bup,
        sum_bdown,
        sum_gain_one,
        sum_shift_one,
        sum_gain_two,
        sum_shift_two,
    )


def solution(mesh):
    placed = (
        P("scene", "seq", None),
        P("scene", "seq"),
        P("scene", "seq", None),
        P(),
        P(),
        P(),
        P(),
        P(),
        P(),
        P(),
        P(),
        P(),
        P(),
        P(),
        P(),
        P(),
        P(),
        P(),
    )
    scenes, n = mesh.shape["scene"], mesh.shape["seq"]
    if (scenes, n) == (2, HEADS):
        on_device = functools.partial(layer_on_device, scenes, n)
    else:
        on_device = on_any_device
    return jax.shard_map(
        on_device,
        mesh=mesh,
        in_specs=placed,
        out_specs=(
            P("scene", "seq", None),
            P("scene", "seq", None),
            P(("scene", "seq"), None),
            P(("scene", "seq"), None),
            P(("scene", "seq"), None),
            P(("scene", "seq"), None),
            P(("scene", "seq"), None),
            P(("scene", "seq"), None),
            P(("scene", "seq")),
            P(("scene", "seq")),
            P(("scene", "seq")),
            P(("scene", "seq")),
            P(("scene", "seq")),
            P(("scene", "seq")),
            P(("scene", "seq")),
            P(("scene", "seq")),
            P(("scene", "seq")),
        ),
        check_vma=False,
    )
```

```python
import functools

import jax
import jax.numpy as jnp
from jax import lax
from jax.experimental import pallas as pl
from jax.experimental.pallas import tpu as pltpu
from jax.sharding import PartitionSpec as P

HEADS = 16
HEAD_DIM = 64
MESH = pl.DeviceIdType.MESH
f32 = jnp.float32
bf16 = jnp.bfloat16

norm_eps = 1e-05
score_scale = 0.125
FORWARD_LIMIT = 60 << 20
gelu_coef = 0.7978845608028654


def matmul(left, right):
    return jnp.dot(left, right, preferred_element_type=jnp.float32)


def contract(left, right, left_dim, right_dim):
    return lax.dot_general(
        left, right, (((left_dim,), (right_dim,)), ((), ())), preferred_element_type=jnp.float32
    )


def matmul_tn(left, right):
    return contract(left, right, 0, 0)


def matmul_nt(left, right):
    return contract(left, right, 1, 1)


def normalise(values):
    row_mean = jnp.mean(values, axis=-1, keepdims=True)
    centred = values - row_mean
    row_var = jnp.mean(centred * centred, axis=-1, keepdims=True)
    inverse = lax.rsqrt(row_var + norm_eps)
    return centred * inverse, inverse


def norm_back(grad, scaled, inverse, gain):
    weighted = grad * gain
    back = inverse * (
        weighted
        - jnp.mean(weighted, axis=-1, keepdims=True)
        - scaled * jnp.mean(weighted * scaled, axis=-1, keepdims=True)
    )
    return back, jnp.sum(grad * scaled, axis=0), jnp.sum(grad, axis=0)


def greet(partners):
    barrier = pltpu.get_barrier_semaphore()
    for partner in partners:
        pl.semaphore_signal(barrier, inc=1, device_id=partner, device_id_type=MESH)
    return lambda: pl.semaphore_wait(barrier, len(partners))


def remote(src, dst, send_sem, recv_sem, device):
    return pltpu.make_async_remote_copy(
        src_ref=src,
        dst_ref=dst,
        send_sem=send_sem,
        recv_sem=recv_sem,
        device_id=device,
        device_id_type=MESH,
    )


def flipped(index, other):
    out = 0
    for weight in (1, 2, 4, 8):
        bit, turn = lax.rem(index // weight, 2), lax.rem(other // weight, 2)
        out = out + weight * (bit + turn - 2 * bit * turn)
    return out


def forward_kernel(n, tok, *refs):
    (
        tokens_ref,
        gain_ref,
        shift_ref,
        wq_ref,
        wk_ref,
        wv_ref,
        bq_ref,
        bv_ref,
        att_ref,
        normed_out,
        q_out,
        k_out,
        v_out,
        o_out,
        lse_out,
        rows_in,
        gain,
        shift,
        b_query,
        b_value,
        land,
        w_pair,
        w_head,
        bias,
        q_all,
        k_all,
        v_all,
        k_nat,
        o_all,
        lse_all,
        stats,
        att_send,
        load_sem,
        gather_send,
        gather_recv,
        save_sem,
        out_send,
        out_recv,
        out_local,
        last_sem,
    ) = refs
    me = lax.axis_index("seq")
    scene = lax.axis_index("scene")
    core = lax.rem(me, 2)
    chips = n // 2
    wide = 2 * tok
    half_rows = tok // 2
    devices = [flipped(me, s) for s in range(n)]

    def rows(head):
        return pl.ds(pl.multiple_of(head * HEAD_DIM, HEAD_DIM), HEAD_DIM)

    def lanes(block, width=tok):
        return pl.ds(pl.multiple_of(block * width, width), width)

    tokens_load = pltpu.make_async_copy(tokens_ref, rows_in, load_sem.at[0])
    tokens_load.start()
    weight_loads = [
        pltpu.make_async_copy(ref.at[:, lanes(me // 2, 128)], w_pair.at[i], load_sem.at[1 + i])
        for i, ref in enumerate((wk_ref, wq_ref, wv_ref))
    ]
    vector_loads = [
        pltpu.make_async_copy(src, dst, load_sem.at[4 + i])
        for i, (src, dst) in enumerate(
            ((gain_ref, gain), (shift_ref, shift), (bq_ref, b_query), (bv_ref, b_value))
        )
    ]
    for load in vector_loads + weight_loads:
        load.start()
    all_here = greet([(scene, devices[s]) for s in range(1, n)])

    def gather_copy(slot, over, part):
        piece = slice(part * half_rows, (part + 1) * half_rows)
        there = slot ^ over
        return remote(
            land.at[slot, piece, :],
            land.at[there, piece, :],
            gather_send.at[there, part],
            gather_recv.at[there, part],
            (scene, devices[over]),
        )

    routes = {0: (4, 2, 8, 1), 8: (4, 2, 1), 4: (2, 1), 12: (2, 1), 2: (1,), 6: (1,), 10: (1,), 14: (1,)}

    def routes_of(slot, part):
        if part == 1 and slot == 12:
            return (1,)
        if part == 1 and slot == 10:
            return (4, 1)
        return routes.get(slot, ())

    def came_over(slot, part):
        for source in range(n):
            for over in routes_of(source, part):
                if source ^ over == slot:
                    return over

    sent = []
    saves = []

    def forward(slot, part):
        for over in routes_of(slot, part):
            copy = gather_copy(slot, over, part)
            copy.start()
            sent.append(copy)

    def arrive(slot, part):
        over = came_over(slot, part)
        gather_copy(slot ^ over, over, part).wait_recv()
        forward(slot, part)

    for load in [tokens_load] + vector_loads:
        load.wait()
    for part in range(2):
        piece = slice(part * half_rows, (part + 1) * half_rows)
        scaled, _ = normalise(rows_in[piece, :].astype(f32))
        land[0, piece, :] = (scaled * gain[...] + shift[...]).astype(bf16)
        if part == 0:
            all_here()
        forward(0, part)

    odd = core == 1
    for i, load in enumerate(weight_loads):
        load.wait()
        pair = w_pair[i].astype(f32)
        w_head[:, HEAD_DIM * i : HEAD_DIM * i + HEAD_DIM] = jnp.where(
            odd, pair[:, HEAD_DIM:], pair[:, :HEAD_DIM]
        ).astype(bf16)
    for i, ref in ((1, b_query), (2, b_value)):
        pair = ref[0:1, lanes(me // 2, 128)]
        bias[0:1, HEAD_DIM * i : HEAD_DIM * i + HEAD_DIM] = jnp.where(
            odd, pair[:, HEAD_DIM:], pair[:, :HEAD_DIM]
        )
    bias[0:1, :HEAD_DIM] = jnp.zeros((1, HEAD_DIM), f32)

    def project(slot):
        made = contract(land[slot], w_head[...], 1, 0) + bias[0:1, :]
        low = made.astype(bf16)
        turned = low.T
        span = slice(slot * tok, (slot + 1) * tok)
        k_nat[span, :] = low[:, :HEAD_DIM]
        k_all[:, span] = turned[:HEAD_DIM]
        q_all[:, span] = turned[HEAD_DIM : 2 * HEAD_DIM] * jnp.asarray(score_scale, bf16)
        v_all[:, span] = turned[2 * HEAD_DIM :]
        save = pltpu.make_async_copy(land.at[slot], normed_out.at[span, :], save_sem.at[slot])
        save.start()
        saves.append(save)

    def attend(span, first, state):
        top, total, acc = state
        keys = slice(first, first + chips // 2 * wide)
        scores = contract(k_nat[keys, :], q_all[:, span], 1, 0)
        here = jnp.max(scores, axis=0, keepdims=True)
        new_top = here if top is None else jnp.maximum(top, here)
        shifted = jnp.exp(scores - new_top)
        part_sum = jnp.sum(shifted, axis=0, keepdims=True)
        part = contract(v_all[:, keys], shifted.astype(bf16), 1, 0)
        if top is None:
            return new_top, part_sum, part
        fade = jnp.exp(top - new_top)
        return new_top, total * fade + part_sum, acc * fade + part

    middle = chips // 2 * wide

    def early(i):
        span = slice(i * wide, (i + 1) * wide)
        top, total, acc = attend(span, 0, (None, None, None))
        stats[0:1, span] = top
        stats[1:2, span] = total
        o_all[:, span] = acc

    def close(i, span, state):
        top, total, acc = state
        out = acc / total
        o_all[:, span] = out
        lse_all[:, span] = jnp.broadcast_to(top + jnp.log(total), (8, wide))
        low = out.astype(bf16)
        att_send[i, 0] = low[:, :tok]
        att_send[i, 1] = low[:, tok:]

    def out_copy(i, flip):
        return remote(
            att_send.at[i, flip],
            att_ref.at[rows(me), :],
            out_send.at[i, flip],
            out_recv.at[i, flip],
            (scene, flipped(me, 2 * i + flip)),
        )

    project(0)
    for part in range(2):
        arrive(1, part)
    project(1)
    for part in range(2):
        arrive(2, part)
        arrive(4, part)
    project(2)
    for slot in (3, 5):
        for part in range(2):
            arrive(slot, part)
    project(3)
    project(4)
    project(5)
    for part in range(2):
        arrive(8, part)
    for slot in (6, 7):
        for part in range(2):
            arrive(slot, part)
    project(6)
    project(7)
    early(0)
    early(1)
    arrive(9, 0)
    arrive(9, 1)
    project(8)
    project(9)
    for part in range(2):
        arrive(12, part)
        arrive(10, part)
    early(2)
    for slot in (11, 13):
        for part in range(2):
            arrive(slot, part)
    project(10)
    project(11)
    early(3)
    project(12)
    project(13)
    arrive(14, 0)
    arrive(14, 1)
    project(14)
    arrive(15, 0)
    arrive(15, 1)
    project(15)
    for i, (src, dst) in enumerate(((q_all, q_out), (k_all, k_out), (v_all, v_out))):
        save = pltpu.make_async_copy(src, dst, last_sem.at[i])
        save.start()
        saves.append(save)

    def late_body(j, carry):
        i = chips - 1 - j
        span = lanes(i, wide)
        close(i, span, attend(span, middle, attend(span, 0, (None, None, None))))
        out_copy(i, 0).start()
        out_copy(i, 1).start()
        return carry

    lax.fori_loop(0, chips // 2, late_body, 0)

    def rest(i, span):
        state = (stats[0:1, span], stats[1:2, span], o_all[:, span])
        close(i, span, attend(span, middle, state))

    def rest_body(j, carry):
        i = chips // 2 - 1 - j
        rest(i, lanes(i, wide))
        out_copy(i, 0).start()
        out_copy(i, 1).start()
        return carry

    lax.fori_loop(0, chips // 2 - 1, rest_body, 0)
    rest(0, slice(0, wide))
    mine = pltpu.make_async_copy(att_send.at[0, 0], att_ref.at[rows(me), :], out_local)
    mine.start()
    out_copy(0, 1).start()
    for i, (src, dst) in enumerate(((o_all, o_out), (lse_all, lse_out))):
        save = pltpu.make_async_copy(src, dst, last_sem.at[3 + i])
        save.start()
        saves.append(save)
    for copy in sent:
        copy.wait_send()
    mine.wait()
    out_copy(0, 1).wait()

    def drain(i, carry):
        out_copy(i, 0).wait()
        out_copy(i, 1).wait()
        return carry

    lax.fori_loop(1, chips, drain, 0)
    for save in saves:
        save.wait()


def attention_forward(n, tokens, gain, shift, w_query, w_key, w_value, b_query, b_value):
    tok, width = tokens.shape
    length = n * tok
    any_spec = pl.BlockSpec(memory_space=pl.ANY)
    head_all = jax.ShapeDtypeStruct((HEAD_DIM, length), bf16)
    dma = pltpu.SemaphoreType.DMA
    return pl.pallas_call(
        functools.partial(forward_kernel, n, tok),
        out_shape=(
            jax.ShapeDtypeStruct((width, tok), bf16),
            jax.ShapeDtypeStruct((length, width), bf16),
            head_all,
            head_all,
            head_all,
            jax.ShapeDtypeStruct((HEAD_DIM, length), f32),
            jax.ShapeDtypeStruct((8, length), f32),
        ),
        in_specs=[any_spec] * 8,
        out_specs=[any_spec] * 7,
        scratch_shapes=[
            pltpu.VMEM((tok, width), bf16),
            pltpu.VMEM((1, width), f32),
            pltpu.VMEM((1, width), f32),
            pltpu.VMEM((1, width), f32),
            pltpu.VMEM((1, width), f32),
            pltpu.VMEM((n, tok, width), bf16),
            pltpu.VMEM((3, width, 2 * HEAD_DIM), bf16),
            pltpu.VMEM((width, 3 * HEAD_DIM), bf16),
            pltpu.VMEM((8, 3 * HEAD_DIM), f32),
            pltpu.VMEM((HEAD_DIM, length), bf16),
            pltpu.VMEM((HEAD_DIM, length), bf16),
            pltpu.VMEM((HEAD_DIM, length), bf16),
            pltpu.VMEM((length, HEAD_DIM), bf16),
            pltpu.VMEM((HEAD_DIM, length), f32),
            pltpu.VMEM((8, length), f32),
            pltpu.VMEM((8, length), f32),
            pltpu.VMEM((n // 2, 2, HEAD_DIM, tok), bf16),
            dma((8,)),
            dma((n, 2)),
            dma((n, 2)),
            dma((n,)),
            dma((n // 2, 2)),
            dma((n // 2, 2)),
            dma,
            dma((5,)),
        ],
        compiler_params=pltpu.CompilerParams(
            collective_id=0, has_side_effects=True, vmem_limit_bytes=FORWARD_LIMIT
        ),
        name="attention_forward",
    )(
        tokens,
        gain[None],
        shift[None],
        w_query,
        w_key,
        w_value,
        b_query[None],
        b_value[None],
    )


CHUNKS = 9
TICKS = CHUNKS + 4
SLOTS = 3


def halving_plan(full, got0, got1a, got1b, got2a, got2b, got3, got4, total, send_sem, recv_sem):
    me = lax.axis_index("seq")
    x = lax.axis_index("scene")
    core = lax.rem(me, 2)
    y = lax.rem(me // 2, 2)
    z0 = lax.rem(me // 4, 2)
    z1 = me // 8
    at_core = (x, me + 1 - 2 * core)
    at_x = (1 - x, me)
    at_y = (x, me + 2 - 4 * y)
    at_z0 = (x, me + 4 - 8 * z0)
    at_z1 = (x, me + 8 - 16 * z1)
    up, low = slice(0, 64), slice(64, 128)

    def copy_of(slot, c):
        src, dst, device = (
            lambda: (full.at[lax.rem(c, SLOTS), :, :, :, :, 1 - core], got0.at[c], at_core),
            lambda: (got0.at[c, 1 - x, :, :, :, up, :], got1a.at[c], at_x),
            lambda: (got0.at[c, :, :, :, 1 - y, low, :], got1b.at[c], at_y),
            lambda: (got1a.at[c, :, 1 - z0], got2a.at[c], at_z0),
            lambda: (got1b.at[c, 1 - x], got2b.at[c], at_x),
            lambda: (got2a.at[c, :, 1 - y], got3.at[c, :, up, :], at_y),
            lambda: (got2b.at[c, :, 1 - z0], got3.at[c, :, low, :], at_z0),
            lambda: (got3.at[c, 1 - z1], got4.at[c], at_z1),
        )[slot]()
        going = send_sem.at[c] if slot == 0 else send_sem.at[CHUNKS + slot]
        return remote(src, dst, going, recv_sem.at[c, slot], device)

    def sum1(c):
        copy_of(0, c).wait_recv()
        got0[c] = got0[c] + full[lax.rem(c, SLOTS), :, :, :, :, core]

    def start1(c):
        copy_of(1, c).start()
        copy_of(2, c).start()

    def stage2(c):
        copy_of(1, c).wait_recv()
        got1a[c] = got1a[c] + got0[c, x, :, :, :, up, :]
        copy_of(3, c).start()
        copy_of(2, c).wait_recv()
        got1b[c] = got1b[c] + got0[c, :, :, :, y, low, :]
        copy_of(4, c).start()

    def stage3(c):
        copy_of(3, c).wait_recv()
        got2a[c] = got2a[c] + got1a[c, :, z0]
        copy_of(5, c).start()
        copy_of(4, c).wait_recv()
        got2b[c] = got2b[c] + got1b[c, x]
        copy_of(6, c).start()

    def stage4(c):
        copy_of(5, c).wait_recv()
        got3[c, :, up, :] = got3[c, :, up, :] + got2a[c, :, y]
        copy_of(6, c).wait_recv()
        got3[c, :, low, :] = got3[c, :, low, :] + got2b[c, :, z0]
        copy_of(7, c).start()

    def stage5(c):
        copy_of(7, c).wait_recv()
        total[c] = got3[c, z1].astype(f32) + got4[c].astype(f32)

    def tick(when):
        for stage, c in (
            (stage5, when - 4),
            (stage4, when - 3),
            (stage3, when - 2),
            (stage2, when - 1),
            (start1, when + 1),
        ):

            @pl.when((c >= 0) & (c < CHUNKS))
            def _(stage=stage, c=c):
                stage(c)

    def settle():
        for slot, src in enumerate((got1a, got1a, got1b, got2a, got2b, got3, got3, got4)):
            if slot:
                everything = src.at[:, :, up, :] if slot in (5, 6) else src
                pltpu.make_async_copy(everything, everything, send_sem.at[CHUNKS + slot]).wait()

    return copy_of, sum1, start1, tick, settle


def tail_kernel(n, tok, *refs):
    (
        q_ref,
        k_ref,
        v_ref,
        o_ref,
        lse_ref,
        masked_ref,
        att_ref,
        normed_ref,
        wd_ref,
        wu_ref,
        wo_ref,
        wq_ref,
        wk_ref,
        wv_ref,
        tokens_ref,
        gain_ref,
        gain_two_ref,
        b_down_ref,
        b_up_ref,
        b_out_ref,
        shift_two_ref,
        mask_ref,
        block_out,
        tokens_out,
        total,
        pack_got,
        small_got,
        early_got,
        q_all,
        k_all,
        v_all,
        d_all,
        d_send,
        o_all,
        lse_all,
        low,
        act,
        masked,
        two,
        hidden,
        att,
        resid_low,
        act_t,
        two_t,
        full,
        got0,
        got1a,
        got1b,
        got2a,
        got2b,
        got3,
        got4,
        land,
        rows_in,
        resid,
        gain_one,
        gain_two,
        b_down,
        b_up,
        b_out,
        shift_two,
        mask,
        pack,
        small,
        early,
        load_sem,
        ring_sem,
        weight_sem,
        normed_sem,
        in_send,
        in_recv,
        in_local,
        kv_send,
        kv_recv,
        kv_local,
        q_send,
        q_recv,
        q_local,
        half_send,
        half_recv,
        last_send,
        last_recv,
        last_local,
    ) = refs
    me = lax.axis_index("seq")
    scene = lax.axis_index("scene")
    chips = n // 2
    length = n * tok
    wide = 2 * tok
    devices = 2 * n
    width = masked.shape[1]
    mine = scene * n + me

    def rows(head):
        return pl.ds(pl.multiple_of(head * HEAD_DIM, HEAD_DIM), HEAD_DIM)

    def lanes(block, width=tok):
        return pl.ds(pl.multiple_of(block * width, width), width)

    loads = [
        pltpu.make_async_copy(src, dst, load_sem.at[i])
        for i, (src, dst) in enumerate(
            (
                (att_ref, att),
                (b_up_ref, b_up),
                (masked_ref, masked),
                (q_ref, q_all),
                (k_ref, k_all),
                (v_ref, v_all),
                (o_ref, o_all),
                (lse_ref, lse_all),
                (b_out_ref, b_out),
                (shift_two_ref, shift_two),
                (tokens_ref, rows_in),
                (gain_ref, gain_one),
                (gain_two_ref, gain_two),
                (b_down_ref, b_down),
                (mask_ref, mask),
            )
        )
    ]
    for load in loads:
        load.start()

    def peer(j):
        index = lax.rem(mine + j, devices)
        return index, (index // n, lax.rem(index, n))

    all_here = greet([peer(j)[1] for j in range(1, devices)])

    half, sum1, start1, tick, settle = halving_plan(
        full, got0, got1a, got1b, got2a, got2b, got3, got4, total, half_send, half_recv
    )

    def chunk_begin(c):
        @pl.when(c >= SLOTS)
        def _():
            half(0, c - SLOTS).wait_send()

        return lax.rem(c, SLOTS)

    def chunk_end(c):
        half(0, c).start()

        @pl.when((c >= 1) & (c != 4))
        def _():
            sum1(c - 1)

    def down_chunk(c):
        slot = chunk_begin(c)
        columns = masked[:, lanes(c, 256)]
        for block in range(4):
            part = contract(act_t[1024 * block : 1024 * block + 1024, :], columns, 1, 0)
            full[slot, block // 2, block % 2] = part.astype(bf16).reshape(2, 2, 2, 128, 256)
        chunk_end(c)

    def narrow_chunk(c, left, right):
        slot = chunk_begin(c)
        for block in range(4):
            part = contract(left, right[:, 256 * block : 256 * block + 256], 1, 0)
            full[slot, :, :, :, :, :, 32 * block : 32 * block + 32, :] = part.astype(bf16).reshape(
                2, 2, 2, 2, 2, 32, 256
            )
        chunk_end(c)

    def first_chunk(c, carry):
        down_chunk(c)

        @pl.when((c >= 1) & (c <= 2))
        def _():
            start1(c - 1)

        return carry

    def feed_forward(ring, slope, out_acc, two_acc):
        def weight_load(i):
            if i in (-1, 12):
                src = wo_ref
            elif 4 <= i < 8:
                src = wd_ref.at[1024 * (i - 4) : 1024 * (i - 4) + 1024, :]
            else:
                src = wu_ref.at[:, 1024 * (i % 4) : 1024 * (i % 4) + 1024]
            return pltpu.make_async_copy(src, ring.at[i % 2], ring_sem.at[i % 2])

        for i in (-1, 0):
            weight_load(i).start()
        for i in (0, 1, *range(8, 14)):
            loads[i].wait()
        turned = att[...].T
        weight_load(-1).wait()
        resid[...] = rows_in[...].astype(f32) + contract(turned, ring[1], 1, 0) + b_out[...]
        weight_load(1).start()
        scaled, _ = normalise(resid[...])
        two[...] = (scaled * gain_two[...] + shift_two[...]).astype(bf16)
        for i in range(4):
            weight_load(i).wait()
            grown = contract(two[...], ring[i % 2], 1, 0) + b_up[:, 1024 * i : 1024 * i + 1024]
            weight_load(i + 2).start()
            value, slope[i] = gelu_both(grown)
            value = value.astype(bf16)
            act[tok * i : tok * i + tok, :] = value
            act_t[1024 * i : 1024 * i + 1024, :] = value.T
        loads[2].wait()
        loads[14].wait()
        column = jnp.broadcast_to(mask[...].astype(f32), (128, tok)).T[:, 0:1]
        masked[...] = (masked[...].astype(f32) * column).astype(bf16)
        all_here()
        lax.fori_loop(0, 4, first_chunk, 0)
        masked_sum = jnp.sum(masked[...].astype(f32), axis=0, keepdims=True)
        for i in range(4):
            weight_load(4 + i).wait()
            there = slice(tok * i, tok * i + tok)
            part = contract(act[there, :], ring[i % 2], 1, 0)
            out_acc[...] = resid[...] + b_down[...] + part if i == 0 else out_acc[...] + part
            grown = contract(masked[...], ring[i % 2], 1, 1) * slope[i]
            weight_load(6 + i).start()
            grown = grown.astype(bf16)
            hidden[there, :] = grown
            sums = jnp.sum(grown.astype(f32), axis=0, keepdims=True)
            for j in range(8):
                early[8 * i + j, 4:5, :] = sums[:, 128 * j : 128 * j + 128]
            if i == 1:
                tick(1)
        block_out[...] = out_acc[...].astype(bf16)
        sum1(3)
        for i in range(4):
            weight_load(8 + i).wait()
            part = contract(hidden[tok * i : tok * i + tok, :], ring[i % 2], 1, 1)
            two_acc[...] = part if i == 0 else two_acc[...] + part
            if i < 3:
                weight_load(10 + i).start()
            if i == 1:
                tick(2)
        scaled, inverse = normalise(resid[...])
        part, gain_grad, shift_grad = norm_back(two_acc[...], scaled, inverse, gain_two[...])
        resid[...] = masked[...].astype(f32) + part
        resid_low[...] = resid[...].astype(bf16)
        low_sum = jnp.sum(resid_low[...].astype(f32), axis=0, keepdims=True)
        for row, vector in enumerate((low_sum, masked_sum, gain_grad[None], shift_grad[None])):
            for d in range(devices):
                start = 128 * (d // 4)
                early[d, row : row + 1, :] = vector[:, start : start + 128]
        weight_load(12).wait()
        d_send[...] = contract(ring[0], resid_low[...], 1, 1).astype(bf16)

    pl.run_scoped(
        feed_forward,
        pltpu.VMEM((2, 1024, 1024), bf16),
        pltpu.VMEM((4, tok, 1024), f32),
        pltpu.VMEM((tok, width), f32),
        pltpu.VMEM((tok, width), f32),
    )

    copies = []
    for s in reversed(range(1, n)):
        head = flipped(me, s)
        copies.append(
            remote(
                d_send.at[rows(head), :],
                d_all.at[:, s * tok : s * tok + tok],
                in_send,
                in_recv,
                (scene, head),
            )
        )
        copies[-1].start()
    local = pltpu.make_async_copy(d_send.at[rows(me), :], d_all.at[:, :tok], in_local)
    local.start()

    def pack_copy(j):
        index, device = peer(j)
        return remote(pack.at[index], pack_got.at[mine], last_send.at[0], last_recv.at[0], device)

    def small_copy(j):
        index, device = peer(j)
        return remote(
            small.at[0:4, lanes(index // 4, 128)],
            small_got.at[mine, 0:4, :],
            last_send.at[1],
            last_recv.at[1],
            device,
        )

    def early_copy(j):
        index, device = peer(j)
        return remote(
            early.at[index, 0:5, :],
            early_got.at[mine, 0:5, :],
            last_send.at[2],
            last_recv.at[2],
            device,
        )

    kept = [
        pltpu.make_async_copy(pack.at[mine], pack_got.at[mine], last_local.at[0]),
        pltpu.make_async_copy(
            small.at[0:4, lanes(mine // 4, 128)], small_got.at[mine, 0:4, :], last_local.at[1]
        ),
        pltpu.make_async_copy(
            early.at[mine, 0:5, :], early_got.at[mine, 0:5, :], last_local.at[2]
        ),
    ]
    kept[2].start()

    def early_body(j, carry):
        early_copy(j).start()
        return carry

    lax.fori_loop(1, devices, early_body, 0)
    two_t[...] = two[...].T
    for load in loads[3:8]:
        load.wait()

    def chunk(step):
        @pl.when(step == 0)
        def _():
            narrow_chunk(step + 7, two_t[...], hidden[3 * tok :, :])
            normed_load(0).start()

        @pl.when(step == 1)
        def _():
            narrow_chunk(step + 7, att[...], resid_low[...])
            normed_load(1).start()

        @pl.when(step == 2)
        def _():
            sum1(CHUNKS - 1)

    def normed_load(i):
        return pltpu.make_async_copy(
            normed_ref.at[1024 * i : 1024 * i + 1024, :],
            (act, hidden)[i % 2],
            normed_sem.at[i % 2],
        )

    def q_copy(step, flip):
        slot = 2 * step + flip
        return remote(
            low.at[0, :, lanes(slot)],
            land.at[0, rows(me), :],
            q_send,
            q_recv,
            (scene, flipped(me, slot)),
        )

    def kv_copy(step, flip):
        slot = 2 * step + flip
        return remote(
            low.at[1:3, :, lanes(slot)],
            land.at[1:3, rows(me), :],
            kv_send,
            kv_recv,
            (scene, flipped(me, slot)),
        )

    own = [
        pltpu.make_async_copy(low.at[0, :, :tok], land.at[0, rows(me), :], q_local),
        pltpu.make_async_copy(low.at[1:3, :, :tok], land.at[1:3, rows(me), :], kv_local),
    ]

    weight_loads = [
        pltpu.make_async_copy(
            ref.at[:, :, :, :, 256 * block : 256 * block + 256],
            full.at[a, block // 2, block % 2],
            weight_sem.at[a, block],
        )
        for a, ref in enumerate((wq_ref, wk_ref, wv_ref))
        for block in range(4)
    ]

    def load_weights():
        for c in range(CHUNKS - SLOTS, CHUNKS):
            half(0, c).wait_send()
        for load in weight_loads:
            load.start()

    def attention(q_nat, k_nat, v_nat, d_nat, delta, dq_acc):
        q_nat[...] = q_all[...].T
        k_nat[...] = k_all[...].T
        v_nat[...] = v_all[...].T
        dq_acc[...] = jnp.zeros_like(dq_acc)

        def middle_chunk(i, carry):
            there = pl.ds(pl.multiple_of(i * tok, tok), tok)
            narrow_chunk(4 + i, two_t[...], hidden[there, :])

            @pl.when(i == 1)
            def _():
                tick(3)

            return carry

        lax.fori_loop(0, 3, middle_chunk, 0)
        local.wait()
        pltpu.make_async_copy(d_all.at[:, tok:], d_all.at[:, tok:], in_recv).wait()
        d_nat[...] = d_all[...].T
        delta[...] = jnp.broadcast_to(
            jnp.sum(d_all[...].astype(f32) * o_all[...], axis=0, keepdims=True), delta.shape
        )

        def keys(step, last):
            span = lanes(step, wide)
            k_here, v_here, kt_here = k_nat[span, :], v_nat[span, :], k_all[:, span]
            dk = dv = None
            for i in reversed(range(chips)):
                if not last and i == 5:
                    tick(chips - 1 - step + 4)
                there = slice(i * wide, (i + 1) * wide)
                scores = contract(k_here, q_all[:, there], 1, 0)
                prob = jnp.exp(scores - lse_all[0:1, there])
                dprob = contract(v_here, d_all[:, there], 1, 0)
                dscore = (prob * (dprob - delta[0:1, there])).astype(bf16)
                v_part = contract(prob.astype(bf16), d_nat[there, :], 1, 0)
                k_part = contract(dscore, q_nat[there, :], 1, 0)
                dk = k_part if dk is None else dk + k_part
                dv = v_part if dv is None else dv + v_part
                dq = dq_acc[:, there] + contract(kt_here, dscore, 1, 0)
                if last:
                    low[0, :, there] = (dq * score_scale).astype(bf16)
                    if i == 0:
                        own[0].start()
                    else:
                        q_copy(i, 0).start()
                    q_copy(i, 1).start()
                else:
                    dq_acc[:, there] = dq
            low[1, :, span] = dk.astype(bf16).T
            low[2, :, span] = dv.astype(bf16).T

        def step_body(step, carry):
            chunk(step)
            keys(chips - 1 - step, False)

            kv_copy(chips - 1 - step, 0).start()
            kv_copy(chips - 1 - step, 1).start()
            return carry

        lax.fori_loop(0, chips - 1, step_body, 0)
        load_weights()
        tick(11)
        keys(0, True)
        own[1].start()
        kv_copy(0, 1).start()

    pl.run_scoped(
        attention,
        *(pltpu.VMEM((length, HEAD_DIM), bf16) for _ in range(4)),
        pltpu.VMEM((8, length), f32),
        pltpu.VMEM((HEAD_DIM, length), f32),
    )

    head_acc = None
    for i in range(length // 1024):
        normed_load(i).wait()
        left = low[:, :, 1024 * i : 1024 * i + 1024].reshape(3 * HEAD_DIM, 1024)
        part = contract(left, (act, hidden)[i % 2][...], 1, 0)
        head_acc = part if head_acc is None else head_acc + part
        if i + 2 < length // 1024:
            normed_load(i + 2).start()
    by_row = head_acc.T
    share = width // devices
    pack[:, :share, :] = by_row[:, : 2 * HEAD_DIM].astype(bf16).reshape(devices, share, 2 * HEAD_DIM)
    third = by_row[:, 2 * HEAD_DIM :].astype(bf16).reshape(devices, 2, share // 2, HEAD_DIM)
    pack[:, share:, :] = jnp.concatenate([third[:, 0], third[:, 1]], axis=-1)

    kept[0].start()

    def pack_body(j, carry):
        pack_copy(j).start()
        return carry

    lax.fori_loop(1, devices, pack_body, 0)

    for copy in own:
        copy.wait()
    for sem, others in ((q_recv, land.at[0, HEAD_DIM:, :]), (kv_recv, land.at[1:3, HEAD_DIM:, :])):
        pltpu.make_async_copy(others, others, sem).wait()
    for load in weight_loads:
        load.wait()
    def first_norm(back_in):
        for i in range(4):
            part = None
            for a in range(3):
                left = jnp.concatenate(
                    [full[a, b // 2, b % 2, i // 2, i % 2].reshape(256, 256) for b in range(4)],
                    axis=1,
                )
                here = contract(left, land[a], 1, 0)
                part = here if part is None else part + here
            back_in[:, 256 * i : 256 * i + 256] = part.T
        scaled, inverse = normalise(rows_in[...].astype(f32))
        token_part, gain_grad, shift_grad = norm_back(back_in[...], scaled, inverse, gain_one[...])
        tokens_out[...] = (resid[...] + token_part).astype(bf16)
        small[2:3, :] = gain_grad[None]
        small[3:4, :] = shift_grad[None]

    pl.run_scoped(first_norm, pltpu.VMEM((tok, width), f32))
    ones = jnp.ones((8, tok), bf16)
    small[0:1, :] = contract(ones, land[0], 1, 1)[0:1]
    small[1:2, :] = contract(ones, land[2], 1, 1)[0:1]
    kept[1].start()

    def small_body(j, carry):
        small_copy(j).start()
        return carry

    lax.fori_loop(1, devices, small_body, 0)

    tick(12)
    for copy in kept:
        copy.wait()
    for i, src in enumerate(
        (pack.at[1:], small_got.at[1:, 0:4, :], early_got.at[1:, 0:5, :])
    ):
        pltpu.make_async_copy(src, src, last_recv.at[i]).wait()
        pltpu.make_async_copy(src, src, last_send.at[i]).wait()
    for sem, others in (
        (in_send, low.at[0, :, tok:]),
        (q_send, low.at[0, :, tok:]),
        (kv_send, low.at[1:3, :, tok:]),
    ):
        pltpu.make_async_copy(others, others, sem).wait()

    settle()


def tail(n, tok, width, hidden_width, *arrays):
    length = n * tok
    chips = n // 2
    devices = 2 * n
    share = width // devices
    any_spec = pl.BlockSpec(memory_space=pl.ANY)
    vmem = pl.BlockSpec(memory_space=pltpu.VMEM)
    dma = pltpu.SemaphoreType.DMA

    def space(*shape, kind=bf16):
        return pltpu.VMEM(shape, kind)

    def out(*shape, kind=f32):
        return jax.ShapeDtypeStruct(shape, kind)

    pieces = CHUNKS
    scratch = (
        [space(HEAD_DIM, length)] * 4
        + [
            space(width, tok),
            space(HEAD_DIM, length, kind=f32),
            space(8, length, kind=f32),
            space(3, HEAD_DIM, length),
            space(hidden_width // 1024 * tok, 1024),
            space(tok, width),
            space(tok, width),
            space(hidden_width // 1024 * tok, 1024),
            space(width, tok),
            space(tok, width),
            space(hidden_width, tok),
            space(width, tok),
            space(SLOTS, 2, 2, 2, 2, 2, 128, 256),
            space(pieces, 2, 2, 2, 2, 128, 256),
            space(pieces, 2, 2, 2, 64, 256),
            space(pieces, 2, 2, 2, 64, 256),
            space(pieces, 2, 2, 64, 256),
            space(pieces, 2, 2, 64, 256),
            space(pieces, 2, 128, 256),
            space(pieces, 128, 256),
            space(3, width, tok),
            space(tok, width),
            space(tok, width, kind=f32),
            space(1, width, kind=f32),
            space(1, width, kind=f32),
            space(1, width, kind=f32),
            space(1, hidden_width, kind=f32),
            space(1, width, kind=f32),
            space(1, width, kind=f32),
            space(1, tok, kind=jnp.int32),
            space(devices, share + share // 2, 128),
            space(8, width, kind=f32),
            space(devices, 8, 128, kind=f32),
            dma((15,)),
            dma((2,)),
            dma((3, 4)),
            dma((2,)),
            dma,
            dma,
            dma,
            dma,
            dma,
            dma,
            dma,
            dma,
            dma,
            dma((pieces + 8,)),
            dma((pieces, 8)),
        ]
        + [dma((3,))] * 3
    )
    return pl.pallas_call(
        functools.partial(tail_kernel, n, tok),
        out_shape=(
            out(tok, width, kind=bf16),
            out(tok, width, kind=bf16),
            out(pieces, 128, 256),
            out(devices, share + share // 2, 128, kind=bf16),
            out(devices, 8, 128),
            out(devices, 8, 128),
        ),
        in_specs=[any_spec] * 22,
        out_specs=[vmem] * 6,
        scratch_shapes=scratch,
        compiler_params=pltpu.CompilerParams(
            collective_id=1, has_side_effects=True, vmem_limit_bytes=63 << 20
        ),
        name="tail",
    )(*arrays)


def finish_kernel(n, *refs):
    block_in, tokens_in, total, pack_got, small_got, early_got = refs[:6]
    block_out, tokens_out, query_out, key_out, value_out, out_out, up_out, down_out = refs[6:14]
    vectors, up_vector = refs[14:22], refs[22]
    block_out[...] = block_in[...]
    tokens_out[...] = tokens_in[...]
    mine = lax.axis_index("scene") * n + lax.axis_index("seq")
    share = query_out.shape[0]
    for head in range(0, n, 2):
        pair = [
            pack_got[head + i].astype(f32) + pack_got[n + head + i].astype(f32) for i in range(2)
        ]
        columns = slice(head * HEAD_DIM, head * HEAD_DIM + 2 * HEAD_DIM)

        def joined(first, last, start):
            return jnp.concatenate(
                [part[first:last, start : start + HEAD_DIM] for part in pair], axis=1
            )

        query_out[:, columns] = joined(0, share, 0)
        key_out[:, columns] = joined(0, share, HEAD_DIM)
        value_out[: share // 2, columns] = joined(share, share + share // 2, 0)
        value_out[share // 2 :, columns] = joined(share, share + share // 2, HEAD_DIM)
    for i in range(4):
        down_out[:, 256 * i : 256 * i + 256] = total[i]
        out_out[:, 256 * i : 256 * i + 256] = total[8, 32 * i : 32 * i + 32, :]
    for i in range(16):
        up_out[:, 256 * i : 256 * i + 256] = total[4 + i // 4, 32 * (i % 4) : 32 * (i % 4) + 32, :]
    turn = lax.rem(128 - 32 * lax.rem(mine, 4), 128)
    late = pltpu.roll(jnp.sum(small_got[...], axis=0), turn, 1)
    early = jnp.sum(early_got[...], axis=0)
    up_vector[...] = early[4]
    early = pltpu.roll(early, turn, 1)
    for i in range(4):
        vectors[i][...] = late[i, :share]
        vectors[4 + i][...] = early[i, :share]


def finish(n, block_rows, tokens_grad, total, pack_got, small_got, early_got):
    tok, width = tokens_grad.shape
    devices = 2 * n
    share = width // devices
    vmem = pl.BlockSpec(memory_space=pltpu.VMEM)

    def out(*shape):
        return jax.ShapeDtypeStruct(shape, f32)

    return pl.pallas_call(
        functools.partial(finish_kernel, n),
        out_shape=(
            jax.ShapeDtypeStruct((tok, width), bf16),
            jax.ShapeDtypeStruct((tok, width), bf16),
            out(share, width),
            out(share, width),
            out(share, width),
            out(share, width),
            out(share, 4 * width),
            out(4 * share, width),
        )
        + (out(share),) * 8
        + (out(4 * share),),
        in_specs=[vmem] * 6,
        out_specs=[vmem] * 17,
        compiler_params=pltpu.CompilerParams(vmem_limit_bytes=60 << 20),
        name="finish",
    )(block_rows, tokens_grad, total, pack_got, small_got, early_got)


def gelu_both(values):
    cubic = gelu_coef * (values + 0.044715 * values * values * values)
    bend = jnp.tanh(cubic)
    slope = gelu_coef * (1.0 + 3.0 * 0.044715 * values * values)
    grad = 0.5 * (1.0 + bend) + 0.5 * values * (1.0 - bend * bend) * slope
    return 0.5 * values * (1.0 + bend), grad


def layer_on_device(
    scenes,
    n,
    tokens,
    surface_mask,
    out_grad,
    w_query,
    w_key,
    w_value,
    w_out,
    w_up,
    w_down,
    b_query,
    b_value,
    b_out,
    b_up,
    b_down,
    gain_one,
    shift_one,
    gain_two,
    shift_two,
):
    _, tok, width = tokens.shape
    att_t, normed_all, q_all, k_all, v_all, o_all, lse_all = attention_forward(
        n, tokens[0], gain_one, shift_one, w_query, w_key, w_value, b_query, b_value
    )

    arrived = tail(
        n,
        tok,
        width,
        w_up.shape[1],
        q_all,
        k_all,
        v_all,
        o_all,
        lse_all,
        out_grad[0],
        att_t,
        normed_all,
        w_down,
        w_up,
        w_out,
        *(w.reshape(2, 2, 2, 128, width) for w in (w_query, w_key, w_value)),
        tokens[0],
        gain_one[None],
        gain_two[None],
        b_down[None],
        b_up[None],
        b_out[None],
        shift_two[None],
        surface_mask,
    )
    block_out, tokens_grad, *sums = finish(n, *arrived)
    bquery, bvalue, gone, sone, bout, bdown, gtwo, stwo, bup = sums[6:]
    return (
        block_out[None],
        tokens_grad[None],
        *sums[:6],
        bquery,
        bvalue,
        bout,
        bup,
        bdown,
        gone,
        sone,
        gtwo,
        stwo,
    )


def norm_rows(values, gain, shift):
    row_mean = jnp.mean(values, axis=-1, keepdims=True)
    centred = values - row_mean
    row_var = jnp.mean(centred * centred, axis=-1, keepdims=True)
    return centred * lax.rsqrt(row_var + norm_eps) * gain + shift


def gelu_tanh(values):
    return (
        0.5 * values * (1.0 + jnp.tanh(gelu_coef * (values + 0.044715 * values * values * values)))
    )


def take_pair(array_in, pair_index):
    pair_width = 2 * HEAD_DIM
    sliced = lax.dynamic_slice_in_dim(array_in, pair_index * pair_width, pair_width, 2)
    return sliced.reshape(sliced.shape[:2] + (2, HEAD_DIM))


def take_stats(array_in, pair_index):
    return lax.dynamic_slice_in_dim(array_in, pair_index * 2, 2, 1)


def join_pairs(stacked):
    moved = jnp.moveaxis(stacked, 0, 2)
    return moved.reshape(moved.shape[:2] + (moved.shape[2] * moved.shape[3],))


def join_stats(stacked):
    moved = jnp.moveaxis(stacked, 0, 1)
    return moved.reshape((moved.shape[0], moved.shape[1] * moved.shape[2], moved.shape[3]))


def merge_heads(pair_part):
    return pair_part.reshape(pair_part.shape[:2] + (2 * HEAD_DIM,))


def attend(q_scene, k_gathered, v_gathered):

    def attend_pair_step(unused, pair_index):
        q_pair = take_pair(q_scene, pair_index)
        k_pair = take_pair(k_gathered, pair_index)
        v_pair = take_pair(v_gathered, pair_index)
        scores = (
            jnp.einsum("sqhe,skhe->shqk", q_pair, k_pair, preferred_element_type=jnp.float32)
            * score_scale
        )
        row_max = jnp.max(scores, axis=-1, keepdims=True)
        shifted = jnp.exp(scores - row_max)
        row_sum = jnp.sum(shifted, axis=-1, keepdims=True)
        prob_low = (shifted / row_sum).astype(jnp.bfloat16)
        pair_out = jnp.einsum(
            "shqk,skhe->sqhe", prob_low, v_pair, preferred_element_type=jnp.float32
        )
        pair_lse = (row_max + jnp.log(row_sum))[..., 0]
        return (unused, (merge_heads(pair_out), pair_lse))

    pair_count = HEADS // 2
    _, (pair_outs, pair_lses) = lax.scan(
        attend_pair_step, jnp.zeros((), jnp.float32), jnp.arange(pair_count, dtype=jnp.int32)
    )
    return (join_pairs(pair_outs), join_stats(pair_lses))


def query_side(q_scene, k_gathered, v_gathered, row_lse, att_grad):

    def query_pair_step(unused, pair_index):
        q_pair = take_pair(q_scene, pair_index)
        k_pair = take_pair(k_gathered, pair_index)
        v_pair = take_pair(v_gathered, pair_index)
        d_pair = take_pair(att_grad, pair_index)
        l_pair = take_stats(row_lse, pair_index)
        scores = (
            jnp.einsum("sqhe,skhe->shqk", q_pair, k_pair, preferred_element_type=jnp.float32)
            * score_scale
        )
        attn_prob = jnp.exp(scores - l_pair[..., None])
        dprob = jnp.einsum("sqhe,skhe->shqk", d_pair, v_pair, preferred_element_type=jnp.float32)
        row_delta = jnp.sum(attn_prob * dprob, axis=-1)
        dscore = (attn_prob * (dprob - row_delta[..., None])).astype(jnp.bfloat16)
        q_part = (
            jnp.einsum("shqk,skhe->sqhe", dscore, k_pair, preferred_element_type=jnp.float32)
            * score_scale
        )
        results = (merge_heads(q_part), row_delta)
        prob_low = attn_prob.astype(jnp.bfloat16)
        k_part = (
            jnp.einsum("shqk,sqhe->skhe", dscore, q_pair, preferred_element_type=jnp.float32)
            * score_scale
        )
        v_part = jnp.einsum("shqk,sqhe->skhe", prob_low, d_pair, preferred_element_type=jnp.float32)
        results = results + (merge_heads(k_part), merge_heads(v_part))
        return (unused, results)

    pair_count = HEADS // 2
    _, results = lax.scan(
        query_pair_step, jnp.zeros((), jnp.float32), jnp.arange(pair_count, dtype=jnp.int32)
    )
    return results


def on_any_device(
    tokens,
    surface_mask,
    out_grad,
    w_query,
    w_key,
    w_value,
    w_out,
    w_up,
    w_down,
    b_query,
    b_value,
    b_out,
    b_up,
    b_down,
    gain_one,
    shift_one,
    gain_two,
    shift_two,
):
    scenes, local_len, model_width = tokens.shape
    row_count = scenes * local_len
    flat_rows = tokens.astype(jnp.float32).reshape(row_count, model_width)
    normed, norm_one_pull = jax.vjp(norm_rows, flat_rows, gain_one, shift_one)
    normed_low = normed.astype(jnp.bfloat16)
    q_low = (matmul(normed_low, w_query) + b_query).astype(jnp.bfloat16)
    k_low = matmul(normed_low, w_key).astype(jnp.bfloat16)
    v_low = (matmul(normed_low, w_value) + b_value).astype(jnp.bfloat16)
    q_scene = q_low.reshape(scenes, local_len, model_width)
    k_scene = k_low.reshape(scenes, local_len, model_width)
    v_scene = v_low.reshape(scenes, local_len, model_width)
    k_gathered, v_gathered = (
        lax.all_gather(k_scene, "seq", axis=1, tiled=True),
        lax.all_gather(v_scene, "seq", axis=1, tiled=True),
    )
    attended, row_lse = attend(q_scene, k_gathered, v_gathered)
    att_low = attended.reshape(row_count, model_width).astype(jnp.bfloat16)
    residual = flat_rows + matmul(att_low, w_out) + b_out
    normed_two, norm_two_pull = jax.vjp(norm_rows, residual, gain_two, shift_two)
    normed_two_low = normed_two.astype(jnp.bfloat16)
    hidden = matmul(normed_two_low, w_up) + b_up
    activated, gelu_pull = jax.vjp(gelu_tanh, hidden)
    act_low = activated.astype(jnp.bfloat16)
    block_rows = residual + matmul(act_low, w_down) + b_down
    block_out = block_rows.reshape(scenes, local_len, model_width).astype(jnp.bfloat16)
    masked_f = out_grad.astype(jnp.float32) * surface_mask.astype(jnp.float32)[..., None]
    masked_rows = masked_f.reshape(row_count, model_width)
    masked_low = masked_rows.astype(jnp.bfloat16)
    grad_down = matmul_tn(act_low, masked_low)
    grad_bdown = jnp.sum(masked_rows, axis=0)
    act_grad = matmul_nt(masked_low, w_down)
    hidden_low = gelu_pull(act_grad)[0].astype(jnp.bfloat16)
    grad_up = matmul_tn(normed_two_low, hidden_low)
    grad_bup = jnp.sum(hidden_low.astype(jnp.float32), axis=0)
    norm_two_in = matmul_nt(hidden_low, w_up)
    resid_part, grad_gain_two, grad_shift_two = norm_two_pull(norm_two_in)
    resid_grad = masked_rows + resid_part
    resid_low = resid_grad.astype(jnp.bfloat16)
    grad_out = matmul_tn(att_low, resid_low)
    grad_bout = jnp.sum(resid_low.astype(jnp.float32), axis=0)
    att_grad = (
        matmul_nt(resid_low, w_out).astype(jnp.bfloat16).reshape(scenes, local_len, model_width)
    )
    q_parts, delta_parts, k_parts, v_parts = query_side(
        q_scene, k_gathered, v_gathered, row_lse, att_grad
    )
    k_summed, v_summed = (
        lax.psum_scatter(
            k_parts.astype(jnp.bfloat16), "seq", scatter_dimension=2, tiled=True
        ).astype(jnp.float32),
        lax.psum_scatter(
            v_parts.astype(jnp.bfloat16), "seq", scatter_dimension=2, tiled=True
        ).astype(jnp.float32),
    )
    k_grad = join_pairs(k_summed)
    v_grad = join_pairs(v_summed)
    q_grad = join_pairs(q_parts)
    q_grad_low = q_grad.reshape(row_count, model_width).astype(jnp.bfloat16)
    k_grad_low = k_grad.reshape(row_count, model_width).astype(jnp.bfloat16)
    v_grad_low = v_grad.reshape(row_count, model_width).astype(jnp.bfloat16)
    grad_query = matmul_tn(normed_low, q_grad_low)
    grad_key = matmul_tn(normed_low, k_grad_low)
    grad_value = matmul_tn(normed_low, v_grad_low)
    grad_bquery = jnp.sum(q_grad_low.astype(jnp.float32), axis=0)
    grad_bvalue = jnp.sum(v_grad_low.astype(jnp.float32), axis=0)
    norm_one_in = (
        matmul_nt(q_grad_low, w_query)
        + matmul_nt(k_grad_low, w_key)
        + matmul_nt(v_grad_low, w_value)
    )
    token_part, grad_gain_one, grad_shift_one = norm_one_pull(norm_one_in)
    tokens_grad = (
        (resid_grad + token_part).reshape(scenes, local_len, model_width).astype(jnp.bfloat16)
    )
    (
        sum_query,
        sum_key,
        sum_value,
        sum_out,
        sum_bquery,
        sum_bvalue,
        sum_bout,
        sum_gain_one,
        sum_shift_one,
        sum_up,
        sum_down,
        sum_bup,
        sum_bdown,
        sum_gain_two,
        sum_shift_two,
    ) = (
        lax.psum_scatter(grad_query, ("scene", "seq"), scatter_dimension=0, tiled=True),
        lax.psum_scatter(grad_key, ("scene", "seq"), scatter_dimension=0, tiled=True),
        lax.psum_scatter(grad_value, ("scene", "seq"), scatter_dimension=0, tiled=True),
        lax.psum_scatter(grad_out, ("scene", "seq"), scatter_dimension=0, tiled=True),
        lax.psum_scatter(grad_bquery, ("scene", "seq"), scatter_dimension=0, tiled=True),
        lax.psum_scatter(grad_bvalue, ("scene", "seq"), scatter_dimension=0, tiled=True),
        lax.psum_scatter(grad_bout, ("scene", "seq"), scatter_dimension=0, tiled=True),
        lax.psum_scatter(grad_gain_one, ("scene", "seq"), scatter_dimension=0, tiled=True),
        lax.psum_scatter(grad_shift_one, ("scene", "seq"), scatter_dimension=0, tiled=True),
        lax.psum_scatter(grad_up, ("scene", "seq"), scatter_dimension=0, tiled=True),
        lax.psum_scatter(grad_down, ("scene", "seq"), scatter_dimension=0, tiled=True),
        lax.psum_scatter(grad_bup, ("scene", "seq"), scatter_dimension=0, tiled=True),
        lax.psum_scatter(grad_bdown, ("scene", "seq"), scatter_dimension=0, tiled=True),
        lax.psum_scatter(grad_gain_two, ("scene", "seq"), scatter_dimension=0, tiled=True),
        lax.psum_scatter(grad_shift_two, ("scene", "seq"), scatter_dimension=0, tiled=True),
    )
    return (
        block_out,
        tokens_grad,
        sum_query,
        sum_key,
        sum_value,
        sum_out,
        sum_up,
        sum_down,
        sum_bquery,
        sum_bvalue,
        sum_bout,
        sum_bup,
        sum_bdown,
        sum_gain_one,
        sum_shift_one,
        sum_gain_two,
        sum_shift_two,
    )


def solution(mesh):
    placed = (
        P("scene", "seq", None),
        P("scene", "seq"),
        P("scene", "seq", None),
        P(),
        P(),
        P(),
        P(),
        P(),
        P(),
        P(),
        P(),
        P(),
        P(),
        P(),
        P(),
        P(),
        P(),
        P(),
    )
    scenes, n = mesh.shape["scene"], mesh.shape["seq"]
    if (scenes, n) == (2, HEADS):
        on_device = functools.partial(layer_on_device, scenes, n)
    else:
        on_device = on_any_device
    return jax.shard_map(
        on_device,
        mesh=mesh,
        in_specs=placed,
        out_specs=(
            P("scene", "seq", None),
            P("scene", "seq", None),
            P(("scene", "seq"), None),
            P(("scene", "seq"), None),
            P(("scene", "seq"), None),
            P(("scene", "seq"), None),
            P(("scene", "seq"), None),
            P(("scene", "seq"), None),
            P(("scene", "seq")),
            P(("scene", "seq")),
            P(("scene", "seq")),
            P(("scene", "seq")),
            P(("scene", "seq")),
            P(("scene", "seq")),
            P(("scene", "seq")),
            P(("scene", "seq")),
            P(("scene", "seq")),
        ),
        check_vma=False,
    )
```
